32 devices in a mesh: fsdp: 32 (over z, y, x, core).
Axes of the slice: x: 2, y: 2, z: 4, core: 2. Of those that a mesh axis runs over, the one named last changes fastest.
Arguments:
- token_ids: int32 [16384], P('fsdp'), may hold values from 0 to 31999, as said below
- loss_rows: int32 [2048], P('fsdp'), may hold values from 256 to 511, as said below
- targets: int32 [2048], P('fsdp'), may hold values from 0 to 31999
- flat_master: float32 [9833280], P('fsdp'), may hold values from -3 to 3
- flat_m: float32 [9833280], P('fsdp'), may hold values from -1 to 1
- flat_v: float32 [9833280], P('fsdp'), may hold values from 0 to 1
- table_master: float32 [32000, 960], P('fsdp'), may hold values from -2 to 2
- table_m: float32 [32000, 960], P('fsdp'), may hold values from -1 to 1
- table_v: float32 [32000, 960], P('fsdp'), may hold values from 0 to 1
Outputs:
- loss: float32 [], replicated
- grad_norm: float32 [], replicated
- flat_m_new: float32 [9833280], P('fsdp')
- flat_v_new: float32 [9833280], P('fsdp')
- flat_update: float32 [9833280], P('fsdp')
- table_m_new: float32 [32000, 960], P('fsdp')
- table_v_new: float32 [32000, 960], P('fsdp')
- table_update: float32 [32000, 960], P('fsdp')
The draws below stay inside these ranges and needn't reach their ends.
Inputs may be any that keep to these rules, and one draw needn't show every extreme that they name: `token_ids`: the owner of an id is id // 1000. Among the 512 tokens of one group no owner is named more than 32 times, and in every draw one owner is named exactly 32 times by every group. `loss_rows`: the 64 entries of one group are distinct indices into that group's own tokens, all in its continuations.
All inputs are finite; a program needn't handle non-finite values.
Results may differ from the reference program's by a relative error of at most 0.0051.
The reference program's roundings to bfloat16 on the way count: a program that leaves them out, or rounds other values in their place, can miss the bound.
Values may be sent and summed in bfloat16 or wider, within the bound.
No kernel may reach another device: no remote copies, remote signals or barrier semaphores. Data moves between devices by JAX's collectives and lax.ppermute only.
A program may use at most 256 MiB of HBM per device.

```python
import math
import jax
import jax.numpy as jnp
from jax import lax

D = 960
QUERY_HEADS = 15
KEY_VALUE_HEADS = 5
HEAD_SIZE = 64
FF = 2560
V = 32000
PL = 256
NC = 2
CL = 128
LOSS_DEV = 64
STEP = 10
QKV = 1600
GROUP_TOKENS = 512
GROUPS = 32
TOKENS = 16384
LOSS_TOTAL = 2048
VOCAB_DEV = 1000
CAP = 32
FLAT = 9833280


def draw_token_ids(key, part):
    groups = TOKENS // GROUP_TOKENS
    slot_count = groups * CAP
    key_full, key_order, key_offset = jax.random.split(key, 3)
    full_owner = jax.random.randint(key_full, (), 0, groups)
    labels = jnp.arange(slot_count, dtype=jnp.int32)
    label_owner = labels // CAP

    def one_device(device_key):
        key_rank, key_mix = jax.random.split(device_key)
        rank_order = jax.random.permutation(key_rank, slot_count).astype(jnp.int32)
        priority = jnp.where(label_owner == full_owner, labels - 2 * slot_count, rank_order)
        chosen = jnp.argsort(priority)[:GROUP_TOKENS]
        owners = label_owner[chosen]
        return owners[jax.random.permutation(key_mix, GROUP_TOKENS)]
    owners = jax.vmap(one_device)(jax.random.split(key_order, groups))
    offsets = jax.random.randint(key_offset, (groups, GROUP_TOKENS), 0, VOCAB_DEV)
    return (owners * VOCAB_DEV + offsets).reshape(TOKENS).astype(jnp.int32)


def draw_loss_rows(key, part):
    groups = LOSS_TOTAL // LOSS_DEV

    def one_device(device_key):
        order_list = jax.random.permutation(device_key, NC * CL).astype(jnp.int32)
        return order_list[:LOSS_DEV] + PL
    return jax.vmap(one_device)(jax.random.split(key, groups)).reshape(LOSS_TOTAL).astype(jnp.int32)


def draw_flat_master(key, part):
    position = jnp.arange(FLAT, dtype=jnp.int32)
    edge_gain = 3 * D
    edge_qkv = edge_gain + D * QKV
    edge_out = edge_qkv + QUERY_HEADS * HEAD_SIZE * D
    edge_gu = edge_out + 2 * D * FF
    edge_down = edge_gu + FF * D
    scale = jnp.full((FLAT,), 0.02, jnp.float32)
    scale = jnp.where(position < edge_qkv, D ** (-0.5), scale)
    scale = jnp.where((position >= edge_qkv) & (position < edge_out), ((PL + CL) / (3.0 * QUERY_HEADS * HEAD_SIZE)) ** 0.5, scale)
    scale = jnp.where((position >= edge_out) & (position < edge_gu), D ** (-0.5), scale)
    scale = jnp.where((position >= edge_gu) & (position < edge_down), 1.7 * FF ** (-0.5), scale)
    key_noise, key_gain = jax.random.split(key)
    noise = jax.random.truncated_normal(key_noise, -4.0, 4.0, (FLAT,), jnp.float32)
    gain_values = jax.random.uniform(key_gain, (FLAT,), jnp.float32, 0.5, 1.5)
    value_rows = jnp.where(position < edge_gain, gain_values, noise * scale)
    return value_rows.astype(jnp.float32)


def draw_table_master(key, part):
    key_noise, key_level, key_sign = jax.random.split(jax.random.fold_in(key, 15), 3)
    shard_count = V // VOCAB_DEV
    base_scale = (D // 4) ** (-0.5)
    noise = jax.random.truncated_normal(key_noise, -4.0, 4.0, (V, D), jnp.float32) * base_scale
    ramp = jnp.arange(shard_count, dtype=jnp.int32).astype(jnp.float32) / max(shard_count - 1, 1)
    jitter = jax.random.uniform(key_level, (shard_count,), jnp.float32, -0.1, 0.1)
    levels = jnp.exp(math.log(0.4) + ramp * (math.log(4.0) - math.log(0.4)) + jitter)
    signs = (2 * jax.random.randint(key_sign, (D,), 0, 2) - 1).astype(jnp.float32) * D ** (-0.5)
    shard_of_row = jnp.arange(V, dtype=jnp.int32) // VOCAB_DEV
    common = levels[shard_of_row][:, None] * 0.6 * signs[None, :]
    return (noise + common).astype(jnp.float32)


def moment_base():
    return 25.0 / math.sqrt(LOSS_TOTAL * (FLAT + V * D))


def first_moment(key, shape):
    scale = 0.11 * moment_base()
    value_rows = jax.random.truncated_normal(key, -4.0, 4.0, shape, jnp.float32) * scale
    return value_rows.astype(jnp.float32)


def second_moment(key, shape, low_factor, high_factor):
    base_sq = moment_base() * moment_base()
    lower = low_factor * base_sq
    upper = high_factor * base_sq
    value_rows = jnp.exp(jax.random.uniform(key, shape, jnp.float32, math.log(lower), math.log(upper)))
    return value_rows.astype(jnp.float32)


def draw_flat_m(key, part):
    return first_moment(jax.random.fold_in(key, 11), (FLAT,))


def draw_flat_v(key, part):
    return second_moment(jax.random.fold_in(key, 12), (FLAT,), 0.15, 15.0)


def draw_table_m(key, part):
    return first_moment(jax.random.fold_in(key, 13), (V, D))


def draw_table_v(key, part):
    return second_moment(jax.random.fold_in(key, 14), (V, D), 0.005, 0.5)


def set_ends(result, own_key, low, top_value):
    longest = result.shape.index(max(result.shape))
    spots = []
    for shift in (0, 1):
        where = [jax.random.randint(jax.random.fold_in(own_key, axis), (), 0, length) for axis, length in enumerate(result.shape)]
        where[longest] = (where[longest] + shift) % result.shape[longest]
        spots.append(tuple(where))
    return result.at[spots[0]].set(low).at[spots[1]].set(top_value)


def setup_inputs(seed: int = 0) -> dict:
    keys = jax.random.split(jax.random.key(seed), 10)
    token_ids = draw_token_ids(jax.random.fold_in(keys[9], 71), 0)
    loss_rows = draw_loss_rows(jax.random.fold_in(keys[9], 71), 0)
    targets = set_ends(jax.random.randint(keys[2], (LOSS_TOTAL,), 0, V), jax.random.fold_in(keys[2], 1), 0, V - 1).astype(jnp.int32)
    flat_master = draw_flat_master(jax.random.fold_in(keys[9], 71), 0)
    flat_m = draw_flat_m(jax.random.fold_in(keys[9], 71), 0)
    flat_v = draw_flat_v(jax.random.fold_in(keys[9], 71), 0)
    table_master = draw_table_master(jax.random.fold_in(keys[9], 71), 0)
    table_m = draw_table_m(jax.random.fold_in(keys[9], 71), 0)
    table_v = draw_table_v(jax.random.fold_in(keys[9], 71), 0)
    return dict(token_ids=token_ids, loss_rows=loss_rows, targets=targets, flat_master=flat_master, flat_m=flat_m, flat_v=flat_v, table_master=table_master, table_m=table_m, table_v=table_v)


@jax.custom_vjp
def reduced_precision(v):
    return lax.optimization_barrier(v.astype(jnp.bfloat16)).astype(jnp.float32)

@jax.custom_vjp
def low_back(v):
    return v

def low_keep(v):
    return (reduced_precision(v), None)

def low_pass(kept, grad):
    return (grad,)

def back_keep(v):
    return (v, None)

def back_low(kept, grad):
    return (reduced_precision(grad),)
reduced_precision.defvjp(low_keep, low_pass)
low_back.defvjp(back_keep, back_low)
EPS = 1e-05
SMOOTH = 0.1
ZCOEF = 0.0001
BETA1 = 0.9
BETA2 = 0.95
ADAM_EPS = 1e-08
DECAY = 0.1
RATE = 0.03
CLIP_C = 25.0
NEGATIVE = -1e+30
HIGH = lax.Precision.HIGHEST

def matmul_high(left, right):
    return jnp.dot(left, right, precision=HIGH, preferred_element_type=jnp.float32)

def norm_gain(value_rows, gain):
    return value_rows * lax.rsqrt(lax.optimization_barrier(jnp.mean(value_rows * value_rows, axis=-1, keepdims=True)) + EPS) * gain

def rotate_head_pairs(value_rows, cosine_table, sine_table):
    half_dim = value_rows.shape[-1] // 2
    turned = jnp.concatenate([-value_rows[..., half_dim:], value_rows[..., :half_dim]], axis=-1)
    return value_rows * cosine_table[:, None, :] + turned * sine_table[:, None, :]

def rope_tables(count, head_dim):
    index_row = jnp.arange(count, dtype=jnp.int32)
    position = jnp.where(index_row < PL, index_row, PL + (index_row - PL) % CL).astype(jnp.float32)
    freqs = 10000.0 ** (-(jnp.arange(head_dim // 2, dtype=jnp.int32).astype(jnp.float32) * 2.0 / head_dim))
    angles = position[:, None] * freqs[None, :]
    angles = jnp.concatenate([angles, angles], axis=-1)
    return (jnp.cos(angles), jnp.sin(angles))

def allowed_mask(query_rows, count):
    query_pos = query_rows[:, None]
    key_pos = jnp.arange(count, dtype=jnp.int32)[None, :]
    query_seg = jnp.where(query_pos < PL, 0, 1 + (query_pos - PL) // CL)
    key_seg = jnp.where(key_pos < PL, 0, 1 + (key_pos - PL) // CL)
    return (key_pos <= query_pos) & ((key_seg == 0) | (key_seg == query_seg))

def unpack(flat):
    edge_qkv = 3 * D
    edge_out = edge_qkv + D * QKV
    edge_gu = edge_out + QUERY_HEADS * HEAD_SIZE * D
    edge_down = edge_gu + 2 * D * FF
    edge_end = edge_down + FF * D
    gains = flat[:edge_qkv].reshape(3, D)
    w_qkv = flat[edge_qkv:edge_out].reshape(D, QKV)
    w_out = flat[edge_out:edge_gu].reshape(QUERY_HEADS * HEAD_SIZE, D)
    w_gu = flat[edge_gu:edge_down].reshape(D, 2 * FF)
    w_down = flat[edge_down:edge_end].reshape(FF, D)
    return (gains, w_qkv, w_out, w_gu, w_down)

def gated_unit(gate_up):
    gate = gate_up[:, :FF]
    return gate * jax.nn.sigmoid(gate) * gate_up[:, FF:]

def group_loss(params, table_low, group_ids, group_rows, group_targets):
    gains, w_qkv, w_out, w_gu, w_down = params
    query_groups = QUERY_HEADS // KEY_VALUE_HEADS
    x_embed = table_low[group_ids] * (math.sqrt(D) * 0.5)
    h_attn = reduced_precision(norm_gain(x_embed, gains[0]))
    query_key_value = low_back(matmul_high(h_attn, w_qkv))
    cosine_table, sine_table = rope_tables(GROUP_TOKENS, HEAD_SIZE)
    query_matrix = reduced_precision(rotate_head_pairs(query_key_value[:, :QUERY_HEADS * HEAD_SIZE].reshape(GROUP_TOKENS, QUERY_HEADS, HEAD_SIZE), cosine_table, sine_table))
    key_rows = reduced_precision(rotate_head_pairs(query_key_value[:, QUERY_HEADS * HEAD_SIZE:(QUERY_HEADS + KEY_VALUE_HEADS) * HEAD_SIZE].reshape(GROUP_TOKENS, KEY_VALUE_HEADS, HEAD_SIZE), cosine_table, sine_table))
    value_rows = reduced_precision(query_key_value[:, (QUERY_HEADS + KEY_VALUE_HEADS) * HEAD_SIZE:].reshape(GROUP_TOKENS, KEY_VALUE_HEADS, HEAD_SIZE))
    query_matrix = query_matrix.reshape(GROUP_TOKENS, KEY_VALUE_HEADS, query_groups, HEAD_SIZE)
    scores = low_back(jnp.einsum('qhgd,khd->hgqk', query_matrix, key_rows, precision=HIGH) * HEAD_SIZE ** (-0.5))
    allowed = allowed_mask(jnp.arange(GROUP_TOKENS, dtype=jnp.int32), GROUP_TOKENS)
    scores = jnp.where(allowed[None, None], scores, NEGATIVE)
    row_peak = lax.optimization_barrier(jnp.max(scores, axis=-1, keepdims=True))
    exp_scores = jnp.exp(scores - row_peak)
    probs = exp_scores / lax.optimization_barrier(jnp.sum(exp_scores, axis=-1, keepdims=True))
    mixed = jnp.einsum('hgqk,khd->qhgd', reduced_precision(probs), value_rows, precision=HIGH).reshape(GROUP_TOKENS, QUERY_HEADS * HEAD_SIZE)
    attended = reduced_precision(low_back(mixed))
    x_one = x_embed + low_back(matmul_high(attended, w_out))
    h_mlp = reduced_precision(norm_gain(x_one, gains[1]))
    gate_up = low_back(matmul_high(h_mlp, w_gu))
    act = reduced_precision(gated_unit(gate_up))
    x_two = x_one + low_back(matmul_high(act, w_down))
    hidden = reduced_precision(norm_gain(x_two[group_rows], gains[2]))
    logits = low_back(matmul_high(hidden, table_low.T))
    top_logit = lax.optimization_barrier(jnp.max(logits, axis=-1, keepdims=True))
    log_total = (top_logit + jnp.log(lax.optimization_barrier(jnp.sum(jnp.exp(logits - top_logit), axis=-1, keepdims=True))))[:, 0]
    target_logit = jnp.take_along_axis(logits, group_targets[:, None], axis=1)[:, 0]
    mean_logit = lax.optimization_barrier(jnp.mean(logits, axis=-1))
    row_loss = log_total - (1.0 - SMOOTH) * target_logit - SMOOTH * mean_logit + ZCOEF * log_total * log_total
    return jnp.sum(row_loss)

def total_loss(flat, table, token_ids, loss_rows, targets):
    params = unpack(reduced_precision(flat))
    table_low = reduced_precision(table)
    group_ids = token_ids.reshape(GROUPS, GROUP_TOKENS)
    group_rows = loss_rows.reshape(GROUPS, LOSS_DEV)
    group_targets = targets.reshape(GROUPS, LOSS_DEV)

    def scan_group(running, items):
        return (running + group_loss(params, table_low, items[0], items[1], items[2]), None)
    summed, _ = lax.scan(jax.checkpoint(scan_group), jnp.zeros((), jnp.float32), (group_ids, group_rows, group_targets))
    return summed / LOSS_TOTAL

def adamw_step(param, gradient, moment_one, moment_two, clip_factor):
    gradient = gradient * clip_factor
    new_one = BETA1 * moment_one + (1.0 - BETA1) * gradient
    new_two = BETA2 * moment_two + (1.0 - BETA2) * gradient * gradient
    ratio = new_one / (1.0 - BETA1 ** STEP) / (jnp.sqrt(new_two / (1.0 - BETA2 ** STEP)) + ADAM_EPS)
    return (new_one, new_two, -RATE * (ratio + DECAY * param))

def reference(token_ids, loss_rows, targets, flat_master, flat_m, flat_v, table_master, table_m, table_v):

    def loss_of(flat, table):
        return total_loss(flat, table, token_ids, loss_rows, targets)
    loss, pullback = jax.vjp(loss_of, flat_master, table_master)
    flat_grad, table_grad = pullback(jnp.ones((), jnp.float32))
    squares = jnp.sum(flat_grad * flat_grad) + jnp.sum(table_grad * table_grad)
    grad_norm = jnp.sqrt(squares)
    limit = CLIP_C / math.sqrt(LOSS_TOTAL)
    clip_factor = limit / jnp.maximum(grad_norm, limit)
    flat_one, flat_two, flat_update = adamw_step(flat_master, flat_grad, flat_m, flat_v, clip_factor)
    table_one, table_two, table_update = adamw_step(table_master, table_grad, table_m, table_v, clip_factor)
    return (loss, grad_norm, flat_one, flat_two, flat_update, table_one, table_two, table_update)
```

```python
import math

import jax
import jax.numpy as jnp
import numpy as np
from jax import lax
from jax.sharding import Mesh, PartitionSpec as P

D = 960
QUERY_HEADS = 15
KEY_VALUE_HEADS = 5
HEAD_SIZE = 64
FF = 2560
V = 32000
PL = 256
CL = 128
STEP = 10
QKV = 1600

EPS = 1e-05
SMOOTH = 0.1
ZCOEF = 0.0001
BETA1 = 0.9
BETA2 = 0.95
ADAM_EPS = 1e-08
DECAY = 0.1
RATE = 0.03
CLIP_C = 25.0
NEGATIVE = -1e30

UNIT = 320
GAINS = 3 * D
GAIN_UNITS = GAINS // UNIT
QKV_UNITS = D * QKV // UNIT
OUT_UNITS = D * D // UNIT
GU_UNITS = D * 2 * FF // UNIT
DOWN_UNITS = FF * D // UNIT
ALL_UNITS = QKV_UNITS + OUT_UNITS + GU_UNITS + DOWN_UNITS
PLANE = ("y", "x", "c")
ALL = ("q", "y", "x", "c")
SHARE = FF // 8

bf16 = jnp.bfloat16
f32 = jnp.float32


def dot(left, right, left_dim=1, right_dim=0):
    return lax.dot_general(
        left, right, (((left_dim,), (right_dim,)), ((), ())), preferred_element_type=f32
    )


def hot(index, count):
    return (index[:, None] == jnp.arange(count, dtype=jnp.int32)[None, :]).astype(bf16)


def scale_of(rows):
    return lax.rsqrt(jnp.mean(rows * rows, axis=-1, keepdims=True) + EPS)


def norm_back(rows, gain, grad):
    scale = scale_of(rows)
    normed = rows * scale
    grad_gain = jnp.sum(grad * normed, axis=0)
    scaled = grad * gain
    return scale * (scaled - normed * jnp.mean(scaled * normed, axis=-1, keepdims=True)), grad_gain


def flip(rows, axes, bits, size):
    return lax.ppermute(rows, axes, [(i, i ^ bits) for i in range(size)])


def rope_tables(count):
    row = np.arange(count)
    position = np.where(row < PL, row, PL + (row - PL) % CL).astype(np.float32)
    half = np.arange(HEAD_SIZE // 2, dtype=np.float32)
    freqs = np.float32(10000.0) ** (-(half * np.float32(2.0) / np.float32(HEAD_SIZE)))
    angles = (position[:, None] * freqs[None, :].astype(np.float32)).astype(np.float64)
    angles = np.concatenate([angles, angles], axis=-1)
    return np.cos(angles).astype(np.float32), np.sin(angles).astype(np.float32)


def rotate(rows, cosine, sine):
    heads = rows.reshape(rows.shape[0], -1, HEAD_SIZE)
    half = HEAD_SIZE // 2
    turned = jnp.concatenate([-heads[..., half:], heads[..., :half]], axis=-1)
    return (heads * cosine[:, None, :] + turned * sine[:, None, :]).reshape(rows.shape)


def rotate_back(grad, cosine, sine):
    heads = grad.reshape(grad.shape[0], -1, HEAD_SIZE)
    half = HEAD_SIZE // 2
    spun = heads * sine[:, None, :]
    turned = jnp.concatenate([spun[..., half:], -spun[..., :half]], axis=-1)
    return (heads * cosine[:, None, :] + turned).reshape(grad.shape)


def adamw_step(param, gradient, moment_one, moment_two, clip_factor):
    gradient = gradient * clip_factor
    new_one = BETA1 * moment_one + (1.0 - BETA1) * gradient
    new_two = BETA2 * moment_two + (1.0 - BETA2) * gradient * gradient
    ratio = new_one / (1.0 - BETA1**STEP) / (jnp.sqrt(new_two / (1.0 - BETA2**STEP)) + ADAM_EPS)
    return (new_one, new_two, -RATE * (ratio + DECAY * param))


def fold_plane(parts):
    got = flip(parts[1], "c", 1, 2)
    mine = parts[0].astype(f32) + got.astype(f32)
    low = mine.astype(parts[1].dtype)
    total = mine[0]
    for k in (1, 2, 3):
        total = total + flip(low[k], ("y", "x"), k, 4).astype(f32)
    return total


def spread_plane(rows):
    four = jnp.stack([rows] + [flip(rows, ("y", "x"), k, 4) for k in (1, 2, 3)])
    return jnp.stack([four, flip(four, "c", 1, 2)])


def local(
    token_ids, loss_rows, targets, flat_master, flat_m, flat_v, table_master, table_m, table_v
):
    devices = lax.axis_size(ALL)
    rows_q = lax.axis_size("q")
    me = lax.axis_index(ALL)
    q_index = lax.axis_index("q")
    p_index = lax.axis_index(PLANE)
    c_index = lax.axis_index("c")
    yx_index = lax.axis_index(("y", "x"))
    tokens = token_ids.shape[0]
    vocab_dev = table_master.shape[0]
    loss_dev = loss_rows.shape[0]
    loss_total = loss_dev * devices
    capacity = max(2, 2 * tokens // devices)
    slots = devices * capacity
    groups = QUERY_HEADS // KEY_VALUE_HEADS
    emb_mult = math.sqrt(D) * 0.5
    shard = flat_master.shape[0]
    units = ALL_UNITS // devices
    span = units * UNIT
    drift = shard - span
    aligned = devices == 32

    place = np.array([kq * 8 + kyx * 2 + kc for kc in range(2) for kyx in range(4) for kq in range(rows_q)])
    rank_of = np.argsort(place)
    source_of = me ^ jnp.asarray(place, jnp.int32)
    order_of = jnp.take(jnp.asarray(rank_of, jnp.int32), me ^ jnp.arange(devices, dtype=jnp.int32))

    flat_low = flat_master.astype(bf16)
    table_low = table_master.astype(bf16)
    ahead = lax.ppermute(flat_low[:GAINS], ALL, [(i + 1, i) for i in range(devices - 1)])
    back = max(0, drift * (devices - 1) - GAINS)
    pieces = [flat_low, ahead]
    if back:
        pieces = [lax.ppermute(flat_low[shard - back :], ALL, [(i, i + 1) for i in range(devices - 1)])] + pieces
    chunk = lax.dynamic_slice(jnp.concatenate(pieces), (back + GAINS - drift * me,), (span,)).reshape(units, UNIT)
    gain_rows = flat_low[:GAINS].reshape(GAIN_UNITS, UNIT)
    extra = jnp.concatenate([gain_rows, jnp.zeros((16 - GAIN_UNITS, UNIT), bf16)])
    if aligned:
        by_five = chunk.reshape(192, 5, UNIT).transpose(1, 0, 2).reshape(units, UNIT)
        by_three = chunk.reshape(320, 3, UNIT).transpose(1, 0, 2).reshape(units, UNIT)
        sent = chunk.reshape(60, 2, 8, UNIT).transpose(2, 1, 0, 3).reshape(8, 120, UNIT)
        got = lax.all_to_all(sent, PLANE, split_axis=0, concat_axis=0, tiled=True)
        by_share = got.reshape(8, 2, 60, UNIT).transpose(1, 0, 2, 3).reshape(units, UNIT)
        mixed = jnp.where((q_index == 0) & (p_index < 5), by_five, by_three)
        mixed = jnp.where((q_index == 1) | (q_index == 2), by_share, mixed)
        column = lax.all_gather(jnp.concatenate([mixed, extra]), "q")
        level = lax.all_gather(column[0], PLANE)
        gains = level[0, units : units + GAIN_UNITS].astype(f32).reshape(3, D)
        w_qkv = level[:5, :units].reshape(5, 5, 192, UNIT).transpose(1, 0, 2, 3).reshape(5, D, UNIT)
        w_out = level[5:, :units].reshape(3, 3, 320, UNIT).transpose(1, 0, 2, 3).reshape(3, D, UNIT)
        w_gate = jnp.concatenate([column[1, :480], column[2, :480]])
        w_up = jnp.concatenate([column[1, 480:units], column[2, 480:units]])
        w_down = column[3, :units].reshape(3, SHARE, UNIT)
    else:
        full = lax.all_gather(jnp.concatenate([chunk, extra]), ALL)
        gains = full[0, units : units + GAIN_UNITS].astype(f32).reshape(3, D)
        full = full[:, :units].reshape(ALL_UNITS, UNIT)
        edge = np.cumsum([QKV_UNITS, OUT_UNITS, GU_UNITS])
        w_qkv = full[: edge[0]].reshape(D, 5, UNIT).transpose(1, 0, 2)
        w_out = full[edge[0] : edge[1]].reshape(D, 3, UNIT).transpose(1, 0, 2)
        both = lax.dynamic_index_in_dim(full[edge[1] : edge[2]].reshape(D, 2, 8, UNIT), p_index, 2, False)
        w_gate, w_up = both[:, 0], both[:, 1]
        w_down = lax.dynamic_index_in_dim(full[edge[2] :].reshape(8, SHARE, 3, UNIT), p_index, 0, False).transpose(1, 0, 2)

    owner = token_ids // vocab_dev
    owner_hot = hot(owner, devices)
    before = (lax.broadcasted_iota(jnp.int32, (tokens, tokens), 0) > lax.broadcasted_iota(jnp.int32, (tokens, tokens), 1)).astype(bf16)
    slot = jnp.sum(dot(before, owner_hot) * owner_hot.astype(f32), axis=1).astype(jnp.int32)
    spot = hot(owner * capacity + slot, slots)
    marked = token_ids + 1
    halves = jnp.stack([marked // 256, marked % 256]).astype(bf16)
    found = dot(halves, spot).astype(jnp.int32)
    requests = (found[0] * 256 + found[1] - 1).reshape(devices, capacity)
    ask = jnp.concatenate([requests, jnp.broadcast_to(targets[None], (devices, loss_dev))], axis=1)
    asked = lax.all_to_all(ask, ALL, split_axis=0, concat_axis=0, tiled=True)
    row_hot = hot(asked[:, :capacity].reshape(-1) - me * vocab_dev, vocab_dev)
    answer = dot(row_hot, table_low).astype(bf16).reshape(devices, capacity, D)
    returned = lax.all_to_all(answer, ALL, split_axis=0, concat_axis=0, tiled=True).reshape(slots, D)
    x_low = dot(spot, returned).astype(bf16)
    x_embed = x_low.astype(f32) * emb_mult

    pick = hot(loss_rows, tokens)
    cosine, sine = (jnp.asarray(t) for t in rope_tables(tokens))
    cosine_pick, sine_pick = cosine[loss_rows], sine[loss_rows]
    h_attn = (x_embed * scale_of(x_embed) * gains[0]).astype(bf16)
    h_pick = dot(pick, h_attn).astype(bf16)
    x_pick = dot(pick, x_low) * emb_mult
    q_raw = jnp.concatenate([dot(h_pick, w_qkv[j]) for j in range(3)], axis=1)
    query = rotate(q_raw, cosine_pick, sine_pick).astype(bf16)
    key = rotate(dot(h_attn, w_qkv[3]), cosine, sine).astype(bf16)
    value = dot(h_attn, w_qkv[4]).astype(bf16)

    def heads_of(rows):
        return rows.reshape(loss_dev, KEY_VALUE_HEADS, groups, HEAD_SIZE).transpose(1, 2, 0, 3).reshape(KEY_VALUE_HEADS, groups * loss_dev, HEAD_SIZE)

    def heads_back(rows):
        return rows.reshape(KEY_VALUE_HEADS, groups, loss_dev, HEAD_SIZE).transpose(2, 0, 1, 3).reshape(loss_dev, D)

    query_h = heads_of(query)
    key_h = key.reshape(tokens, KEY_VALUE_HEADS, HEAD_SIZE).transpose(1, 0, 2)
    value_h = value.reshape(tokens, KEY_VALUE_HEADS, HEAD_SIZE).transpose(1, 0, 2)
    key_pos = jnp.arange(tokens, dtype=jnp.int32)[None, :]
    ask_pos = jnp.tile(loss_rows, groups)[:, None]
    key_seg = jnp.where(key_pos < PL, 0, 1 + (key_pos - PL) // CL)
    ask_seg = jnp.where(ask_pos < PL, 0, 1 + (ask_pos - PL) // CL)
    allowed = (key_pos <= ask_pos) & ((key_seg == 0) | (key_seg == ask_seg))
    scores = jnp.einsum("hqd,hkd->hqk", query_h, key_h, preferred_element_type=f32) * HEAD_SIZE**-0.5
    scores = jnp.where(allowed[None], scores, NEGATIVE)
    exp_scores = jnp.exp(scores - jnp.max(scores, axis=-1, keepdims=True))
    probs = exp_scores / jnp.sum(exp_scores, axis=-1, keepdims=True)
    probs_low = probs.astype(bf16)
    mixed_heads = jnp.einsum("hqk,hkd->hqd", probs_low, value_h, preferred_element_type=f32)
    attended = heads_back(mixed_heads.astype(bf16))
    x_one = x_pick + jnp.concatenate([dot(attended, w_out[j]) for j in range(3)], axis=1)

    h_mlp = (x_one * scale_of(x_one) * gains[1]).astype(bf16)
    plane_rows = 8 * loss_dev
    h_all = spread_plane(h_mlp).reshape(plane_rows, D)
    gate = dot(h_all, w_gate)
    up = dot(h_all, w_up)
    sig = jax.nn.sigmoid(gate)
    act = (gate * sig * up).astype(bf16)
    part = jnp.concatenate([dot(act, w_down[j]) for j in range(3)], axis=1)
    x_two = x_one + fold_plane(part.reshape(2, 4, loss_dev, D))

    hidden = (x_two * scale_of(x_two) * gains[2]).astype(bf16)
    across = jnp.stack([hidden] + [flip(hidden, "q", k, rows_q) for k in range(1, rows_q)])
    hidden_all = spread_plane(across).reshape(loss_total, D)
    logits = dot(hidden_all, table_low, 1, 1)
    targets_all = jnp.take(asked[:, capacity:], source_of, axis=0).reshape(loss_total)
    column_id = targets_all - me * vocab_dev
    hit = column_id[:, None] == jnp.arange(vocab_dev, dtype=jnp.int32)[None, :]
    local_peak = jnp.max(logits, axis=1)
    local_total = jnp.sum(jnp.exp(logits - local_peak[:, None]), axis=1)
    local_target = jnp.sum(jnp.where(hit, logits, 0.0), axis=1)
    local_sum = jnp.sum(logits, axis=1)
    stats = jnp.stack([local_peak, local_total, local_target, local_sum]).reshape(4, devices, loss_dev)
    stats = jnp.take(stats, order_of, axis=1).transpose(1, 0, 2)
    stats = lax.all_to_all(stats, ALL, split_axis=0, concat_axis=0, tiled=True)
    peak = jnp.max(stats[:, 0], axis=0)
    total = jnp.sum(stats[:, 1] * jnp.exp(stats[:, 0] - peak[None]), axis=0)
    my_log = peak + jnp.log(total)
    my_loss = jnp.sum(
        my_log
        - (1.0 - SMOOTH) * jnp.sum(stats[:, 2], axis=0)
        - SMOOTH / V * jnp.sum(stats[:, 3], axis=0)
        + ZCOEF * my_log * my_log
    )
    logs = lax.all_to_all(jnp.broadcast_to(my_log[None, None], (devices, 1, loss_dev)), ALL, split_axis=0, concat_axis=0, tiled=True)
    log_total = jnp.take(logs[:, 0], source_of, axis=0).reshape(loss_total, 1)
    d_logits = (
        (1.0 + 2.0 * ZCOEF * log_total) * jnp.exp(logits - log_total)
        - jnp.where(hit, 1.0 - SMOOTH, 0.0)
        - SMOOTH / V
    ) / loss_total
    d_logits = d_logits.astype(bf16)
    d_hidden = dot(d_logits, table_low).reshape(2, 4, rows_q, loss_dev, D)
    d_hidden = d_hidden.at[1].get().astype(bf16), d_hidden[0]
    d_hidden = fold_plane([d_hidden[1], d_hidden[0]])
    d_low = d_hidden.astype(bf16)
    total_hidden = d_hidden[0]
    for k in range(1, rows_q):
        total_hidden = total_hidden + flip(d_low[k], "q", k, rows_q).astype(f32)
    head_grad = dot(d_logits, hidden_all, 0, 0)

    d_x_two, grad_final = norm_back(x_two, gains[2], total_hidden)
    d_down = spread_plane(d_x_two.astype(bf16)).reshape(plane_rows, D)
    d_act = sum(dot(d_down[:, UNIT * j : UNIT * (j + 1)], w_down[j], 1, 1) for j in range(3))
    d_gate = (d_act * up * sig * (1.0 + gate * (1.0 - sig))).astype(bf16)
    d_up = (d_act * gate * sig).astype(bf16)
    grad_down = [dot(act, d_down[:, UNIT * j : UNIT * (j + 1)], 0, 0).astype(bf16) for j in range(3)]
    grad_gate = dot(h_all, d_gate, 0, 0).astype(bf16)
    grad_up = dot(h_all, d_up, 0, 0).astype(bf16)
    d_h = dot(d_gate, w_gate, 1, 1) + dot(d_up, w_up, 1, 1)
    d_h_mlp = fold_plane(d_h.reshape(2, 4, loss_dev, D))
    d_x_mlp, grad_mlp = norm_back(x_one, gains[1], d_h_mlp)
    d_x_one = d_x_two + d_x_mlp

    d_branch = d_x_one.astype(bf16)
    grad_out = [dot(attended, d_branch[:, UNIT * j : UNIT * (j + 1)], 0, 0).astype(bf16) for j in range(3)]
    d_attended = sum(dot(d_branch[:, UNIT * j : UNIT * (j + 1)], w_out[j], 1, 1) for j in range(3))
    d_mixed = heads_of(d_attended.astype(bf16))
    d_probs = jnp.einsum("hqd,hkd->hqk", d_mixed, value_h, preferred_element_type=f32)
    delta = jnp.sum(probs * d_probs, axis=-1, keepdims=True)
    d_scores = (probs * (d_probs - delta)).astype(bf16)
    d_query = jnp.einsum("hqk,hkd->hqd", d_scores, key_h, preferred_element_type=f32) * HEAD_SIZE**-0.5
    d_key = jnp.einsum("hqk,hqd->khd", d_scores, query_h, preferred_element_type=f32) * HEAD_SIZE**-0.5
    d_value = jnp.einsum("hqk,hqd->khd", probs_low, d_mixed, preferred_element_type=f32)
    d_q = rotate_back(heads_back(d_query), cosine_pick, sine_pick).astype(bf16)
    d_k = rotate_back(d_key.reshape(tokens, UNIT), cosine, sine).astype(bf16)
    d_v = d_value.reshape(tokens, UNIT).astype(bf16)
    grad_qkv = [dot(h_pick, d_q[:, UNIT * j : UNIT * (j + 1)], 0, 0).astype(bf16) for j in range(3)]
    grad_qkv += [dot(h_attn, d_k, 0, 0).astype(bf16), dot(h_attn, d_v, 0, 0).astype(bf16)]
    d_h_pick = sum(dot(d_q[:, UNIT * j : UNIT * (j + 1)], w_qkv[j], 1, 1) for j in range(3))
    high = d_h_pick.astype(bf16)
    rest = (d_h_pick - high.astype(f32)).astype(bf16)
    d_h_attn = dot(d_k, w_qkv[3], 1, 1) + dot(d_v, w_qkv[4], 1, 1) + dot(pick, high, 0, 0) + dot(pick, rest, 0, 0)
    d_x_attn, grad_attn = norm_back(x_embed, gains[0], d_h_attn)
    high = d_x_one.astype(bf16)
    rest = (d_x_one - high.astype(f32)).astype(bf16)
    d_x_embed = d_x_attn + dot(pick, high, 0, 0) + dot(pick, rest, 0, 0)

    sending = dot(spot, (d_x_embed * emb_mult).astype(bf16), 0, 0).astype(bf16).reshape(devices, capacity, D)
    arrived = lax.all_to_all(sending, ALL, split_axis=0, concat_axis=0, tiled=True).reshape(slots, D)
    table_grad = head_grad + dot(row_hot, arrived, 0, 0)

    gain_grads = jnp.concatenate([grad_attn, grad_mlp, grad_final]).reshape(GAIN_UNITS, UNIT)
    if aligned:
        lower = jnp.stack(grad_qkv).reshape(5, 5, 192, UNIT).transpose(1, 0, 2, 3).reshape(5, units, UNIT)
        upper = jnp.stack(grad_out).reshape(3, 3, 320, UNIT).transpose(1, 0, 2, 3).reshape(3, units, UNIT)
        room = jnp.zeros((8, 64, UNIT), bf16).at[0, :GAIN_UNITS].set(gain_grads.astype(bf16))
        level = jnp.concatenate([jnp.concatenate([lower, upper]), room], axis=1).reshape(4, 2, units + 64, UNIT)
        keep = lax.dynamic_index_in_dim(level, c_index, 1, False)
        give = lax.dynamic_index_in_dim(level, 1 - c_index, 1, False)
        level = keep.astype(f32) + flip(give, "c", 1, 2).astype(f32)
        own = lax.dynamic_index_in_dim(level, yx_index, 0, False)
        for k in (1, 2, 3):
            piece = lax.dynamic_index_in_dim(level, yx_index ^ k, 0, False).astype(bf16)
            own = own + flip(piece, ("y", "x"), k, 4).astype(f32)
        own = own.reshape(4, (units + 64) // 4, UNIT)
        quarter = lax.dynamic_index_in_dim(own, q_index, 0, False)
        for k in (1, 2, 3):
            piece = lax.dynamic_index_in_dim(own, q_index ^ k, 0, False).astype(bf16)
            quarter = quarter + flip(piece, "q", k, 4).astype(f32)
        quarter = quarter.astype(bf16)
        quarters = [quarter] + [lax.ppermute(quarter, "q", [(k, 0)]) for k in (1, 2, 3)]
        first = jnp.concatenate(quarters)
        gain_out = first[units : units + GAIN_UNITS]
        first = first[:units]
        blocks = jnp.concatenate(
            [jnp.zeros((units, UNIT), bf16)]
            + [grad_gate[:480], grad_up[:480], grad_gate[480:], grad_up[480:]]
            + grad_down
        )
        share = lax.psum_scatter(blocks, "q", scatter_dimension=0, tiled=True)
        sent = share.reshape(2, 8, 60, UNIT).transpose(1, 0, 2, 3).reshape(8, 120, UNIT)
        got = lax.all_to_all(sent, PLANE, split_axis=0, concat_axis=0, tiled=True)
        by_share = got.reshape(8, 2, 60, UNIT).transpose(2, 1, 0, 3).reshape(units, UNIT)
        by_five = first.reshape(5, 192, UNIT).transpose(1, 0, 2).reshape(units, UNIT)
        by_three = jnp.where(q_index == 0, first, share).reshape(3, 320, UNIT).transpose(1, 0, 2).reshape(units, UNIT)
        mixed = jnp.where((q_index == 0) & (p_index < 5), by_five, by_three)
        mine = jnp.where((q_index == 1) | (q_index == 2), by_share, mixed)
    else:
        zero = jnp.zeros((D, 2, 8, UNIT), bf16)
        both = lax.dynamic_update_index_in_dim(zero, jnp.stack([grad_gate, grad_up], axis=1), p_index, 2)
        downs = lax.dynamic_update_index_in_dim(jnp.zeros((8, SHARE, 3, UNIT), bf16), jnp.stack(grad_down, axis=1), p_index, 0)
        full = jnp.concatenate(
            [
                jnp.stack(grad_qkv, axis=1).reshape(-1, UNIT),
                jnp.stack(grad_out, axis=1).reshape(-1, UNIT),
                both.reshape(-1, UNIT),
                downs.reshape(-1, UNIT),
            ]
        ).reshape(devices, units, UNIT)
        room = jnp.zeros((devices, 16, UNIT), bf16).at[0, :GAIN_UNITS].set(gain_grads.astype(bf16))
        full = jnp.concatenate([full, room], axis=1)
        summed = lax.psum_scatter(full, ALL, scatter_dimension=0, tiled=False)
        mine, gain_out = summed[:units], summed[units : units + GAIN_UNITS]
    behind = lax.ppermute(mine[units - GAIN_UNITS :], ALL, [(i, i + 1) for i in range(devices - 1)])
    behind = jnp.where(me == 0, gain_out, behind)
    tail = max(0, drift * (devices - 1) + shard - GAINS - span)
    stream = jnp.concatenate([behind.reshape(-1), mine.reshape(-1), jnp.zeros((tail,), bf16)])
    layer_grad = lax.dynamic_slice(stream, (drift * me,), (shard,)).astype(f32)

    squares = jnp.sum(layer_grad * layer_grad) + jnp.sum(table_grad * table_grad)
    sums = jnp.broadcast_to(jnp.stack([squares, my_loss])[None], (devices, 2))
    sums = jnp.sum(lax.all_to_all(sums, ALL, split_axis=0, concat_axis=0, tiled=True), axis=0)
    grad_norm = jnp.sqrt(sums[0])
    loss = sums[1] / loss_total
    limit = CLIP_C / math.sqrt(loss_total)
    clip_factor = limit / jnp.maximum(grad_norm, limit)
    flat_one, flat_two, flat_update = adamw_step(flat_master, layer_grad, flat_m, flat_v, clip_factor)
    table_one, table_two, table_update = adamw_step(table_master, table_grad, table_m, table_v, clip_factor)
    return (loss, grad_norm, flat_one, flat_two, flat_update, table_one, table_two, table_update)


def solution(mesh):
    count = mesh.devices.size
    grid = Mesh(mesh.devices.reshape(count // 8, 2, 2, 2), ALL)
    rows, matrix = P(ALL), P(ALL, None)
    in_specs = (rows,) * 6 + (matrix,) * 3
    out_specs = (P(), P()) + (rows,) * 3 + (matrix,) * 3
    return jax.shard_map(local, mesh=grid, in_specs=in_specs, out_specs=out_specs, check_vma=False)
```

```python
import math

import jax
import jax.numpy as jnp
import numpy as np
from jax import lax
from jax.sharding import Mesh, PartitionSpec as P

D = 960
QUERY_HEADS = 15
KEY_VALUE_HEADS = 5
HEAD_SIZE = 64
FF = 2560
V = 32000
PL = 256
CL = 128
STEP = 10
QKV = 1600

EPS = 1e-05
SMOOTH = 0.1
ZCOEF = 0.0001
BETA1 = 0.9
BETA2 = 0.95
ADAM_EPS = 1e-08
DECAY = 0.1
RATE = 0.03
CLIP_C = 25.0
NEGATIVE = -1e30

UNIT = 320
GAINS = 3 * D
GAIN_UNITS = GAINS // UNIT
QKV_UNITS = D * QKV // UNIT
OUT_UNITS = D * D // UNIT
GU_UNITS = D * 2 * FF // UNIT
DOWN_UNITS = FF * D // UNIT
ALL_UNITS = QKV_UNITS + OUT_UNITS + GU_UNITS + DOWN_UNITS
PLANE = ("y", "x", "c")
ALL = ("q", "y", "x", "c")
SHARE = FF // 8

bf16 = jnp.bfloat16
f32 = jnp.float32


def dot(left, right, left_dim=1, right_dim=0):
    return lax.dot_general(
        left, right, (((left_dim,), (right_dim,)), ((), ())), preferred_element_type=f32
    )


def hot(index, count):
    return (index[:, None] == jnp.arange(count, dtype=jnp.int32)[None, :]).astype(bf16)


def scale_of(rows):
    return lax.rsqrt(jnp.mean(rows * rows, axis=-1, keepdims=True) + EPS)


def norm_back(rows, gain, grad):
    scale = scale_of(rows)
    normed = rows * scale
    grad_gain = jnp.sum(grad * normed, axis=0)
    scaled = grad * gain
    return scale * (scaled - normed * jnp.mean(scaled * normed, axis=-1, keepdims=True)), grad_gain


def flip(rows, axes, bits, size):
    return lax.ppermute(rows, axes, [(i, i ^ bits) for i in range(size)])


def rope_tables(count):
    row = np.arange(count)
    position = np.where(row < PL, row, PL + (row - PL) % CL).astype(np.float32)
    half = np.arange(HEAD_SIZE // 2, dtype=np.float32)
    freqs = np.float32(10000.0) ** (-(half * np.float32(2.0) / np.float32(HEAD_SIZE)))
    angles = (position[:, None] * freqs[None, :].astype(np.float32)).astype(np.float64)
    angles = np.concatenate([angles, angles], axis=-1)
    return np.cos(angles).astype(np.float32), np.sin(angles).astype(np.float32)


def rotate(rows, cosine, sine):
    heads = rows.reshape(rows.shape[0], -1, HEAD_SIZE)
    half = HEAD_SIZE // 2
    turned = jnp.concatenate([-heads[..., half:], heads[..., :half]], axis=-1)
    return (heads * cosine[:, None, :] + turned * sine[:, None, :]).reshape(rows.shape)


def rotate_back(grad, cosine, sine):
    heads = grad.reshape(grad.shape[0], -1, HEAD_SIZE)
    half = HEAD_SIZE // 2
    spun = heads * sine[:, None, :]
    turned = jnp.concatenate([spun[..., half:], -spun[..., :half]], axis=-1)
    return (heads * cosine[:, None, :] + turned).reshape(grad.shape)


def adamw_step(param, gradient, moment_one, moment_two, clip_factor):
    gradient = gradient * clip_factor
    new_one = BETA1 * moment_one + (1.0 - BETA1) * gradient
    new_two = BETA2 * moment_two + (1.0 - BETA2) * gradient * gradient
    ratio = new_one / (1.0 - BETA1**STEP) / (jnp.sqrt(new_two / (1.0 - BETA2**STEP)) + ADAM_EPS)
    return (new_one, new_two, -RATE * (ratio + DECAY * param))


def fold_plane(parts):
    got = flip(parts[1], "c", 1, 2)
    mine = parts[0].astype(f32) + got.astype(f32)
    low = mine.astype(parts[1].dtype)
    total = mine[0]
    for k in (1, 2, 3):
        total = total + flip(low[k], ("y", "x"), k, 4).astype(f32)
    return total


def spread_plane(rows):
    four = jnp.stack([rows] + [flip(rows, ("y", "x"), k, 4) for k in (1, 2, 3)])
    return jnp.stack([four, flip(four, "c", 1, 2)])


def local(
    token_ids, loss_rows, targets, flat_master, flat_m, flat_v, table_master, table_m, table_v
):
    devices = lax.axis_size(ALL)
    rows_q = lax.axis_size("q")
    me = lax.axis_index(ALL)
    q_index = lax.axis_index("q")
    p_index = lax.axis_index(PLANE)
    c_index = lax.axis_index("c")
    yx_index = lax.axis_index(("y", "x"))
    tokens = token_ids.shape[0]
    vocab_dev = table_master.shape[0]
    loss_dev = loss_rows.shape[0]
    loss_total = loss_dev * devices
    capacity = max(2, 2 * tokens // devices)
    slots = devices * capacity
    groups = QUERY_HEADS // KEY_VALUE_HEADS
    emb_mult = math.sqrt(D) * 0.5
    shard = flat_master.shape[0]
    units = ALL_UNITS // devices
    span = units * UNIT
    drift = shard - span
    aligned = devices == 32

    place = np.array([kq * 8 + kyx * 2 + kc for kc in range(2) for kyx in range(4) for kq in range(rows_q)])
    rank_of = np.argsort(place)
    source_of = me ^ jnp.asarray(place, jnp.int32)
    order_of = jnp.take(jnp.asarray(rank_of, jnp.int32), me ^ jnp.arange(devices, dtype=jnp.int32))

    table_low = table_master.astype(bf16)
    owner = token_ids // vocab_dev
    owner_hot = hot(owner, devices)
    before = (lax.broadcasted_iota(jnp.int32, (tokens, tokens), 0) > lax.broadcasted_iota(jnp.int32, (tokens, tokens), 1)).astype(bf16)
    slot = jnp.sum(dot(before, owner_hot) * owner_hot.astype(f32), axis=1).astype(jnp.int32)
    spot = hot(owner * capacity + slot, slots)
    marked = token_ids + 1
    halves = jnp.stack([marked // 256, marked % 256]).astype(bf16)
    found = dot(halves, spot).astype(jnp.int32)
    requests = (found[0] * 256 + found[1] - 1).reshape(devices, capacity)
    ask = jnp.concatenate([requests, jnp.broadcast_to(targets[None], (devices, loss_dev))], axis=1)
    asked = lax.all_to_all(ask, ALL, split_axis=0, concat_axis=0, tiled=True)
    row_hot = hot(asked[:, :capacity].reshape(-1) - me * vocab_dev, vocab_dev)
    answer = dot(row_hot, table_low).astype(bf16).reshape(devices, capacity, D)

    flat_low = flat_master.astype(bf16)
    ahead = lax.ppermute(flat_low[:GAINS], ALL, [(i + 1, i) for i in range(devices - 1)])
    back = max(0, drift * (devices - 1) - GAINS)
    pieces = [flat_low, ahead]
    if back:
        pieces = [lax.ppermute(flat_low[shard - back :], ALL, [(i, i + 1) for i in range(devices - 1)])] + pieces
    chunk = lax.dynamic_slice(jnp.concatenate(pieces), (back + GAINS - drift * me,), (span,)).reshape(units, UNIT)
    gain_rows = flat_low[:GAINS].reshape(GAIN_UNITS, UNIT)
    extra = jnp.concatenate([gain_rows, jnp.zeros((16 - GAIN_UNITS, UNIT), bf16)])
    if aligned:
        by_five = chunk.reshape(192, 5, UNIT).transpose(1, 0, 2).reshape(units, UNIT)
        by_three = chunk.reshape(320, 3, UNIT).transpose(1, 0, 2).reshape(units, UNIT)
        sent = chunk.reshape(60, 2, 8, UNIT).transpose(2, 1, 0, 3).reshape(8, 120, UNIT)
        got = lax.all_to_all(sent, PLANE, split_axis=0, concat_axis=0, tiled=True)
        first = jnp.concatenate([jnp.where(p_index < 5, by_five, by_three), extra])
        jumped = lax.ppermute(first, "q", [(0, 2)])
        first = jnp.where(q_index == 2, jumped, first)
        stepped = lax.ppermute(first, "q", [(0, 1), (2, 3)])
        first = jnp.where((q_index == 1) | (q_index == 3), stepped, first)
        answer, first, got = lax.optimization_barrier((answer, first, got))
        returned = lax.all_to_all(answer, ALL, split_axis=0, concat_axis=0, tiled=True).reshape(slots, D)
        level = lax.all_gather(first, PLANE)
        gains = level[0, units : units + GAIN_UNITS].astype(f32).reshape(3, D)
        w_qkv = level[:5, :units].reshape(5, 5, 192, UNIT).transpose(1, 0, 2, 3).reshape(5, D, UNIT)
        w_out = level[5:, :units].reshape(3, 3, 320, UNIT).transpose(1, 0, 2, 3).reshape(3, D, UNIT)
        by_share = got.reshape(8, 2, 60, UNIT).transpose(1, 0, 2, 3).reshape(units, UNIT)
        mixed = jnp.where(q_index == 3, by_three, by_share)
        mixed, returned = lax.optimization_barrier((mixed, returned))
        column = lax.all_gather(mixed, "q")
        w_gate = jnp.concatenate([column[1, :480], column[2, :480]])
        w_up = jnp.concatenate([column[1, 480:], column[2, 480:]])
        w_down = column[3].reshape(3, SHARE, UNIT)
    else:
        returned = lax.all_to_all(answer, ALL, split_axis=0, concat_axis=0, tiled=True).reshape(slots, D)
        full = lax.all_gather(jnp.concatenate([chunk, extra]), ALL)
        gains = full[0, units : units + GAIN_UNITS].astype(f32).reshape(3, D)
        full = full[:, :units].reshape(ALL_UNITS, UNIT)
        edge = np.cumsum([QKV_UNITS, OUT_UNITS, GU_UNITS])
        w_qkv = full[: edge[0]].reshape(D, 5, UNIT).transpose(1, 0, 2)
        w_out = full[edge[0] : edge[1]].reshape(D, 3, UNIT).transpose(1, 0, 2)
        both = lax.dynamic_index_in_dim(full[edge[1] : edge[2]].reshape(D, 2, 8, UNIT), p_index, 2, False)
        w_gate, w_up = both[:, 0], both[:, 1]
        w_down = lax.dynamic_index_in_dim(full[edge[2] :].reshape(8, SHARE, 3, UNIT), p_index, 0, False).transpose(1, 0, 2)
    x_low = dot(spot, returned).astype(bf16)
    x_embed = x_low.astype(f32) * emb_mult

    pick = hot(loss_rows, tokens)
    cosine, sine = (jnp.asarray(t) for t in rope_tables(tokens))
    cosine_pick, sine_pick = cosine[loss_rows], sine[loss_rows]
    h_attn = (x_embed * scale_of(x_embed) * gains[0]).astype(bf16)
    h_pick = dot(pick, h_attn).astype(bf16)
    x_pick = dot(pick, x_low) * emb_mult
    q_raw = jnp.concatenate([dot(h_pick, w_qkv[j]) for j in range(3)], axis=1)
    query = rotate(q_raw, cosine_pick, sine_pick).astype(bf16)
    key = rotate(dot(h_attn, w_qkv[3]), cosine, sine).astype(bf16)
    value = dot(h_attn, w_qkv[4]).astype(bf16)

    def heads_of(rows):
        return rows.reshape(loss_dev, KEY_VALUE_HEADS, groups, HEAD_SIZE).transpose(1, 2, 0, 3).reshape(KEY_VALUE_HEADS, groups * loss_dev, HEAD_SIZE)

    def heads_back(rows):
        return rows.reshape(KEY_VALUE_HEADS, groups, loss_dev, HEAD_SIZE).transpose(2, 0, 1, 3).reshape(loss_dev, D)

    query_h = heads_of(query)
    key_h = key.reshape(tokens, KEY_VALUE_HEADS, HEAD_SIZE).transpose(1, 0, 2)
    value_h = value.reshape(tokens, KEY_VALUE_HEADS, HEAD_SIZE).transpose(1, 0, 2)
    key_pos = jnp.arange(tokens, dtype=jnp.int32)[None, :]
    ask_pos = jnp.tile(loss_rows, groups)[:, None]
    key_seg = jnp.where(key_pos < PL, 0, 1 + (key_pos - PL) // CL)
    ask_seg = jnp.where(ask_pos < PL, 0, 1 + (ask_pos - PL) // CL)
    allowed = (key_pos <= ask_pos) & ((key_seg == 0) | (key_seg == ask_seg))
    scores = jnp.einsum("hqd,hkd->hqk", query_h, key_h, preferred_element_type=f32) * HEAD_SIZE**-0.5
    scores = jnp.where(allowed[None], scores, NEGATIVE)
    exp_scores = jnp.exp(scores - jnp.max(scores, axis=-1, keepdims=True))
    probs = exp_scores / jnp.sum(exp_scores, axis=-1, keepdims=True)
    probs_low = probs.astype(bf16)
    mixed_heads = jnp.einsum("hqk,hkd->hqd", probs_low, value_h, preferred_element_type=f32)
    attended = heads_back(mixed_heads.astype(bf16))
    x_one = x_pick + jnp.concatenate([dot(attended, w_out[j]) for j in range(3)], axis=1)

    h_mlp = (x_one * scale_of(x_one) * gains[1]).astype(bf16)
    plane_rows = 8 * loss_dev
    h_all = spread_plane(h_mlp).reshape(plane_rows, D)
    gate = dot(h_all, w_gate)
    up = dot(h_all, w_up)
    sig = jax.nn.sigmoid(gate)
    act = (gate * sig * up).astype(bf16)
    part = jnp.concatenate([dot(act, w_down[j]) for j in range(3)], axis=1)
    x_two = x_one + fold_plane(part.reshape(2, 4, loss_dev, D))

    hidden = (x_two * scale_of(x_two) * gains[2]).astype(bf16)
    across = jnp.stack([hidden] + [flip(hidden, "q", k, rows_q) for k in range(1, rows_q)])
    hidden_all = spread_plane(across).reshape(loss_total, D)
    logits = dot(hidden_all, table_low, 1, 1)
    targets_all = jnp.take(asked[:, capacity:], source_of, axis=0).reshape(loss_total)
    column_id = targets_all - me * vocab_dev
    hit = column_id[:, None] == jnp.arange(vocab_dev, dtype=jnp.int32)[None, :]
    local_peak = jnp.max(logits, axis=1)
    local_total = jnp.sum(jnp.exp(logits - local_peak[:, None]), axis=1)
    local_target = jnp.sum(jnp.where(hit, logits, 0.0), axis=1)
    local_sum = jnp.sum(logits, axis=1)
    stats = jnp.stack([local_peak, local_total, local_target, local_sum]).reshape(4, devices, loss_dev)
    stats = jnp.take(stats, order_of, axis=1).transpose(1, 0, 2)
    stats = lax.all_to_all(stats, ALL, split_axis=0, concat_axis=0, tiled=True)
    peak = jnp.max(stats[:, 0], axis=0)
    total = jnp.sum(stats[:, 1] * jnp.exp(stats[:, 0] - peak[None]), axis=0)
    my_log = peak + jnp.log(total)
    my_loss = jnp.sum(
        my_log
        - (1.0 - SMOOTH) * jnp.sum(stats[:, 2], axis=0)
        - SMOOTH / V * jnp.sum(stats[:, 3], axis=0)
        + ZCOEF * my_log * my_log
    )
    logs = lax.all_to_all(jnp.broadcast_to(my_log[None, None], (devices, 1, loss_dev)), ALL, split_axis=0, concat_axis=0, tiled=True)
    log_total = jnp.take(logs[:, 0], source_of, axis=0).reshape(loss_total, 1)
    d_logits = (
        (1.0 + 2.0 * ZCOEF * log_total) * jnp.exp(logits - log_total)
        - jnp.where(hit, 1.0 - SMOOTH, 0.0)
        - SMOOTH / V
    ) / loss_total
    d_logits = d_logits.astype(bf16)
    d_hidden = dot(d_logits, table_low).reshape(2, 4, rows_q, loss_dev, D)
    d_hidden = d_hidden.at[1].get().astype(bf16), d_hidden[0]
    d_hidden = fold_plane([d_hidden[1], d_hidden[0]])
    d_low = d_hidden.astype(bf16)
    total_hidden = d_hidden[0]
    for k in range(1, rows_q):
        total_hidden = total_hidden + flip(d_low[k], "q", k, rows_q).astype(f32)
    head_grad = dot(d_logits, hidden_all, 0, 0)

    d_x_two, grad_final = norm_back(x_two, gains[2], total_hidden)
    d_down = spread_plane(d_x_two.astype(bf16)).reshape(plane_rows, D)
    d_act = sum(dot(d_down[:, UNIT * j : UNIT * (j + 1)], w_down[j], 1, 1) for j in range(3))
    d_gate = (d_act * up * sig * (1.0 + gate * (1.0 - sig))).astype(bf16)
    d_up = (d_act * gate * sig).astype(bf16)
    grad_down = [dot(act, d_down[:, UNIT * j : UNIT * (j + 1)], 0, 0).astype(bf16) for j in range(3)]
    grad_gate = dot(h_all, d_gate, 0, 0).astype(bf16)
    grad_up = dot(h_all, d_up, 0, 0).astype(bf16)
    d_h = dot(d_gate, w_gate, 1, 1) + dot(d_up, w_up, 1, 1)
    d_h_mlp = fold_plane(d_h.reshape(2, 4, loss_dev, D))
    d_x_mlp, grad_mlp = norm_back(x_one, gains[1], d_h_mlp)
    d_x_one = d_x_two + d_x_mlp

    d_branch = d_x_one.astype(bf16)
    d_attended = sum(dot(d_branch[:, UNIT * j : UNIT * (j + 1)], w_out[j], 1, 1) for j in range(3))
    d_mixed = heads_of(d_attended.astype(bf16))
    d_probs = jnp.einsum("hqd,hkd->hqk", d_mixed, value_h, preferred_element_type=f32)
    delta = jnp.sum(probs * d_probs, axis=-1, keepdims=True)
    d_scores = (probs * (d_probs - delta)).astype(bf16)
    d_query = jnp.einsum("hqk,hkd->hqd", d_scores, key_h, preferred_element_type=f32) * HEAD_SIZE**-0.5
    d_key = jnp.einsum("hqk,hqd->khd", d_scores, query_h, preferred_element_type=f32) * HEAD_SIZE**-0.5
    d_value = jnp.einsum("hqk,hqd->khd", probs_low, d_mixed, preferred_element_type=f32)
    d_q = rotate_back(heads_back(d_query), cosine_pick, sine_pick).astype(bf16)
    d_k = rotate_back(d_key.reshape(tokens, UNIT), cosine, sine).astype(bf16)
    d_v = d_value.reshape(tokens, UNIT).astype(bf16)
    d_h_pick = sum(dot(d_q[:, UNIT * j : UNIT * (j + 1)], w_qkv[j], 1, 1) for j in range(3))
    high = d_h_pick.astype(bf16)
    rest = (d_h_pick - high.astype(f32)).astype(bf16)
    d_h_attn = dot(d_k, w_qkv[3], 1, 1) + dot(d_v, w_qkv[4], 1, 1) + dot(pick, high, 0, 0) + dot(pick, rest, 0, 0)
    d_x_attn, grad_attn = norm_back(x_embed, gains[0], d_h_attn)
    high = d_x_one.astype(bf16)
    rest = (d_x_one - high.astype(f32)).astype(bf16)
    d_x_embed = d_x_attn + dot(pick, high, 0, 0) + dot(pick, rest, 0, 0)

    sending = dot(spot, (d_x_embed * emb_mult).astype(bf16), 0, 0).astype(bf16).reshape(devices, capacity, D)
    if aligned:
        blocks = jnp.concatenate(
            [jnp.zeros((units, UNIT), bf16)]
            + [grad_gate[:480], grad_up[:480], grad_gate[480:], grad_up[480:]]
            + grad_down
        )
        share = lax.psum_scatter(blocks, "q", scatter_dimension=0, tiled=True)
        sending, share = lax.optimization_barrier((sending, share))
    sending, d_q, d_k, d_v, attended = lax.optimization_barrier((sending, d_q, d_k, d_v, attended))
    arrived = lax.all_to_all(sending, ALL, split_axis=0, concat_axis=0, tiled=True).reshape(slots, D)
    grad_out = [dot(attended, d_branch[:, UNIT * j : UNIT * (j + 1)], 0, 0).astype(bf16) for j in range(3)]
    grad_qkv = [dot(h_pick, d_q[:, UNIT * j : UNIT * (j + 1)], 0, 0).astype(bf16) for j in range(3)]
    grad_qkv += [dot(h_attn, d_k, 0, 0).astype(bf16), dot(h_attn, d_v, 0, 0).astype(bf16)]

    gain_grads = jnp.concatenate([grad_attn, grad_mlp, grad_final]).reshape(GAIN_UNITS, UNIT)
    if aligned:
        lower = jnp.stack(grad_qkv).reshape(5, 5, 192, UNIT).transpose(1, 0, 2, 3).reshape(5, units, UNIT)
        upper = jnp.stack(grad_out).reshape(3, 3, 320, UNIT).transpose(1, 0, 2, 3).reshape(3, units, UNIT)
        room = jnp.zeros((8, 64, UNIT), bf16).at[0, :GAIN_UNITS].set(gain_grads.astype(bf16))
        level = jnp.concatenate([jnp.concatenate([lower, upper]), room], axis=1).reshape(4, 2, units + 64, UNIT)
        level, arrived = lax.optimization_barrier((level, arrived))
        keep = lax.dynamic_index_in_dim(level, c_index, 1, False)
        give = lax.dynamic_index_in_dim(level, 1 - c_index, 1, False)
        level = keep.astype(f32) + flip(give, "c", 1, 2).astype(f32)
        own = lax.dynamic_index_in_dim(level, yx_index, 0, False)
        for k in (1, 2, 3):
            piece = lax.dynamic_index_in_dim(level, yx_index ^ k, 0, False).astype(bf16)
            own = own + flip(piece, ("y", "x"), k, 4).astype(f32)
        own = own.reshape(4, (units + 64) // 4, UNIT)
        quarter = lax.dynamic_index_in_dim(own, q_index, 0, False)
        for k in (1, 2, 3):
            piece = lax.dynamic_index_in_dim(own, q_index ^ k, 0, False).astype(bf16)
            quarter = quarter + flip(piece, "q", k, 4).astype(f32)
        quarter = quarter.astype(bf16)
        quarters = [quarter] + [lax.ppermute(quarter, "q", [(k, 0)]) for k in (1, 2, 3)]
        first = jnp.concatenate(quarters)
        gain_out = first[units : units + GAIN_UNITS]
        first = first[:units]
        sent = share.reshape(2, 8, 60, UNIT).transpose(1, 0, 2, 3).reshape(8, 120, UNIT)
        got = lax.all_to_all(sent, PLANE, split_axis=0, concat_axis=0, tiled=True)
        by_share = got.reshape(8, 2, 60, UNIT).transpose(2, 1, 0, 3).reshape(units, UNIT)
        by_five = first.reshape(5, 192, UNIT).transpose(1, 0, 2).reshape(units, UNIT)
        by_three = jnp.where(q_index == 0, first, share).reshape(3, 320, UNIT).transpose(1, 0, 2).reshape(units, UNIT)
        mixed = jnp.where((q_index == 0) & (p_index < 5), by_five, by_three)
        mine = jnp.where((q_index == 1) | (q_index == 2), by_share, mixed)
    else:
        zero = jnp.zeros((D, 2, 8, UNIT), bf16)
        both = lax.dynamic_update_index_in_dim(zero, jnp.stack([grad_gate, grad_up], axis=1), p_index, 2)
        downs = lax.dynamic_update_index_in_dim(jnp.zeros((8, SHARE, 3, UNIT), bf16), jnp.stack(grad_down, axis=1), p_index, 0)
        full = jnp.concatenate(
            [
                jnp.stack(grad_qkv, axis=1).reshape(-1, UNIT),
                jnp.stack(grad_out, axis=1).reshape(-1, UNIT),
                both.reshape(-1, UNIT),
                downs.reshape(-1, UNIT),
            ]
        ).reshape(devices, units, UNIT)
        room = jnp.zeros((devices, 16, UNIT), bf16).at[0, :GAIN_UNITS].set(gain_grads.astype(bf16))
        full = jnp.concatenate([full, room], axis=1)
        summed = lax.psum_scatter(full, ALL, scatter_dimension=0, tiled=False)
        mine, gain_out = summed[:units], summed[units : units + GAIN_UNITS]
    behind = lax.ppermute(mine[units - GAIN_UNITS :], ALL, [(i, i + 1) for i in range(devices - 1)])
    behind = jnp.where(me == 0, gain_out, behind)
    tail = max(0, drift * (devices - 1) + shard - GAINS - span)
    stream = jnp.concatenate([behind.reshape(-1), mine.reshape(-1), jnp.zeros((tail,), bf16)])
    layer_grad = lax.dynamic_slice(stream, (drift * me,), (shard,)).astype(f32)

    table_grad = head_grad + dot(row_hot, arrived, 0, 0)
    squares = jnp.sum(layer_grad * layer_grad) + jnp.sum(table_grad * table_grad)
    sums = jnp.broadcast_to(jnp.stack([squares, my_loss])[None], (devices, 2))
    sums = jnp.sum(lax.all_to_all(sums, ALL, split_axis=0, concat_axis=0, tiled=True), axis=0)
    grad_norm = jnp.sqrt(sums[0])
    loss = sums[1] / loss_total
    limit = CLIP_C / math.sqrt(loss_total)
    clip_factor = limit / jnp.maximum(grad_norm, limit)
    flat_one, flat_two, flat_update = adamw_step(flat_master, layer_grad, flat_m, flat_v, clip_factor)
    table_one, table_two, table_update = adamw_step(table_master, table_grad, table_m, table_v, clip_factor)
    return (loss, grad_norm, flat_one, flat_two, flat_update, table_one, table_two, table_update)


def solution(mesh):
    count = mesh.devices.size
    grid = Mesh(mesh.devices.reshape(count // 8, 2, 2, 2), ALL)
    rows, matrix = P(ALL), P(ALL, None)
    in_specs = (rows,) * 6 + (matrix,) * 3
    out_specs = (P(), P()) + (rows,) * 3 + (matrix,) * 3
    return jax.shard_map(local, mesh=grid, in_specs=in_specs, out_specs=out_specs, check_vma=False)
```

```python
import math

import jax
import jax.numpy as jnp
import numpy as np
from jax import lax
from jax.sharding import Mesh, PartitionSpec as P

D = 960
QUERY_HEADS = 15
KEY_VALUE_HEADS = 5
HEAD_SIZE = 64
FF = 2560
V = 32000
PL = 256
CL = 128
STEP = 10
QKV = 1600

EPS = 1e-05
SMOOTH = 0.1
ZCOEF = 0.0001
BETA1 = 0.9
BETA2 = 0.95
ADAM_EPS = 1e-08
DECAY = 0.1
RATE = 0.03
CLIP_C = 25.0
NEGATIVE = -1e30

UNIT = 320
GAINS = 3 * D
GAIN_UNITS = GAINS // UNIT
QKV_UNITS = D * QKV // UNIT
OUT_UNITS = D * D // UNIT
GU_UNITS = D * 2 * FF // UNIT
DOWN_UNITS = FF * D // UNIT
ALL_UNITS = QKV_UNITS + OUT_UNITS + GU_UNITS + DOWN_UNITS
PLANE = ("y", "x", "c")
ALL = ("q", "y", "x", "c")
SHARE = FF // 8
LINES = D * (QKV + D + 3 * FF) // 32 // 128
EXTRA = 32

bf16 = jnp.bfloat16
f32 = jnp.float32


def dot(left, right, left_dim=1, right_dim=0):
    return lax.dot_general(
        left, right, (((left_dim,), (right_dim,)), ((), ())), preferred_element_type=f32
    )


def hot(index, count):
    return (index[:, None] == jnp.arange(count, dtype=jnp.int32)[None, :]).astype(bf16)


def scale_of(rows):
    return lax.rsqrt(jnp.mean(rows * rows, axis=-1, keepdims=True) + EPS)


def norm_back(rows, gain, grad):
    scale = scale_of(rows)
    normed = rows * scale
    grad_gain = jnp.sum(grad * normed, axis=0)
    scaled = grad * gain
    return scale * (scaled - normed * jnp.mean(scaled * normed, axis=-1, keepdims=True)), grad_gain


def flip(rows, axes, bits, size):
    return lax.ppermute(rows, axes, [(i, i ^ bits) for i in range(size)])


def rope_tables(count):
    row = np.arange(count)
    position = np.where(row < PL, row, PL + (row - PL) % CL).astype(np.float32)
    half = np.arange(HEAD_SIZE // 2, dtype=np.float32)
    freqs = np.float32(10000.0) ** (-(half * np.float32(2.0) / np.float32(HEAD_SIZE)))
    angles = (position[:, None] * freqs[None, :].astype(np.float32)).astype(np.float64)
    angles = np.concatenate([angles, angles], axis=-1)
    return np.cos(angles).astype(np.float32), np.sin(angles).astype(np.float32)


def rotate(rows, cosine, sine):
    heads = rows.reshape(rows.shape[0], -1, HEAD_SIZE)
    half = HEAD_SIZE // 2
    turned = jnp.concatenate([-heads[..., half:], heads[..., :half]], axis=-1)
    return (heads * cosine[:, None, :] + turned * sine[:, None, :]).reshape(rows.shape)


def rotate_back(grad, cosine, sine):
    heads = grad.reshape(grad.shape[0], -1, HEAD_SIZE)
    half = HEAD_SIZE // 2
    spun = heads * sine[:, None, :]
    turned = jnp.concatenate([spun[..., half:], -spun[..., :half]], axis=-1)
    return (heads * cosine[:, None, :] + turned).reshape(grad.shape)


def adamw_step(param, gradient, moment_one, moment_two, clip_factor):
    gradient = gradient * clip_factor
    new_one = BETA1 * moment_one + (1.0 - BETA1) * gradient
    new_two = BETA2 * moment_two + (1.0 - BETA2) * gradient * gradient
    ratio = new_one / (1.0 - BETA1**STEP) / (jnp.sqrt(new_two / (1.0 - BETA2**STEP)) + ADAM_EPS)
    return (new_one, new_two, -RATE * (ratio + DECAY * param))


def fold_plane(left, right, right_dim):
    half = left.shape[0] // 2
    got = flip(dot(left[half:], right, 1, right_dim).astype(bf16), "c", 1, 2)
    mine = (dot(left[:half], right, 1, right_dim) + got.astype(f32)).reshape(4, half // 4, D)
    low = mine.astype(bf16)
    total = mine[0]
    for k in (1, 2, 3):
        total = total + flip(low[k], ("y", "x"), k, 4).astype(f32)
    return total


def down_pack(rows):
    side = jnp.concatenate([rows[: SHARE // 2, 640:], rows[SHARE // 2 :, 640:]], axis=1)
    return jnp.concatenate([rows[:, :640], side])


def down_unpack(rows):
    side = jnp.concatenate([rows[SHARE:, :UNIT], rows[SHARE:, UNIT:]])
    return jnp.concatenate([rows[:SHARE], side], axis=1)


def spread_plane(rows):
    four = jnp.stack([rows] + [flip(rows, ("y", "x"), k, 4) for k in (1, 2, 3)])
    return jnp.stack([four, flip(four, "c", 1, 2)])


def local(
    token_ids, loss_rows, targets, flat_master, flat_m, flat_v, table_master, table_m, table_v
):
    devices = lax.axis_size(ALL)
    rows_q = lax.axis_size("q")
    me = lax.axis_index(ALL)
    q_index = lax.axis_index("q")
    p_index = lax.axis_index(PLANE)
    c_index = lax.axis_index("c")
    yx_index = lax.axis_index(("y", "x"))
    tokens = token_ids.shape[0]
    vocab_dev = table_master.shape[0]
    loss_dev = loss_rows.shape[0]
    loss_total = loss_dev * devices
    capacity = max(2, 2 * tokens // devices)
    slots = devices * capacity
    groups = QUERY_HEADS // KEY_VALUE_HEADS
    emb_mult = math.sqrt(D) * 0.5
    shard = flat_master.shape[0]
    units = ALL_UNITS // devices
    span = units * UNIT
    drift = shard - span
    aligned = devices == 32

    place = np.array([kq * 8 + kyx * 2 + kc for kc in range(2) for kyx in range(4) for kq in range(rows_q)])
    rank_of = np.argsort(place)
    source_of = me ^ jnp.asarray(place, jnp.int32)
    order_of = jnp.take(jnp.asarray(rank_of, jnp.int32), me ^ jnp.arange(devices, dtype=jnp.int32))

    table_low = table_master.astype(bf16)
    owner = token_ids // vocab_dev
    owner_hot = hot(owner, devices)
    before = (lax.broadcasted_iota(jnp.int32, (tokens, tokens), 0) > lax.broadcasted_iota(jnp.int32, (tokens, tokens), 1)).astype(bf16)
    slot = jnp.sum(dot(before, owner_hot) * owner_hot.astype(f32), axis=1).astype(jnp.int32)
    spot = hot(owner * capacity + slot, slots)
    marked = token_ids + 1
    halves = jnp.stack([marked // 256, marked % 256]).astype(bf16)
    found = dot(halves, spot).astype(jnp.int32)
    requests = (found[0] * 256 + found[1] - 1).reshape(devices, capacity)
    ask = jnp.concatenate([requests, jnp.broadcast_to(targets[None], (devices, loss_dev))], axis=1)
    asked = lax.all_to_all(ask, ALL, split_axis=0, concat_axis=0, tiled=True)
    row_hot = hot(asked[:, :capacity].reshape(-1) - me * vocab_dev, vocab_dev)
    answer = dot(row_hot, table_low).astype(bf16).reshape(devices, capacity, D)

    flat_low = flat_master.astype(bf16)
    ahead = lax.ppermute(flat_low[:GAINS], ALL, [(i + 1, i) for i in range(devices - 1)])
    back = max(0, drift * (devices - 1) - GAINS)
    pieces = [flat_low, ahead]
    if back:
        pieces = [lax.ppermute(flat_low[shard - back :], ALL, [(i, i + 1) for i in range(devices - 1)])] + pieces
    chunk = lax.dynamic_slice(jnp.concatenate(pieces), (back + GAINS - drift * me,), (span,))
    if aligned:
        sent = chunk.reshape(60, 2, 8, UNIT).transpose(2, 0, 1, 3).reshape(8, 60, 2 * UNIT)
        got = lax.all_to_all(sent, PLANE, split_axis=0, concat_axis=0, tiled=True)
        first = jnp.concatenate([chunk, flat_low[:GAINS], jnp.zeros((EXTRA * 128 - GAINS,), bf16)]).reshape(LINES + EXTRA, 128)
        jumped = lax.ppermute(first, "q", [(0, 2)])
        first = jnp.where(q_index == 2, jumped, first)
        stepped = lax.ppermute(first, "q", [(0, 1), (2, 3)])
        first = jnp.where((q_index == 1) | (q_index == 3), stepped, first)
        answer, first, got = lax.optimization_barrier((answer, first, got))
        returned = lax.all_to_all(answer, ALL, split_axis=0, concat_axis=0, tiled=True).reshape(slots, D)
        level = lax.all_gather(first, PLANE)
        gains = level[0, LINES:].reshape(-1)[:GAINS].astype(f32).reshape(3, D)
        w_qkv = level[:5, :LINES].reshape(D, QKV)
        w_out = level[5:, :LINES].reshape(D, D)
        mixed = jnp.where(q_index == 3, down_pack(chunk.reshape(SHARE, D)), got.reshape(480, 2 * UNIT))
        mixed, returned = lax.optimization_barrier((mixed, returned))
        column = lax.all_gather(mixed, "q")
        w_gu = column[1:3].reshape(D, 2 * SHARE)
        w_down = down_unpack(column[3])
    else:
        returned = lax.all_to_all(answer, ALL, split_axis=0, concat_axis=0, tiled=True).reshape(slots, D)
        extra = jnp.zeros((16 * UNIT,), bf16).at[:GAINS].set(flat_low[:GAINS])
        full = lax.all_gather(jnp.concatenate([chunk, extra]).reshape(units + 16, UNIT), ALL)
        gains = full[0, units : units + GAIN_UNITS].astype(f32).reshape(3, D)
        full = full[:, :units].reshape(ALL_UNITS, UNIT)
        edge = np.cumsum([QKV_UNITS, OUT_UNITS, GU_UNITS])
        w_qkv = full[: edge[0]].reshape(D, QKV)
        w_out = full[edge[0] : edge[1]].reshape(D, D)
        both = lax.dynamic_index_in_dim(full[edge[1] : edge[2]].reshape(D, 2, 8, UNIT), p_index, 2, False)
        w_gu = both.reshape(D, 2 * SHARE)
        w_down = lax.dynamic_index_in_dim(full[edge[2] :].reshape(8, SHARE, D), p_index, 0, False)
    x_low = dot(spot, returned).astype(bf16)
    x_embed = x_low.astype(f32) * emb_mult

    pick = hot(loss_rows, tokens)
    cosine, sine = (jnp.asarray(t) for t in rope_tables(tokens))
    cosine_pick, sine_pick = cosine[loss_rows], sine[loss_rows]
    h_attn = (x_embed * scale_of(x_embed) * gains[0]).astype(bf16)
    h_pick = dot(pick, h_attn).astype(bf16)
    x_pick = dot(pick, x_low) * emb_mult
    query = rotate(dot(h_pick, w_qkv[:, :D]), cosine_pick, sine_pick).astype(bf16)
    w_kv = w_qkv[:, D:]
    key_value = dot(h_attn, w_kv)
    key = rotate(key_value[:, :UNIT], cosine, sine).astype(bf16)
    value = key_value[:, UNIT:].astype(bf16)

    def heads_of(rows):
        return rows.reshape(loss_dev, KEY_VALUE_HEADS, groups, HEAD_SIZE).transpose(1, 2, 0, 3).reshape(KEY_VALUE_HEADS, groups * loss_dev, HEAD_SIZE)

    def heads_back(rows):
        return rows.reshape(KEY_VALUE_HEADS, groups, loss_dev, HEAD_SIZE).transpose(2, 0, 1, 3).reshape(loss_dev, D)

    query_h = heads_of(query)
    key_h = key.reshape(tokens, KEY_VALUE_HEADS, HEAD_SIZE).transpose(1, 0, 2)
    value_h = value.reshape(tokens, KEY_VALUE_HEADS, HEAD_SIZE).transpose(1, 0, 2)
    key_pos = jnp.arange(tokens, dtype=jnp.int32)[None, :]
    ask_pos = jnp.tile(loss_rows, groups)[:, None]
    key_seg = jnp.where(key_pos < PL, 0, 1 + (key_pos - PL) // CL)
    ask_seg = jnp.where(ask_pos < PL, 0, 1 + (ask_pos - PL) // CL)
    allowed = (key_pos <= ask_pos) & ((key_seg == 0) | (key_seg == ask_seg))
    scores = jnp.einsum("hqd,hkd->hqk", query_h, key_h, preferred_element_type=f32) * HEAD_SIZE**-0.5
    scores = jnp.where(allowed[None], scores, NEGATIVE)
    exp_scores = jnp.exp(scores - jnp.max(scores, axis=-1, keepdims=True))
    probs = exp_scores / jnp.sum(exp_scores, axis=-1, keepdims=True)
    probs_low = probs.astype(bf16)
    mixed_heads = jnp.einsum("hqk,hkd->hqd", probs_low, value_h, preferred_element_type=f32)
    attended = heads_back(mixed_heads.astype(bf16))
    x_one = x_pick + dot(attended, w_out)

    h_mlp = (x_one * scale_of(x_one) * gains[1]).astype(bf16)
    plane_rows = 8 * loss_dev
    h_all = spread_plane(h_mlp).reshape(plane_rows, D)
    gate_up = dot(h_all, w_gu)
    gate, up = gate_up[:, :SHARE], gate_up[:, SHARE:]
    sig = jax.nn.sigmoid(gate)
    act = (gate * sig * up).astype(bf16)
    x_two = x_one + fold_plane(act, w_down, 0)

    hidden = (x_two * scale_of(x_two) * gains[2]).astype(bf16)
    across = jnp.stack([hidden] + [flip(hidden, "q", k, rows_q) for k in range(1, rows_q)])
    by_x, by_y = flip(across, "x", 1, 2), flip(across, "y", 1, 2)
    cut = rows_q // 2
    corner = [flip(by_x[:cut], "y", 1, 2), flip(by_y[cut:], "x", 1, 2)]
    near = jnp.stack([across, by_x, by_y, jnp.concatenate(corner)]).reshape(loss_total // 2, D)
    sides = [near, flip(near, "c", 1, 2)]
    targets_all = jnp.take(asked[:, capacity:], source_of, axis=0).reshape(2, loss_total // 2)
    logits, hits, stats = [], [], []
    for side, rows in enumerate(sides):
        z = dot(rows, table_low, 1, 1)
        column_id = targets_all[side] - me * vocab_dev
        hit = column_id[:, None] == jnp.arange(vocab_dev, dtype=jnp.int32)[None, :]
        local_peak = jnp.max(z, axis=1)
        local_total = jnp.sum(jnp.exp(z - local_peak[:, None]), axis=1)
        local_target = jnp.sum(jnp.where(hit, z, 0.0), axis=1)
        local_sum = jnp.sum(z, axis=1)
        logits.append(z)
        hits.append(hit)
        stats.append(jnp.stack([local_peak, local_total, local_target, local_sum]))
    stats = jnp.concatenate(stats, axis=1).reshape(4, devices, loss_dev)
    stats = jnp.take(stats, order_of, axis=1).transpose(1, 0, 2)
    stats = lax.all_to_all(stats, ALL, split_axis=0, concat_axis=0, tiled=True)
    peak = jnp.max(stats[:, 0], axis=0)
    total = jnp.sum(stats[:, 1] * jnp.exp(stats[:, 0] - peak[None]), axis=0)
    my_log = peak + jnp.log(total)
    my_loss = jnp.sum(
        my_log
        - (1.0 - SMOOTH) * jnp.sum(stats[:, 2], axis=0)
        - SMOOTH / V * jnp.sum(stats[:, 3], axis=0)
        + ZCOEF * my_log * my_log
    )
    logs = lax.all_to_all(jnp.broadcast_to(my_log[None, None], (devices, 1, loss_dev)), ALL, split_axis=0, concat_axis=0, tiled=True)
    log_total = jnp.take(logs[:, 0], source_of, axis=0).reshape(2, loss_total // 2, 1)
    d_logits = [
        (
            (
                (1.0 + 2.0 * ZCOEF * log_total[side]) * jnp.exp(logits[side] - log_total[side])
                - jnp.where(hits[side], 1.0 - SMOOTH, 0.0)
                - SMOOTH / V
            )
            / loss_total
        ).astype(bf16)
        for side in (1, 0)
    ]
    got = flip(dot(d_logits[0], table_low).astype(bf16), "c", 1, 2)
    d_hidden = (dot(d_logits[1], table_low) + got.astype(f32)).reshape(4, rows_q, loss_dev, D)
    d_low = d_hidden.astype(bf16)
    d_hidden = d_hidden[0]
    for k in (1, 2, 3):
        d_hidden = d_hidden + flip(d_low[k], ("y", "x"), k, 4).astype(f32)
    d_low = d_hidden.astype(bf16)
    total_hidden = d_hidden[0]
    for k in range(1, rows_q):
        total_hidden = total_hidden + flip(d_low[k], "q", k, rows_q).astype(f32)
    head_grad = dot(d_logits[1], sides[0], 0, 0) + dot(d_logits[0], sides[1], 0, 0)
    head_grad, total_hidden = lax.optimization_barrier((head_grad, total_hidden))

    d_x_two, grad_final = norm_back(x_two, gains[2], total_hidden)
    d_down = spread_plane(d_x_two.astype(bf16)).reshape(plane_rows, D)
    d_act = dot(d_down, w_down, 1, 1)
    d_gate = d_act * up * sig * (1.0 + gate * (1.0 - sig))
    d_gu = jnp.concatenate([d_gate, d_act * gate * sig], axis=1).astype(bf16)
    d_h_mlp = fold_plane(d_gu, w_gu, 1)
    grad_down = dot(act, d_down, 0, 0).astype(bf16)
    grad_gu = dot(h_all, d_gu, 0, 0).astype(bf16)
    d_x_mlp, grad_mlp = norm_back(x_one, gains[1], d_h_mlp)
    d_x_one = d_x_two + d_x_mlp

    d_branch = d_x_one.astype(bf16)
    d_attended = dot(d_branch, w_out, 1, 1)
    d_mixed = heads_of(d_attended.astype(bf16))
    d_probs = jnp.einsum("hqd,hkd->hqk", d_mixed, value_h, preferred_element_type=f32)
    delta = jnp.sum(probs * d_probs, axis=-1, keepdims=True)
    d_scores = (probs * (d_probs - delta)).astype(bf16)
    d_query = jnp.einsum("hqk,hkd->hqd", d_scores, key_h, preferred_element_type=f32) * HEAD_SIZE**-0.5
    d_key = jnp.einsum("hqk,hqd->khd", d_scores, query_h, preferred_element_type=f32) * HEAD_SIZE**-0.5
    d_value = jnp.einsum("hqk,hqd->khd", probs_low, d_mixed, preferred_element_type=f32)
    d_q = rotate_back(heads_back(d_query), cosine_pick, sine_pick).astype(bf16)
    d_k = rotate_back(d_key.reshape(tokens, UNIT), cosine, sine)
    d_kv = jnp.concatenate([d_k, d_value.reshape(tokens, UNIT)], axis=1).astype(bf16)
    d_h_pick = dot(d_q, w_qkv[:, :D], 1, 1)
    high = d_h_pick.astype(bf16)
    rest = (d_h_pick - high.astype(f32)).astype(bf16)
    d_h_attn = dot(d_kv, w_kv, 1, 1) + dot(pick, high, 0, 0) + dot(pick, rest, 0, 0)
    d_x_attn, grad_attn = norm_back(x_embed, gains[0], d_h_attn)
    high = d_x_one.astype(bf16)
    rest = (d_x_one - high.astype(f32)).astype(bf16)
    d_x_embed = d_x_attn + dot(pick, high, 0, 0) + dot(pick, rest, 0, 0)

    sending = dot(spot, (d_x_embed * emb_mult).astype(bf16), 0, 0).astype(bf16).reshape(devices, capacity, D)
    if aligned:
        blocks = jnp.concatenate([jnp.zeros((1, 480, 640), bf16), grad_gu.reshape(2, 480, 640), down_pack(grad_down)[None]])
        share = lax.psum_scatter(blocks, "q", scatter_dimension=0, tiled=False)
        sending, d_q, d_kv, attended = lax.optimization_barrier((sending, d_q, d_kv, attended))
        share, d_q, d_kv, attended = lax.optimization_barrier((share, d_q, d_kv, attended))
    arrived = lax.all_to_all(sending, ALL, split_axis=0, concat_axis=0, tiled=True).reshape(slots, D)
    grad_out = dot(attended, d_branch, 0, 0).astype(bf16)
    grad_qkv = jnp.concatenate([dot(h_pick, d_q, 0, 0), dot(h_attn, d_kv, 0, 0)], axis=1).astype(bf16)

    gain_grads = jnp.concatenate([grad_attn, grad_mlp, grad_final]).astype(bf16)
    if aligned:
        level = jnp.concatenate([grad_qkv.reshape(5, LINES, 128), grad_out.reshape(3, LINES, 128)])
        room = jnp.zeros((8, EXTRA * 128), bf16).at[0, :GAINS].set(gain_grads).reshape(8, EXTRA, 128)
        level = jnp.concatenate([level, room], axis=1).reshape(4, 2, LINES + EXTRA, 128)
        level, arrived = lax.optimization_barrier((level, arrived))
        keep = lax.dynamic_index_in_dim(level, c_index, 1, False)
        give = lax.dynamic_index_in_dim(level, 1 - c_index, 1, False)
        level = keep.astype(f32) + flip(give, "c", 1, 2).astype(f32)
        own = lax.dynamic_index_in_dim(level, yx_index, 0, False)
        for k in (1, 2, 3):
            piece = lax.dynamic_index_in_dim(level, yx_index ^ k, 0, False).astype(bf16)
            own = own + flip(piece, ("y", "x"), k, 4).astype(f32)
        own = own.reshape(4, (LINES + EXTRA) // 4, 128)
        own, share = lax.optimization_barrier((own, share))
        got = lax.all_to_all(share.reshape(8, 60, 640), PLANE, split_axis=0, concat_axis=0, tiled=True)
        quarter = lax.dynamic_index_in_dim(own, q_index, 0, False)
        for k in (1, 2, 3):
            piece = lax.dynamic_index_in_dim(own, q_index ^ k, 0, False).astype(bf16)
            quarter = quarter + flip(piece, "q", k, 4).astype(f32)
        quarter = quarter.astype(bf16)
        quarters = [quarter] + [lax.ppermute(quarter, "q", [(k, 0)]) for k in (1, 2, 3)]
        first = jnp.concatenate(quarters)
        gain_out = first[LINES:].reshape(-1)[:GAINS]
        first = first[:LINES].reshape(-1)
        by_share = got.reshape(8, 60, 2, UNIT).transpose(1, 2, 0, 3).reshape(-1)
        mine = jnp.where(q_index == 3, down_unpack(share).reshape(-1), by_share)
        mine = jnp.where(q_index == 0, first, mine)
    else:
        both = lax.dynamic_update_index_in_dim(jnp.zeros((D, 2, 8, UNIT), bf16), grad_gu.reshape(D, 2, UNIT), p_index, 2)
        downs = lax.dynamic_update_index_in_dim(jnp.zeros((8, SHARE, D), bf16), grad_down, p_index, 0)
        full = jnp.concatenate([part.reshape(-1, UNIT) for part in (grad_qkv, grad_out, both, downs)]).reshape(devices, units, UNIT)
        room = jnp.zeros((devices, 16, UNIT), bf16).at[0, :GAIN_UNITS].set(gain_grads.reshape(GAIN_UNITS, UNIT))
        full = jnp.concatenate([full, room], axis=1)
        summed = lax.psum_scatter(full, ALL, scatter_dimension=0, tiled=False)
        mine, gain_out = summed[:units].reshape(-1), summed[units : units + GAIN_UNITS].reshape(-1)
    behind = lax.ppermute(mine[span - GAINS :], ALL, [(i, i + 1) for i in range(devices - 1)])
    behind = jnp.where(me == 0, gain_out, behind)
    tail = max(0, drift * (devices - 1) + shard - GAINS - span)
    stream = jnp.concatenate([behind, mine, jnp.zeros((tail,), bf16)])
    layer_grad = lax.dynamic_slice(stream, (drift * me,), (shard,)).astype(f32)

    table_grad = head_grad + dot(row_hot, arrived, 0, 0)
    squares = jnp.sum(layer_grad * layer_grad) + jnp.sum(table_grad * table_grad)
    sums = jnp.broadcast_to(jnp.stack([squares, my_loss])[None], (devices, 2))
    sums = jnp.sum(lax.all_to_all(sums, ALL, split_axis=0, concat_axis=0, tiled=True), axis=0)
    grad_norm = jnp.sqrt(sums[0])
    loss = sums[1] / loss_total
    limit = CLIP_C / math.sqrt(loss_total)
    clip_factor = limit / jnp.maximum(grad_norm, limit)
    flat_one, flat_two, flat_update = adamw_step(flat_master, layer_grad, flat_m, flat_v, clip_factor)
    table_one, table_two, table_update = adamw_step(table_master, table_grad, table_m, table_v, clip_factor)
    return (loss, grad_norm, flat_one, flat_two, flat_update, table_one, table_two, table_update)


def solution(mesh):
    count = mesh.devices.size
    grid = Mesh(mesh.devices.reshape(count // 8, 2, 2, 2), ALL)
    rows, matrix = P(ALL), P(ALL, None)
    in_specs = (rows,) * 6 + (matrix,) * 3
    out_specs = (P(), P()) + (rows,) * 3 + (matrix,) * 3
    return jax.shard_map(local, mesh=grid, in_specs=in_specs, out_specs=out_specs, check_vma=False)
```

```python
import math

import jax
import jax.numpy as jnp
import numpy as np
from jax import lax
from jax.sharding import Mesh, PartitionSpec as P

D = 960
QUERY_HEADS = 15
KEY_VALUE_HEADS = 5
HEAD_SIZE = 64
FF = 2560
V = 32000
PL = 256
CL = 128
STEP = 10
QKV = 1600

EPS = 1e-05
SMOOTH = 0.1
ZCOEF = 0.0001
BETA1 = 0.9
BETA2 = 0.95
ADAM_EPS = 1e-08
DECAY = 0.1
RATE = 0.03
CLIP_C = 25.0
NEGATIVE = -1e30

UNIT = 320
GAINS = 3 * D
GAIN_UNITS = GAINS // UNIT
QKV_UNITS = D * QKV // UNIT
OUT_UNITS = D * D // UNIT
GU_UNITS = D * 2 * FF // UNIT
DOWN_UNITS = FF * D // UNIT
ALL_UNITS = QKV_UNITS + OUT_UNITS + GU_UNITS + DOWN_UNITS
PLANE = ("y", "x", "c")
ALL = ("q", "y", "x", "c")
SHARE = FF // 8
LINES = D * (QKV + D + 3 * FF) // 32 // 128
EXTRA = 32
WIDE = 1024

bf16 = jnp.bfloat16
f32 = jnp.float32


def dot(left, right, left_dim=1, right_dim=0):
    return lax.dot_general(
        left, right, (((left_dim,), (right_dim,)), ((), ())), preferred_element_type=f32
    )


def hot(index, count):
    return (index[:, None] == jnp.arange(count, dtype=jnp.int32)[None, :]).astype(bf16)


def scale_of(rows):
    return lax.rsqrt(jnp.mean(rows * rows, axis=-1, keepdims=True) + EPS)


def norm_back(rows, gain, grad):
    scale = scale_of(rows)
    normed = rows * scale
    grad_gain = jnp.sum(grad * normed, axis=0)
    scaled = grad * gain
    return scale * (scaled - normed * jnp.mean(scaled * normed, axis=-1, keepdims=True)), grad_gain


def flip(rows, axes, bits, size):
    return lax.ppermute(rows, axes, [(i, i ^ bits) for i in range(size)])


def rope_tables(count):
    row = np.arange(count)
    position = np.where(row < PL, row, PL + (row - PL) % CL).astype(np.float32)
    half = np.arange(HEAD_SIZE // 2, dtype=np.float32)
    freqs = np.float32(10000.0) ** (-(half * np.float32(2.0) / np.float32(HEAD_SIZE)))
    angles = (position[:, None] * freqs[None, :].astype(np.float32)).astype(np.float64)
    angles = np.concatenate([angles, angles], axis=-1)
    return np.cos(angles).astype(np.float32), np.sin(angles).astype(np.float32)


def rotate(rows, cosine, sine):
    heads = rows.reshape(rows.shape[0], -1, HEAD_SIZE)
    half = HEAD_SIZE // 2
    turned = jnp.concatenate([-heads[..., half:], heads[..., :half]], axis=-1)
    return (heads * cosine[:, None, :] + turned * sine[:, None, :]).reshape(rows.shape)


def rotate_back(grad, cosine, sine):
    heads = grad.reshape(grad.shape[0], -1, HEAD_SIZE)
    half = HEAD_SIZE // 2
    spun = heads * sine[:, None, :]
    turned = jnp.concatenate([spun[..., half:], -spun[..., :half]], axis=-1)
    return (heads * cosine[:, None, :] + turned).reshape(grad.shape)


def adamw_step(param, gradient, moment_one, moment_two, clip_factor):
    gradient = gradient * clip_factor
    new_one = BETA1 * moment_one + (1.0 - BETA1) * gradient
    new_two = BETA2 * moment_two + (1.0 - BETA2) * gradient * gradient
    ratio = new_one / (1.0 - BETA1**STEP) / (jnp.sqrt(new_two / (1.0 - BETA2**STEP)) + ADAM_EPS)
    return (new_one, new_two, -RATE * (ratio + DECAY * param))


def pick_block(blocks, index, axis=0):
    return lax.dynamic_index_in_dim(blocks, index, axis, False)


def widen(rows):
    return jnp.pad(rows, ((0, 0), (0, WIDE - D)))


def fold_plane(left, right, right_dim):
    c_index, yx_index = lax.axis_index("c"), lax.axis_index(("y", "x"))
    rows = left.reshape(4, 2, left.shape[0] // 8, left.shape[1])
    far = pick_block(rows, 1 - c_index, 1).reshape(-1, left.shape[1])
    near = pick_block(rows, c_index, 1).reshape(-1, left.shape[1])
    got = flip(dot(far, right, 1, right_dim).astype(bf16), "c", 1, 2)
    mine = (dot(near, right, 1, right_dim) + got.astype(f32)).reshape(4, -1, WIDE)
    low = mine.astype(bf16)
    total = pick_block(mine, yx_index)
    for k in (1, 2, 3):
        total = total + flip(pick_block(low, yx_index ^ k), ("y", "x"), k, 4).astype(f32)
    return total[:, :D]


def down_pack(rows):
    side = jnp.concatenate([rows[: SHARE // 2, 640:], rows[SHARE // 2 :, 640:]], axis=1)
    return jnp.concatenate([rows[:, :640], side])


def down_unpack(rows):
    side = jnp.concatenate([rows[SHARE:, :UNIT], rows[SHARE:, UNIT:]])
    return jnp.concatenate([rows[:SHARE], side], axis=1)


def spread_plane(rows):
    return widen(lax.all_gather(rows, PLANE).reshape(-1, D))


def local(
    token_ids, loss_rows, targets, flat_master, flat_m, flat_v, table_master, table_m, table_v
):
    devices = lax.axis_size(ALL)
    rows_q = lax.axis_size("q")
    me = lax.axis_index(ALL)
    q_index = lax.axis_index("q")
    p_index = lax.axis_index(PLANE)
    c_index = lax.axis_index("c")
    yx_index = lax.axis_index(("y", "x"))
    tokens = token_ids.shape[0]
    vocab_dev = table_master.shape[0]
    loss_dev = loss_rows.shape[0]
    loss_total = loss_dev * devices
    capacity = max(2, 2 * tokens // devices)
    slots = devices * capacity
    groups = QUERY_HEADS // KEY_VALUE_HEADS
    emb_mult = math.sqrt(D) * 0.5
    shard = flat_master.shape[0]
    units = ALL_UNITS // devices
    span = units * UNIT
    drift = shard - span
    aligned = devices == 32

    place = np.array([q * 8 + kyx * 2 + kc for kc in range(2) for kyx in range(4) for q in range(rows_q)])
    rank_of = np.argsort(place)
    source_of = p_index ^ jnp.asarray(place, jnp.int32)
    order_of = jnp.take(jnp.asarray(rank_of, jnp.int32), p_index ^ jnp.arange(devices, dtype=jnp.int32))

    table_low = table_master.astype(bf16)
    owner = token_ids // vocab_dev
    owner_hot = hot(owner, devices)
    before = (lax.broadcasted_iota(jnp.int32, (tokens, tokens), 0) > lax.broadcasted_iota(jnp.int32, (tokens, tokens), 1)).astype(bf16)
    slot = jnp.sum(dot(before, owner_hot) * owner_hot.astype(f32), axis=1).astype(jnp.int32)
    spot = hot(owner * capacity + slot, slots)
    marked = token_ids + 1
    halves = jnp.stack([marked // 256, marked % 256]).astype(bf16)
    found = dot(halves, spot).astype(jnp.int32)
    requests = (found[0] * 256 + found[1] - 1).reshape(devices, capacity)
    ask = jnp.concatenate([requests, jnp.broadcast_to(targets[None], (devices, loss_dev))], axis=1)
    asked = lax.all_to_all(ask, ALL, split_axis=0, concat_axis=0, tiled=True)
    row_hot = hot(asked[:, :capacity].reshape(-1) - me * vocab_dev, vocab_dev)
    answer = dot(row_hot, table_low).astype(bf16).reshape(devices, capacity, D)

    flat_low = flat_master.astype(bf16)
    ahead = lax.ppermute(flat_low[:GAINS], ALL, [(i + 1, i) for i in range(devices - 1)])
    back = max(0, drift * (devices - 1) - GAINS)
    pieces = [flat_low, ahead]
    if back:
        pieces = [lax.ppermute(flat_low[shard - back :], ALL, [(i, i + 1) for i in range(devices - 1)])] + pieces
    chunk = lax.dynamic_slice(jnp.concatenate(pieces), (back + GAINS - drift * me,), (span,))
    if aligned:
        sent = chunk.reshape(60, 2, 8, UNIT).transpose(2, 0, 1, 3).reshape(8, 60, 2 * UNIT)
        got = lax.all_to_all(sent, PLANE, split_axis=0, concat_axis=0, tiled=True)
        first = jnp.concatenate([chunk, flat_low[:GAINS], jnp.zeros((EXTRA * 128 - GAINS,), bf16)]).reshape(LINES + EXTRA, 128)
        jumped = lax.ppermute(first, "q", [(0, 2)])
        first = jnp.where(q_index == 2, jumped, first)
        stepped = lax.ppermute(first, "q", [(0, 1), (2, 3)])
        first = jnp.where((q_index == 1) | (q_index == 3), stepped, first)
        answer, first, got = lax.optimization_barrier((answer, first, got))
        returned = lax.all_to_all(answer, ALL, split_axis=0, concat_axis=0, tiled=True).reshape(slots, D)
        level = lax.all_gather(first, PLANE)
        gains = level[0, LINES:].reshape(-1)[:GAINS].astype(f32).reshape(3, D)
        w_qkv = level[:5, :LINES].reshape(D, QKV)
        w_out = level[5:, :LINES].reshape(D, D)
        mixed = jnp.where(q_index == 3, down_pack(chunk.reshape(SHARE, D)), got.reshape(480, 2 * UNIT))
        mixed, w_qkv, w_out = lax.optimization_barrier((mixed, w_qkv, w_out))
        returned, w_qkv, w_out = lax.optimization_barrier((returned, w_qkv, w_out))
        column = lax.all_gather(mixed, "q")
        w_gu = column[1:3].reshape(D, 2 * SHARE)
        w_down = down_unpack(column[3])
    else:
        returned = lax.all_to_all(answer, ALL, split_axis=0, concat_axis=0, tiled=True).reshape(slots, D)
        extra = jnp.zeros((16 * UNIT,), bf16).at[:GAINS].set(flat_low[:GAINS])
        full = lax.all_gather(jnp.concatenate([chunk, extra]).reshape(units + 16, UNIT), ALL)
        gains = full[0, units : units + GAIN_UNITS].astype(f32).reshape(3, D)
        full = full[:, :units].reshape(ALL_UNITS, UNIT)
        edge = np.cumsum([QKV_UNITS, OUT_UNITS, GU_UNITS])
        w_qkv = full[: edge[0]].reshape(D, QKV)
        w_out = full[edge[0] : edge[1]].reshape(D, D)
        both = lax.dynamic_index_in_dim(full[edge[1] : edge[2]].reshape(D, 2, 8, UNIT), p_index, 2, False)
        w_gu = both.reshape(D, 2 * SHARE)
        w_down = lax.dynamic_index_in_dim(full[edge[2] :].reshape(8, SHARE, D), p_index, 0, False)
    w_gu = jnp.pad(w_gu, ((0, WIDE - D), (0, 0)))
    w_down = widen(w_down)
    x_low = dot(spot, returned).astype(bf16)
    x_embed = x_low.astype(f32) * emb_mult

    pick = hot(loss_rows, tokens)
    cosine, sine = (jnp.asarray(t) for t in rope_tables(tokens))
    cosine_pick, sine_pick = cosine[loss_rows], sine[loss_rows]
    h_attn = (x_embed * scale_of(x_embed) * gains[0]).astype(bf16)
    h_pick = dot(pick, h_attn).astype(bf16)
    x_pick = dot(pick, x_low) * emb_mult
    query = rotate(dot(h_pick, w_qkv[:, :D]), cosine_pick, sine_pick).astype(bf16)
    w_kv = w_qkv[:, D:]
    key_value = dot(h_attn, w_kv)
    key = rotate(key_value[:, :UNIT], cosine, sine).astype(bf16)
    value = key_value[:, UNIT:].astype(bf16)

    def heads_of(rows):
        return rows.reshape(loss_dev, KEY_VALUE_HEADS, groups, HEAD_SIZE).transpose(1, 2, 0, 3).reshape(KEY_VALUE_HEADS, groups * loss_dev, HEAD_SIZE)

    def heads_back(rows):
        return rows.reshape(KEY_VALUE_HEADS, groups, loss_dev, HEAD_SIZE).transpose(2, 0, 1, 3).reshape(loss_dev, D)

    query_h = heads_of(query)
    key_h = key.reshape(tokens, KEY_VALUE_HEADS, HEAD_SIZE).transpose(1, 0, 2)
    value_h = value.reshape(tokens, KEY_VALUE_HEADS, HEAD_SIZE).transpose(1, 0, 2)
    key_pos = jnp.arange(tokens, dtype=jnp.int32)[None, :]
    ask_pos = jnp.tile(loss_rows, groups)[:, None]
    key_seg = jnp.where(key_pos < PL, 0, 1 + (key_pos - PL) // CL)
    ask_seg = jnp.where(ask_pos < PL, 0, 1 + (ask_pos - PL) // CL)
    allowed = (key_pos <= ask_pos) & ((key_seg == 0) | (key_seg == ask_seg))
    scores = jnp.einsum("hqd,hkd->hqk", query_h, key_h, preferred_element_type=f32) * HEAD_SIZE**-0.5
    scores = jnp.where(allowed[None], scores, NEGATIVE)
    exp_scores = jnp.exp(scores - jnp.max(scores, axis=-1, keepdims=True))
    probs = exp_scores / jnp.sum(exp_scores, axis=-1, keepdims=True)
    probs_low = probs.astype(bf16)
    mixed_heads = jnp.einsum("hqk,hkd->hqd", probs_low, value_h, preferred_element_type=f32)
    attended = heads_back(mixed_heads.astype(bf16))
    x_one = x_pick + dot(attended, w_out)

    h_mlp = (x_one * scale_of(x_one) * gains[1]).astype(bf16)
    h_all = spread_plane(h_mlp)
    gate_up = dot(h_all, w_gu)
    gate, up = gate_up[:, :SHARE], gate_up[:, SHARE:]
    sig = jax.nn.sigmoid(gate)
    act = (gate * sig * up).astype(bf16)
    x_two = x_one + fold_plane(act, w_down, 0)

    hidden = (x_two * scale_of(x_two) * gains[2]).astype(bf16)
    wide_table = widen(table_low)
    across = lax.all_gather(widen(hidden), "q")
    by_x, by_y = flip(across, "x", 1, 2), flip(across, "y", 1, 2)
    cut = rows_q // 2
    corner = [flip(by_x[:cut], "y", 1, 2), flip(by_y[cut:], "x", 1, 2)]
    near = jnp.concatenate([across, by_x, by_y] + corner).reshape(loss_total // 2, WIDE)
    sides = [near, flip(near, "c", 1, 2)]
    targets_all = jnp.take(asked[:, capacity:], source_of, axis=0).reshape(2, loss_total // 2)
    logits, hits, stats = [], [], []
    for side, rows in enumerate(sides):
        z = dot(rows, wide_table, 1, 1)
        column_id = targets_all[side] - me * vocab_dev
        hit = column_id[:, None] == jnp.arange(vocab_dev, dtype=jnp.int32)[None, :]
        local_peak = jnp.max(z, axis=1)
        local_total = jnp.sum(jnp.exp(z - local_peak[:, None]), axis=1)
        local_target = jnp.sum(jnp.where(hit, z, 0.0), axis=1)
        local_sum = jnp.sum(z, axis=1)
        logits.append(z)
        hits.append(hit)
        stats.append(jnp.stack([local_peak, local_total, local_target, local_sum]))
    stats = jnp.concatenate(stats, axis=1).reshape(4, devices, loss_dev)
    stats = jnp.take(stats, order_of, axis=1).transpose(1, 0, 2)
    stats = lax.all_to_all(stats, ALL, split_axis=0, concat_axis=0, tiled=True)
    peak = jnp.max(stats[:, 0], axis=0)
    total = jnp.sum(stats[:, 1] * jnp.exp(stats[:, 0] - peak[None]), axis=0)
    my_log = peak + jnp.log(total)
    my_loss = jnp.sum(
        my_log
        - (1.0 - SMOOTH) * jnp.sum(stats[:, 2], axis=0)
        - SMOOTH / V * jnp.sum(stats[:, 3], axis=0)
        + ZCOEF * my_log * my_log
    )
    logs = lax.all_to_all(jnp.broadcast_to(my_log[None, None], (devices, 1, loss_dev)), ALL, split_axis=0, concat_axis=0, tiled=True)
    log_total = jnp.take(logs[:, 0], source_of, axis=0).reshape(2, loss_total // 2, 1)
    d_logits = [
        (
            (
                (1.0 + 2.0 * ZCOEF * log_total[side]) * jnp.exp(logits[side] - log_total[side])
                - jnp.where(hits[side], 1.0 - SMOOTH, 0.0)
                - SMOOTH / V
            )
            / loss_total
        ).astype(bf16)
        for side in (1, 0)
    ]
    got = flip(dot(d_logits[0], wide_table).astype(bf16), "c", 1, 2)
    d_hidden = (dot(d_logits[1], wide_table) + got.astype(f32)).reshape(4, rows_q, loss_dev, WIDE)
    d_low = d_hidden.astype(bf16)
    d_hidden = d_hidden[0]
    for k in (1, 2, 3):
        d_hidden = d_hidden + flip(d_low[k], ("y", "x"), k, 4).astype(f32)
    d_low = d_hidden.astype(bf16)
    total_hidden = pick_block(d_hidden, q_index)
    for k in range(1, rows_q):
        total_hidden = total_hidden + flip(pick_block(d_low, q_index ^ k), "q", k, rows_q).astype(f32)
    total_hidden = total_hidden[:, :D]
    head_grad = dot(d_logits[1], sides[0], 0, 0) + dot(d_logits[0], sides[1], 0, 0)
    head_grad, total_hidden = lax.optimization_barrier((head_grad, total_hidden))

    d_x_two, grad_final = norm_back(x_two, gains[2], total_hidden)
    d_down = spread_plane(d_x_two.astype(bf16))
    d_act = dot(d_down, w_down, 1, 1)
    d_gate = d_act * up * sig * (1.0 + gate * (1.0 - sig))
    d_gu = jnp.concatenate([d_gate, d_act * gate * sig], axis=1).astype(bf16)
    d_h_mlp = fold_plane(d_gu, w_gu, 1)
    grad_down = dot(act, d_down, 0, 0)[:, :D].astype(bf16)
    grad_gu = dot(h_all, d_gu, 0, 0)[:D].astype(bf16)
    d_x_mlp, grad_mlp = norm_back(x_one, gains[1], d_h_mlp)
    d_x_one = d_x_two + d_x_mlp

    d_branch = d_x_one.astype(bf16)
    d_attended = dot(d_branch, w_out, 1, 1)
    d_mixed = heads_of(d_attended.astype(bf16))
    d_probs = jnp.einsum("hqd,hkd->hqk", d_mixed, value_h, preferred_element_type=f32)
    delta = jnp.sum(probs * d_probs, axis=-1, keepdims=True)
    d_scores = (probs * (d_probs - delta)).astype(bf16)
    d_query = jnp.einsum("hqk,hkd->hqd", d_scores, key_h, preferred_element_type=f32) * HEAD_SIZE**-0.5
    d_key = jnp.einsum("hqk,hqd->khd", d_scores, query_h, preferred_element_type=f32) * HEAD_SIZE**-0.5
    d_value = jnp.einsum("hqk,hqd->khd", probs_low, d_mixed, preferred_element_type=f32)
    d_q = rotate_back(heads_back(d_query), cosine_pick, sine_pick).astype(bf16)
    d_k = rotate_back(d_key.reshape(tokens, UNIT), cosine, sine)
    d_kv = jnp.concatenate([d_k, d_value.reshape(tokens, UNIT)], axis=1).astype(bf16)
    d_h_pick = dot(d_q, w_qkv[:, :D], 1, 1)
    high = d_h_pick.astype(bf16)
    rest = (d_h_pick - high.astype(f32)).astype(bf16)
    d_h_attn = dot(d_kv, w_kv, 1, 1) + dot(pick, high, 0, 0) + dot(pick, rest, 0, 0)
    d_x_attn, grad_attn = norm_back(x_embed, gains[0], d_h_attn)
    high = d_x_one.astype(bf16)
    rest = (d_x_one - high.astype(f32)).astype(bf16)
    d_x_embed = d_x_attn + dot(pick, high, 0, 0) + dot(pick, rest, 0, 0)

    part = capacity // 2
    scaled = (d_x_embed * emb_mult).astype(bf16)
    sending = []
    for side in range(2):
        inside = (slot >= side * part) & (slot < (side + 1) * part)
        place_of = jnp.where(inside, owner * part + slot - side * part, -1)
        sending.append(dot(hot(place_of, devices * part), scaled, 0, 0).astype(bf16).reshape(devices, part, D))
    if aligned:
        blocks = jnp.concatenate([jnp.zeros((1, 480, 640), bf16), grad_gu.reshape(2, 480, 640), down_pack(grad_down)[None]])
        share = lax.psum_scatter(blocks, "q", scatter_dimension=0, tiled=False)
        sending, d_q, d_kv, attended = lax.optimization_barrier((sending, d_q, d_kv, attended))
        share, d_q, d_kv, attended = lax.optimization_barrier((share, d_q, d_kv, attended))
    arrived = [lax.all_to_all(rows, ALL, split_axis=0, concat_axis=0, tiled=True).reshape(-1, D) for rows in sending]
    grad_out = dot(attended, d_branch, 0, 0).astype(bf16)
    grad_qkv = jnp.concatenate([dot(h_pick, d_q, 0, 0), dot(h_attn, d_kv, 0, 0)], axis=1).astype(bf16)

    gain_grads = jnp.concatenate([grad_attn, grad_mlp, grad_final]).astype(bf16)
    if aligned:
        level = jnp.concatenate([grad_qkv.reshape(5, LINES, 128), grad_out.reshape(3, LINES, 128)])
        room = jnp.zeros((8, EXTRA * 128), bf16).at[0, :GAINS].set(gain_grads).reshape(8, EXTRA, 128)
        level = jnp.concatenate([level, room], axis=1).reshape(4, 2, LINES + EXTRA, 128)
        level, arrived[0] = lax.optimization_barrier((level, arrived[0]))
        keep = lax.dynamic_index_in_dim(level, c_index, 1, False)
        give = lax.dynamic_index_in_dim(level, 1 - c_index, 1, False)
        level = keep.astype(f32) + flip(give, "c", 1, 2).astype(f32)
        own = lax.dynamic_index_in_dim(level, yx_index, 0, False)
        for k in (1, 2, 3):
            piece = lax.dynamic_index_in_dim(level, yx_index ^ k, 0, False).astype(bf16)
            own = own + flip(piece, ("y", "x"), k, 4).astype(f32)
        own = own.reshape(4, (LINES + EXTRA) // 4, 128)
        own, share, arrived[1] = lax.optimization_barrier((own, share, arrived[1]))
        got = lax.all_to_all(share.reshape(8, 60, 640), PLANE, split_axis=0, concat_axis=0, tiled=True)
        quarter = lax.dynamic_index_in_dim(own, q_index, 0, False)
        for k in (1, 2, 3):
            piece = lax.dynamic_index_in_dim(own, q_index ^ k, 0, False).astype(bf16)
            quarter = quarter + flip(piece, "q", k, 4).astype(f32)
        quarter = quarter.astype(bf16)
        quarters = [quarter] + [lax.ppermute(quarter, "q", [(k, 0)]) for k in (1, 2, 3)]
        first = jnp.concatenate(quarters)
        gain_out = first[LINES:].reshape(-1)[:GAINS]
        first = first[:LINES].reshape(-1)
        by_share = got.reshape(8, 60, 2, UNIT).transpose(1, 2, 0, 3).reshape(-1)
        mine = jnp.where(q_index == 3, down_unpack(share).reshape(-1), by_share)
        mine = jnp.where(q_index == 0, first, mine)
    else:
        both = lax.dynamic_update_index_in_dim(jnp.zeros((D, 2, 8, UNIT), bf16), grad_gu.reshape(D, 2, UNIT), p_index, 2)
        downs = lax.dynamic_update_index_in_dim(jnp.zeros((8, SHARE, D), bf16), grad_down, p_index, 0)
        full = jnp.concatenate([part.reshape(-1, UNIT) for part in (grad_qkv, grad_out, both, downs)]).reshape(devices, units, UNIT)
        room = jnp.zeros((devices, 16, UNIT), bf16).at[0, :GAIN_UNITS].set(gain_grads.reshape(GAIN_UNITS, UNIT))
        full = jnp.concatenate([full, room], axis=1)
        summed = lax.psum_scatter(full, ALL, scatter_dimension=0, tiled=False)
        mine, gain_out = summed[:units].reshape(-1), summed[units : units + GAIN_UNITS].reshape(-1)
    behind = lax.ppermute(mine[span - GAINS :], ALL, [(i, i + 1) for i in range(devices - 1)])
    behind = jnp.where(me == 0, gain_out, behind)
    tail = max(0, drift * (devices - 1) + shard - GAINS - span)
    stream = jnp.concatenate([behind, mine, jnp.zeros((tail,), bf16)])
    layer_grad = lax.dynamic_slice(stream, (drift * me,), (shard,)).astype(f32)

    table_grad = head_grad[:, :D]
    for side in range(2):
        rows = asked[:, side * part : (side + 1) * part].reshape(-1) - me * vocab_dev
        table_grad = table_grad + dot(hot(rows, vocab_dev), arrived[side], 0, 0)
    squares = jnp.sum(layer_grad * layer_grad) + jnp.sum(table_grad * table_grad)
    sums = jnp.broadcast_to(jnp.stack([squares, my_loss])[None], (devices, 2))
    sums = jnp.sum(lax.all_to_all(sums, ALL, split_axis=0, concat_axis=0, tiled=True), axis=0)
    grad_norm = jnp.sqrt(sums[0])
    loss = sums[1] / loss_total
    limit = CLIP_C / math.sqrt(loss_total)
    clip_factor = limit / jnp.maximum(grad_norm, limit)
    flat_one, flat_two, flat_update = adamw_step(flat_master, layer_grad, flat_m, flat_v, clip_factor)
    table_one, table_two, table_update = adamw_step(table_master, table_grad, table_m, table_v, clip_factor)
    return (loss, grad_norm, flat_one, flat_two, flat_update, table_one, table_two, table_update)


def solution(mesh):
    count = mesh.devices.size
    grid = Mesh(mesh.devices.reshape(count // 8, 2, 2, 2), ALL)
    rows, matrix = P(ALL), P(ALL, None)
    in_specs = (rows,) * 6 + (matrix,) * 3
    out_specs = (P(), P()) + (rows,) * 3 + (matrix,) * 3
    return jax.shard_map(local, mesh=grid, in_specs=in_specs, out_specs=out_specs, check_vma=False)
```

```python
import math

import jax
import jax.numpy as jnp
import numpy as np
from jax import lax
from jax.sharding import Mesh, PartitionSpec as P

D = 960
QUERY_HEADS = 15
KEY_VALUE_HEADS = 5
HEAD_SIZE = 64
FF = 2560
V = 32000
PL = 256
CL = 128
STEP = 10
QKV = 1600

EPS = 1e-05
SMOOTH = 0.1
ZCOEF = 0.0001
BETA1 = 0.9
BETA2 = 0.95
ADAM_EPS = 1e-08
DECAY = 0.1
RATE = 0.03
CLIP_C = 25.0
NEGATIVE = -1e30

UNIT = 320
GAINS = 3 * D
GAIN_UNITS = GAINS // UNIT
QKV_UNITS = D * QKV // UNIT
OUT_UNITS = D * D // UNIT
GU_UNITS = D * 2 * FF // UNIT
DOWN_UNITS = FF * D // UNIT
ALL_UNITS = QKV_UNITS + OUT_UNITS + GU_UNITS + DOWN_UNITS
PLANE = ("y", "x", "c")
ALL = ("q", "y", "x", "c")
SHARE = FF // 8
TOP = D // 5
KV = QKV - D
ROOM = 32
WIDE = 1024

bf16 = jnp.bfloat16
f32 = jnp.float32


def dot(left, right, left_dim=1, right_dim=0):
    return lax.dot_general(
        left, right, (((left_dim,), (right_dim,)), ((), ())), preferred_element_type=f32
    )


def hot(index, count):
    return (index[:, None] == jnp.arange(count, dtype=jnp.int32)[None, :]).astype(bf16)


def scale_of(rows):
    return lax.rsqrt(jnp.mean(rows * rows, axis=-1, keepdims=True) + EPS)


def norm_back(rows, gain, grad):
    scale = scale_of(rows)
    normed = rows * scale
    grad_gain = jnp.sum(grad * normed, axis=0)
    scaled = grad * gain
    return scale * (scaled - normed * jnp.mean(scaled * normed, axis=-1, keepdims=True)), grad_gain


def flip(rows, axes, bits, size):
    return lax.ppermute(rows, axes, [(i, i ^ bits) for i in range(size)])


def rope_tables(count):
    row = np.arange(count)
    position = np.where(row < PL, row, PL + (row - PL) % CL).astype(np.float32)
    half = np.arange(HEAD_SIZE // 2, dtype=np.float32)
    freqs = np.float32(10000.0) ** (-(half * np.float32(2.0) / np.float32(HEAD_SIZE)))
    angles = (position[:, None] * freqs[None, :].astype(np.float32)).astype(np.float64)
    angles = np.concatenate([angles, angles], axis=-1)
    return np.cos(angles).astype(np.float32), np.sin(angles).astype(np.float32)


def rotate(rows, cosine, sine):
    heads = rows.reshape(rows.shape[0], -1, HEAD_SIZE)
    half = HEAD_SIZE // 2
    turned = jnp.concatenate([-heads[..., half:], heads[..., :half]], axis=-1)
    return (heads * cosine[:, None, :] + turned * sine[:, None, :]).reshape(rows.shape)


def rotate_back(grad, cosine, sine):
    heads = grad.reshape(grad.shape[0], -1, HEAD_SIZE)
    half = HEAD_SIZE // 2
    spun = heads * sine[:, None, :]
    turned = jnp.concatenate([spun[..., half:], -spun[..., :half]], axis=-1)
    return (heads * cosine[:, None, :] + turned).reshape(grad.shape)


def adamw_step(param, gradient, moment_one, moment_two, clip_factor):
    gradient = gradient * clip_factor
    new_one = BETA1 * moment_one + (1.0 - BETA1) * gradient
    new_two = BETA2 * moment_two + (1.0 - BETA2) * gradient * gradient
    ratio = new_one / (1.0 - BETA1**STEP) / (jnp.sqrt(new_two / (1.0 - BETA2**STEP)) + ADAM_EPS)
    return (new_one, new_two, -RATE * (ratio + DECAY * param))


def pick_block(blocks, index, axis=0):
    return lax.dynamic_index_in_dim(blocks, index, axis, False)


def widen(rows):
    return jnp.pad(rows, ((0, 0), (0, WIDE - D)))


def fold_plane(left, right, right_dim):
    c_index, yx_index = lax.axis_index("c"), lax.axis_index(("y", "x"))
    rows = left.reshape(4, 2, left.shape[0] // 8, left.shape[1])
    far = pick_block(rows, 1 - c_index, 1).reshape(-1, left.shape[1])
    near = pick_block(rows, c_index, 1).reshape(-1, left.shape[1])
    got = flip(dot(far, right, 1, right_dim).astype(bf16), "c", 1, 2)
    mine = (dot(near, right, 1, right_dim) + got.astype(f32)).reshape(4, -1, WIDE)
    low = mine.astype(bf16)
    total = pick_block(mine, yx_index)
    for k in (1, 2, 3):
        total = total + flip(pick_block(low, yx_index ^ k), ("y", "x"), k, 4).astype(f32)
    return total[:, :D]


def down_pack(rows):
    side = jnp.concatenate([rows[: SHARE // 2, 640:], rows[SHARE // 2 :, 640:]], axis=1)
    return jnp.concatenate([rows[:, :640], side])


def down_unpack(rows):
    side = jnp.concatenate([rows[SHARE:, :UNIT], rows[SHARE:, UNIT:]])
    return jnp.concatenate([rows[:SHARE], side], axis=1)


def spread_plane(rows):
    return widen(lax.all_gather(rows, PLANE).reshape(-1, D))


def local(
    token_ids, loss_rows, targets, flat_master, flat_m, flat_v, table_master, table_m, table_v
):
    devices = lax.axis_size(ALL)
    rows_q = lax.axis_size("q")
    me = lax.axis_index(ALL)
    q_index = lax.axis_index("q")
    p_index = lax.axis_index(PLANE)
    c_index = lax.axis_index("c")
    yx_index = lax.axis_index(("y", "x"))
    tokens = token_ids.shape[0]
    vocab_dev = table_master.shape[0]
    loss_dev = loss_rows.shape[0]
    loss_total = loss_dev * devices
    capacity = max(2, 2 * tokens // devices)
    slots = devices * capacity
    groups = QUERY_HEADS // KEY_VALUE_HEADS
    emb_mult = math.sqrt(D) * 0.5
    shard = flat_master.shape[0]
    units = ALL_UNITS // devices
    span = units * UNIT
    drift = shard - span
    aligned = devices == 32

    place = np.array([q * 8 + kyx * 2 + kc for kc in range(2) for kyx in range(4) for q in range(rows_q)])
    rank_of = np.argsort(place)
    source_of = p_index ^ jnp.asarray(place, jnp.int32)
    order_of = jnp.take(jnp.asarray(rank_of, jnp.int32), p_index ^ jnp.arange(devices, dtype=jnp.int32))

    table_low = table_master.astype(bf16)
    owner = token_ids // vocab_dev
    owner_hot = hot(owner, devices)
    before = (lax.broadcasted_iota(jnp.int32, (tokens, tokens), 0) > lax.broadcasted_iota(jnp.int32, (tokens, tokens), 1)).astype(bf16)
    slot = jnp.sum(dot(before, owner_hot) * owner_hot.astype(f32), axis=1).astype(jnp.int32)
    spot = hot(owner * capacity + slot, slots)
    marked = token_ids + 1
    halves = jnp.stack([marked // 256, marked % 256]).astype(bf16)
    found = dot(halves, spot).astype(jnp.int32)
    requests = (found[0] * 256 + found[1] - 1).reshape(devices, capacity)
    ask = jnp.concatenate([requests, jnp.broadcast_to(targets[None], (devices, loss_dev))], axis=1)

    flat_low = flat_master.astype(bf16)
    ahead = lax.ppermute(flat_low[:GAINS], ALL, [(i + 1, i) for i in range(devices - 1)])
    back = max(0, drift * (devices - 1) - GAINS)
    pieces = [flat_low, ahead]
    if back:
        pieces = [lax.ppermute(flat_low[shard - back :], ALL, [(i, i + 1) for i in range(devices - 1)])] + pieces
    chunk = lax.dynamic_slice(jnp.concatenate(pieces), (back + GAINS - drift * me,), (span,))
    if aligned:
        sent = chunk.reshape(60, 2, 8, UNIT).transpose(2, 0, 1, 3).reshape(8, 60, 2 * UNIT)
        got = lax.all_to_all(sent, PLANE, split_axis=0, concat_axis=0, tiled=True)
        both = chunk.reshape(TOP, QKV)
        both = jnp.concatenate([both[:, :D], both[:, D:].reshape(SHARE - TOP, D)])
        first = jnp.where(p_index < 5, both, chunk.reshape(SHARE, D))
        first = jnp.concatenate([first, flat_low[:GAINS].reshape(3, D), jnp.zeros((5, D), bf16)])
        first, ask = lax.optimization_barrier((first, ask))
        asked = lax.all_to_all(ask, ALL, split_axis=0, concat_axis=0, tiled=True)
        row_hot = hot(asked[:, :capacity].reshape(-1) - me * vocab_dev, vocab_dev)
        answer = dot(row_hot, table_low).astype(bf16).reshape(devices, capacity, D)
        jumped = lax.ppermute(first, "q", [(0, 2)])
        first = jnp.where(q_index == 2, jumped, first)
        stepped = lax.ppermute(first, "q", [(0, 1), (2, 3)])
        first = jnp.where((q_index == 1) | (q_index == 3), stepped, first)
        answer, first, got = lax.optimization_barrier((answer, first, got))
        returned = lax.all_to_all(answer, ALL, split_axis=0, concat_axis=0, tiled=True).reshape(slots, D)
        level = lax.all_gather(first, PLANE)
        mixed = jnp.where(q_index == 3, down_pack(chunk.reshape(SHARE, D)), got.reshape(480, 2 * UNIT))
        mixed, level = lax.optimization_barrier((mixed, level))
        gains = level[0, SHARE : SHARE + 3].astype(f32)
        w_q = level[:5, :TOP].reshape(D, D)
        w_kv = level[:5, TOP:SHARE].reshape(D, KV)
        w_out = level[5:, :SHARE].reshape(D, D)
        returned, w_q, w_kv, w_out = lax.optimization_barrier((returned, w_q, w_kv, w_out))
        column = lax.all_gather(mixed, "q")
    else:
        asked = lax.all_to_all(ask, ALL, split_axis=0, concat_axis=0, tiled=True)
        row_hot = hot(asked[:, :capacity].reshape(-1) - me * vocab_dev, vocab_dev)
        answer = dot(row_hot, table_low).astype(bf16).reshape(devices, capacity, D)
        returned = lax.all_to_all(answer, ALL, split_axis=0, concat_axis=0, tiled=True).reshape(slots, D)
        extra = jnp.zeros((16 * UNIT,), bf16).at[:GAINS].set(flat_low[:GAINS])
        full = lax.all_gather(jnp.concatenate([chunk, extra]).reshape(units + 16, UNIT), ALL)
        gains = full[0, units : units + GAIN_UNITS].astype(f32).reshape(3, D)
        full = full[:, :units].reshape(ALL_UNITS, UNIT)
        edge = np.cumsum([QKV_UNITS, OUT_UNITS, GU_UNITS])
        w_qkv = full[: edge[0]].reshape(D, QKV)
        w_q, w_kv = w_qkv[:, :D], w_qkv[:, D:]
        w_out = full[edge[0] : edge[1]].reshape(D, D)
        both = lax.dynamic_index_in_dim(full[edge[1] : edge[2]].reshape(D, 2, 8, UNIT), p_index, 2, False)
        w_gu = both.reshape(D, 2 * SHARE)
        w_down = lax.dynamic_index_in_dim(full[edge[2] :].reshape(8, SHARE, D), p_index, 0, False)
    x_low = dot(spot, returned).astype(bf16)
    x_embed = x_low.astype(f32) * emb_mult

    pick = hot(loss_rows, tokens)
    cosine, sine = (jnp.asarray(t) for t in rope_tables(tokens))
    cosine_pick, sine_pick = cosine[loss_rows], sine[loss_rows]
    h_attn = (x_embed * scale_of(x_embed) * gains[0]).astype(bf16)
    h_pick = dot(pick, h_attn).astype(bf16)
    x_pick = dot(pick, x_low) * emb_mult
    query = rotate(dot(h_pick, w_q), cosine_pick, sine_pick).astype(bf16)
    key_value = dot(h_attn, w_kv)
    key = rotate(key_value[:, :UNIT], cosine, sine).astype(bf16)
    value = key_value[:, UNIT:].astype(bf16)

    def heads_of(rows):
        return rows.reshape(loss_dev, KEY_VALUE_HEADS, groups, HEAD_SIZE).transpose(1, 2, 0, 3).reshape(KEY_VALUE_HEADS, groups * loss_dev, HEAD_SIZE)

    def heads_back(rows):
        return rows.reshape(KEY_VALUE_HEADS, groups, loss_dev, HEAD_SIZE).transpose(2, 0, 1, 3).reshape(loss_dev, D)

    query_h = heads_of(query)
    key_h = key.reshape(tokens, KEY_VALUE_HEADS, HEAD_SIZE).transpose(1, 0, 2)
    value_h = value.reshape(tokens, KEY_VALUE_HEADS, HEAD_SIZE).transpose(1, 0, 2)
    key_pos = jnp.arange(tokens, dtype=jnp.int32)[None, :]
    ask_pos = jnp.tile(loss_rows, groups)[:, None]
    key_seg = jnp.where(key_pos < PL, 0, 1 + (key_pos - PL) // CL)
    ask_seg = jnp.where(ask_pos < PL, 0, 1 + (ask_pos - PL) // CL)
    allowed = (key_pos <= ask_pos) & ((key_seg == 0) | (key_seg == ask_seg))
    scores = jnp.einsum("hqd,hkd->hqk", query_h, key_h, preferred_element_type=f32) * HEAD_SIZE**-0.5
    scores = jnp.where(allowed[None], scores, NEGATIVE)
    exp_scores = jnp.exp(scores - jnp.max(scores, axis=-1, keepdims=True))
    probs = exp_scores / jnp.sum(exp_scores, axis=-1, keepdims=True)
    probs_low = probs.astype(bf16)
    mixed_heads = jnp.einsum("hqk,hkd->hqd", probs_low, value_h, preferred_element_type=f32)
    attended = heads_back(mixed_heads.astype(bf16))
    x_one = x_pick + dot(attended, w_out)

    if aligned:
        column, x_one = lax.optimization_barrier((column, x_one))
        w_gu = column[1:3].reshape(D, 2 * SHARE)
        w_down = down_unpack(column[3])
    w_gu = jnp.pad(w_gu, ((0, WIDE - D), (0, 0)))
    w_down = widen(w_down)
    h_mlp = (x_one * scale_of(x_one) * gains[1]).astype(bf16)
    h_all = spread_plane(h_mlp)
    gate_up = dot(h_all, w_gu)
    gate, up = gate_up[:, :SHARE], gate_up[:, SHARE:]
    sig = jax.nn.sigmoid(gate)
    act = (gate * sig * up).astype(bf16)
    x_two = x_one + fold_plane(act, w_down, 0)

    hidden = (x_two * scale_of(x_two) * gains[2]).astype(bf16)
    wide_table = widen(table_low)
    across = lax.all_gather(widen(hidden), "q")
    by_x, by_y = flip(across, "x", 1, 2), flip(across, "y", 1, 2)
    cut = rows_q // 2
    corner = [flip(by_x[:cut], "y", 1, 2), flip(by_y[cut:], "x", 1, 2)]
    near = jnp.concatenate([across, by_x, by_y] + corner).reshape(loss_total // 2, WIDE)
    sides = [near, flip(near, "c", 1, 2)]
    targets_all = jnp.take(asked[:, capacity:], source_of, axis=0).reshape(2, loss_total // 2)
    logits, hits, stats = [], [], []
    for side, rows in enumerate(sides):
        z = dot(rows, wide_table, 1, 1)
        column_id = targets_all[side] - me * vocab_dev
        hit = column_id[:, None] == jnp.arange(vocab_dev, dtype=jnp.int32)[None, :]
        local_peak = jnp.max(z, axis=1)
        local_total = jnp.sum(jnp.exp(z - local_peak[:, None]), axis=1)
        local_target = jnp.sum(jnp.where(hit, z, 0.0), axis=1)
        local_sum = jnp.sum(z, axis=1)
        logits.append(z)
        hits.append(hit)
        stats.append(jnp.stack([local_peak, local_total, local_target, local_sum]))
    stats = jnp.concatenate(stats, axis=1).reshape(4, devices, loss_dev)
    stats = jnp.take(stats, order_of, axis=1).transpose(1, 0, 2)
    stats = lax.all_to_all(stats, ALL, split_axis=0, concat_axis=0, tiled=True)
    peak = jnp.max(stats[:, 0], axis=0)
    total = jnp.sum(stats[:, 1] * jnp.exp(stats[:, 0] - peak[None]), axis=0)
    my_log = peak + jnp.log(total)
    my_loss = jnp.sum(
        my_log
        - (1.0 - SMOOTH) * jnp.sum(stats[:, 2], axis=0)
        - SMOOTH / V * jnp.sum(stats[:, 3], axis=0)
        + ZCOEF * my_log * my_log
    )
    logs = lax.all_to_all(jnp.broadcast_to(my_log[None, None], (devices, 1, loss_dev)), ALL, split_axis=0, concat_axis=0, tiled=True)
    log_total = jnp.take(logs[:, 0], source_of, axis=0).reshape(2, loss_total // 2, 1)
    d_logits = [
        (
            (
                (1.0 + 2.0 * ZCOEF * log_total[side]) * jnp.exp(logits[side] - log_total[side])
                - jnp.where(hits[side], 1.0 - SMOOTH, 0.0)
                - SMOOTH / V
            )
            / loss_total
        ).astype(bf16)
        for side in (1, 0)
    ]
    got = flip(dot(d_logits[0], wide_table).astype(bf16), "c", 1, 2)
    d_hidden = (dot(d_logits[1], wide_table) + got.astype(f32)).reshape(4, rows_q, loss_dev, WIDE)
    d_low = d_hidden.astype(bf16)
    d_hidden = d_hidden[0]
    for k in (1, 2, 3):
        d_hidden = d_hidden + flip(d_low[k], ("y", "x"), k, 4).astype(f32)
    d_low = d_hidden.astype(bf16)
    total_hidden = pick_block(d_hidden, q_index)
    for k in range(1, rows_q):
        total_hidden = total_hidden + flip(pick_block(d_low, q_index ^ k), "q", k, rows_q).astype(f32)
    total_hidden = total_hidden[:, :D]
    head_grad = (dot(d_logits[1], sides[0], 0, 0) + dot(d_logits[0], sides[1], 0, 0))[:, :D]
    head_grad, total_hidden = lax.optimization_barrier((head_grad, total_hidden))

    d_x_two, grad_final = norm_back(x_two, gains[2], total_hidden)
    d_down = spread_plane(d_x_two.astype(bf16))
    d_act = dot(d_down, w_down, 1, 1)
    d_gate = d_act * up * sig * (1.0 + gate * (1.0 - sig))
    d_gu = jnp.concatenate([d_gate, d_act * gate * sig], axis=1).astype(bf16)
    d_h_mlp = fold_plane(d_gu, w_gu, 1)
    grad_down = dot(act, d_down, 0, 0)[:, :D].astype(bf16)
    grad_gu = dot(h_all, d_gu, 0, 0)[:D].astype(bf16)
    d_x_mlp, grad_mlp = norm_back(x_one, gains[1], d_h_mlp)
    d_x_one = d_x_two + d_x_mlp

    d_branch = d_x_one.astype(bf16)
    d_attended = dot(d_branch, w_out, 1, 1)
    d_mixed = heads_of(d_attended.astype(bf16))
    d_probs = jnp.einsum("hqd,hkd->hqk", d_mixed, value_h, preferred_element_type=f32)
    delta = jnp.sum(probs * d_probs, axis=-1, keepdims=True)
    d_scores = (probs * (d_probs - delta)).astype(bf16)
    d_query = jnp.einsum("hqk,hkd->hqd", d_scores, key_h, preferred_element_type=f32) * HEAD_SIZE**-0.5
    d_key = jnp.einsum("hqk,hqd->khd", d_scores, query_h, preferred_element_type=f32) * HEAD_SIZE**-0.5
    d_value = jnp.einsum("hqk,hqd->khd", probs_low, d_mixed, preferred_element_type=f32)
    d_q = rotate_back(heads_back(d_query), cosine_pick, sine_pick).astype(bf16)
    d_k = rotate_back(d_key.reshape(tokens, UNIT), cosine, sine)
    d_kv = jnp.concatenate([d_k, d_value.reshape(tokens, UNIT)], axis=1).astype(bf16)
    d_h_pick = dot(d_q, w_q, 1, 1)
    high = d_h_pick.astype(bf16)
    rest = (d_h_pick - high.astype(f32)).astype(bf16)
    d_h_attn = dot(d_kv, w_kv, 1, 1) + dot(pick, high, 0, 0) + dot(pick, rest, 0, 0)
    d_x_attn, grad_attn = norm_back(x_embed, gains[0], d_h_attn)
    high = d_x_one.astype(bf16)
    rest = (d_x_one - high.astype(f32)).astype(bf16)
    d_x_embed = d_x_attn + dot(pick, high, 0, 0) + dot(pick, rest, 0, 0)

    part = capacity // 2
    scaled = (d_x_embed * emb_mult).astype(bf16)
    sending = []
    for side in range(2):
        inside = (slot >= side * part) & (slot < (side + 1) * part)
        place_of = jnp.where(inside, owner * part + slot - side * part, -1)
        sending.append(dot(hot(place_of, devices * part), scaled, 0, 0).astype(bf16).reshape(devices, part, D))
    if aligned:
        blocks = jnp.concatenate([jnp.zeros((1, 480, 640), bf16), grad_gu.reshape(2, 480, 640), down_pack(grad_down)[None]])
        share = lax.psum_scatter(blocks, "q", scatter_dimension=0, tiled=False)
        sending, d_q, d_kv, attended = lax.optimization_barrier((sending, d_q, d_kv, attended))
        share, d_q, d_kv, attended = lax.optimization_barrier((share, d_q, d_kv, attended))
    arrived = [lax.all_to_all(rows, ALL, split_axis=0, concat_axis=0, tiled=True).reshape(-1, D) for rows in sending]
    grad_out = dot(attended, d_branch, 0, 0).astype(bf16)
    grad_q = dot(h_pick, d_q, 0, 0).astype(bf16)
    grad_kv = dot(h_attn, d_kv, 0, 0).astype(bf16)

    gain_grads = jnp.concatenate([grad_attn, grad_mlp, grad_final]).astype(bf16)
    if aligned:
        lower = jnp.concatenate([grad_q.reshape(5, TOP, D), grad_kv.reshape(5, SHARE - TOP, D)], axis=1)
        level = jnp.concatenate([lower, grad_out.reshape(3, SHARE, D)])
        room = jnp.zeros((8, ROOM, D), bf16).at[0, :3].set(gain_grads.reshape(3, D))
        level = jnp.concatenate([level, room], axis=1).reshape(4, 2, SHARE + ROOM, D)
        level, arrived[0] = lax.optimization_barrier((level, arrived[0]))
        keep = lax.dynamic_index_in_dim(level, c_index, 1, False)
        give = lax.dynamic_index_in_dim(level, 1 - c_index, 1, False)
        level = keep.astype(f32) + flip(give, "c", 1, 2).astype(f32)
        own = lax.dynamic_index_in_dim(level, yx_index, 0, False)
        for k in (1, 2, 3):
            piece = lax.dynamic_index_in_dim(level, yx_index ^ k, 0, False).astype(bf16)
            own = own + flip(piece, ("y", "x"), k, 4).astype(f32)
        own = own.reshape(4, (SHARE + ROOM) // 4, D)
        own, share, arrived[1] = lax.optimization_barrier((own, share, arrived[1]))
        got = lax.all_to_all(share.reshape(8, 60, 640), PLANE, split_axis=0, concat_axis=0, tiled=True)
        quarter = lax.dynamic_index_in_dim(own, q_index, 0, False)
        for k in (1, 2, 3):
            piece = lax.dynamic_index_in_dim(own, q_index ^ k, 0, False).astype(bf16)
            quarter = quarter + flip(piece, "q", k, 4).astype(f32)
        quarter = quarter.astype(bf16)
        quarters = [quarter] + [lax.ppermute(quarter, "q", [(k, 0)]) for k in (1, 2, 3)]
        first = jnp.concatenate(quarters)
        gain_out = first[SHARE : SHARE + 3].reshape(-1)
        both = jnp.concatenate([first[:TOP], first[TOP:SHARE].reshape(TOP, KV)], axis=1)
        first = jnp.where(p_index < 5, both.reshape(-1), first[:SHARE].reshape(-1))
        by_share = got.reshape(8, 60, 2, UNIT).transpose(1, 2, 0, 3).reshape(-1)
        mine = jnp.where(q_index == 3, down_unpack(share).reshape(-1), by_share)
        mine = jnp.where(q_index == 0, first, mine)
    else:
        both = lax.dynamic_update_index_in_dim(jnp.zeros((D, 2, 8, UNIT), bf16), grad_gu.reshape(D, 2, UNIT), p_index, 2)
        downs = lax.dynamic_update_index_in_dim(jnp.zeros((8, SHARE, D), bf16), grad_down, p_index, 0)
        full = jnp.concatenate([part.reshape(-1, UNIT) for part in (jnp.concatenate([grad_q, grad_kv], axis=1), grad_out, both, downs)]).reshape(devices, units, UNIT)
        room = jnp.zeros((devices, 16, UNIT), bf16).at[0, :GAIN_UNITS].set(gain_grads.reshape(GAIN_UNITS, UNIT))
        full = jnp.concatenate([full, room], axis=1)
        summed = lax.psum_scatter(full, ALL, scatter_dimension=0, tiled=False)
        mine, gain_out = summed[:units].reshape(-1), summed[units : units + GAIN_UNITS].reshape(-1)
    behind = lax.ppermute(mine[span - GAINS :], ALL, [(i, i + 1) for i in range(devices - 1)])
    behind = jnp.where(me == 0, gain_out, behind)
    tail = max(0, drift * (devices - 1) + shard - GAINS - span)
    stream = jnp.concatenate([behind, mine, jnp.zeros((tail,), bf16)])
    layer_grad = lax.dynamic_slice(stream, (drift * me,), (shard,)).astype(f32)

    table_grad = head_grad
    for side in range(2):
        rows = asked[:, side * part : (side + 1) * part].reshape(-1) - me * vocab_dev
        table_grad = table_grad + dot(hot(rows, vocab_dev), arrived[side], 0, 0)
    squares = jnp.sum(layer_grad * layer_grad) + jnp.sum(table_grad * table_grad)
    sums = jnp.broadcast_to(jnp.stack([squares, my_loss])[None], (devices, 2))
    sums = jnp.sum(lax.all_to_all(sums, ALL, split_axis=0, concat_axis=0, tiled=True), axis=0)
    grad_norm = jnp.sqrt(sums[0])
    loss = sums[1] / loss_total
    limit = CLIP_C / math.sqrt(loss_total)
    clip_factor = limit / jnp.maximum(grad_norm, limit)
    flat_one, flat_two, flat_update = adamw_step(flat_master, layer_grad, flat_m, flat_v, clip_factor)
    table_one, table_two, table_update = adamw_step(table_master, table_grad, table_m, table_v, clip_factor)
    return (loss, grad_norm, flat_one, flat_two, flat_update, table_one, table_two, table_update)


def solution(mesh):
    count = mesh.devices.size
    grid = Mesh(mesh.devices.reshape(count // 8, 2, 2, 2), ALL)
    rows, matrix = P(ALL), P(ALL, None)
    in_specs = (rows,) * 6 + (matrix,) * 3
    out_specs = (P(), P()) + (rows,) * 3 + (matrix,) * 3
    return jax.shard_map(local, mesh=grid, in_specs=in_specs, out_specs=out_specs, check_vma=False)
```

```python
import math

import jax
import jax.numpy as jnp
import numpy as np
from jax import lax
from jax.sharding import Mesh, PartitionSpec as P

D = 960
QUERY_HEADS = 15
KEY_VALUE_HEADS = 5
HEAD_SIZE = 64
FF = 2560
V = 32000
PL = 256
CL = 128
STEP = 10
QKV = 1600

EPS = 1e-05
SMOOTH = 0.1
ZCOEF = 0.0001
BETA1 = 0.9
BETA2 = 0.95
ADAM_EPS = 1e-08
DECAY = 0.1
RATE = 0.03
CLIP_C = 25.0
NEGATIVE = -1e30

UNIT = 320
GAINS = 3 * D
GAIN_UNITS = GAINS // UNIT
QKV_UNITS = D * QKV // UNIT
OUT_UNITS = D * D // UNIT
GU_UNITS = D * 2 * FF // UNIT
DOWN_UNITS = FF * D // UNIT
ALL_UNITS = QKV_UNITS + OUT_UNITS + GU_UNITS + DOWN_UNITS
PLANE = ("y", "x", "c")
ALL = ("q", "y", "x", "c")
SHARE = FF // 8
TOP = D // 5
KV = QKV - D
ROOM = 32
WIDE = 1024

bf16 = jnp.bfloat16
f32 = jnp.float32


def dot(left, right, left_dim=1, right_dim=0):
    return lax.dot_general(
        left, right, (((left_dim,), (right_dim,)), ((), ())), preferred_element_type=f32
    )


def hot(index, count):
    return (index[:, None] == jnp.arange(count, dtype=jnp.int32)[None, :]).astype(bf16)


def scale_of(rows):
    return lax.rsqrt(jnp.mean(rows * rows, axis=-1, keepdims=True) + EPS)


def norm_back(rows, gain, grad):
    scale = scale_of(rows)
    normed = rows * scale
    grad_gain = jnp.sum(grad * normed, axis=0)
    scaled = grad * gain
    return scale * (scaled - normed * jnp.mean(scaled * normed, axis=-1, keepdims=True)), grad_gain


def flip(rows, axes, bits, size):
    return lax.ppermute(rows, axes, [(i, i ^ bits) for i in range(size)])


def rope_tables(count):
    row = np.arange(count)
    position = np.where(row < PL, row, PL + (row - PL) % CL).astype(np.float32)
    half = np.arange(HEAD_SIZE // 2, dtype=np.float32)
    freqs = np.float32(10000.0) ** (-(half * np.float32(2.0) / np.float32(HEAD_SIZE)))
    angles = (position[:, None] * freqs[None, :].astype(np.float32)).astype(np.float64)
    angles = np.concatenate([angles, angles], axis=-1)
    return np.cos(angles).astype(np.float32), np.sin(angles).astype(np.float32)


def rotate(rows, cosine, sine):
    heads = rows.reshape(rows.shape[0], -1, HEAD_SIZE)
    half = HEAD_SIZE // 2
    turned = jnp.concatenate([-heads[..., half:], heads[..., :half]], axis=-1)
    return (heads * cosine[:, None, :] + turned * sine[:, None, :]).reshape(rows.shape)


def rotate_back(grad, cosine, sine):
    heads = grad.reshape(grad.shape[0], -1, HEAD_SIZE)
    half = HEAD_SIZE // 2
    spun = heads * sine[:, None, :]
    turned = jnp.concatenate([spun[..., half:], -spun[..., :half]], axis=-1)
    return (heads * cosine[:, None, :] + turned).reshape(grad.shape)


def adamw_step(param, gradient, moment_one, moment_two, clip_factor):
    gradient = gradient * clip_factor
    new_one = BETA1 * moment_one + (1.0 - BETA1) * gradient
    new_two = BETA2 * moment_two + (1.0 - BETA2) * gradient * gradient
    ratio = new_one / (1.0 - BETA1**STEP) / (jnp.sqrt(new_two / (1.0 - BETA2**STEP)) + ADAM_EPS)
    return (new_one, new_two, -RATE * (ratio + DECAY * param))


def pick_block(blocks, index, axis=0):
    return lax.dynamic_index_in_dim(blocks, index, axis, False)


def widen(rows):
    return jnp.pad(rows, ((0, 0), (0, WIDE - D)))


def fold_plane(left, right, right_dim):
    c_index, yx_index = lax.axis_index("c"), lax.axis_index(("y", "x"))
    rows = left.reshape(4, 2, left.shape[0] // 8, left.shape[1])
    far = pick_block(rows, 1 - c_index, 1).reshape(-1, left.shape[1])
    near = pick_block(rows, c_index, 1).reshape(-1, left.shape[1])
    got = flip(dot(far, right, 1, right_dim).astype(bf16), "c", 1, 2)
    mine = (dot(near, right, 1, right_dim) + got.astype(f32)).reshape(4, -1, WIDE)
    low = mine.astype(bf16)
    total = pick_block(mine, yx_index)
    for k in (1, 2, 3):
        total = total + flip(pick_block(low, yx_index ^ k), ("y", "x"), k, 4).astype(f32)
    return total[:, :D]


def down_pack(rows):
    side = jnp.concatenate([rows[: SHARE // 2, 640:], rows[SHARE // 2 :, 640:]], axis=1)
    return jnp.concatenate([rows[:, :640], side])


def down_unpack(rows):
    side = jnp.concatenate([rows[SHARE:, :UNIT], rows[SHARE:, UNIT:]])
    return jnp.concatenate([rows[:SHARE], side], axis=1)


def spread_plane(rows):
    return widen(lax.all_gather(rows, PLANE).reshape(-1, D))


def local(
    token_ids, loss_rows, targets, flat_master, flat_m, flat_v, table_master, table_m, table_v
):
    devices = lax.axis_size(ALL)
    rows_q = lax.axis_size("q")
    me = lax.axis_index(ALL)
    q_index = lax.axis_index("q")
    p_index = lax.axis_index(PLANE)
    c_index = lax.axis_index("c")
    yx_index = lax.axis_index(("y", "x"))
    tokens = token_ids.shape[0]
    vocab_dev = table_master.shape[0]
    loss_dev = loss_rows.shape[0]
    loss_total = loss_dev * devices
    capacity = max(2, 2 * tokens // devices)
    slots = devices * capacity
    groups = QUERY_HEADS // KEY_VALUE_HEADS
    emb_mult = math.sqrt(D) * 0.5
    shard = flat_master.shape[0]
    units = ALL_UNITS // devices
    span = units * UNIT
    drift = shard - span
    aligned = devices == 32

    place = np.array([q * 8 + kyx * 2 + kc for kc in range(2) for kyx in range(4) for q in range(rows_q)])
    rank_of = np.argsort(place)
    source_of = p_index ^ jnp.asarray(place, jnp.int32)
    order_of = jnp.take(jnp.asarray(rank_of, jnp.int32), p_index ^ jnp.arange(devices, dtype=jnp.int32))

    table_low = table_master.astype(bf16)
    owner = token_ids // vocab_dev
    owner_hot = hot(owner, devices)
    before = (lax.broadcasted_iota(jnp.int32, (tokens, tokens), 0) > lax.broadcasted_iota(jnp.int32, (tokens, tokens), 1)).astype(bf16)
    slot = jnp.sum(dot(before, owner_hot) * owner_hot.astype(f32), axis=1).astype(jnp.int32)
    spot = hot(owner * capacity + slot, slots)

    def spot_between(low, high):
        inside = (slot >= low) & (slot < high)
        return hot(jnp.where(inside, owner * (high - low) + slot - low, -1), devices * (high - low))

    def rows_between(low, high):
        return hot(asked[:, low:high].reshape(-1) - me * vocab_dev, vocab_dev)

    def exchange(blocks):
        return lax.all_to_all(blocks, ALL, split_axis=0, concat_axis=0, tiled=True).reshape(-1, D)

    cuts = (0, 3 * capacity // 4, capacity)
    cuts_back = (0, capacity // 4, capacity)
    marked = token_ids + 1
    halves = jnp.stack([marked // 256, marked % 256]).astype(bf16)
    found = dot(halves, spot).astype(jnp.int32)
    requests = (found[0] * 256 + found[1] - 1).reshape(devices, capacity)
    ask = jnp.concatenate([requests, jnp.broadcast_to(targets[None], (devices, loss_dev))], axis=1)

    flat_low = flat_master.astype(bf16)
    ahead = lax.ppermute(flat_low[:GAINS], ALL, [(i + 1, i) for i in range(devices - 1)])
    back = max(0, drift * (devices - 1) - GAINS)
    pieces = [flat_low, ahead]
    if back:
        pieces = [lax.ppermute(flat_low[shard - back :], ALL, [(i, i + 1) for i in range(devices - 1)])] + pieces
    chunk = lax.dynamic_slice(jnp.concatenate(pieces), (back + GAINS - drift * me,), (span,))
    if aligned:
        sent = chunk.reshape(60, 2, 8, UNIT).transpose(2, 0, 1, 3).reshape(8, 60, 2 * UNIT)
        got = lax.all_to_all(sent, PLANE, split_axis=0, concat_axis=0, tiled=True)
        both = chunk.reshape(TOP, QKV)
        both = jnp.concatenate([both[:, :D], both[:, D:].reshape(SHARE - TOP, D)])
        first = jnp.where(p_index < 5, both, chunk.reshape(SHARE, D))
        first = jnp.concatenate([first, flat_low[:GAINS].reshape(3, D), jnp.zeros((5, D), bf16)])
        first, ask = lax.optimization_barrier((first, ask))
        asked = lax.all_to_all(ask, ALL, split_axis=0, concat_axis=0, tiled=True)
        answer = [dot(rows_between(low, high), table_low).astype(bf16).reshape(devices, high - low, D) for low, high in zip(cuts, cuts[1:])]
        jumped = lax.ppermute(first, "q", [(0, 2)])
        first = jnp.where(q_index == 2, jumped, first)
        stepped = lax.ppermute(first, "q", [(0, 1), (2, 3)])
        first = jnp.where((q_index == 1) | (q_index == 3), stepped, first)
        answer, first, got = lax.optimization_barrier((answer, first, got))
        returned = [exchange(blocks) for blocks in answer]
        level = jnp.stack([first] + [flip(first, ("y", "x"), k, 4) for k in (1, 2, 3)])
        mixed = jnp.where(q_index == 3, down_pack(chunk.reshape(SHARE, D)), got.reshape(480, 2 * UNIT))
        level, returned[0] = lax.optimization_barrier((level, returned[0]))
        level = jnp.concatenate([level, flip(level, "c", 1, 2)])

        def from_place(p):
            k = p_index ^ p
            return pick_block(level, (k & 1) * 4 + (k >> 1))

        gains = from_place(0)[SHARE : SHARE + 3].astype(f32)
        w_q = jnp.concatenate([from_place(p)[:TOP] for p in range(5)])
        w_kv = jnp.concatenate([from_place(p)[TOP:SHARE] for p in range(5)]).reshape(D, KV)
        w_out = jnp.concatenate([from_place(p)[:SHARE] for p in range(5, 8)])
        returned[1], w_q, w_kv, w_out = lax.optimization_barrier((returned[1], w_q, w_kv, w_out))
        column = lax.all_gather(mixed, "q")
    else:
        asked = lax.all_to_all(ask, ALL, split_axis=0, concat_axis=0, tiled=True)
        answer = [dot(rows_between(low, high), table_low).astype(bf16).reshape(devices, high - low, D) for low, high in zip(cuts, cuts[1:])]
        returned = [exchange(blocks) for blocks in answer]
        extra = jnp.zeros((16 * UNIT,), bf16).at[:GAINS].set(flat_low[:GAINS])
        full = lax.all_gather(jnp.concatenate([chunk, extra]).reshape(units + 16, UNIT), ALL)
        gains = full[0, units : units + GAIN_UNITS].astype(f32).reshape(3, D)
        full = full[:, :units].reshape(ALL_UNITS, UNIT)
        edge = np.cumsum([QKV_UNITS, OUT_UNITS, GU_UNITS])
        w_qkv = full[: edge[0]].reshape(D, QKV)
        w_q, w_kv = w_qkv[:, :D], w_qkv[:, D:]
        w_out = full[edge[0] : edge[1]].reshape(D, D)
        both = lax.dynamic_index_in_dim(full[edge[1] : edge[2]].reshape(D, 2, 8, UNIT), p_index, 2, False)
        w_gu = both.reshape(D, 2 * SHARE)
        w_down = lax.dynamic_index_in_dim(full[edge[2] :].reshape(8, SHARE, D), p_index, 0, False)
    x_low = sum(dot(spot_between(low, high), rows) for low, high, rows in zip(cuts, cuts[1:], returned)).astype(bf16)
    x_embed = x_low.astype(f32) * emb_mult

    pick = hot(loss_rows, tokens)
    cosine, sine = (jnp.asarray(t) for t in rope_tables(tokens))
    cosine_pick, sine_pick = cosine[loss_rows], sine[loss_rows]
    h_attn = (x_embed * scale_of(x_embed) * gains[0]).astype(bf16)
    h_pick = dot(pick, h_attn).astype(bf16)
    x_pick = dot(pick, x_low) * emb_mult
    query = rotate(dot(h_pick, w_q), cosine_pick, sine_pick).astype(bf16)
    key_value = dot(h_attn, w_kv)
    if aligned:
        column, key_value = lax.optimization_barrier((column, key_value))
    key = rotate(key_value[:, :UNIT], cosine, sine).astype(bf16)
    value = key_value[:, UNIT:].astype(bf16)

    def heads_of(rows):
        return rows.reshape(loss_dev, KEY_VALUE_HEADS, groups, HEAD_SIZE).transpose(1, 2, 0, 3).reshape(KEY_VALUE_HEADS, groups * loss_dev, HEAD_SIZE)

    def heads_back(rows):
        return rows.reshape(KEY_VALUE_HEADS, groups, loss_dev, HEAD_SIZE).transpose(2, 0, 1, 3).reshape(loss_dev, D)

    query_h = heads_of(query)
    key_h = key.reshape(tokens, KEY_VALUE_HEADS, HEAD_SIZE).transpose(1, 0, 2)
    value_h = value.reshape(tokens, KEY_VALUE_HEADS, HEAD_SIZE).transpose(1, 0, 2)
    key_pos = jnp.arange(tokens, dtype=jnp.int32)[None, :]
    ask_pos = jnp.tile(loss_rows, groups)[:, None]
    key_seg = jnp.where(key_pos < PL, 0, 1 + (key_pos - PL) // CL)
    ask_seg = jnp.where(ask_pos < PL, 0, 1 + (ask_pos - PL) // CL)
    allowed = (key_pos <= ask_pos) & ((key_seg == 0) | (key_seg == ask_seg))
    scores = jnp.einsum("hqd,hkd->hqk", query_h, key_h, preferred_element_type=f32) * HEAD_SIZE**-0.5
    scores = jnp.where(allowed[None], scores, NEGATIVE)
    exp_scores = jnp.exp(scores - jnp.max(scores, axis=-1, keepdims=True))
    probs = exp_scores / jnp.sum(exp_scores, axis=-1, keepdims=True)
    probs_low = probs.astype(bf16)
    mixed_heads = jnp.einsum("hqk,hkd->hqd", probs_low, value_h, preferred_element_type=f32)
    attended = heads_back(mixed_heads.astype(bf16))
    x_one = x_pick + dot(attended, w_out)

    if aligned:
        w_gu = column[1:3].reshape(D, 2 * SHARE)
        w_down = down_unpack(column[3])
    w_gu = jnp.pad(w_gu, ((0, WIDE - D), (0, 0)))
    w_down = widen(w_down)
    h_mlp = (x_one * scale_of(x_one) * gains[1]).astype(bf16)
    h_all = spread_plane(h_mlp)
    gate_up = dot(h_all, w_gu)
    gate, up = gate_up[:, :SHARE], gate_up[:, SHARE:]
    sig = jax.nn.sigmoid(gate)
    act = (gate * sig * up).astype(bf16)
    x_two = x_one + fold_plane(act, w_down, 0)

    hidden = (x_two * scale_of(x_two) * gains[2]).astype(bf16)
    wide_table = widen(table_low)
    across = lax.all_gather(widen(hidden), "q")
    by_x, by_y = flip(across, "x", 1, 2), flip(across, "y", 1, 2)
    cut = rows_q // 2
    corner = [flip(by_x[:cut], "y", 1, 2), flip(by_y[cut:], "x", 1, 2)]
    near = jnp.concatenate([across, by_x, by_y] + corner).reshape(loss_total // 2, WIDE)
    sides = [near, flip(near, "c", 1, 2)]
    targets_all = jnp.take(asked[:, capacity:], source_of, axis=0).reshape(2, loss_total // 2)
    logits, hits, stats = [], [], []
    for side, rows in enumerate(sides):
        z = dot(rows, wide_table, 1, 1)
        column_id = targets_all[side] - me * vocab_dev
        hit = column_id[:, None] == jnp.arange(vocab_dev, dtype=jnp.int32)[None, :]
        local_peak = jnp.max(z, axis=1)
        local_total = jnp.sum(jnp.exp(z - local_peak[:, None]), axis=1)
        local_target = jnp.sum(jnp.where(hit, z, 0.0), axis=1)
        local_sum = jnp.sum(z, axis=1)
        logits.append(z)
        hits.append(hit)
        stats.append(jnp.stack([local_peak, local_total, local_target, local_sum]))
    stats = jnp.concatenate(stats, axis=1).reshape(4, devices, loss_dev)
    stats = jnp.take(stats, order_of, axis=1).transpose(1, 0, 2)
    stats = lax.all_to_all(stats, ALL, split_axis=0, concat_axis=0, tiled=True)
    peak = jnp.max(stats[:, 0], axis=0)
    total = jnp.sum(stats[:, 1] * jnp.exp(stats[:, 0] - peak[None]), axis=0)
    my_log = peak + jnp.log(total)
    my_loss = jnp.sum(
        my_log
        - (1.0 - SMOOTH) * jnp.sum(stats[:, 2], axis=0)
        - SMOOTH / V * jnp.sum(stats[:, 3], axis=0)
        + ZCOEF * my_log * my_log
    )
    logs = lax.all_to_all(jnp.broadcast_to(my_log[None, None], (devices, 1, loss_dev)), ALL, split_axis=0, concat_axis=0, tiled=True)
    log_total = jnp.take(logs[:, 0], source_of, axis=0).reshape(2, loss_total // 2, 1)
    d_logits = [
        (
            (
                (1.0 + 2.0 * ZCOEF * log_total[side]) * jnp.exp(logits[side] - log_total[side])
                - jnp.where(hits[side], 1.0 - SMOOTH, 0.0)
                - SMOOTH / V
            )
            / loss_total
        ).astype(bf16)
        for side in (1, 0)
    ]
    got = flip(dot(d_logits[0], wide_table).astype(bf16), "c", 1, 2)
    d_hidden = (dot(d_logits[1], wide_table) + got.astype(f32)).reshape(4, rows_q, loss_dev, WIDE)
    d_low = d_hidden.astype(bf16)
    d_hidden = d_hidden[0]
    for k in (1, 2, 3):
        d_hidden = d_hidden + flip(d_low[k], ("y", "x"), k, 4).astype(f32)
    d_low = d_hidden.astype(bf16)
    total_hidden = pick_block(d_hidden, q_index)
    for k in range(1, rows_q):
        total_hidden = total_hidden + flip(pick_block(d_low, q_index ^ k), "q", k, rows_q).astype(f32)
    total_hidden = total_hidden[:, :D]
    head_grad = (dot(d_logits[1], sides[0], 0, 0) + dot(d_logits[0], sides[1], 0, 0))[:, :D]
    head_grad, total_hidden = lax.optimization_barrier((head_grad, total_hidden))

    d_x_two, grad_final = norm_back(x_two, gains[2], total_hidden)
    d_down = spread_plane(d_x_two.astype(bf16))
    d_act = dot(d_down, w_down, 1, 1)
    d_gate = d_act * up * sig * (1.0 + gate * (1.0 - sig))
    d_gu = jnp.concatenate([d_gate, d_act * gate * sig], axis=1).astype(bf16)
    d_h_mlp = fold_plane(d_gu, w_gu, 1)
    grad_down = dot(act, d_down, 0, 0)[:, :D].astype(bf16)
    grad_gu = dot(h_all, d_gu, 0, 0)[:D].astype(bf16)
    d_x_mlp, grad_mlp = norm_back(x_one, gains[1], d_h_mlp)
    d_x_one = d_x_two + d_x_mlp

    d_branch = d_x_one.astype(bf16)
    d_attended = dot(d_branch, w_out, 1, 1)
    d_mixed = heads_of(d_attended.astype(bf16))
    d_probs = jnp.einsum("hqd,hkd->hqk", d_mixed, value_h, preferred_element_type=f32)
    delta = jnp.sum(probs * d_probs, axis=-1, keepdims=True)
    d_scores = (probs * (d_probs - delta)).astype(bf16)
    d_query = jnp.einsum("hqk,hkd->hqd", d_scores, key_h, preferred_element_type=f32) * HEAD_SIZE**-0.5
    d_key = jnp.einsum("hqk,hqd->khd", d_scores, query_h, preferred_element_type=f32) * HEAD_SIZE**-0.5
    d_value = jnp.einsum("hqk,hqd->khd", probs_low, d_mixed, preferred_element_type=f32)
    d_q = rotate_back(heads_back(d_query), cosine_pick, sine_pick).astype(bf16)
    d_k = rotate_back(d_key.reshape(tokens, UNIT), cosine, sine)
    d_kv = jnp.concatenate([d_k, d_value.reshape(tokens, UNIT)], axis=1).astype(bf16)
    d_h_pick = dot(d_q, w_q, 1, 1)
    high = d_h_pick.astype(bf16)
    rest = (d_h_pick - high.astype(f32)).astype(bf16)
    d_h_attn = dot(d_kv, w_kv, 1, 1) + dot(pick, high, 0, 0) + dot(pick, rest, 0, 0)
    d_x_attn, grad_attn = norm_back(x_embed, gains[0], d_h_attn)
    high = d_x_one.astype(bf16)
    rest = (d_x_one - high.astype(f32)).astype(bf16)
    d_x_embed = d_x_attn + dot(pick, high, 0, 0) + dot(pick, rest, 0, 0)

    scaled = (d_x_embed * emb_mult).astype(bf16)
    sending = [
        dot(spot_between(low, high), scaled, 0, 0).astype(bf16).reshape(devices, high - low, D)
        for low, high in zip(cuts_back, cuts_back[1:])
    ]
    if aligned:
        blocks = jnp.concatenate([jnp.zeros((1, 480, 640), bf16), grad_gu.reshape(2, 480, 640), down_pack(grad_down)[None]])
        share = lax.psum_scatter(blocks, "q", scatter_dimension=0, tiled=False)
        sending, d_q, d_kv, attended = lax.optimization_barrier((sending, d_q, d_kv, attended))
        share, d_q, d_kv, attended = lax.optimization_barrier((share, d_q, d_kv, attended))
    arrived = [exchange(blocks) for blocks in sending]
    grad_out = dot(attended, d_branch, 0, 0).astype(bf16)
    grad_q = dot(h_pick, d_q, 0, 0).astype(bf16)
    grad_kv = dot(h_attn, d_kv, 0, 0).astype(bf16)

    gain_grads = jnp.concatenate([grad_attn, grad_mlp, grad_final]).astype(bf16)
    if aligned:
        lower = jnp.concatenate([grad_q.reshape(5, TOP, D), grad_kv.reshape(5, SHARE - TOP, D)], axis=1)
        level = jnp.concatenate([lower, grad_out.reshape(3, SHARE, D)])
        room = jnp.zeros((8, ROOM, D), bf16).at[0, :3].set(gain_grads.reshape(3, D))
        level = jnp.concatenate([level, room], axis=1).reshape(4, 2, SHARE + ROOM, D)
        level, arrived[0] = lax.optimization_barrier((level, arrived[0]))
        keep = lax.dynamic_index_in_dim(level, c_index, 1, False)
        give = lax.dynamic_index_in_dim(level, 1 - c_index, 1, False)
        level = keep.astype(f32) + flip(give, "c", 1, 2).astype(f32)
        own = lax.dynamic_index_in_dim(level, yx_index, 0, False)
        for k in (1, 2, 3):
            piece = lax.dynamic_index_in_dim(level, yx_index ^ k, 0, False).astype(bf16)
            own = own + flip(piece, ("y", "x"), k, 4).astype(f32)
        own = own.reshape(4, (SHARE + ROOM) // 4, D)
        own, share, arrived[1] = lax.optimization_barrier((own, share, arrived[1]))
        got = lax.all_to_all(share.reshape(8, 60, 640), PLANE, split_axis=0, concat_axis=0, tiled=True)
        quarter = lax.dynamic_index_in_dim(own, q_index, 0, False)
        for k in (1, 2, 3):
            piece = lax.dynamic_index_in_dim(own, q_index ^ k, 0, False).astype(bf16)
            quarter = quarter + flip(piece, "q", k, 4).astype(f32)
        table_grad = head_grad
        for low, high, rows in zip(cuts_back, cuts_back[1:], arrived):
            table_grad = table_grad + dot(rows_between(low, high), rows, 0, 0)
        table_squares = jnp.sum(table_grad * table_grad)
        quarter, table_squares = lax.optimization_barrier((quarter.astype(bf16), table_squares))
        quarters = [quarter] + [lax.ppermute(quarter, "q", [(k, 0)]) for k in (1, 2, 3)]
        first = jnp.concatenate(quarters)
        gain_out = first[SHARE : SHARE + 3].reshape(-1)
        both = jnp.concatenate([first[:TOP], first[TOP:SHARE].reshape(TOP, KV)], axis=1)
        first = jnp.where(p_index < 5, both.reshape(-1), first[:SHARE].reshape(-1))
        by_share = got.reshape(8, 60, 2, UNIT).transpose(1, 2, 0, 3).reshape(-1)
        mine = jnp.where(q_index == 3, down_unpack(share).reshape(-1), by_share)
        mine = jnp.where(q_index == 0, first, mine)
    else:
        table_grad = head_grad
        for low, high, rows in zip(cuts_back, cuts_back[1:], arrived):
            table_grad = table_grad + dot(rows_between(low, high), rows, 0, 0)
        table_squares = jnp.sum(table_grad * table_grad)
        both = lax.dynamic_update_index_in_dim(jnp.zeros((D, 2, 8, UNIT), bf16), grad_gu.reshape(D, 2, UNIT), p_index, 2)
        downs = lax.dynamic_update_index_in_dim(jnp.zeros((8, SHARE, D), bf16), grad_down, p_index, 0)
        full = jnp.concatenate([part.reshape(-1, UNIT) for part in (jnp.concatenate([grad_q, grad_kv], axis=1), grad_out, both, downs)]).reshape(devices, units, UNIT)
        room = jnp.zeros((devices, 16, UNIT), bf16).at[0, :GAIN_UNITS].set(gain_grads.reshape(GAIN_UNITS, UNIT))
        full = jnp.concatenate([full, room], axis=1)
        summed = lax.psum_scatter(full, ALL, scatter_dimension=0, tiled=False)
        mine, gain_out = summed[:units].reshape(-1), summed[units : units + GAIN_UNITS].reshape(-1)
    behind = lax.ppermute(mine[span - GAINS :], ALL, [(i, i + 1) for i in range(devices - 1)])
    behind = jnp.where(me == 0, gain_out, behind)
    tail = max(0, drift * (devices - 1) + shard - GAINS - span)
    stream = jnp.concatenate([behind, mine, jnp.zeros((tail,), bf16)])
    layer_grad = lax.dynamic_slice(stream, (drift * me,), (shard,)).astype(f32)

    squares = jnp.sum(layer_grad * layer_grad) + table_squares
    sums = jnp.broadcast_to(jnp.stack([squares, my_loss])[None], (devices, 2))
    sums = jnp.sum(lax.all_to_all(sums, ALL, split_axis=0, concat_axis=0, tiled=True), axis=0)
    grad_norm = jnp.sqrt(sums[0])
    loss = sums[1] / loss_total
    limit = CLIP_C / math.sqrt(loss_total)
    clip_factor = limit / jnp.maximum(grad_norm, limit)
    flat_one, flat_two, flat_update = adamw_step(flat_master, layer_grad, flat_m, flat_v, clip_factor)
    table_one, table_two, table_update = adamw_step(table_master, table_grad, table_m, table_v, clip_factor)
    return (loss, grad_norm, flat_one, flat_two, flat_update, table_one, table_two, table_update)


def solution(mesh):
    count = mesh.devices.size
    grid = Mesh(mesh.devices.reshape(count // 8, 2, 2, 2), ALL)
    rows, matrix = P(ALL), P(ALL, None)
    in_specs = (rows,) * 6 + (matrix,) * 3
    out_specs = (P(), P()) + (rows,) * 3 + (matrix,) * 3
    return jax.shard_map(local, mesh=grid, in_specs=in_specs, out_specs=out_specs, check_vma=False)
```

```python
import math

import jax
import jax.numpy as jnp
import numpy as np
from jax import lax
from jax.sharding import Mesh, PartitionSpec as P

D = 960
QUERY_HEADS = 15
KEY_VALUE_HEADS = 5
HEAD_SIZE = 64
FF = 2560
V = 32000
PL = 256
CL = 128
STEP = 10
QKV = 1600

EPS = 1e-05
SMOOTH = 0.1
ZCOEF = 0.0001
BETA1 = 0.9
BETA2 = 0.95
ADAM_EPS = 1e-08
DECAY = 0.1
RATE = 0.03
CLIP_C = 25.0
NEGATIVE = -1e30

UNIT = 320
GAINS = 3 * D
GAIN_UNITS = GAINS // UNIT
QKV_UNITS = D * QKV // UNIT
OUT_UNITS = D * D // UNIT
GU_UNITS = D * 2 * FF // UNIT
DOWN_UNITS = FF * D // UNIT
ALL_UNITS = QKV_UNITS + OUT_UNITS + GU_UNITS + DOWN_UNITS
PLANE = ("y", "x", "c")
ALL = ("q", "y", "x", "c")
SHARE = FF // 8
TOP = D // 5
KV = QKV - D
ROOM = 32
WIDE = 1024

bf16 = jnp.bfloat16
f32 = jnp.float32


def dot(left, right, left_dim=1, right_dim=0):
    return lax.dot_general(
        left, right, (((left_dim,), (right_dim,)), ((), ())), preferred_element_type=f32
    )


def hot(index, count):
    return (index[:, None] == jnp.arange(count, dtype=jnp.int32)[None, :]).astype(bf16)


def scale_of(rows):
    return lax.rsqrt(jnp.mean(rows * rows, axis=-1, keepdims=True) + EPS)


def norm_back(rows, gain, grad):
    scale = scale_of(rows)
    normed = rows * scale
    grad_gain = jnp.sum(grad * normed, axis=0)
    scaled = grad * gain
    return scale * (scaled - normed * jnp.mean(scaled * normed, axis=-1, keepdims=True)), grad_gain


def flip(rows, axes, bits, size):
    return lax.ppermute(rows, axes, [(i, i ^ bits) for i in range(size)])


def rope_tables(count):
    row = np.arange(count)
    position = np.where(row < PL, row, PL + (row - PL) % CL).astype(np.float32)
    half = np.arange(HEAD_SIZE // 2, dtype=np.float32)
    freqs = np.float32(10000.0) ** (-(half * np.float32(2.0) / np.float32(HEAD_SIZE)))
    angles = (position[:, None] * freqs[None, :].astype(np.float32)).astype(np.float64)
    angles = np.concatenate([angles, angles], axis=-1)
    return np.cos(angles).astype(np.float32), np.sin(angles).astype(np.float32)


def rotate(rows, cosine, sine):
    heads = rows.reshape(rows.shape[0], -1, HEAD_SIZE)
    half = HEAD_SIZE // 2
    turned = jnp.concatenate([-heads[..., half:], heads[..., :half]], axis=-1)
    return (heads * cosine[:, None, :] + turned * sine[:, None, :]).reshape(rows.shape)


def rotate_back(grad, cosine, sine):
    heads = grad.reshape(grad.shape[0], -1, HEAD_SIZE)
    half = HEAD_SIZE // 2
    spun = heads * sine[:, None, :]
    turned = jnp.concatenate([spun[..., half:], -spun[..., :half]], axis=-1)
    return (heads * cosine[:, None, :] + turned).reshape(grad.shape)


def adamw_step(param, gradient, moment_one, moment_two, clip_factor):
    gradient = gradient * clip_factor
    new_one = BETA1 * moment_one + (1.0 - BETA1) * gradient
    new_two = BETA2 * moment_two + (1.0 - BETA2) * gradient * gradient
    ratio = new_one / (1.0 - BETA1**STEP) / (jnp.sqrt(new_two / (1.0 - BETA2**STEP)) + ADAM_EPS)
    return (new_one, new_two, -RATE * (ratio + DECAY * param))


def pick_block(blocks, index, axis=0):
    return lax.dynamic_index_in_dim(blocks, index, axis, False)


def widen(rows):
    return jnp.pad(rows, ((0, 0), (0, WIDE - D)))


def fold_plane(left, right, right_dim):
    c_index, yx_index = lax.axis_index("c"), lax.axis_index(("y", "x"))
    rows = left.reshape(4, 2, left.shape[0] // 8, left.shape[1])
    far = pick_block(rows, 1 - c_index, 1).reshape(-1, left.shape[1])
    near = pick_block(rows, c_index, 1).reshape(-1, left.shape[1])
    got = flip(dot(far, right, 1, right_dim).astype(bf16), "c", 1, 2)
    mine = (dot(near, right, 1, right_dim) + got.astype(f32)).reshape(4, -1, WIDE)
    low = mine.astype(bf16)
    total = pick_block(mine, yx_index)
    for k in (1, 2, 3):
        total = total + flip(pick_block(low, yx_index ^ k), ("y", "x"), k, 4).astype(f32)
    return total[:, :D]


def down_pack(rows):
    side = jnp.concatenate([rows[: SHARE // 2, 640:], rows[SHARE // 2 :, 640:]], axis=1)
    return jnp.concatenate([rows[:, :640], side])


def down_unpack(rows):
    side = jnp.concatenate([rows[SHARE:, :UNIT], rows[SHARE:, UNIT:]])
    return jnp.concatenate([rows[:SHARE], side], axis=1)


def spread_plane(rows):
    return widen(lax.all_gather(rows, PLANE).reshape(-1, D))


def local(
    token_ids, loss_rows, targets, flat_master, flat_m, flat_v, table_master, table_m, table_v
):
    devices = lax.axis_size(ALL)
    rows_q = lax.axis_size("q")
    me = lax.axis_index(ALL)
    q_index = lax.axis_index("q")
    p_index = lax.axis_index(PLANE)
    c_index = lax.axis_index("c")
    yx_index = lax.axis_index(("y", "x"))
    tokens = token_ids.shape[0]
    vocab_dev = table_master.shape[0]
    loss_dev = loss_rows.shape[0]
    loss_total = loss_dev * devices
    capacity = max(2, 2 * tokens // devices)
    slots = devices * capacity
    groups = QUERY_HEADS // KEY_VALUE_HEADS
    emb_mult = math.sqrt(D) * 0.5
    shard = flat_master.shape[0]
    units = ALL_UNITS // devices
    span = units * UNIT
    drift = shard - span
    aligned = devices == 32

    place = np.array([q * 8 + kyx * 2 + kc for kc in range(2) for kyx in range(4) for q in range(rows_q)])
    rank_of = np.argsort(place)
    source_of = p_index ^ jnp.asarray(place, jnp.int32)
    order_of = jnp.take(jnp.asarray(rank_of, jnp.int32), p_index ^ jnp.arange(devices, dtype=jnp.int32))

    table_low = table_master.astype(bf16)
    owner = token_ids // vocab_dev
    owner_hot = hot(owner, devices)
    before = (lax.broadcasted_iota(jnp.int32, (tokens, tokens), 0) > lax.broadcasted_iota(jnp.int32, (tokens, tokens), 1)).astype(bf16)
    slot = jnp.sum(dot(before, owner_hot) * owner_hot.astype(f32), axis=1).astype(jnp.int32)
    spot = hot(owner * capacity + slot, slots)

    def spot_between(low, high):
        inside = (slot >= low) & (slot < high)
        return hot(jnp.where(inside, owner * (high - low) + slot - low, -1), devices * (high - low))

    def rows_between(low, high):
        return hot(asked[:, low:high].reshape(-1) - me * vocab_dev, vocab_dev)

    def exchange(blocks):
        return lax.all_to_all(blocks, ALL, split_axis=0, concat_axis=0, tiled=True).reshape(-1, D)

    cuts = (0, 3 * capacity // 4, capacity)
    cuts_back = (0, capacity // 4, capacity)
    marked = token_ids + 1
    halves = jnp.stack([marked // 256, marked % 256]).astype(bf16)
    found = dot(halves, spot).astype(jnp.int32)
    requests = (found[0] * 256 + found[1] - 1).reshape(devices, capacity)
    ask = jnp.concatenate([requests, jnp.broadcast_to(targets[None], (devices, loss_dev))], axis=1)

    flat_low = flat_master.astype(bf16)
    ahead = lax.ppermute(flat_low[:GAINS], ALL, [(i + 1, i) for i in range(devices - 1)])
    back = max(0, drift * (devices - 1) - GAINS)
    pieces = [flat_low, ahead]
    if back:
        pieces = [lax.ppermute(flat_low[shard - back :], ALL, [(i, i + 1) for i in range(devices - 1)])] + pieces
    chunk = lax.dynamic_slice(jnp.concatenate(pieces), (back + GAINS - drift * me,), (span,))
    if aligned:
        sent = chunk.reshape(60, 2, 8, UNIT).transpose(2, 0, 1, 3).reshape(8, 60, 2 * UNIT)
        got = lax.all_to_all(sent, PLANE, split_axis=0, concat_axis=0, tiled=True)
        both = chunk.reshape(TOP, QKV)
        both = jnp.concatenate([both[:, :D], both[:, D:].reshape(SHARE - TOP, D)])
        first = jnp.where(p_index < 5, both, chunk.reshape(SHARE, D))
        first = jnp.concatenate([first, flat_low[:GAINS].reshape(3, D), jnp.zeros((5, D), bf16)])
        first, ask = lax.optimization_barrier((first, ask))
        asked = lax.all_to_all(ask, ALL, split_axis=0, concat_axis=0, tiled=True)
        answer = [dot(rows_between(low, high), table_low).astype(bf16).reshape(devices, high - low, D) for low, high in zip(cuts, cuts[1:])]
        jumped = lax.ppermute(first, "q", [(0, 2)])
        first = jnp.where(q_index == 2, jumped, first)
        stepped = lax.ppermute(first, "q", [(0, 1), (2, 3)])
        first = jnp.where((q_index == 1) | (q_index == 3), stepped, first)
        answer, first, got = lax.optimization_barrier((answer, first, got))
        returned = [exchange(blocks) for blocks in answer]
        level = lax.all_gather(first, ("y", "x"))
        mixed = jnp.where(q_index == 3, down_pack(chunk.reshape(SHARE, D)), got.reshape(480, 2 * UNIT))
        mixed, level = lax.optimization_barrier((mixed, level))
        level, returned[0] = lax.optimization_barrier((level, returned[0]))
        other = flip(level, "c", 1, 2)

        def from_place(p, low, high):
            mine, theirs = level[p // 2, low:high], other[p // 2, low:high]
            return jnp.where(c_index == p % 2, mine, theirs)

        gains = from_place(0, SHARE, SHARE + 3).astype(f32)
        w_q = jnp.concatenate([from_place(p, 0, TOP) for p in range(5)])
        w_kv = jnp.concatenate([from_place(p, TOP, SHARE) for p in range(5)]).reshape(D, KV)
        w_out = jnp.concatenate([from_place(p, 0, SHARE) for p in range(5, 8)])
        returned[1], w_q, w_kv, w_out = lax.optimization_barrier((returned[1], w_q, w_kv, w_out))
        column = lax.all_gather(mixed, "q")
    else:
        asked = lax.all_to_all(ask, ALL, split_axis=0, concat_axis=0, tiled=True)
        answer = [dot(rows_between(low, high), table_low).astype(bf16).reshape(devices, high - low, D) for low, high in zip(cuts, cuts[1:])]
        returned = [exchange(blocks) for blocks in answer]
        extra = jnp.zeros((16 * UNIT,), bf16).at[:GAINS].set(flat_low[:GAINS])
        full = lax.all_gather(jnp.concatenate([chunk, extra]).reshape(units + 16, UNIT), ALL)
        gains = full[0, units : units + GAIN_UNITS].astype(f32).reshape(3, D)
        full = full[:, :units].reshape(ALL_UNITS, UNIT)
        edge = np.cumsum([QKV_UNITS, OUT_UNITS, GU_UNITS])
        w_qkv = full[: edge[0]].reshape(D, QKV)
        w_q, w_kv = w_qkv[:, :D], w_qkv[:, D:]
        w_out = full[edge[0] : edge[1]].reshape(D, D)
        both = lax.dynamic_index_in_dim(full[edge[1] : edge[2]].reshape(D, 2, 8, UNIT), p_index, 2, False)
        w_gu = both.reshape(D, 2 * SHARE)
        w_down = lax.dynamic_index_in_dim(full[edge[2] :].reshape(8, SHARE, D), p_index, 0, False)
    x_low = sum(dot(spot_between(low, high), rows) for low, high, rows in zip(cuts, cuts[1:], returned)).astype(bf16)
    x_embed = x_low.astype(f32) * emb_mult

    pick = hot(loss_rows, tokens)
    cosine, sine = (jnp.asarray(t) for t in rope_tables(tokens))
    cosine_pick, sine_pick = cosine[loss_rows], sine[loss_rows]
    h_attn = (x_embed * scale_of(x_embed) * gains[0]).astype(bf16)
    h_pick = dot(pick, h_attn).astype(bf16)
    x_pick = dot(pick, x_low) * emb_mult
    query = rotate(dot(h_pick, w_q), cosine_pick, sine_pick).astype(bf16)
    key_value = dot(h_attn, w_kv)
    key = rotate(key_value[:, :UNIT], cosine, sine).astype(bf16)
    value = key_value[:, UNIT:].astype(bf16)

    def heads_of(rows):
        return rows.reshape(loss_dev, KEY_VALUE_HEADS, groups, HEAD_SIZE).transpose(1, 2, 0, 3).reshape(KEY_VALUE_HEADS, groups * loss_dev, HEAD_SIZE)

    def heads_back(rows):
        return rows.reshape(KEY_VALUE_HEADS, groups, loss_dev, HEAD_SIZE).transpose(2, 0, 1, 3).reshape(loss_dev, D)

    query_h = heads_of(query)
    key_h = key.reshape(tokens, KEY_VALUE_HEADS, HEAD_SIZE).transpose(1, 0, 2)
    value_h = value.reshape(tokens, KEY_VALUE_HEADS, HEAD_SIZE).transpose(1, 0, 2)
    key_pos = jnp.arange(tokens, dtype=jnp.int32)[None, :]
    ask_pos = jnp.tile(loss_rows, groups)[:, None]
    key_seg = jnp.where(key_pos < PL, 0, 1 + (key_pos - PL) // CL)
    ask_seg = jnp.where(ask_pos < PL, 0, 1 + (ask_pos - PL) // CL)
    allowed = (key_pos <= ask_pos) & ((key_seg == 0) | (key_seg == ask_seg))
    scores = jnp.einsum("hqd,hkd->hqk", query_h, key_h, preferred_element_type=f32) * HEAD_SIZE**-0.5
    scores = jnp.where(allowed[None], scores, NEGATIVE)
    exp_scores = jnp.exp(scores - jnp.max(scores, axis=-1, keepdims=True))
    probs = exp_scores / jnp.sum(exp_scores, axis=-1, keepdims=True)
    probs_low = probs.astype(bf16)
    mixed_heads = jnp.einsum("hqk,hkd->hqd", probs_low, value_h, preferred_element_type=f32)
    attended = heads_back(mixed_heads.astype(bf16))
    x_one = x_pick + dot(attended, w_out)

    if aligned:
        column, x_one = lax.optimization_barrier((column, x_one))
        w_gu = column[1:3].reshape(D, 2 * SHARE)
        w_down = down_unpack(column[3])
    w_gu = jnp.pad(w_gu, ((0, WIDE - D), (0, 0)))
    w_down = widen(w_down)
    h_mlp = (x_one * scale_of(x_one) * gains[1]).astype(bf16)
    h_all = spread_plane(h_mlp)
    gate_up = dot(h_all, w_gu)
    gate, up = gate_up[:, :SHARE], gate_up[:, SHARE:]
    sig = jax.nn.sigmoid(gate)
    act = (gate * sig * up).astype(bf16)
    x_two = x_one + fold_plane(act, w_down, 0)

    hidden = (x_two * scale_of(x_two) * gains[2]).astype(bf16)
    wide_table = widen(table_low)
    across = lax.all_gather(widen(hidden), "q")
    by_x, by_y = flip(across, "x", 1, 2), flip(across, "y", 1, 2)
    cut = rows_q // 2
    corner = [flip(by_x[:cut], "y", 1, 2), flip(by_y[cut:], "x", 1, 2)]
    near = jnp.concatenate([across, by_x, by_y] + corner).reshape(loss_total // 2, WIDE)
    sides = [near, flip(near, "c", 1, 2)]
    targets_all = jnp.take(asked[:, capacity:], source_of, axis=0).reshape(2, loss_total // 2)
    logits, hits, stats = [], [], []
    for side, rows in enumerate(sides):
        z = dot(rows, wide_table, 1, 1)
        column_id = targets_all[side] - me * vocab_dev
        hit = column_id[:, None] == jnp.arange(vocab_dev, dtype=jnp.int32)[None, :]
        local_peak = jnp.max(z, axis=1)
        local_total = jnp.sum(jnp.exp(z - local_peak[:, None]), axis=1)
        local_target = jnp.sum(jnp.where(hit, z, 0.0), axis=1)
        local_sum = jnp.sum(z, axis=1)
        logits.append(z)
        hits.append(hit)
        stats.append(jnp.stack([local_peak, local_total, local_target, local_sum]))
    stats = jnp.concatenate(stats, axis=1).reshape(4, devices, loss_dev)
    stats = jnp.take(stats, order_of, axis=1).transpose(1, 0, 2)
    stats = lax.all_to_all(stats, ALL, split_axis=0, concat_axis=0, tiled=True)
    peak = jnp.max(stats[:, 0], axis=0)
    total = jnp.sum(stats[:, 1] * jnp.exp(stats[:, 0] - peak[None]), axis=0)
    my_log = peak + jnp.log(total)
    my_loss = jnp.sum(
        my_log
        - (1.0 - SMOOTH) * jnp.sum(stats[:, 2], axis=0)
        - SMOOTH / V * jnp.sum(stats[:, 3], axis=0)
        + ZCOEF * my_log * my_log
    )
    logs = lax.all_to_all(jnp.broadcast_to(my_log[None, None], (devices, 1, loss_dev)), ALL, split_axis=0, concat_axis=0, tiled=True)
    log_total = jnp.take(logs[:, 0], source_of, axis=0).reshape(2, loss_total // 2, 1)
    d_logits = [
        (
            (
                (1.0 + 2.0 * ZCOEF * log_total[side]) * jnp.exp(logits[side] - log_total[side])
                - jnp.where(hits[side], 1.0 - SMOOTH, 0.0)
                - SMOOTH / V
            )
            / loss_total
        ).astype(bf16)
        for side in (1, 0)
    ]
    got = flip(dot(d_logits[0], wide_table).astype(bf16), "c", 1, 2)
    d_hidden = (dot(d_logits[1], wide_table) + got.astype(f32)).reshape(4, rows_q, loss_dev, WIDE)
    d_low = d_hidden.astype(bf16)
    d_hidden = d_hidden[0]
    for k in (1, 2, 3):
        d_hidden = d_hidden + flip(d_low[k], ("y", "x"), k, 4).astype(f32)
    d_low = d_hidden.astype(bf16)
    total_hidden = pick_block(d_hidden, q_index)
    for k in range(1, rows_q):
        total_hidden = total_hidden + flip(pick_block(d_low, q_index ^ k), "q", k, rows_q).astype(f32)
    total_hidden = total_hidden[:, :D]
    head_grad = (dot(d_logits[1], sides[0], 0, 0) + dot(d_logits[0], sides[1], 0, 0))[:, :D]
    head_grad, total_hidden = lax.optimization_barrier((head_grad, total_hidden))

    d_x_two, grad_final = norm_back(x_two, gains[2], total_hidden)
    d_down = spread_plane(d_x_two.astype(bf16))
    d_act = dot(d_down, w_down, 1, 1)
    d_gate = d_act * up * sig * (1.0 + gate * (1.0 - sig))
    d_gu = jnp.concatenate([d_gate, d_act * gate * sig], axis=1).astype(bf16)
    d_h_mlp = fold_plane(d_gu, w_gu, 1)
    grad_down = dot(act, d_down, 0, 0)[:, :D].astype(bf16)
    grad_gu = dot(h_all, d_gu, 0, 0)[:D].astype(bf16)
    d_x_mlp, grad_mlp = norm_back(x_one, gains[1], d_h_mlp)
    d_x_one = d_x_two + d_x_mlp

    d_branch = d_x_one.astype(bf16)
    d_attended = dot(d_branch, w_out, 1, 1)
    d_mixed = heads_of(d_attended.astype(bf16))
    d_probs = jnp.einsum("hqd,hkd->hqk", d_mixed, value_h, preferred_element_type=f32)
    delta = jnp.sum(probs * d_probs, axis=-1, keepdims=True)
    d_scores = (probs * (d_probs - delta)).astype(bf16)
    d_query = jnp.einsum("hqk,hkd->hqd", d_scores, key_h, preferred_element_type=f32) * HEAD_SIZE**-0.5
    d_key = jnp.einsum("hqk,hqd->khd", d_scores, query_h, preferred_element_type=f32) * HEAD_SIZE**-0.5
    d_value = jnp.einsum("hqk,hqd->khd", probs_low, d_mixed, preferred_element_type=f32)
    d_q = rotate_back(heads_back(d_query), cosine_pick, sine_pick).astype(bf16)
    d_k = rotate_back(d_key.reshape(tokens, UNIT), cosine, sine)
    d_kv = jnp.concatenate([d_k, d_value.reshape(tokens, UNIT)], axis=1).astype(bf16)
    d_h_pick = dot(d_q, w_q, 1, 1)
    high = d_h_pick.astype(bf16)
    rest = (d_h_pick - high.astype(f32)).astype(bf16)
    d_h_attn = dot(d_kv, w_kv, 1, 1) + dot(pick, high, 0, 0) + dot(pick, rest, 0, 0)
    d_x_attn, grad_attn = norm_back(x_embed, gains[0], d_h_attn)
    high = d_x_one.astype(bf16)
    rest = (d_x_one - high.astype(f32)).astype(bf16)
    d_x_embed = d_x_attn + dot(pick, high, 0, 0) + dot(pick, rest, 0, 0)

    scaled = (d_x_embed * emb_mult).astype(bf16)
    sending = [
        dot(spot_between(low, high), scaled, 0, 0).astype(bf16).reshape(devices, high - low, D)
        for low, high in zip(cuts_back, cuts_back[1:])
    ]
    if aligned:
        blocks = jnp.concatenate([jnp.zeros((1, 480, 640), bf16), grad_gu.reshape(2, 480, 640), down_pack(grad_down)[None]])
        share = lax.psum_scatter(blocks, "q", scatter_dimension=0, tiled=False)
        sending, d_q, d_kv, attended = lax.optimization_barrier((sending, d_q, d_kv, attended))
        share, d_q, d_kv, attended = lax.optimization_barrier((share, d_q, d_kv, attended))
    arrived = [exchange(blocks) for blocks in sending]
    grad_out = dot(attended, d_branch, 0, 0).astype(bf16)
    grad_q = dot(h_pick, d_q, 0, 0).astype(bf16)
    grad_kv = dot(h_attn, d_kv, 0, 0).astype(bf16)

    gain_grads = jnp.concatenate([grad_attn, grad_mlp, grad_final]).astype(bf16)
    if aligned:
        lower = jnp.concatenate([grad_q.reshape(5, TOP, D), grad_kv.reshape(5, SHARE - TOP, D)], axis=1)
        level = jnp.concatenate([lower, grad_out.reshape(3, SHARE, D)])
        room = jnp.zeros((8, ROOM, D), bf16).at[0, :3].set(gain_grads.reshape(3, D))
        level = jnp.concatenate([level, room], axis=1).reshape(4, 2, SHARE + ROOM, D)
        level, arrived[0] = lax.optimization_barrier((level, arrived[0]))
        keep = lax.dynamic_index_in_dim(level, c_index, 1, False)
        give = lax.dynamic_index_in_dim(level, 1 - c_index, 1, False)
        level = keep.astype(f32) + flip(give, "c", 1, 2).astype(f32)
        own = lax.dynamic_index_in_dim(level, yx_index, 0, False)
        for k in (1, 2, 3):
            piece = lax.dynamic_index_in_dim(level, yx_index ^ k, 0, False).astype(bf16)
            own = own + flip(piece, ("y", "x"), k, 4).astype(f32)
        own = own.reshape(4, (SHARE + ROOM) // 4, D)
        own, share, arrived[1] = lax.optimization_barrier((own, share, arrived[1]))
        got = lax.all_to_all(share.reshape(8, 60, 640), PLANE, split_axis=0, concat_axis=0, tiled=True)
        quarter = lax.dynamic_index_in_dim(own, q_index, 0, False)
        for k in (1, 2, 3):
            piece = lax.dynamic_index_in_dim(own, q_index ^ k, 0, False).astype(bf16)
            quarter = quarter + flip(piece, "q", k, 4).astype(f32)
        table_grad = head_grad
        for low, high, rows in zip(cuts_back, cuts_back[1:], arrived):
            table_grad = table_grad + dot(rows_between(low, high), rows, 0, 0)
        table_squares = jnp.sum(table_grad * table_grad)
        quarter = quarter.astype(bf16)
        squares = jnp.sum(quarter.astype(f32) ** 2) + jnp.sum(share.astype(f32) ** 2) + table_squares
        quarter, squares = lax.optimization_barrier((quarter, squares))
        quarters = [quarter] + [lax.ppermute(quarter, "q", [(k, 0)]) for k in (1, 2, 3)]
        first = jnp.concatenate(quarters)
        gain_out = first[SHARE : SHARE + 3].reshape(-1)
        both = jnp.concatenate([first[:TOP], first[TOP:SHARE].reshape(TOP, KV)], axis=1)
        first = jnp.where(p_index < 5, both.reshape(-1), first[:SHARE].reshape(-1))
        by_share = got.reshape(8, 60, 2, UNIT).transpose(1, 2, 0, 3).reshape(-1)
        mine = jnp.where(q_index == 3, down_unpack(share).reshape(-1), by_share)
        mine = jnp.where(q_index == 0, first, mine)
    else:
        table_grad = head_grad
        for low, high, rows in zip(cuts_back, cuts_back[1:], arrived):
            table_grad = table_grad + dot(rows_between(low, high), rows, 0, 0)
        table_squares = jnp.sum(table_grad * table_grad)
        both = lax.dynamic_update_index_in_dim(jnp.zeros((D, 2, 8, UNIT), bf16), grad_gu.reshape(D, 2, UNIT), p_index, 2)
        downs = lax.dynamic_update_index_in_dim(jnp.zeros((8, SHARE, D), bf16), grad_down, p_index, 0)
        full = jnp.concatenate([part.reshape(-1, UNIT) for part in (jnp.concatenate([grad_q, grad_kv], axis=1), grad_out, both, downs)]).reshape(devices, units, UNIT)
        room = jnp.zeros((devices, 16, UNIT), bf16).at[0, :GAIN_UNITS].set(gain_grads.reshape(GAIN_UNITS, UNIT))
        full = jnp.concatenate([full, room], axis=1)
        summed = lax.psum_scatter(full, ALL, scatter_dimension=0, tiled=False)
        mine, gain_out = summed[:units].reshape(-1), summed[units : units + GAIN_UNITS].reshape(-1)
    behind = lax.ppermute(mine[span - GAINS :], ALL, [(i, i + 1) for i in range(devices - 1)])
    behind = jnp.where(me == 0, gain_out, behind)
    tail = max(0, drift * (devices - 1) + shard - GAINS - span)
    stream = jnp.concatenate([behind, mine, jnp.zeros((tail,), bf16)])
    layer_grad = lax.dynamic_slice(stream, (drift * me,), (shard,)).astype(f32)

    if not aligned:
        squares = jnp.sum(layer_grad * layer_grad) + table_squares
    sums = jnp.broadcast_to(jnp.stack([squares, my_loss])[None], (devices, 2))
    sums = jnp.sum(lax.all_to_all(sums, ALL, split_axis=0, concat_axis=0, tiled=True), axis=0)
    grad_norm = jnp.sqrt(sums[0])
    loss = sums[1] / loss_total
    limit = CLIP_C / math.sqrt(loss_total)
    clip_factor = limit / jnp.maximum(grad_norm, limit)
    flat_one, flat_two, flat_update = adamw_step(flat_master, layer_grad, flat_m, flat_v, clip_factor)
    table_one, table_two, table_update = adamw_step(table_master, table_grad, table_m, table_v, clip_factor)
    return (loss, grad_norm, flat_one, flat_two, flat_update, table_one, table_two, table_update)


def solution(mesh):
    count = mesh.devices.size
    grid = Mesh(mesh.devices.reshape(count // 8, 2, 2, 2), ALL)
    rows, matrix = P(ALL), P(ALL, None)
    in_specs = (rows,) * 6 + (matrix,) * 3
    out_specs = (P(), P()) + (rows,) * 3 + (matrix,) * 3
    return jax.shard_map(local, mesh=grid, in_specs=in_specs, out_specs=out_specs, check_vma=False)
```

```python
import math

import jax
import jax.numpy as jnp
import numpy as np
from jax import lax
from jax.sharding import Mesh, PartitionSpec as P

D = 960
QUERY_HEADS = 15
KEY_VALUE_HEADS = 5
HEAD_SIZE = 64
FF = 2560
V = 32000
PL = 256
CL = 128
STEP = 10
QKV = 1600

EPS = 1e-05
SMOOTH = 0.1
ZCOEF = 0.0001
BETA1 = 0.9
BETA2 = 0.95
ADAM_EPS = 1e-08
DECAY = 0.1
RATE = 0.03
CLIP_C = 25.0
NEGATIVE = -1e30

UNIT = 320
GAINS = 3 * D
GAIN_UNITS = GAINS // UNIT
QKV_UNITS = D * QKV // UNIT
OUT_UNITS = D * D // UNIT
GU_UNITS = D * 2 * FF // UNIT
DOWN_UNITS = FF * D // UNIT
ALL_UNITS = QKV_UNITS + OUT_UNITS + GU_UNITS + DOWN_UNITS
PLANE = ("y", "x", "c")
ALL = ("q", "y", "x", "c")
SHARE = FF // 8
TOP = D // 5
KV = QKV - D
ROOM = 32
WIDE = 1024

bf16 = jnp.bfloat16
f32 = jnp.float32


def dot(left, right, left_dim=1, right_dim=0):
    return lax.dot_general(
        left, right, (((left_dim,), (right_dim,)), ((), ())), preferred_element_type=f32
    )


def hot(index, count):
    return (index[:, None] == jnp.arange(count, dtype=jnp.int32)[None, :]).astype(bf16)


def scale_of(rows):
    return lax.rsqrt(jnp.mean(rows * rows, axis=-1, keepdims=True) + EPS)


def norm_back(rows, gain, grad):
    scale = scale_of(rows)
    normed = rows * scale
    grad_gain = jnp.sum(grad * normed, axis=0)
    scaled = grad * gain
    return scale * (scaled - normed * jnp.mean(scaled * normed, axis=-1, keepdims=True)), grad_gain


def flip(rows, axes, bits, size):
    return lax.ppermute(rows, axes, [(i, i ^ bits) for i in range(size)])


def rope_tables(count):
    row = np.arange(count)
    position = np.where(row < PL, row, PL + (row - PL) % CL).astype(np.float32)
    half = np.arange(HEAD_SIZE // 2, dtype=np.float32)
    freqs = np.float32(10000.0) ** (-(half * np.float32(2.0) / np.float32(HEAD_SIZE)))
    angles = (position[:, None] * freqs[None, :].astype(np.float32)).astype(np.float64)
    angles = np.concatenate([angles, angles], axis=-1)
    return np.cos(angles).astype(np.float32), np.sin(angles).astype(np.float32)


def rotate(rows, cosine, sine):
    heads = rows.reshape(rows.shape[0], -1, HEAD_SIZE)
    half = HEAD_SIZE // 2
    turned = jnp.concatenate([-heads[..., half:], heads[..., :half]], axis=-1)
    return (heads * cosine[:, None, :] + turned * sine[:, None, :]).reshape(rows.shape)


def rotate_back(grad, cosine, sine):
    heads = grad.reshape(grad.shape[0], -1, HEAD_SIZE)
    half = HEAD_SIZE // 2
    spun = heads * sine[:, None, :]
    turned = jnp.concatenate([spun[..., half:], -spun[..., :half]], axis=-1)
    return (heads * cosine[:, None, :] + turned).reshape(grad.shape)


def adamw_step(param, gradient, moment_one, moment_two, clip_factor):
    gradient = gradient * clip_factor
    new_one = BETA1 * moment_one + (1.0 - BETA1) * gradient
    new_two = BETA2 * moment_two + (1.0 - BETA2) * gradient * gradient
    ratio = new_one / (1.0 - BETA1**STEP) / (jnp.sqrt(new_two / (1.0 - BETA2**STEP)) + ADAM_EPS)
    return (new_one, new_two, -RATE * (ratio + DECAY * param))


def pick_block(blocks, index, axis=0):
    return lax.dynamic_index_in_dim(blocks, index, axis, False)


def widen(rows):
    return jnp.pad(rows, ((0, 0), (0, WIDE - D)))


def fold_plane(left, right, right_dim):
    c_index, yx_index = lax.axis_index("c"), lax.axis_index(("y", "x"))
    rows = left.reshape(4, 2, left.shape[0] // 8, left.shape[1])
    far = pick_block(rows, 1 - c_index, 1).reshape(-1, left.shape[1])
    near = pick_block(rows, c_index, 1).reshape(-1, left.shape[1])
    got = flip(dot(far, right, 1, right_dim).astype(bf16), "c", 1, 2)
    mine = (dot(near, right, 1, right_dim) + got.astype(f32)).reshape(4, -1, WIDE)
    low = mine.astype(bf16)
    total = pick_block(mine, yx_index)
    for k in (1, 2, 3):
        total = total + flip(pick_block(low, yx_index ^ k), ("y", "x"), k, 4).astype(f32)
    return total[:, :D]


def down_pack(rows):
    side = jnp.concatenate([rows[: SHARE // 2, 640:], rows[SHARE // 2 :, 640:]], axis=1)
    return jnp.concatenate([rows[:, :640], side])


def down_unpack(rows):
    side = jnp.concatenate([rows[SHARE:, :UNIT], rows[SHARE:, UNIT:]])
    return jnp.concatenate([rows[:SHARE], side], axis=1)


def spread_plane(rows):
    return widen(lax.all_gather(rows, PLANE).reshape(-1, D))


def local(
    token_ids, loss_rows, targets, flat_master, flat_m, flat_v, table_master, table_m, table_v
):
    devices = lax.axis_size(ALL)
    rows_q = lax.axis_size("q")
    me = lax.axis_index(ALL)
    q_index = lax.axis_index("q")
    p_index = lax.axis_index(PLANE)
    c_index = lax.axis_index("c")
    yx_index = lax.axis_index(("y", "x"))
    tokens = token_ids.shape[0]
    vocab_dev = table_master.shape[0]
    loss_dev = loss_rows.shape[0]
    loss_total = loss_dev * devices
    capacity = max(2, 2 * tokens // devices)
    slots = devices * capacity
    groups = QUERY_HEADS // KEY_VALUE_HEADS
    emb_mult = math.sqrt(D) * 0.5
    shard = flat_master.shape[0]
    units = ALL_UNITS // devices
    span = units * UNIT
    drift = shard - span
    aligned = devices == 32

    place = np.array([q * 8 + kyx * 2 + kc for kc in range(2) for kyx in range(4) for q in range(rows_q)])
    rank_of = np.argsort(place)
    source_of = p_index ^ jnp.asarray(place, jnp.int32)
    order_of = jnp.take(jnp.asarray(rank_of, jnp.int32), p_index ^ jnp.arange(devices, dtype=jnp.int32))

    table_low = table_master.astype(bf16)
    owner = token_ids // vocab_dev
    owner_hot = hot(owner, devices)
    before = (lax.broadcasted_iota(jnp.int32, (tokens, tokens), 0) > lax.broadcasted_iota(jnp.int32, (tokens, tokens), 1)).astype(bf16)
    slot = jnp.sum(dot(before, owner_hot) * owner_hot.astype(f32), axis=1).astype(jnp.int32)
    spot = hot(owner * capacity + slot, slots)

    def spot_between(low, high):
        inside = (slot >= low) & (slot < high)
        return hot(jnp.where(inside, owner * (high - low) + slot - low, -1), devices * (high - low))

    def rows_between(low, high):
        return hot(asked[:, low:high].reshape(-1) - me * vocab_dev, vocab_dev)

    def exchange(blocks):
        return lax.all_to_all(blocks, ALL, split_axis=0, concat_axis=0, tiled=True).reshape(-1, D)

    cuts_back = (0, capacity // 4, capacity)
    marked = token_ids + 1
    halves = jnp.stack([marked // 256, marked % 256]).astype(bf16)
    found = dot(halves, spot).astype(jnp.int32)
    requests = (found[0] * 256 + found[1] - 1).reshape(devices, capacity)
    ask = jnp.concatenate([requests, jnp.broadcast_to(targets[None], (devices, loss_dev))], axis=1)

    flat_low = flat_master.astype(bf16)
    ahead = lax.ppermute(flat_low[:GAINS], ALL, [(i + 1, i) for i in range(devices - 1)])
    back = max(0, drift * (devices - 1) - GAINS)
    pieces = [flat_low, ahead]
    if back:
        pieces = [lax.ppermute(flat_low[shard - back :], ALL, [(i, i + 1) for i in range(devices - 1)])] + pieces
    chunk = lax.dynamic_slice(jnp.concatenate(pieces), (back + GAINS - drift * me,), (span,))
    if aligned:
        sent = chunk.reshape(60, 2, 8, UNIT).transpose(2, 0, 1, 3).reshape(8, 60, 2 * UNIT)
        got = lax.all_to_all(sent, PLANE, split_axis=0, concat_axis=0, tiled=True)
        both = chunk.reshape(TOP, QKV)
        both = jnp.concatenate([both[:, :D], both[:, D:].reshape(SHARE - TOP, D)])
        first = jnp.where(p_index < 5, both, chunk.reshape(SHARE, D))
        first = jnp.concatenate([first, flat_low[:GAINS].reshape(3, D), jnp.zeros((5, D), bf16)])
        first, ask = lax.optimization_barrier((first, ask))
        asked = lax.all_to_all(ask, ALL, split_axis=0, concat_axis=0, tiled=True)
        answer = dot(rows_between(0, capacity), table_low).astype(bf16).reshape(devices, capacity, D)
        jumped = lax.ppermute(first, "q", [(0, 2)])
        first = jnp.where(q_index == 2, jumped, first)
        stepped = lax.ppermute(first, "q", [(0, 1), (2, 3)])
        first = jnp.where((q_index == 1) | (q_index == 3), stepped, first)
        answer, first, got = lax.optimization_barrier((answer, first, got))
        returned = exchange(answer)
        level = lax.all_gather(first, PLANE)
        mixed = jnp.where(q_index == 3, down_pack(chunk.reshape(SHARE, D)), got.reshape(480, 2 * UNIT))
        mixed, level = lax.optimization_barrier((mixed, level))
        gains = level[0, SHARE : SHARE + 3].astype(f32)
        w_q = level[:5, :TOP].reshape(D, D)
        w_kv = level[:5, TOP:SHARE].reshape(D, KV)
        w_out = level[5:, :SHARE].reshape(D, D)
        returned, w_q, w_kv, w_out = lax.optimization_barrier((returned, w_q, w_kv, w_out))
        column = lax.all_gather(mixed, "q")
    else:
        asked = lax.all_to_all(ask, ALL, split_axis=0, concat_axis=0, tiled=True)
        answer = dot(rows_between(0, capacity), table_low).astype(bf16).reshape(devices, capacity, D)
        returned = exchange(answer)
        extra = jnp.zeros((16 * UNIT,), bf16).at[:GAINS].set(flat_low[:GAINS])
        full = lax.all_gather(jnp.concatenate([chunk, extra]).reshape(units + 16, UNIT), ALL)
        gains = full[0, units : units + GAIN_UNITS].astype(f32).reshape(3, D)
        full = full[:, :units].reshape(ALL_UNITS, UNIT)
        edge = np.cumsum([QKV_UNITS, OUT_UNITS, GU_UNITS])
        w_qkv = full[: edge[0]].reshape(D, QKV)
        w_q, w_kv = w_qkv[:, :D], w_qkv[:, D:]
        w_out = full[edge[0] : edge[1]].reshape(D, D)
        both = lax.dynamic_index_in_dim(full[edge[1] : edge[2]].reshape(D, 2, 8, UNIT), p_index, 2, False)
        w_gu = both.reshape(D, 2 * SHARE)
        w_down = lax.dynamic_index_in_dim(full[edge[2] :].reshape(8, SHARE, D), p_index, 0, False)
    x_low = dot(spot, returned).astype(bf16)
    x_embed = x_low.astype(f32) * emb_mult

    pick = hot(loss_rows, tokens)
    cosine, sine = (jnp.asarray(t) for t in rope_tables(tokens))
    cosine_pick, sine_pick = cosine[loss_rows], sine[loss_rows]
    h_attn = (x_embed * scale_of(x_embed) * gains[0]).astype(bf16)
    h_pick = dot(pick, h_attn).astype(bf16)
    x_pick = dot(pick, x_low) * emb_mult
    query = rotate(dot(h_pick, w_q), cosine_pick, sine_pick).astype(bf16)
    key_value = dot(h_attn, w_kv)
    key = rotate(key_value[:, :UNIT], cosine, sine).astype(bf16)
    value = key_value[:, UNIT:].astype(bf16)

    def heads_of(rows):
        return rows.reshape(loss_dev, KEY_VALUE_HEADS, groups, HEAD_SIZE).transpose(1, 2, 0, 3).reshape(KEY_VALUE_HEADS, groups * loss_dev, HEAD_SIZE)

    def heads_back(rows):
        return rows.reshape(KEY_VALUE_HEADS, groups, loss_dev, HEAD_SIZE).transpose(2, 0, 1, 3).reshape(loss_dev, D)

    query_h = heads_of(query)
    key_h = key.reshape(tokens, KEY_VALUE_HEADS, HEAD_SIZE).transpose(1, 0, 2)
    value_h = value.reshape(tokens, KEY_VALUE_HEADS, HEAD_SIZE).transpose(1, 0, 2)
    key_pos = jnp.arange(tokens, dtype=jnp.int32)[None, :]
    ask_pos = jnp.tile(loss_rows, groups)[:, None]
    key_seg = jnp.where(key_pos < PL, 0, 1 + (key_pos - PL) // CL)
    ask_seg = jnp.where(ask_pos < PL, 0, 1 + (ask_pos - PL) // CL)
    allowed = (key_pos <= ask_pos) & ((key_seg == 0) | (key_seg == ask_seg))
    scores = jnp.einsum("hqd,hkd->hqk", query_h, key_h, preferred_element_type=f32) * HEAD_SIZE**-0.5
    scores = jnp.where(allowed[None], scores, NEGATIVE)
    exp_scores = jnp.exp(scores - jnp.max(scores, axis=-1, keepdims=True))
    probs = exp_scores / jnp.sum(exp_scores, axis=-1, keepdims=True)
    probs_low = probs.astype(bf16)
    mixed_heads = jnp.einsum("hqk,hkd->hqd", probs_low, value_h, preferred_element_type=f32)
    attended = heads_back(mixed_heads.astype(bf16))
    x_one = x_pick + dot(attended, w_out)

    h_mlp = (x_one * scale_of(x_one) * gains[1]).astype(bf16)
    h_all = spread_plane(h_mlp)
    if aligned:
        column, h_all = lax.optimization_barrier((column, h_all))
        w_gu = column[1:3].reshape(D, 2 * SHARE)
        w_down = down_unpack(column[3])
    w_gu = jnp.pad(w_gu, ((0, WIDE - D), (0, 0)))
    w_down = widen(w_down)
    gate_up = dot(h_all, w_gu)
    gate, up = gate_up[:, :SHARE], gate_up[:, SHARE:]
    sig = jax.nn.sigmoid(gate)
    act = (gate * sig * up).astype(bf16)
    x_two = x_one + fold_plane(act, w_down, 0)

    hidden = (x_two * scale_of(x_two) * gains[2]).astype(bf16)
    wide_table = widen(table_low)
    across = lax.all_gather(widen(hidden), "q")
    by_x, by_y = flip(across, "x", 1, 2), flip(across, "y", 1, 2)
    cut = rows_q // 2
    corner = [flip(by_x[:cut], "y", 1, 2), flip(by_y[cut:], "x", 1, 2)]
    near = jnp.concatenate([across, by_x, by_y] + corner).reshape(loss_total // 2, WIDE)
    sides = [near, flip(near, "c", 1, 2)]
    targets_all = jnp.take(asked[:, capacity:], source_of, axis=0).reshape(2, loss_total // 2)
    logits, hits, stats = [], [], []
    for side, rows in enumerate(sides):
        z = dot(rows, wide_table, 1, 1)
        column_id = targets_all[side] - me * vocab_dev
        hit = column_id[:, None] == jnp.arange(vocab_dev, dtype=jnp.int32)[None, :]
        local_peak = jnp.max(z, axis=1)
        local_total = jnp.sum(jnp.exp(z - local_peak[:, None]), axis=1)
        local_target = jnp.sum(jnp.where(hit, z, 0.0), axis=1)
        local_sum = jnp.sum(z, axis=1)
        logits.append(z)
        hits.append(hit)
        stats.append(jnp.stack([local_peak, local_total, local_target, local_sum]))
    stats = jnp.concatenate(stats, axis=1).reshape(4, devices, loss_dev)
    stats = jnp.take(stats, order_of, axis=1).transpose(1, 0, 2)
    stats = lax.all_to_all(stats, ALL, split_axis=0, concat_axis=0, tiled=True)
    peak = jnp.max(stats[:, 0], axis=0)
    total = jnp.sum(stats[:, 1] * jnp.exp(stats[:, 0] - peak[None]), axis=0)
    my_log = peak + jnp.log(total)
    my_loss = jnp.sum(
        my_log
        - (1.0 - SMOOTH) * jnp.sum(stats[:, 2], axis=0)
        - SMOOTH / V * jnp.sum(stats[:, 3], axis=0)
        + ZCOEF * my_log * my_log
    )
    logs = lax.all_to_all(jnp.broadcast_to(my_log[None, None], (devices, 1, loss_dev)), ALL, split_axis=0, concat_axis=0, tiled=True)
    log_total = jnp.take(logs[:, 0], source_of, axis=0).reshape(2, loss_total // 2, 1)
    d_logits = [
        (
            (
                (1.0 + 2.0 * ZCOEF * log_total[side]) * jnp.exp(logits[side] - log_total[side])
                - jnp.where(hits[side], 1.0 - SMOOTH, 0.0)
                - SMOOTH / V
            )
            / loss_total
        ).astype(bf16)
        for side in (1, 0)
    ]
    got = flip(dot(d_logits[0], wide_table).astype(bf16), "c", 1, 2)
    d_hidden = (dot(d_logits[1], wide_table) + got.astype(f32)).reshape(4, rows_q, loss_dev, WIDE)
    d_low = d_hidden.astype(bf16)
    d_hidden = d_hidden[0]
    for k in (1, 2, 3):
        d_hidden = d_hidden + flip(d_low[k], ("y", "x"), k, 4).astype(f32)
    d_low = d_hidden.astype(bf16)
    total_hidden = pick_block(d_hidden, q_index)
    for k in range(1, rows_q):
        total_hidden = total_hidden + flip(pick_block(d_low, q_index ^ k), "q", k, rows_q).astype(f32)
    total_hidden = total_hidden[:, :D]
    head_grad = (dot(d_logits[1], sides[0], 0, 0) + dot(d_logits[0], sides[1], 0, 0))[:, :D]
    head_grad, total_hidden = lax.optimization_barrier((head_grad, total_hidden))

    d_x_two, grad_final = norm_back(x_two, gains[2], total_hidden)
    d_down = spread_plane(d_x_two.astype(bf16))
    d_act = dot(d_down, w_down, 1, 1)
    d_gate = d_act * up * sig * (1.0 + gate * (1.0 - sig))
    d_gu = jnp.concatenate([d_gate, d_act * gate * sig], axis=1).astype(bf16)
    d_h_mlp = fold_plane(d_gu, w_gu, 1)
    grad_down = dot(act, d_down, 0, 0)[:, :D].astype(bf16)
    grad_gu = dot(h_all, d_gu, 0, 0)[:D].astype(bf16)
    d_x_mlp, grad_mlp = norm_back(x_one, gains[1], d_h_mlp)
    d_x_one = d_x_two + d_x_mlp

    d_branch = d_x_one.astype(bf16)
    d_attended = dot(d_branch, w_out, 1, 1)
    d_mixed = heads_of(d_attended.astype(bf16))
    d_probs = jnp.einsum("hqd,hkd->hqk", d_mixed, value_h, preferred_element_type=f32)
    delta = jnp.sum(probs * d_probs, axis=-1, keepdims=True)
    d_scores = (probs * (d_probs - delta)).astype(bf16)
    d_query = jnp.einsum("hqk,hkd->hqd", d_scores, key_h, preferred_element_type=f32) * HEAD_SIZE**-0.5
    d_key = jnp.einsum("hqk,hqd->khd", d_scores, query_h, preferred_element_type=f32) * HEAD_SIZE**-0.5
    d_value = jnp.einsum("hqk,hqd->khd", probs_low, d_mixed, preferred_element_type=f32)
    d_q = rotate_back(heads_back(d_query), cosine_pick, sine_pick).astype(bf16)
    d_k = rotate_back(d_key.reshape(tokens, UNIT), cosine, sine)
    d_kv = jnp.concatenate([d_k, d_value.reshape(tokens, UNIT)], axis=1).astype(bf16)
    d_h_pick = dot(d_q, w_q, 1, 1)
    high = d_h_pick.astype(bf16)
    rest = (d_h_pick - high.astype(f32)).astype(bf16)
    d_h_attn = dot(d_kv, w_kv, 1, 1) + dot(pick, high, 0, 0) + dot(pick, rest, 0, 0)
    d_x_attn, grad_attn = norm_back(x_embed, gains[0], d_h_attn)
    high = d_x_one.astype(bf16)
    rest = (d_x_one - high.astype(f32)).astype(bf16)
    d_x_embed = d_x_attn + dot(pick, high, 0, 0) + dot(pick, rest, 0, 0)

    scaled = (d_x_embed * emb_mult).astype(bf16)
    sending = [
        dot(spot_between(low, high), scaled, 0, 0).astype(bf16).reshape(devices, high - low, D)
        for low, high in zip(cuts_back, cuts_back[1:])
    ]
    if aligned:
        blocks = jnp.concatenate([jnp.zeros((1, 480, 640), bf16), grad_gu.reshape(2, 480, 640), down_pack(grad_down)[None]])
        share = lax.psum_scatter(blocks, "q", scatter_dimension=0, tiled=False)
        sending, d_q, d_kv, attended = lax.optimization_barrier((sending, d_q, d_kv, attended))
        share, d_q, d_kv, attended = lax.optimization_barrier((share, d_q, d_kv, attended))
    arrived = [exchange(blocks) for blocks in sending]
    grad_out = dot(attended, d_branch, 0, 0).astype(bf16)
    grad_q = dot(h_pick, d_q, 0, 0).astype(bf16)
    grad_kv = dot(h_attn, d_kv, 0, 0).astype(bf16)

    def finish(squares, table_grad):
        sums = jnp.broadcast_to(jnp.stack([squares, my_loss])[None], (devices, 2))
        sums = jnp.sum(lax.all_to_all(sums, ALL, split_axis=0, concat_axis=0, tiled=True), axis=0)
        grad_norm = jnp.sqrt(sums[0])
        loss = sums[1] / loss_total
        limit = CLIP_C / math.sqrt(loss_total)
        clip_factor = limit / jnp.maximum(grad_norm, limit)
        return loss, grad_norm, clip_factor, adamw_step(table_master, table_grad, table_m, table_v, clip_factor)

    gain_grads = jnp.concatenate([grad_attn, grad_mlp, grad_final]).astype(bf16)
    if aligned:
        lower = jnp.concatenate([grad_q.reshape(5, TOP, D), grad_kv.reshape(5, SHARE - TOP, D)], axis=1)
        level = jnp.concatenate([lower, grad_out.reshape(3, SHARE, D)])
        room = jnp.zeros((8, ROOM, D), bf16).at[0, :3].set(gain_grads.reshape(3, D))
        level = jnp.concatenate([level, room], axis=1).reshape(4, 2, SHARE + ROOM, D)
        level, arrived[0] = lax.optimization_barrier((level, arrived[0]))
        keep = lax.dynamic_index_in_dim(level, c_index, 1, False)
        give = lax.dynamic_index_in_dim(level, 1 - c_index, 1, False)
        level = keep.astype(f32) + flip(give, "c", 1, 2).astype(f32)
        level = level.reshape(2, 2, SHARE + ROOM, D)
        middle = (SHARE + ROOM) // 2
        x_index, y_index = lax.axis_index("x"), lax.axis_index("y")
        left, right = pick_block(level[:, :, :middle], x_index, 1), pick_block(level[:, :, middle:], y_index, 0)
        left = left + flip(pick_block(level[:, :, :middle], 1 - x_index, 1).astype(bf16), "x", 1, 2).astype(f32)
        right = right + flip(pick_block(level[:, :, middle:], 1 - y_index, 0).astype(bf16), "y", 1, 2).astype(f32)
        left = pick_block(left, y_index) + flip(pick_block(left, 1 - y_index).astype(bf16), "y", 1, 2).astype(f32)
        right = pick_block(right, x_index) + flip(pick_block(right, 1 - x_index).astype(bf16), "x", 1, 2).astype(f32)
        own = jnp.concatenate([left, right])
        own = own.reshape(4, (SHARE + ROOM) // 4, D)
        own, share, arrived[1] = lax.optimization_barrier((own, share, arrived[1]))
        got = lax.all_to_all(share.reshape(8, 60, 640), PLANE, split_axis=0, concat_axis=0, tiled=True)
        quarter = lax.dynamic_index_in_dim(own, q_index, 0, False)
        for k in (1, 2, 3):
            piece = lax.dynamic_index_in_dim(own, q_index ^ k, 0, False).astype(bf16)
            quarter = quarter + flip(piece, "q", k, 4).astype(f32)
        table_grad = head_grad
        for low, high, rows in zip(cuts_back, cuts_back[1:], arrived):
            table_grad = table_grad + dot(rows_between(low, high), rows, 0, 0)
        table_squares = jnp.sum(table_grad * table_grad)
        quarter = quarter.astype(bf16)
        squares = jnp.sum(quarter.astype(f32) ** 2) + jnp.sum(share.astype(f32) ** 2) + table_squares
        quarter, squares = lax.optimization_barrier((quarter, squares))
        quarters = [quarter] + [lax.ppermute(quarter, "q", [(k, 0)]) for k in (1, 2, 3)]
        first = jnp.concatenate(quarters)
        gain_out = first[SHARE : SHARE + 3].reshape(-1)
        both = jnp.concatenate([first[:TOP], first[TOP:SHARE].reshape(TOP, KV)], axis=1)
        first = jnp.where(p_index < 5, both.reshape(-1), first[:SHARE].reshape(-1))
        loss, grad_norm, clip_factor, table_new = finish(squares, table_grad)
        got, table_new = lax.optimization_barrier((got, table_new))
        by_share = got.reshape(8, 60, 2, UNIT).transpose(1, 2, 0, 3).reshape(-1)
        mine = jnp.where(q_index == 3, down_unpack(share).reshape(-1), by_share)
        mine = jnp.where(q_index == 0, first, mine)
    else:
        table_grad = head_grad
        for low, high, rows in zip(cuts_back, cuts_back[1:], arrived):
            table_grad = table_grad + dot(rows_between(low, high), rows, 0, 0)
        table_squares = jnp.sum(table_grad * table_grad)
        both = lax.dynamic_update_index_in_dim(jnp.zeros((D, 2, 8, UNIT), bf16), grad_gu.reshape(D, 2, UNIT), p_index, 2)
        downs = lax.dynamic_update_index_in_dim(jnp.zeros((8, SHARE, D), bf16), grad_down, p_index, 0)
        full = jnp.concatenate([part.reshape(-1, UNIT) for part in (jnp.concatenate([grad_q, grad_kv], axis=1), grad_out, both, downs)]).reshape(devices, units, UNIT)
        room = jnp.zeros((devices, 16, UNIT), bf16).at[0, :GAIN_UNITS].set(gain_grads.reshape(GAIN_UNITS, UNIT))
        full = jnp.concatenate([full, room], axis=1)
        summed = lax.psum_scatter(full, ALL, scatter_dimension=0, tiled=False)
        mine, gain_out = summed[:units].reshape(-1), summed[units : units + GAIN_UNITS].reshape(-1)
    behind = lax.ppermute(mine[span - GAINS :], ALL, [(i, i + 1) for i in range(devices - 1)])
    behind = jnp.where(me == 0, gain_out, behind)
    tail = max(0, drift * (devices - 1) + shard - GAINS - span)
    stream = jnp.concatenate([behind, mine, jnp.zeros((tail,), bf16)])
    layer_grad = lax.dynamic_slice(stream, (drift * me,), (shard,)).astype(f32)

    if not aligned:
        squares = jnp.sum(layer_grad * layer_grad) + table_squares
        loss, grad_norm, clip_factor, table_new = finish(squares, table_grad)
    flat_new = adamw_step(flat_master, layer_grad, flat_m, flat_v, clip_factor)
    return (loss, grad_norm) + flat_new + table_new


def solution(mesh):
    count = mesh.devices.size
    grid = Mesh(mesh.devices.reshape(count // 8, 2, 2, 2), ALL)
    rows, matrix = P(ALL), P(ALL, None)
    in_specs = (rows,) * 6 + (matrix,) * 3
    out_specs = (P(), P()) + (rows,) * 3 + (matrix,) * 3
    return jax.shard_map(local, mesh=grid, in_specs=in_specs, out_specs=out_specs, check_vma=False)
```

```python
import math

import jax
import jax.numpy as jnp
import numpy as np
from jax import lax
from jax.sharding import Mesh, PartitionSpec as P

D = 960
QUERY_HEADS = 15
KEY_VALUE_HEADS = 5
HEAD_SIZE = 64
FF = 2560
V = 32000
PL = 256
CL = 128
STEP = 10
QKV = 1600

EPS = 1e-05
SMOOTH = 0.1
ZCOEF = 0.0001
BETA1 = 0.9
BETA2 = 0.95
ADAM_EPS = 1e-08
DECAY = 0.1
RATE = 0.03
CLIP_C = 25.0
NEGATIVE = -1e30

UNIT = 320
GAINS = 3 * D
GAIN_UNITS = GAINS // UNIT
QKV_UNITS = D * QKV // UNIT
OUT_UNITS = D * D // UNIT
GU_UNITS = D * 2 * FF // UNIT
DOWN_UNITS = FF * D // UNIT
ALL_UNITS = QKV_UNITS + OUT_UNITS + GU_UNITS + DOWN_UNITS
PLANE = ("y", "x", "c")
ALL = ("q", "y", "x", "c")
SHARE = FF // 8
TOP = D // 5
KV = QKV - D
ROOM = 32
WIDE = 1024

bf16 = jnp.bfloat16
f32 = jnp.float32


def dot(left, right, left_dim=1, right_dim=0):
    return lax.dot_general(
        left, right, (((left_dim,), (right_dim,)), ((), ())), preferred_element_type=f32
    )


def hot(index, count):
    return (index[:, None] == jnp.arange(count, dtype=jnp.int32)[None, :]).astype(bf16)


def scale_of(rows):
    return lax.rsqrt(jnp.mean(rows * rows, axis=-1, keepdims=True) + EPS)


def norm_back(rows, gain, grad):
    scale = scale_of(rows)
    normed = rows * scale
    grad_gain = jnp.sum(grad * normed, axis=0)
    scaled = grad * gain
    return scale * (scaled - normed * jnp.mean(scaled * normed, axis=-1, keepdims=True)), grad_gain


def flip(rows, axes, bits, size):
    return lax.ppermute(rows, axes, [(i, i ^ bits) for i in range(size)])


def rope_tables(count):
    row = np.arange(count)
    position = np.where(row < PL, row, PL + (row - PL) % CL).astype(np.float32)
    half = np.arange(HEAD_SIZE // 2, dtype=np.float32)
    freqs = np.float32(10000.0) ** (-(half * np.float32(2.0) / np.float32(HEAD_SIZE)))
    angles = (position[:, None] * freqs[None, :].astype(np.float32)).astype(np.float64)
    angles = np.concatenate([angles, angles], axis=-1)
    return np.cos(angles).astype(np.float32), np.sin(angles).astype(np.float32)


def rotate(rows, cosine, sine):
    heads = rows.reshape(rows.shape[0], -1, HEAD_SIZE)
    half = HEAD_SIZE // 2
    turned = jnp.concatenate([-heads[..., half:], heads[..., :half]], axis=-1)
    return (heads * cosine[:, None, :] + turned * sine[:, None, :]).reshape(rows.shape)


def rotate_back(grad, cosine, sine):
    heads = grad.reshape(grad.shape[0], -1, HEAD_SIZE)
    half = HEAD_SIZE // 2
    spun = heads * sine[:, None, :]
    turned = jnp.concatenate([spun[..., half:], -spun[..., :half]], axis=-1)
    return (heads * cosine[:, None, :] + turned).reshape(grad.shape)


def adamw_step(param, gradient, moment_one, moment_two, clip_factor):
    gradient = gradient * clip_factor
    new_one = BETA1 * moment_one + (1.0 - BETA1) * gradient
    new_two = BETA2 * moment_two + (1.0 - BETA2) * gradient * gradient
    ratio = new_one / (1.0 - BETA1**STEP) / (jnp.sqrt(new_two / (1.0 - BETA2**STEP)) + ADAM_EPS)
    return (new_one, new_two, -RATE * (ratio + DECAY * param))


def pick_block(blocks, index, axis=0):
    return lax.dynamic_index_in_dim(blocks, index, axis, False)


def widen(rows):
    return jnp.pad(rows, ((0, 0), (0, WIDE - D)))


def fold_plane(left, right, right_dim):
    c_index, yx_index = lax.axis_index("c"), lax.axis_index(("y", "x"))
    rows = left.reshape(4, 2, left.shape[0] // 8, left.shape[1])
    far = pick_block(rows, 1 - c_index, 1).reshape(-1, left.shape[1])
    near = pick_block(rows, c_index, 1).reshape(-1, left.shape[1])
    got = flip(dot(far, right, 1, right_dim).astype(bf16), "c", 1, 2)
    mine = (dot(near, right, 1, right_dim) + got.astype(f32)).reshape(4, -1, WIDE)
    low = mine.astype(bf16)
    total = pick_block(mine, yx_index)
    for k in (1, 2, 3):
        total = total + flip(pick_block(low, yx_index ^ k), ("y", "x"), k, 4).astype(f32)
    return total[:, :D]


def down_pack(rows):
    side = jnp.concatenate([rows[: SHARE // 2, 640:], rows[SHARE // 2 :, 640:]], axis=1)
    return jnp.concatenate([rows[:, :640], side])


def down_unpack(rows):
    side = jnp.concatenate([rows[SHARE:, :UNIT], rows[SHARE:, UNIT:]])
    return jnp.concatenate([rows[:SHARE], side], axis=1)


def spread_plane(rows):
    return widen(lax.all_gather(rows, PLANE).reshape(-1, D))


def local(
    token_ids, loss_rows, targets, flat_master, flat_m, flat_v, table_master, table_m, table_v
):
    devices = lax.axis_size(ALL)
    rows_q = lax.axis_size("q")
    me = lax.axis_index(ALL)
    q_index = lax.axis_index("q")
    p_index = lax.axis_index(PLANE)
    c_index = lax.axis_index("c")
    yx_index = lax.axis_index(("y", "x"))
    tokens = token_ids.shape[0]
    vocab_dev = table_master.shape[0]
    loss_dev = loss_rows.shape[0]
    loss_total = loss_dev * devices
    capacity = max(2, 2 * tokens // devices)
    slots = devices * capacity
    groups = QUERY_HEADS // KEY_VALUE_HEADS
    emb_mult = math.sqrt(D) * 0.5
    shard = flat_master.shape[0]
    units = ALL_UNITS // devices
    span = units * UNIT
    drift = shard - span
    aligned = devices == 32

    place = np.array([q * 8 + kyx * 2 + kc for kc in range(2) for kyx in range(4) for q in range(rows_q)])
    rank_of = np.argsort(place)
    source_of = p_index ^ jnp.asarray(place, jnp.int32)
    order_of = jnp.take(jnp.asarray(rank_of, jnp.int32), p_index ^ jnp.arange(devices, dtype=jnp.int32))

    table_low = table_master.astype(bf16)
    owner = token_ids // vocab_dev
    owner_hot = hot(owner, devices)
    before = (lax.broadcasted_iota(jnp.int32, (tokens, tokens), 0) > lax.broadcasted_iota(jnp.int32, (tokens, tokens), 1)).astype(bf16)
    slot = jnp.sum(dot(before, owner_hot) * owner_hot.astype(f32), axis=1).astype(jnp.int32)
    spot = hot(owner * capacity + slot, slots)

    def spot_between(low, high):
        inside = (slot >= low) & (slot < high)
        return hot(jnp.where(inside, owner * (high - low) + slot - low, -1), devices * (high - low))

    def rows_between(low, high):
        return hot(asked[:, low:high].reshape(-1) - me * vocab_dev, vocab_dev)

    def exchange(blocks):
        return lax.all_to_all(blocks, ALL, split_axis=0, concat_axis=0, tiled=True).reshape(-1, D)

    cuts_back = (0, capacity // 4, capacity)
    marked = token_ids + 1
    halves = jnp.stack([marked // 256, marked % 256]).astype(bf16)
    found = dot(halves, spot).astype(jnp.int32)
    requests = (found[0] * 256 + found[1] - 1).reshape(devices, capacity)
    ask = jnp.concatenate([requests, jnp.broadcast_to(targets[None], (devices, loss_dev))], axis=1)

    flat_low = flat_master.astype(bf16)
    ahead = lax.ppermute(flat_low[:GAINS], ALL, [(i + 1, i) for i in range(devices - 1)])
    back = max(0, drift * (devices - 1) - GAINS)
    pieces = [flat_low, ahead]
    if back:
        pieces = [lax.ppermute(flat_low[shard - back :], ALL, [(i, i + 1) for i in range(devices - 1)])] + pieces
    chunk = lax.dynamic_slice(jnp.concatenate(pieces), (back + GAINS - drift * me,), (span,))
    if aligned:
        sent = chunk.reshape(60, 2, 8, UNIT).transpose(2, 0, 1, 3).reshape(8, 60, 2 * UNIT)
        got = lax.all_to_all(sent, PLANE, split_axis=0, concat_axis=0, tiled=True)
        both = chunk.reshape(TOP, QKV)
        both = jnp.concatenate([both[:, :D], both[:, D:].reshape(SHARE - TOP, D)])
        first = jnp.where(p_index < 5, both, chunk.reshape(SHARE, D))
        first = jnp.concatenate([first, flat_low[:GAINS].reshape(3, D), jnp.zeros((5, D), bf16)])
        first, ask = lax.optimization_barrier((first, ask))
        asked = lax.all_to_all(ask, ALL, split_axis=0, concat_axis=0, tiled=True)
        answer = dot(rows_between(0, capacity), table_low).astype(bf16).reshape(devices, capacity, D)
        jumped = lax.ppermute(first, "q", [(0, 2)])
        first = jnp.where(q_index == 2, jumped, first)
        stepped = lax.ppermute(first, "q", [(0, 1), (2, 3)])
        first = jnp.where((q_index == 1) | (q_index == 3), stepped, first)
        answer, first, got = lax.optimization_barrier((answer, first, got))
        returned = exchange(answer)
        level = lax.all_gather(first, PLANE)
        mixed = jnp.where(q_index == 3, down_pack(chunk.reshape(SHARE, D)), got.reshape(480, 2 * UNIT))
        mixed, level = lax.optimization_barrier((mixed, level))
        gains = level[0, SHARE : SHARE + 3].astype(f32)
        w_q = level[:5, :TOP].reshape(D, D)
        w_kv = level[:5, TOP:SHARE].reshape(D, KV)
        w_out = level[5:, :SHARE].reshape(D, D)
        returned, w_q, w_kv, w_out = lax.optimization_barrier((returned, w_q, w_kv, w_out))
        column = lax.all_gather(mixed, "q")
    else:
        asked = lax.all_to_all(ask, ALL, split_axis=0, concat_axis=0, tiled=True)
        answer = dot(rows_between(0, capacity), table_low).astype(bf16).reshape(devices, capacity, D)
        returned = exchange(answer)
        extra = jnp.zeros((16 * UNIT,), bf16).at[:GAINS].set(flat_low[:GAINS])
        full = lax.all_gather(jnp.concatenate([chunk, extra]).reshape(units + 16, UNIT), ALL)
        gains = full[0, units : units + GAIN_UNITS].astype(f32).reshape(3, D)
        full = full[:, :units].reshape(ALL_UNITS, UNIT)
        edge = np.cumsum([QKV_UNITS, OUT_UNITS, GU_UNITS])
        w_qkv = full[: edge[0]].reshape(D, QKV)
        w_q, w_kv = w_qkv[:, :D], w_qkv[:, D:]
        w_out = full[edge[0] : edge[1]].reshape(D, D)
        both = lax.dynamic_index_in_dim(full[edge[1] : edge[2]].reshape(D, 2, 8, UNIT), p_index, 2, False)
        w_gu = both.reshape(D, 2 * SHARE)
        w_down = lax.dynamic_index_in_dim(full[edge[2] :].reshape(8, SHARE, D), p_index, 0, False)
    x_low = dot(spot, returned).astype(bf16)
    x_embed = x_low.astype(f32) * emb_mult

    pick = hot(loss_rows, tokens)
    cosine, sine = (jnp.asarray(t) for t in rope_tables(tokens))
    cosine_pick, sine_pick = cosine[loss_rows], sine[loss_rows]
    h_attn = (x_embed * scale_of(x_embed) * gains[0]).astype(bf16)
    h_pick = dot(pick, h_attn).astype(bf16)
    x_pick = dot(pick, x_low) * emb_mult
    query = rotate(dot(h_pick, w_q), cosine_pick, sine_pick).astype(bf16)
    key_value = dot(h_attn, w_kv)
    key = rotate(key_value[:, :UNIT], cosine, sine).astype(bf16)
    value = key_value[:, UNIT:].astype(bf16)

    def heads_of(rows):
        return rows.reshape(loss_dev, KEY_VALUE_HEADS, groups, HEAD_SIZE).transpose(1, 2, 0, 3).reshape(KEY_VALUE_HEADS, groups * loss_dev, HEAD_SIZE)

    def heads_back(rows):
        return rows.reshape(KEY_VALUE_HEADS, groups, loss_dev, HEAD_SIZE).transpose(2, 0, 1, 3).reshape(loss_dev, D)

    query_h = heads_of(query)
    key_h = key.reshape(tokens, KEY_VALUE_HEADS, HEAD_SIZE).transpose(1, 0, 2)
    value_h = value.reshape(tokens, KEY_VALUE_HEADS, HEAD_SIZE).transpose(1, 0, 2)
    key_pos = jnp.arange(tokens, dtype=jnp.int32)[None, :]
    ask_pos = jnp.tile(loss_rows, groups)[:, None]
    key_seg = jnp.where(key_pos < PL, 0, 1 + (key_pos - PL) // CL)
    ask_seg = jnp.where(ask_pos < PL, 0, 1 + (ask_pos - PL) // CL)
    allowed = (key_pos <= ask_pos) & ((key_seg == 0) | (key_seg == ask_seg))
    scores = jnp.einsum("hqd,hkd->hqk", query_h, key_h, preferred_element_type=f32) * HEAD_SIZE**-0.5
    scores = jnp.where(allowed[None], scores, NEGATIVE)
    exp_scores = jnp.exp(scores - jnp.max(scores, axis=-1, keepdims=True))
    probs = exp_scores / jnp.sum(exp_scores, axis=-1, keepdims=True)
    probs_low = probs.astype(bf16)
    mixed_heads = jnp.einsum("hqk,hkd->hqd", probs_low, value_h, preferred_element_type=f32)
    attended = heads_back(mixed_heads.astype(bf16))
    x_one = x_pick + dot(attended, w_out)

    h_mlp = (x_one * scale_of(x_one) * gains[1]).astype(bf16)
    h_all = spread_plane(h_mlp)
    if aligned:
        column, h_all = lax.optimization_barrier((column, h_all))
        w_gu = column[1:3].reshape(D, 2 * SHARE)
        w_down = down_unpack(column[3])
    w_gu = jnp.pad(w_gu, ((0, WIDE - D), (0, 0)))
    w_down = widen(w_down)
    gate_up = dot(h_all, w_gu)
    gate, up = gate_up[:, :SHARE], gate_up[:, SHARE:]
    sig = jax.nn.sigmoid(gate)
    act = (gate * sig * up).astype(bf16)
    x_two = x_one + fold_plane(act, w_down, 0)

    hidden = (x_two * scale_of(x_two) * gains[2]).astype(bf16)
    wide_table = widen(table_low)
    across = lax.all_gather(widen(hidden), "q")
    by_x, by_y = flip(across, "x", 1, 2), flip(across, "y", 1, 2)
    cut = rows_q // 2
    corner = [flip(by_x[:cut], "y", 1, 2), flip(by_y[cut:], "x", 1, 2)]
    near = jnp.concatenate([across, by_x, by_y] + corner).reshape(loss_total // 2, WIDE)
    sides = [near, flip(near, "c", 1, 2)]
    targets_all = jnp.take(asked[:, capacity:], source_of, axis=0).reshape(2, loss_total // 2)
    logits, hits, stats = [], [], []
    for side, rows in enumerate(sides):
        z = dot(rows, wide_table, 1, 1)
        column_id = targets_all[side] - me * vocab_dev
        hit = column_id[:, None] == jnp.arange(vocab_dev, dtype=jnp.int32)[None, :]
        local_peak = jnp.max(z, axis=1)
        local_total = jnp.sum(jnp.exp(z - local_peak[:, None]), axis=1)
        local_target = jnp.sum(jnp.where(hit, z, 0.0), axis=1)
        local_sum = jnp.sum(z, axis=1)
        logits.append(z)
        hits.append(hit)
        stats.append(jnp.stack([local_peak, local_total, local_target, local_sum]))
    stats = jnp.concatenate(stats, axis=1).reshape(4, devices, loss_dev)
    stats = jnp.take(stats, order_of, axis=1).transpose(1, 0, 2)
    stats = lax.all_to_all(stats, ALL, split_axis=0, concat_axis=0, tiled=True)
    peak = jnp.max(stats[:, 0], axis=0)
    total = jnp.sum(stats[:, 1] * jnp.exp(stats[:, 0] - peak[None]), axis=0)
    my_log = peak + jnp.log(total)
    my_loss = jnp.sum(
        my_log
        - (1.0 - SMOOTH) * jnp.sum(stats[:, 2], axis=0)
        - SMOOTH / V * jnp.sum(stats[:, 3], axis=0)
        + ZCOEF * my_log * my_log
    )
    logs = lax.all_to_all(jnp.broadcast_to(my_log[None, None], (devices, 1, loss_dev)), ALL, split_axis=0, concat_axis=0, tiled=True)
    log_total = jnp.take(logs[:, 0], source_of, axis=0).reshape(2, loss_total // 2, 1)
    d_logits = [
        (
            (
                (1.0 + 2.0 * ZCOEF * log_total[side]) * jnp.exp(logits[side] - log_total[side])
                - jnp.where(hits[side], 1.0 - SMOOTH, 0.0)
                - SMOOTH / V
            )
            / loss_total
        ).astype(bf16)
        for side in (1, 0)
    ]
    got = flip(dot(d_logits[0], wide_table).astype(bf16), "c", 1, 2)
    d_hidden = (dot(d_logits[1], wide_table) + got.astype(f32)).reshape(4, rows_q, loss_dev, WIDE)
    d_low = d_hidden.astype(bf16)
    d_hidden = d_hidden[0]
    for k in (1, 2, 3):
        d_hidden = d_hidden + flip(d_low[k], ("y", "x"), k, 4).astype(f32)
    d_low = d_hidden.astype(bf16)
    total_hidden = pick_block(d_hidden, q_index)
    for k in range(1, rows_q):
        total_hidden = total_hidden + flip(pick_block(d_low, q_index ^ k), "q", k, rows_q).astype(f32)
    total_hidden = total_hidden[:, :D]
    head_grad = (dot(d_logits[1], sides[0], 0, 0) + dot(d_logits[0], sides[1], 0, 0))[:, :D]
    head_grad, total_hidden = lax.optimization_barrier((head_grad, total_hidden))

    d_x_two, grad_final = norm_back(x_two, gains[2], total_hidden)
    d_down = spread_plane(d_x_two.astype(bf16))
    d_act = dot(d_down, w_down, 1, 1)
    d_gate = d_act * up * sig * (1.0 + gate * (1.0 - sig))
    d_gu = jnp.concatenate([d_gate, d_act * gate * sig], axis=1).astype(bf16)
    d_h_mlp = fold_plane(d_gu, w_gu, 1)
    grad_down = dot(act, d_down, 0, 0)[:, :D].astype(bf16)
    grad_gu = dot(h_all, d_gu, 0, 0)[:D].astype(bf16)
    d_x_mlp, grad_mlp = norm_back(x_one, gains[1], d_h_mlp)
    d_x_one = d_x_two + d_x_mlp

    d_branch = d_x_one.astype(bf16)
    d_attended = dot(d_branch, w_out, 1, 1)
    d_mixed = heads_of(d_attended.astype(bf16))
    d_probs = jnp.einsum("hqd,hkd->hqk", d_mixed, value_h, preferred_element_type=f32)
    delta = jnp.sum(probs * d_probs, axis=-1, keepdims=True)
    d_scores = (probs * (d_probs - delta)).astype(bf16)
    d_query = jnp.einsum("hqk,hkd->hqd", d_scores, key_h, preferred_element_type=f32) * HEAD_SIZE**-0.5
    d_key = jnp.einsum("hqk,hqd->khd", d_scores, query_h, preferred_element_type=f32) * HEAD_SIZE**-0.5
    d_value = jnp.einsum("hqk,hqd->khd", probs_low, d_mixed, preferred_element_type=f32)
    d_q = rotate_back(heads_back(d_query), cosine_pick, sine_pick).astype(bf16)
    d_k = rotate_back(d_key.reshape(tokens, UNIT), cosine, sine)
    d_kv = jnp.concatenate([d_k, d_value.reshape(tokens, UNIT)], axis=1).astype(bf16)
    d_h_pick = dot(d_q, w_q, 1, 1)
    high = d_h_pick.astype(bf16)
    rest = (d_h_pick - high.astype(f32)).astype(bf16)
    d_h_attn = dot(d_kv, w_kv, 1, 1) + dot(pick, high, 0, 0) + dot(pick, rest, 0, 0)
    d_x_attn, grad_attn = norm_back(x_embed, gains[0], d_h_attn)
    high = d_x_one.astype(bf16)
    rest = (d_x_one - high.astype(f32)).astype(bf16)
    d_x_embed = d_x_attn + dot(pick, high, 0, 0) + dot(pick, rest, 0, 0)

    scaled = (d_x_embed * emb_mult).astype(bf16)
    sending = [
        dot(spot_between(low, high), scaled, 0, 0).astype(bf16).reshape(devices, high - low, D)
        for low, high in zip(cuts_back, cuts_back[1:])
    ]
    if aligned:
        blocks = jnp.concatenate([jnp.zeros((1, 480, 640), bf16), grad_gu.reshape(2, 480, 640), down_pack(grad_down)[None]])
        share = lax.psum_scatter(blocks, "q", scatter_dimension=0, tiled=False)
        sending, d_q, d_kv, attended = lax.optimization_barrier((sending, d_q, d_kv, attended))
        share, d_q, d_kv, attended = lax.optimization_barrier((share, d_q, d_kv, attended))
    arrived = [exchange(blocks) for blocks in sending]
    grad_out = dot(attended, d_branch, 0, 0).astype(bf16)
    grad_q = dot(h_pick, d_q, 0, 0).astype(bf16)
    grad_kv = dot(h_attn, d_kv, 0, 0).astype(bf16)

    def norm_of(squares):
        sums = jnp.broadcast_to(jnp.stack([squares, my_loss])[None], (devices, 2))
        sums = jnp.sum(lax.all_to_all(sums, ALL, split_axis=0, concat_axis=0, tiled=True), axis=0)
        grad_norm = jnp.sqrt(sums[0])
        limit = CLIP_C / math.sqrt(loss_total)
        return sums[1] / loss_total, grad_norm, limit / jnp.maximum(grad_norm, limit)

    gain_grads = jnp.concatenate([grad_attn, grad_mlp, grad_final]).astype(bf16)
    if aligned:
        lower = jnp.concatenate([grad_q.reshape(5, TOP, D), grad_kv.reshape(5, SHARE - TOP, D)], axis=1)
        level = jnp.concatenate([lower, grad_out.reshape(3, SHARE, D)])
        room = jnp.zeros((8, ROOM, D), bf16).at[0, :3].set(gain_grads.reshape(3, D))
        level = jnp.concatenate([level, room], axis=1).reshape(4, 2, SHARE + ROOM, D)
        level, arrived[0] = lax.optimization_barrier((level, arrived[0]))
        keep = lax.dynamic_index_in_dim(level, c_index, 1, False)
        give = lax.dynamic_index_in_dim(level, 1 - c_index, 1, False)
        level = keep.astype(f32) + flip(give, "c", 1, 2).astype(f32)
        level = level.reshape(2, 2, SHARE + ROOM, D)
        middle = (SHARE + ROOM) // 2
        x_index, y_index = lax.axis_index("x"), lax.axis_index("y")
        left, right = pick_block(level[:, :, :middle], x_index, 1), pick_block(level[:, :, middle:], y_index, 0)
        left = left + flip(pick_block(level[:, :, :middle], 1 - x_index, 1).astype(bf16), "x", 1, 2).astype(f32)
        right = right + flip(pick_block(level[:, :, middle:], 1 - y_index, 0).astype(bf16), "y", 1, 2).astype(f32)
        left = pick_block(left, y_index) + flip(pick_block(left, 1 - y_index).astype(bf16), "y", 1, 2).astype(f32)
        right = pick_block(right, x_index) + flip(pick_block(right, 1 - x_index).astype(bf16), "x", 1, 2).astype(f32)
        own = jnp.concatenate([left, right])
        own = own.reshape(4, (SHARE + ROOM) // 4, D)
        own, share, arrived[1] = lax.optimization_barrier((own, share, arrived[1]))
        got = lax.all_to_all(share.reshape(8, 60, 640), PLANE, split_axis=0, concat_axis=0, tiled=True)
        quarter = lax.dynamic_index_in_dim(own, q_index, 0, False)
        for k in (1, 2, 3):
            piece = lax.dynamic_index_in_dim(own, q_index ^ k, 0, False).astype(bf16)
            quarter = quarter + flip(piece, "q", k, 4).astype(f32)
        table_grad = head_grad
        for low, high, rows in zip(cuts_back, cuts_back[1:], arrived):
            table_grad = table_grad + dot(rows_between(low, high), rows, 0, 0)
        table_squares = jnp.sum(table_grad * table_grad)
        quarter = quarter.astype(bf16)
        squares = jnp.sum(quarter.astype(f32) ** 2) + jnp.sum(share.astype(f32) ** 2) + table_squares
        quarter, squares, got = lax.optimization_barrier((quarter, squares, got))
        quarters = [quarter] + [lax.ppermute(quarter, "q", [(k, 0)]) for k in (1, 2, 3)]
        first = jnp.concatenate(quarters)
        gain_out = first[SHARE : SHARE + 3].reshape(-1)
        both = jnp.concatenate([first[:TOP], first[TOP:SHARE].reshape(TOP, KV)], axis=1)
        first = jnp.where(p_index < 5, both.reshape(-1), first[:SHARE].reshape(-1))
        by_share = got.reshape(8, 60, 2, UNIT).transpose(1, 2, 0, 3).reshape(-1)
        mine = jnp.where(q_index == 3, down_unpack(share).reshape(-1), by_share)
        mine = jnp.where(q_index == 0, first, mine)
        loss, grad_norm, clip_factor = norm_of(squares)
        mine, clip_factor = lax.optimization_barrier((mine, clip_factor))
    else:
        table_grad = head_grad
        for low, high, rows in zip(cuts_back, cuts_back[1:], arrived):
            table_grad = table_grad + dot(rows_between(low, high), rows, 0, 0)
        table_squares = jnp.sum(table_grad * table_grad)
        both = lax.dynamic_update_index_in_dim(jnp.zeros((D, 2, 8, UNIT), bf16), grad_gu.reshape(D, 2, UNIT), p_index, 2)
        downs = lax.dynamic_update_index_in_dim(jnp.zeros((8, SHARE, D), bf16), grad_down, p_index, 0)
        full = jnp.concatenate([part.reshape(-1, UNIT) for part in (jnp.concatenate([grad_q, grad_kv], axis=1), grad_out, both, downs)]).reshape(devices, units, UNIT)
        room = jnp.zeros((devices, 16, UNIT), bf16).at[0, :GAIN_UNITS].set(gain_grads.reshape(GAIN_UNITS, UNIT))
        full = jnp.concatenate([full, room], axis=1)
        summed = lax.psum_scatter(full, ALL, scatter_dimension=0, tiled=False)
        mine, gain_out = summed[:units].reshape(-1), summed[units : units + GAIN_UNITS].reshape(-1)
    behind = lax.ppermute(mine[span - GAINS :], ALL, [(i, i + 1) for i in range(devices - 1)])
    behind = jnp.where(me == 0, gain_out, behind)
    tail = max(0, drift * (devices - 1) + shard - GAINS - span)
    stream = jnp.concatenate([behind, mine, jnp.zeros((tail,), bf16)])
    layer_grad = lax.dynamic_slice(stream, (drift * me,), (shard,)).astype(f32)

    if not aligned:
        loss, grad_norm, clip_factor = norm_of(jnp.sum(layer_grad * layer_grad) + table_squares)
    flat_new = adamw_step(flat_master, layer_grad, flat_m, flat_v, clip_factor)
    table_new = adamw_step(table_master, table_grad, table_m, table_v, clip_factor)
    return (loss, grad_norm) + flat_new + table_new


def solution(mesh):
    count = mesh.devices.size
    grid = Mesh(mesh.devices.reshape(count // 8, 2, 2, 2), ALL)
    rows, matrix = P(ALL), P(ALL, None)
    in_specs = (rows,) * 6 + (matrix,) * 3
    out_specs = (P(), P()) + (rows,) * 3 + (matrix,) * 3
    return jax.shard_map(local, mesh=grid, in_specs=in_specs, out_specs=out_specs, check_vma=False)
```

```python
import math

import jax
import jax.numpy as jnp
import numpy as np
from jax import lax
from jax.sharding import Mesh, PartitionSpec as P

D = 960
QUERY_HEADS = 15
KEY_VALUE_HEADS = 5
HEAD_SIZE = 64
FF = 2560
V = 32000
PL = 256
CL = 128
STEP = 10
QKV = 1600

EPS = 1e-05
SMOOTH = 0.1
ZCOEF = 0.0001
BETA1 = 0.9
BETA2 = 0.95
ADAM_EPS = 1e-08
DECAY = 0.1
RATE = 0.03
CLIP_C = 25.0
NEGATIVE = -1e30

UNIT = 320
GAINS = 3 * D
GAIN_UNITS = GAINS // UNIT
QKV_UNITS = D * QKV // UNIT
OUT_UNITS = D * D // UNIT
GU_UNITS = D * 2 * FF // UNIT
DOWN_UNITS = FF * D // UNIT
ALL_UNITS = QKV_UNITS + OUT_UNITS + GU_UNITS + DOWN_UNITS
PLANE = ("y", "x", "c")
ALL = ("q", "y", "x", "c")
SHARE = FF // 8
TOP = D // 5
KV = QKV - D
ROOM = 32
WIDE = 1024

bf16 = jnp.bfloat16
f32 = jnp.float32


def dot(left, right, left_dim=1, right_dim=0):
    return lax.dot_general(
        left, right, (((left_dim,), (right_dim,)), ((), ())), preferred_element_type=f32
    )


def hot(index, count):
    return (index[:, None] == jnp.arange(count, dtype=jnp.int32)[None, :]).astype(bf16)


def scale_of(rows):
    return lax.rsqrt(jnp.mean(rows * rows, axis=-1, keepdims=True) + EPS)


def norm_back(rows, gain, grad):
    scale = scale_of(rows)
    normed = rows * scale
    grad_gain = jnp.sum(grad * normed, axis=0)
    scaled = grad * gain
    return scale * (scaled - normed * jnp.mean(scaled * normed, axis=-1, keepdims=True)), grad_gain


def flip(rows, axes, bits, size):
    return lax.ppermute(rows, axes, [(i, i ^ bits) for i in range(size)])


def rope_tables(count):
    row = np.arange(count)
    position = np.where(row < PL, row, PL + (row - PL) % CL).astype(np.float32)
    half = np.arange(HEAD_SIZE // 2, dtype=np.float32)
    freqs = np.float32(10000.0) ** (-(half * np.float32(2.0) / np.float32(HEAD_SIZE)))
    angles = (position[:, None] * freqs[None, :].astype(np.float32)).astype(np.float64)
    angles = np.concatenate([angles, angles], axis=-1)
    return np.cos(angles).astype(np.float32), np.sin(angles).astype(np.float32)


def rotate(rows, cosine, sine):
    heads = rows.reshape(rows.shape[0], -1, HEAD_SIZE)
    half = HEAD_SIZE // 2
    turned = jnp.concatenate([-heads[..., half:], heads[..., :half]], axis=-1)
    return (heads * cosine[:, None, :] + turned * sine[:, None, :]).reshape(rows.shape)


def rotate_back(grad, cosine, sine):
    heads = grad.reshape(grad.shape[0], -1, HEAD_SIZE)
    half = HEAD_SIZE // 2
    spun = heads * sine[:, None, :]
    turned = jnp.concatenate([spun[..., half:], -spun[..., :half]], axis=-1)
    return (heads * cosine[:, None, :] + turned).reshape(grad.shape)


def adamw_step(param, gradient, moment_one, moment_two, clip_factor):
    gradient = gradient * clip_factor
    new_one = BETA1 * moment_one + (1.0 - BETA1) * gradient
    new_two = BETA2 * moment_two + (1.0 - BETA2) * gradient * gradient
    ratio = new_one / (1.0 - BETA1**STEP) / (jnp.sqrt(new_two / (1.0 - BETA2**STEP)) + ADAM_EPS)
    return (new_one, new_two, -RATE * (ratio + DECAY * param))


def pick_block(blocks, index, axis=0):
    return lax.dynamic_index_in_dim(blocks, index, axis, False)


def widen(rows):
    return jnp.pad(rows, ((0, 0), (0, WIDE - D)))


def fold_plane(left, right, right_dim):
    c_index, yx_index = lax.axis_index("c"), lax.axis_index(("y", "x"))
    rows = left.reshape(4, 2, left.shape[0] // 8, left.shape[1])
    far = pick_block(rows, 1 - c_index, 1).reshape(-1, left.shape[1])
    near = pick_block(rows, c_index, 1).reshape(-1, left.shape[1])
    got = flip(dot(far, right, 1, right_dim).astype(bf16), "c", 1, 2)
    mine = (dot(near, right, 1, right_dim) + got.astype(f32)).reshape(4, -1, WIDE)
    low = mine.astype(bf16)
    total = pick_block(mine, yx_index)
    for k in (1, 2, 3):
        total = total + flip(pick_block(low, yx_index ^ k), ("y", "x"), k, 4).astype(f32)
    return total[:, :D]


def down_pack(rows):
    side = jnp.concatenate([rows[: SHARE // 2, 640:], rows[SHARE // 2 :, 640:]], axis=1)
    return jnp.concatenate([rows[:, :640], side])


def down_unpack(rows):
    side = jnp.concatenate([rows[SHARE:, :UNIT], rows[SHARE:, UNIT:]])
    return jnp.concatenate([rows[:SHARE], side], axis=1)


def spread_plane(rows):
    return widen(lax.all_gather(rows, PLANE).reshape(-1, D))


def local(
    token_ids, loss_rows, targets, flat_master, flat_m, flat_v, table_master, table_m, table_v
):
    devices = lax.axis_size(ALL)
    rows_q = lax.axis_size("q")
    me = lax.axis_index(ALL)
    q_index = lax.axis_index("q")
    p_index = lax.axis_index(PLANE)
    c_index = lax.axis_index("c")
    yx_index = lax.axis_index(("y", "x"))
    tokens = token_ids.shape[0]
    vocab_dev = table_master.shape[0]
    loss_dev = loss_rows.shape[0]
    loss_total = loss_dev * devices
    capacity = max(2, 2 * tokens // devices)
    slots = devices * capacity
    groups = QUERY_HEADS // KEY_VALUE_HEADS
    emb_mult = math.sqrt(D) * 0.5
    shard = flat_master.shape[0]
    units = ALL_UNITS // devices
    span = units * UNIT
    drift = shard - span
    aligned = devices == 32

    place = np.array([q * 8 + kyx * 2 + kc for kc in range(2) for kyx in range(4) for q in range(rows_q)])
    rank_of = np.argsort(place)
    source_of = p_index ^ jnp.asarray(place, jnp.int32)
    order_of = jnp.take(jnp.asarray(rank_of, jnp.int32), p_index ^ jnp.arange(devices, dtype=jnp.int32))

    table_low = table_master.astype(bf16)
    owner = token_ids // vocab_dev
    owner_hot = hot(owner, devices)
    before = (lax.broadcasted_iota(jnp.int32, (tokens, tokens), 0) > lax.broadcasted_iota(jnp.int32, (tokens, tokens), 1)).astype(bf16)
    slot = jnp.sum(dot(before, owner_hot) * owner_hot.astype(f32), axis=1).astype(jnp.int32)
    spot = hot(owner * capacity + slot, slots)

    def spot_between(low, high):
        inside = (slot >= low) & (slot < high)
        return hot(jnp.where(inside, owner * (high - low) + slot - low, -1), devices * (high - low))

    def rows_between(low, high):
        return hot(asked[:, low:high].reshape(-1) - me * vocab_dev, vocab_dev)

    def exchange(blocks):
        return lax.all_to_all(blocks, ALL, split_axis=0, concat_axis=0, tiled=True).reshape(-1, D)

    cuts_back = (0, capacity // 2, capacity)
    marked = token_ids + 1
    halves = jnp.stack([marked // 256, marked % 256]).astype(bf16)
    found = dot(halves, spot).astype(jnp.int32)
    requests = (found[0] * 256 + found[1] - 1).reshape(devices, capacity)
    ask = jnp.concatenate([requests, jnp.broadcast_to(targets[None], (devices, loss_dev))], axis=1)

    flat_low = flat_master.astype(bf16)
    ahead = lax.ppermute(flat_low[:GAINS], ALL, [(i + 1, i) for i in range(devices - 1)])
    back = max(0, drift * (devices - 1) - GAINS)
    pieces = [flat_low, ahead]
    if back:
        pieces = [lax.ppermute(flat_low[shard - back :], ALL, [(i, i + 1) for i in range(devices - 1)])] + pieces
    chunk = lax.dynamic_slice(jnp.concatenate(pieces), (back + GAINS - drift * me,), (span,))
    if aligned:
        sent = chunk.reshape(60, 2, 8, UNIT).transpose(2, 0, 1, 3).reshape(8, 60, 2 * UNIT)
        got = lax.all_to_all(sent, PLANE, split_axis=0, concat_axis=0, tiled=True)
        both = chunk.reshape(TOP, QKV)
        both = jnp.concatenate([both[:, :D], both[:, D:].reshape(SHARE - TOP, D)])
        first = jnp.where(p_index < 5, both, chunk.reshape(SHARE, D))
        first = jnp.concatenate([first, flat_low[:GAINS].reshape(3, D), jnp.zeros((5, D), bf16)])
        first, ask = lax.optimization_barrier((first, ask))
        asked = lax.all_to_all(ask, ALL, split_axis=0, concat_axis=0, tiled=True)
        answer = dot(rows_between(0, capacity), table_low).astype(bf16).reshape(devices, capacity, D)
        jumped = lax.ppermute(first, "q", [(0, 2)])
        first = jnp.where(q_index == 2, jumped, first)
        stepped = lax.ppermute(first, "q", [(0, 1), (2, 3)])
        first = jnp.where((q_index == 1) | (q_index == 3), stepped, first)
        answer, first, got = lax.optimization_barrier((answer, first, got))
        returned = exchange(answer)
        level = lax.all_gather(first, PLANE)
        mixed = jnp.where(q_index == 3, down_pack(chunk.reshape(SHARE, D)), got.reshape(480, 2 * UNIT))
        mixed, level = lax.optimization_barrier((mixed, level))
        gains = level[0, SHARE : SHARE + 3].astype(f32)
        w_q = level[:5, :TOP].reshape(D, D)
        w_kv = level[:5, TOP:SHARE].reshape(D, KV)
        w_out = level[5:, :SHARE].reshape(D, D)
        returned, w_q, w_kv, w_out = lax.optimization_barrier((returned, w_q, w_kv, w_out))
        column = lax.all_gather(mixed, "q")
    else:
        asked = lax.all_to_all(ask, ALL, split_axis=0, concat_axis=0, tiled=True)
        answer = dot(rows_between(0, capacity), table_low).astype(bf16).reshape(devices, capacity, D)
        returned = exchange(answer)
        extra = jnp.zeros((16 * UNIT,), bf16).at[:GAINS].set(flat_low[:GAINS])
        full = lax.all_gather(jnp.concatenate([chunk, extra]).reshape(units + 16, UNIT), ALL)
        gains = full[0, units : units + GAIN_UNITS].astype(f32).reshape(3, D)
        full = full[:, :units].reshape(ALL_UNITS, UNIT)
        edge = np.cumsum([QKV_UNITS, OUT_UNITS, GU_UNITS])
        w_qkv = full[: edge[0]].reshape(D, QKV)
        w_q, w_kv = w_qkv[:, :D], w_qkv[:, D:]
        w_out = full[edge[0] : edge[1]].reshape(D, D)
        both = lax.dynamic_index_in_dim(full[edge[1] : edge[2]].reshape(D, 2, 8, UNIT), p_index, 2, False)
        w_gu = both.reshape(D, 2 * SHARE)
        w_down = lax.dynamic_index_in_dim(full[edge[2] :].reshape(8, SHARE, D), p_index, 0, False)
    x_low = dot(spot, returned).astype(bf16)
    x_embed = x_low.astype(f32) * emb_mult

    pick = hot(loss_rows, tokens)
    cosine, sine = (jnp.asarray(t) for t in rope_tables(tokens))
    cosine_pick, sine_pick = cosine[loss_rows], sine[loss_rows]
    h_attn = (x_embed * scale_of(x_embed) * gains[0]).astype(bf16)
    h_pick = dot(pick, h_attn).astype(bf16)
    x_pick = dot(pick, x_low) * emb_mult
    query = rotate(dot(h_pick, w_q), cosine_pick, sine_pick).astype(bf16)
    key_value = dot(h_attn, w_kv)
    key = rotate(key_value[:, :UNIT], cosine, sine).astype(bf16)
    value = key_value[:, UNIT:].astype(bf16)

    def heads_of(rows):
        return rows.reshape(loss_dev, KEY_VALUE_HEADS, groups, HEAD_SIZE).transpose(1, 2, 0, 3).reshape(KEY_VALUE_HEADS, groups * loss_dev, HEAD_SIZE)

    def heads_back(rows):
        return rows.reshape(KEY_VALUE_HEADS, groups, loss_dev, HEAD_SIZE).transpose(2, 0, 1, 3).reshape(loss_dev, D)

    query_h = heads_of(query)
    key_h = key.reshape(tokens, KEY_VALUE_HEADS, HEAD_SIZE).transpose(1, 0, 2)
    value_h = value.reshape(tokens, KEY_VALUE_HEADS, HEAD_SIZE).transpose(1, 0, 2)
    key_pos = jnp.arange(tokens, dtype=jnp.int32)[None, :]
    ask_pos = jnp.tile(loss_rows, groups)[:, None]
    key_seg = jnp.where(key_pos < PL, 0, 1 + (key_pos - PL) // CL)
    ask_seg = jnp.where(ask_pos < PL, 0, 1 + (ask_pos - PL) // CL)
    allowed = (key_pos <= ask_pos) & ((key_seg == 0) | (key_seg == ask_seg))
    scores = jnp.einsum("hqd,hkd->hqk", query_h, key_h, preferred_element_type=f32) * HEAD_SIZE**-0.5
    scores = jnp.where(allowed[None], scores, NEGATIVE)
    exp_scores = jnp.exp(scores - jnp.max(scores, axis=-1, keepdims=True))
    probs = exp_scores / jnp.sum(exp_scores, axis=-1, keepdims=True)
    probs_low = probs.astype(bf16)
    mixed_heads = jnp.einsum("hqk,hkd->hqd", probs_low, value_h, preferred_element_type=f32)
    attended = heads_back(mixed_heads.astype(bf16))
    x_one = x_pick + dot(attended, w_out)

    h_mlp = (x_one * scale_of(x_one) * gains[1]).astype(bf16)
    h_all = spread_plane(h_mlp)
    if aligned:
        column, h_all = lax.optimization_barrier((column, h_all))
        w_gu = column[1:3].reshape(D, 2 * SHARE)
        w_down = down_unpack(column[3])
    w_gu = jnp.pad(w_gu, ((0, WIDE - D), (0, 0)))
    w_down = widen(w_down)
    gate_up = dot(h_all, w_gu)
    gate, up = gate_up[:, :SHARE], gate_up[:, SHARE:]
    sig = jax.nn.sigmoid(gate)
    act = (gate * sig * up).astype(bf16)
    x_two = x_one + fold_plane(act, w_down, 0)

    hidden = (x_two * scale_of(x_two) * gains[2]).astype(bf16)
    wide_table = widen(table_low)
    across = lax.all_gather(widen(hidden), "q")
    by_x, by_y = flip(across, "x", 1, 2), flip(across, "y", 1, 2)
    cut = rows_q // 2
    corner = [flip(by_x[:cut], "y", 1, 2), flip(by_y[cut:], "x", 1, 2)]
    near = jnp.concatenate([across, by_x, by_y] + corner).reshape(loss_total // 2, WIDE)
    sides = [near, flip(near, "c", 1, 2)]
    targets_all = jnp.take(asked[:, capacity:], source_of, axis=0).reshape(2, loss_total // 2)
    logits, hits, stats = [], [], []
    for side, rows in enumerate(sides):
        z = dot(rows, wide_table, 1, 1)
        column_id = targets_all[side] - me * vocab_dev
        hit = column_id[:, None] == jnp.arange(vocab_dev, dtype=jnp.int32)[None, :]
        local_peak = jnp.max(z, axis=1)
        local_total = jnp.sum(jnp.exp(z - local_peak[:, None]), axis=1)
        local_target = jnp.sum(jnp.where(hit, z, 0.0), axis=1)
        local_sum = jnp.sum(z, axis=1)
        logits.append(z)
        hits.append(hit)
        stats.append(jnp.stack([local_peak, local_total, local_target, local_sum]))
    stats = jnp.concatenate(stats, axis=1).reshape(4, devices, loss_dev)
    stats = jnp.take(stats, order_of, axis=1).transpose(1, 0, 2)
    stats = lax.all_to_all(stats, ALL, split_axis=0, concat_axis=0, tiled=True)
    peak = jnp.max(stats[:, 0], axis=0)
    total = jnp.sum(stats[:, 1] * jnp.exp(stats[:, 0] - peak[None]), axis=0)
    my_log = peak + jnp.log(total)
    my_loss = jnp.sum(
        my_log
        - (1.0 - SMOOTH) * jnp.sum(stats[:, 2], axis=0)
        - SMOOTH / V * jnp.sum(stats[:, 3], axis=0)
        + ZCOEF * my_log * my_log
    )
    logs = lax.all_to_all(jnp.broadcast_to(my_log[None, None], (devices, 1, loss_dev)), ALL, split_axis=0, concat_axis=0, tiled=True)
    log_total = jnp.take(logs[:, 0], source_of, axis=0).reshape(2, loss_total // 2, 1)
    d_logits = [
        (
            (
                (1.0 + 2.0 * ZCOEF * log_total[side]) * jnp.exp(logits[side] - log_total[side])
                - jnp.where(hits[side], 1.0 - SMOOTH, 0.0)
                - SMOOTH / V
            )
            / loss_total
        ).astype(bf16)
        for side in (1, 0)
    ]
    got = flip(dot(d_logits[0], wide_table).astype(bf16), "c", 1, 2)
    d_hidden = (dot(d_logits[1], wide_table) + got.astype(f32)).reshape(4, rows_q, loss_dev, WIDE)
    d_low = d_hidden.astype(bf16)
    d_hidden = d_hidden[0]
    for k in (1, 2, 3):
        d_hidden = d_hidden + flip(d_low[k], ("y", "x"), k, 4).astype(f32)
    d_low = d_hidden.astype(bf16)
    total_hidden = pick_block(d_hidden, q_index)
    for k in range(1, rows_q):
        total_hidden = total_hidden + flip(pick_block(d_low, q_index ^ k), "q", k, rows_q).astype(f32)
    total_hidden = total_hidden[:, :D]
    head_grad = (dot(d_logits[1], sides[0], 0, 0) + dot(d_logits[0], sides[1], 0, 0))[:, :D]
    head_grad, total_hidden = lax.optimization_barrier((head_grad, total_hidden))

    d_x_two, grad_final = norm_back(x_two, gains[2], total_hidden)
    d_down = spread_plane(d_x_two.astype(bf16))
    d_act = dot(d_down, w_down, 1, 1)
    d_gate = d_act * up * sig * (1.0 + gate * (1.0 - sig))
    d_gu = jnp.concatenate([d_gate, d_act * gate * sig], axis=1).astype(bf16)
    d_h_mlp = fold_plane(d_gu, w_gu, 1)
    grad_down = dot(act, d_down, 0, 0)[:, :D].astype(bf16)
    grad_gu = dot(h_all, d_gu, 0, 0)[:D].astype(bf16)
    d_x_mlp, grad_mlp = norm_back(x_one, gains[1], d_h_mlp)
    d_x_one = d_x_two + d_x_mlp

    d_branch = d_x_one.astype(bf16)
    d_attended = dot(d_branch, w_out, 1, 1)
    d_mixed = heads_of(d_attended.astype(bf16))
    d_probs = jnp.einsum("hqd,hkd->hqk", d_mixed, value_h, preferred_element_type=f32)
    delta = jnp.sum(probs * d_probs, axis=-1, keepdims=True)
    d_scores = (probs * (d_probs - delta)).astype(bf16)
    d_query = jnp.einsum("hqk,hkd->hqd", d_scores, key_h, preferred_element_type=f32) * HEAD_SIZE**-0.5
    d_key = jnp.einsum("hqk,hqd->khd", d_scores, query_h, preferred_element_type=f32) * HEAD_SIZE**-0.5
    d_value = jnp.einsum("hqk,hqd->khd", probs_low, d_mixed, preferred_element_type=f32)
    d_q = rotate_back(heads_back(d_query), cosine_pick, sine_pick).astype(bf16)
    d_k = rotate_back(d_key.reshape(tokens, UNIT), cosine, sine)
    d_kv = jnp.concatenate([d_k, d_value.reshape(tokens, UNIT)], axis=1).astype(bf16)
    d_h_pick = dot(d_q, w_q, 1, 1)
    high = d_h_pick.astype(bf16)
    rest = (d_h_pick - high.astype(f32)).astype(bf16)
    d_h_attn = dot(d_kv, w_kv, 1, 1) + dot(pick, high, 0, 0) + dot(pick, rest, 0, 0)
    d_x_attn, grad_attn = norm_back(x_embed, gains[0], d_h_attn)
    high = d_x_one.astype(bf16)
    rest = (d_x_one - high.astype(f32)).astype(bf16)
    d_x_embed = d_x_attn + dot(pick, high, 0, 0) + dot(pick, rest, 0, 0)

    scaled = (d_x_embed * emb_mult).astype(bf16)
    sending = [
        dot(spot_between(low, high), scaled, 0, 0).astype(bf16).reshape(devices, high - low, D)
        for low, high in zip(cuts_back, cuts_back[1:])
    ]
    if aligned:
        blocks = jnp.concatenate([jnp.zeros((1, 480, 640), bf16), grad_gu.reshape(2, 480, 640), down_pack(grad_down)[None]])
        share = lax.psum_scatter(blocks, "q", scatter_dimension=0, tiled=False)
        sending, d_q, d_kv, attended = lax.optimization_barrier((sending, d_q, d_kv, attended))
        share, d_q, d_kv, attended = lax.optimization_barrier((share, d_q, d_kv, attended))
    arrived = [exchange(blocks) for blocks in sending]
    grad_out = dot(attended, d_branch, 0, 0).astype(bf16)
    grad_q = dot(h_pick, d_q, 0, 0).astype(bf16)
    grad_kv = dot(h_attn, d_kv, 0, 0).astype(bf16)

    def norm_of(squares):
        sums = jnp.broadcast_to(jnp.stack([squares, my_loss])[None], (devices, 2))
        sums = jnp.sum(lax.all_to_all(sums, ALL, split_axis=0, concat_axis=0, tiled=True), axis=0)
        grad_norm = jnp.sqrt(sums[0])
        limit = CLIP_C / math.sqrt(loss_total)
        return sums[1] / loss_total, grad_norm, limit / jnp.maximum(grad_norm, limit)

    gain_grads = jnp.concatenate([grad_attn, grad_mlp, grad_final]).astype(bf16)
    if aligned:
        lower = jnp.concatenate([grad_q.reshape(5, TOP, D), grad_kv.reshape(5, SHARE - TOP, D)], axis=1)
        level = jnp.concatenate([lower, grad_out.reshape(3, SHARE, D)])
        room = jnp.zeros((8, ROOM, D), bf16).at[0, :3].set(gain_grads.reshape(3, D))
        level = jnp.concatenate([level, room], axis=1).reshape(4, 2, SHARE + ROOM, D)
        level, arrived[0] = lax.optimization_barrier((level, arrived[0]))
        keep = lax.dynamic_index_in_dim(level, c_index, 1, False)
        give = lax.dynamic_index_in_dim(level, 1 - c_index, 1, False)
        cores = [rows.reshape(2, 2, SHARE + ROOM, D) for rows in (keep, flip(give, "c", 1, 2))]
        middle = (SHARE + ROOM) // 2
        x_index, y_index = lax.axis_index("x"), lax.axis_index("y")

        def upper(index):
            return sum(pick_block(rows[:, :, :middle], index, 1).astype(f32) for rows in cores)

        def under(index):
            return sum(pick_block(rows[:, :, middle:], index, 0).astype(f32) for rows in cores)

        left = upper(x_index) + flip(upper(1 - x_index).astype(bf16), "x", 1, 2).astype(f32)
        right = under(y_index) + flip(under(1 - y_index).astype(bf16), "y", 1, 2).astype(f32)
        left = pick_block(left, y_index) + flip(pick_block(left, 1 - y_index).astype(bf16), "y", 1, 2).astype(f32)
        right = pick_block(right, x_index) + flip(pick_block(right, 1 - x_index).astype(bf16), "x", 1, 2).astype(f32)
        own = jnp.concatenate([left, right])
        own = own.reshape(4, (SHARE + ROOM) // 4, D)
        own, share, arrived[1] = lax.optimization_barrier((own, share, arrived[1]))
        got = lax.all_to_all(share.reshape(8, 60, 640), PLANE, split_axis=0, concat_axis=0, tiled=True)
        quarter = lax.dynamic_index_in_dim(own, q_index, 0, False)
        for k in (1, 2, 3):
            piece = lax.dynamic_index_in_dim(own, q_index ^ k, 0, False).astype(bf16)
            quarter = quarter + flip(piece, "q", k, 4).astype(f32)
        table_grad = head_grad
        for low, high, rows in zip(cuts_back, cuts_back[1:], arrived):
            table_grad = table_grad + dot(rows_between(low, high), rows, 0, 0)
        table_squares = jnp.sum(table_grad * table_grad)
        quarter = quarter.astype(bf16)
        squares = jnp.sum(quarter.astype(f32) ** 2) + jnp.sum(share.astype(f32) ** 2) + table_squares
        quarter, squares, got = lax.optimization_barrier((quarter, squares, got))
        quarters = [quarter] + [lax.ppermute(quarter, "q", [(k, 0)]) for k in (1, 2, 3)]
        loss, grad_norm, clip_factor = norm_of(squares)
        table_new = adamw_step(table_master, table_grad, table_m, table_v, clip_factor)
        quarters, table_new = lax.optimization_barrier((quarters, table_new))
        first = jnp.concatenate(quarters)
        gain_out = first[SHARE : SHARE + 3].reshape(-1)
        both = jnp.concatenate([first[:TOP], first[TOP:SHARE].reshape(TOP, KV)], axis=1)
        first = jnp.where(p_index < 5, both.reshape(-1), first[:SHARE].reshape(-1))
        by_share = got.reshape(8, 60, 2, UNIT).transpose(1, 2, 0, 3).reshape(-1)
        mine = jnp.where(q_index == 3, down_unpack(share).reshape(-1), by_share)
        mine = jnp.where(q_index == 0, first, mine)
    else:
        table_grad = head_grad
        for low, high, rows in zip(cuts_back, cuts_back[1:], arrived):
            table_grad = table_grad + dot(rows_between(low, high), rows, 0, 0)
        table_squares = jnp.sum(table_grad * table_grad)
        both = lax.dynamic_update_index_in_dim(jnp.zeros((D, 2, 8, UNIT), bf16), grad_gu.reshape(D, 2, UNIT), p_index, 2)
        downs = lax.dynamic_update_index_in_dim(jnp.zeros((8, SHARE, D), bf16), grad_down, p_index, 0)
        full = jnp.concatenate([part.reshape(-1, UNIT) for part in (jnp.concatenate([grad_q, grad_kv], axis=1), grad_out, both, downs)]).reshape(devices, units, UNIT)
        room = jnp.zeros((devices, 16, UNIT), bf16).at[0, :GAIN_UNITS].set(gain_grads.reshape(GAIN_UNITS, UNIT))
        full = jnp.concatenate([full, room], axis=1)
        summed = lax.psum_scatter(full, ALL, scatter_dimension=0, tiled=False)
        mine, gain_out = summed[:units].reshape(-1), summed[units : units + GAIN_UNITS].reshape(-1)
    behind = lax.ppermute(mine[span - GAINS :], ALL, [(i, i + 1) for i in range(devices - 1)])
    behind = jnp.where(me == 0, gain_out, behind)
    tail = max(0, drift * (devices - 1) + shard - GAINS - span)
    stream = jnp.concatenate([behind, mine, jnp.zeros((tail,), bf16)])
    layer_grad = lax.dynamic_slice(stream, (drift * me,), (shard,)).astype(f32)

    if not aligned:
        loss, grad_norm, clip_factor = norm_of(jnp.sum(layer_grad * layer_grad) + table_squares)
        table_new = adamw_step(table_master, table_grad, table_m, table_v, clip_factor)
    flat_new = adamw_step(flat_master, layer_grad, flat_m, flat_v, clip_factor)
    return (loss, grad_norm) + flat_new + table_new


def solution(mesh):
    count = mesh.devices.size
    grid = Mesh(mesh.devices.reshape(count // 8, 2, 2, 2), ALL)
    rows, matrix = P(ALL), P(ALL, None)
    in_specs = (rows,) * 6 + (matrix,) * 3
    out_specs = (P(), P()) + (rows,) * 3 + (matrix,) * 3
    return jax.shard_map(local, mesh=grid, in_specs=in_specs, out_specs=out_specs, check_vma=False)
```

```python
import math

import jax
import jax.numpy as jnp
import numpy as np
from jax import lax
from jax.sharding import Mesh, PartitionSpec as P

D = 960
QUERY_HEADS = 15
KEY_VALUE_HEADS = 5
HEAD_SIZE = 64
FF = 2560
V = 32000
PL = 256
CL = 128
STEP = 10
QKV = 1600

EPS = 1e-05
SMOOTH = 0.1
ZCOEF = 0.0001
BETA1 = 0.9
BETA2 = 0.95
ADAM_EPS = 1e-08
DECAY = 0.1
RATE = 0.03
CLIP_C = 25.0
NEGATIVE = -1e30

UNIT = 320
GAINS = 3 * D
GAIN_UNITS = GAINS // UNIT
QKV_UNITS = D * QKV // UNIT
OUT_UNITS = D * D // UNIT
GU_UNITS = D * 2 * FF // UNIT
DOWN_UNITS = FF * D // UNIT
ALL_UNITS = QKV_UNITS + OUT_UNITS + GU_UNITS + DOWN_UNITS
PLANE = ("y", "x", "c")
ALL = ("q", "y", "x", "c")
SHARE = FF // 8
TOP = D // 5
KV = QKV - D
ROOM = 32
WIDE = 1024

bf16 = jnp.bfloat16
f32 = jnp.float32


def dot(left, right, left_dim=1, right_dim=0):
    return lax.dot_general(
        left, right, (((left_dim,), (right_dim,)), ((), ())), preferred_element_type=f32
    )


def hot(index, count):
    return (index[:, None] == jnp.arange(count, dtype=jnp.int32)[None, :]).astype(bf16)


def scale_of(rows):
    return lax.rsqrt(jnp.mean(rows * rows, axis=-1, keepdims=True) + EPS)


def norm_back(rows, gain, grad):
    scale = scale_of(rows)
    normed = rows * scale
    grad_gain = jnp.sum(grad * normed, axis=0)
    scaled = grad * gain
    return scale * (scaled - normed * jnp.mean(scaled * normed, axis=-1, keepdims=True)), grad_gain


def flip(rows, axes, bits, size):
    return lax.ppermute(rows, axes, [(i, i ^ bits) for i in range(size)])


def rope_tables(count):
    row = np.arange(count)
    position = np.where(row < PL, row, PL + (row - PL) % CL).astype(np.float32)
    half = np.arange(HEAD_SIZE // 2, dtype=np.float32)
    freqs = np.float32(10000.0) ** (-(half * np.float32(2.0) / np.float32(HEAD_SIZE)))
    angles = (position[:, None] * freqs[None, :].astype(np.float32)).astype(np.float64)
    angles = np.concatenate([angles, angles], axis=-1)
    return np.cos(angles).astype(np.float32), np.sin(angles).astype(np.float32)


def rotate(rows, cosine, sine):
    heads = rows.reshape(rows.shape[0], -1, HEAD_SIZE)
    half = HEAD_SIZE // 2
    turned = jnp.concatenate([-heads[..., half:], heads[..., :half]], axis=-1)
    return (heads * cosine[:, None, :] + turned * sine[:, None, :]).reshape(rows.shape)


def rotate_back(grad, cosine, sine):
    heads = grad.reshape(grad.shape[0], -1, HEAD_SIZE)
    half = HEAD_SIZE // 2
    spun = heads * sine[:, None, :]
    turned = jnp.concatenate([spun[..., half:], -spun[..., :half]], axis=-1)
    return (heads * cosine[:, None, :] + turned).reshape(grad.shape)


def adamw_step(param, gradient, moment_one, moment_two, clip_factor):
    gradient = gradient * clip_factor
    new_one = BETA1 * moment_one + (1.0 - BETA1) * gradient
    new_two = BETA2 * moment_two + (1.0 - BETA2) * gradient * gradient
    ratio = new_one / (1.0 - BETA1**STEP) / (jnp.sqrt(new_two / (1.0 - BETA2**STEP)) + ADAM_EPS)
    return (new_one, new_two, -RATE * (ratio + DECAY * param))


def merge_stats(one, two):
    peak = jnp.maximum(one[0], two[0])
    total = one[1] * jnp.exp(one[0] - peak) + two[1] * jnp.exp(two[0] - peak)
    return jnp.stack([peak, total, one[2] + two[2], one[3] + two[3]])


def pick_block(blocks, index, axis=0):
    return lax.dynamic_index_in_dim(blocks, index, axis, False)


def widen(rows):
    return jnp.pad(rows, ((0, 0), (0, WIDE - D)))


def fold_plane(left, right, right_dim):
    c_index, yx_index = lax.axis_index("c"), lax.axis_index(("y", "x"))
    rows = left.reshape(4, 2, left.shape[0] // 8, left.shape[1])
    far = pick_block(rows, 1 - c_index, 1).reshape(-1, left.shape[1])
    near = pick_block(rows, c_index, 1).reshape(-1, left.shape[1])
    got = flip(dot(far, right, 1, right_dim).astype(bf16), "c", 1, 2)
    mine = (dot(near, right, 1, right_dim) + got.astype(f32)).reshape(4, -1, WIDE)
    low = mine.astype(bf16)
    total = pick_block(mine, yx_index)
    for k in (1, 2, 3):
        total = total + flip(pick_block(low, yx_index ^ k), ("y", "x"), k, 4).astype(f32)
    return total[:, :D]


def down_pack(rows):
    side = jnp.concatenate([rows[: SHARE // 2, 640:], rows[SHARE // 2 :, 640:]], axis=1)
    return jnp.concatenate([rows[:, :640], side])


def down_unpack(rows):
    side = jnp.concatenate([rows[SHARE:, :UNIT], rows[SHARE:, UNIT:]])
    return jnp.concatenate([rows[:SHARE], side], axis=1)


def spread_plane(rows):
    return widen(lax.all_gather(rows, PLANE).reshape(-1, D))


def local(
    token_ids, loss_rows, targets, flat_master, flat_m, flat_v, table_master, table_m, table_v
):
    devices = lax.axis_size(ALL)
    rows_q = lax.axis_size("q")
    me = lax.axis_index(ALL)
    q_index = lax.axis_index("q")
    p_index = lax.axis_index(PLANE)
    c_index = lax.axis_index("c")
    yx_index = lax.axis_index(("y", "x"))
    tokens = token_ids.shape[0]
    vocab_dev = table_master.shape[0]
    loss_dev = loss_rows.shape[0]
    loss_total = loss_dev * devices
    capacity = max(2, 2 * tokens // devices)
    slots = devices * capacity
    groups = QUERY_HEADS // KEY_VALUE_HEADS
    emb_mult = math.sqrt(D) * 0.5
    shard = flat_master.shape[0]
    units = ALL_UNITS // devices
    span = units * UNIT
    drift = shard - span
    aligned = devices == 32

    place = np.array([q * 8 + kyx * 2 + kc for kc in range(2) for kyx in range(4) for q in range(rows_q)])
    source_of = p_index ^ jnp.asarray(place, jnp.int32)

    table_low = table_master.astype(bf16)
    owner = token_ids // vocab_dev
    owner_hot = hot(owner, devices)
    before = (lax.broadcasted_iota(jnp.int32, (tokens, tokens), 0) > lax.broadcasted_iota(jnp.int32, (tokens, tokens), 1)).astype(bf16)
    slot = jnp.sum(dot(before, owner_hot) * owner_hot.astype(f32), axis=1).astype(jnp.int32)
    spot = hot(owner * capacity + slot, slots)

    def spot_between(low, high):
        inside = (slot >= low) & (slot < high)
        return hot(jnp.where(inside, owner * (high - low) + slot - low, -1), devices * (high - low))

    def rows_between(low, high):
        return hot(asked[:, low:high].reshape(-1) - me * vocab_dev, vocab_dev)

    def exchange(blocks):
        return lax.all_to_all(blocks, ALL, split_axis=0, concat_axis=0, tiled=True).reshape(-1, D)

    cuts_back = (0, capacity // 4, capacity)
    marked = token_ids + 1
    halves = jnp.stack([marked // 256, marked % 256]).astype(bf16)
    found = dot(halves, spot).astype(jnp.int32)
    requests = (found[0] * 256 + found[1] - 1).reshape(devices, capacity)
    ask = jnp.concatenate([requests, jnp.broadcast_to(targets[None], (devices, loss_dev))], axis=1)

    flat_low = flat_master.astype(bf16)
    ahead = lax.ppermute(flat_low[:GAINS], ALL, [(i + 1, i) for i in range(devices - 1)])
    back = max(0, drift * (devices - 1) - GAINS)
    pieces = [flat_low, ahead]
    if back:
        pieces = [lax.ppermute(flat_low[shard - back :], ALL, [(i, i + 1) for i in range(devices - 1)])] + pieces
    chunk = lax.dynamic_slice(jnp.concatenate(pieces), (back + GAINS - drift * me,), (span,))
    if aligned:
        sent = chunk.reshape(60, 2, 8, UNIT).transpose(2, 0, 1, 3).reshape(8, 60, 2 * UNIT)
        got = lax.all_to_all(sent, PLANE, split_axis=0, concat_axis=0, tiled=True)
        both = chunk.reshape(TOP, QKV)
        both = jnp.concatenate([both[:, :D], both[:, D:].reshape(SHARE - TOP, D)])
        first = jnp.where(p_index < 5, both, chunk.reshape(SHARE, D))
        first = jnp.concatenate([first, flat_low[:GAINS].reshape(3, D), jnp.zeros((5, D), bf16)])
        first, ask = lax.optimization_barrier((first, ask))
        asked = lax.all_to_all(ask, ALL, split_axis=0, concat_axis=0, tiled=True)
        answer = dot(rows_between(0, capacity), table_low).astype(bf16).reshape(devices, capacity, D)
        jumped = lax.ppermute(first, "q", [(0, 2)])
        first = jnp.where(q_index == 2, jumped, first)
        stepped = lax.ppermute(first, "q", [(0, 1), (2, 3)])
        first = jnp.where((q_index == 1) | (q_index == 3), stepped, first)
        answer, first, got = lax.optimization_barrier((answer, first, got))
        returned = exchange(answer)
        level = lax.all_gather(first, PLANE)
        mixed = jnp.where(q_index == 3, down_pack(chunk.reshape(SHARE, D)), got.reshape(480, 2 * UNIT))
        mixed, level = lax.optimization_barrier((mixed, level))
        gains = level[0, SHARE : SHARE + 3].astype(f32)
        w_q = level[:5, :TOP].reshape(D, D)
        w_kv = level[:5, TOP:SHARE].reshape(D, KV)
        w_out = level[5:, :SHARE].reshape(D, D)
        returned, w_q, w_kv, w_out = lax.optimization_barrier((returned, w_q, w_kv, w_out))
        column = lax.all_gather(mixed, "q")
    else:
        asked = lax.all_to_all(ask, ALL, split_axis=0, concat_axis=0, tiled=True)
        answer = dot(rows_between(0, capacity), table_low).astype(bf16).reshape(devices, capacity, D)
        returned = exchange(answer)
        extra = jnp.zeros((16 * UNIT,), bf16).at[:GAINS].set(flat_low[:GAINS])
        full = lax.all_gather(jnp.concatenate([chunk, extra]).reshape(units + 16, UNIT), ALL)
        gains = full[0, units : units + GAIN_UNITS].astype(f32).reshape(3, D)
        full = full[:, :units].reshape(ALL_UNITS, UNIT)
        edge = np.cumsum([QKV_UNITS, OUT_UNITS, GU_UNITS])
        w_qkv = full[: edge[0]].reshape(D, QKV)
        w_q, w_kv = w_qkv[:, :D], w_qkv[:, D:]
        w_out = full[edge[0] : edge[1]].reshape(D, D)
        both = lax.dynamic_index_in_dim(full[edge[1] : edge[2]].reshape(D, 2, 8, UNIT), p_index, 2, False)
        w_gu = both.reshape(D, 2 * SHARE)
        w_down = lax.dynamic_index_in_dim(full[edge[2] :].reshape(8, SHARE, D), p_index, 0, False)
    x_low = dot(spot, returned).astype(bf16)
    x_embed = x_low.astype(f32) * emb_mult

    pick = hot(loss_rows, tokens)
    cosine, sine = (jnp.asarray(t) for t in rope_tables(tokens))
    cosine_pick, sine_pick = cosine[loss_rows], sine[loss_rows]
    h_attn = (x_embed * scale_of(x_embed) * gains[0]).astype(bf16)
    h_pick = dot(pick, h_attn).astype(bf16)
    x_pick = dot(pick, x_low) * emb_mult
    query = rotate(dot(h_pick, w_q), cosine_pick, sine_pick).astype(bf16)
    key_value = dot(h_attn, w_kv)
    key = rotate(key_value[:, :UNIT], cosine, sine).astype(bf16)
    value = key_value[:, UNIT:].astype(bf16)

    def heads_of(rows):
        return rows.reshape(loss_dev, KEY_VALUE_HEADS, groups, HEAD_SIZE).transpose(1, 2, 0, 3).reshape(KEY_VALUE_HEADS, groups * loss_dev, HEAD_SIZE)

    def heads_back(rows):
        return rows.reshape(KEY_VALUE_HEADS, groups, loss_dev, HEAD_SIZE).transpose(2, 0, 1, 3).reshape(loss_dev, D)

    query_h = heads_of(query)
    key_h = key.reshape(tokens, KEY_VALUE_HEADS, HEAD_SIZE).transpose(1, 0, 2)
    value_h = value.reshape(tokens, KEY_VALUE_HEADS, HEAD_SIZE).transpose(1, 0, 2)
    key_pos = jnp.arange(tokens, dtype=jnp.int32)[None, :]
    ask_pos = jnp.tile(loss_rows, groups)[:, None]
    key_seg = jnp.where(key_pos < PL, 0, 1 + (key_pos - PL) // CL)
    ask_seg = jnp.where(ask_pos < PL, 0, 1 + (ask_pos - PL) // CL)
    allowed = (key_pos <= ask_pos) & ((key_seg == 0) | (key_seg == ask_seg))
    scores = jnp.einsum("hqd,hkd->hqk", query_h, key_h, preferred_element_type=f32) * HEAD_SIZE**-0.5
    scores = jnp.where(allowed[None], scores, NEGATIVE)
    exp_scores = jnp.exp(scores - jnp.max(scores, axis=-1, keepdims=True))
    probs = exp_scores / jnp.sum(exp_scores, axis=-1, keepdims=True)
    probs_low = probs.astype(bf16)
    mixed_heads = jnp.einsum("hqk,hkd->hqd", probs_low, value_h, preferred_element_type=f32)
    attended = heads_back(mixed_heads.astype(bf16))
    x_one = x_pick + dot(attended, w_out)

    h_mlp = (x_one * scale_of(x_one) * gains[1]).astype(bf16)
    h_all = spread_plane(h_mlp)
    if aligned:
        column, h_all = lax.optimization_barrier((column, h_all))
        w_gu = column[1:3].reshape(D, 2 * SHARE)
        w_down = down_unpack(column[3])
    w_gu = jnp.pad(w_gu, ((0, WIDE - D), (0, 0)))
    w_down = widen(w_down)
    gate_up = dot(h_all, w_gu)
    gate, up = gate_up[:, :SHARE], gate_up[:, SHARE:]
    sig = jax.nn.sigmoid(gate)
    act = (gate * sig * up).astype(bf16)
    x_two = x_one + fold_plane(act, w_down, 0)

    hidden = (x_two * scale_of(x_two) * gains[2]).astype(bf16)
    wide_table = widen(table_low)
    across = lax.all_gather(widen(hidden), "q")
    by_x, by_y = flip(across, "x", 1, 2), flip(across, "y", 1, 2)
    cut = rows_q // 2
    corner = [flip(by_x[:cut], "y", 1, 2), flip(by_y[cut:], "x", 1, 2)]
    near = jnp.concatenate([across, by_x, by_y] + corner).reshape(loss_total // 2, WIDE)
    sides = [near, flip(near, "c", 1, 2)]
    targets_all = jnp.take(asked[:, capacity:], source_of, axis=0).reshape(2, loss_total // 2)
    logits, hits, stats = [], [], []
    for side, rows in enumerate(sides):
        z = dot(rows, wide_table, 1, 1)
        column_id = targets_all[side] - me * vocab_dev
        hit = column_id[:, None] == jnp.arange(vocab_dev, dtype=jnp.int32)[None, :]
        local_peak = jnp.max(z, axis=1)
        local_total = jnp.sum(jnp.exp(z - local_peak[:, None]), axis=1)
        local_target = jnp.sum(jnp.where(hit, z, 0.0), axis=1)
        local_sum = jnp.sum(z, axis=1)
        logits.append(z)
        hits.append(hit)
        stats.append(jnp.stack([local_peak, local_total, local_target, local_sum]))
    stats = jnp.concatenate(stats, axis=1)
    block = rows_q * loss_dev
    for axis, bit in (("c", 4), ("x", 1), ("y", 2)):
        other = flip(stats, axis, 1, 2)
        other = jnp.concatenate([other[:, (k ^ bit) * block : ((k ^ bit) + 1) * block] for k in range(8)], axis=1)
        stats = merge_stats(stats, other)
    bit = 1
    while bit < rows_q:
        stats = merge_stats(stats, flip(stats, "q", bit, rows_q))
        bit *= 2
    log_total = stats[0] + jnp.log(stats[1])
    mine_at = q_index * loss_dev
    my_log, my_target, my_sum = (lax.dynamic_slice(row, (mine_at,), (loss_dev,)) for row in (log_total, stats[2], stats[3]))
    my_loss = jnp.sum(my_log - (1.0 - SMOOTH) * my_target - SMOOTH / V * my_sum + ZCOEF * my_log * my_log)
    log_total = log_total.reshape(2, loss_total // 2, 1)
    d_logits = [
        (
            (
                (1.0 + 2.0 * ZCOEF * log_total[side]) * jnp.exp(logits[side] - log_total[side])
                - jnp.where(hits[side], 1.0 - SMOOTH, 0.0)
                - SMOOTH / V
            )
            / loss_total
        ).astype(bf16)
        for side in (1, 0)
    ]
    got = flip(dot(d_logits[0], wide_table).astype(bf16), "c", 1, 2)
    d_hidden = (dot(d_logits[1], wide_table) + got.astype(f32)).reshape(4, rows_q, loss_dev, WIDE)
    d_low = d_hidden.astype(bf16)
    d_hidden = d_hidden[0]
    for k in (1, 2, 3):
        d_hidden = d_hidden + flip(d_low[k], ("y", "x"), k, 4).astype(f32)
    d_low = d_hidden.astype(bf16)
    total_hidden = pick_block(d_hidden, q_index)
    for k in range(1, rows_q):
        total_hidden = total_hidden + flip(pick_block(d_low, q_index ^ k), "q", k, rows_q).astype(f32)
    total_hidden = total_hidden[:, :D]
    head_grad = (dot(d_logits[1], sides[0], 0, 0) + dot(d_logits[0], sides[1], 0, 0))[:, :D]
    head_grad, total_hidden = lax.optimization_barrier((head_grad, total_hidden))

    d_x_two, grad_final = norm_back(x_two, gains[2], total_hidden)
    d_down = spread_plane(d_x_two.astype(bf16))
    d_act = dot(d_down, w_down, 1, 1)
    d_gate = d_act * up * sig * (1.0 + gate * (1.0 - sig))
    d_gu = jnp.concatenate([d_gate, d_act * gate * sig], axis=1).astype(bf16)
    d_h_mlp = fold_plane(d_gu, w_gu, 1)
    grad_down = dot(act, d_down, 0, 0)[:, :D].astype(bf16)
    grad_gu = dot(h_all, d_gu, 0, 0)[:D].astype(bf16)
    d_x_mlp, grad_mlp = norm_back(x_one, gains[1], d_h_mlp)
    d_x_one = d_x_two + d_x_mlp

    d_branch = d_x_one.astype(bf16)
    d_attended = dot(d_branch, w_out, 1, 1)
    d_mixed = heads_of(d_attended.astype(bf16))
    d_probs = jnp.einsum("hqd,hkd->hqk", d_mixed, value_h, preferred_element_type=f32)
    delta = jnp.sum(probs * d_probs, axis=-1, keepdims=True)
    d_scores = (probs * (d_probs - delta)).astype(bf16)
    d_query = jnp.einsum("hqk,hkd->hqd", d_scores, key_h, preferred_element_type=f32) * HEAD_SIZE**-0.5
    d_key = jnp.einsum("hqk,hqd->khd", d_scores, query_h, preferred_element_type=f32) * HEAD_SIZE**-0.5
    d_value = jnp.einsum("hqk,hqd->khd", probs_low, d_mixed, preferred_element_type=f32)
    d_q = rotate_back(heads_back(d_query), cosine_pick, sine_pick).astype(bf16)
    d_k = rotate_back(d_key.reshape(tokens, UNIT), cosine, sine)
    d_kv = jnp.concatenate([d_k, d_value.reshape(tokens, UNIT)], axis=1).astype(bf16)
    d_h_pick = dot(d_q, w_q, 1, 1)
    high = d_h_pick.astype(bf16)
    rest = (d_h_pick - high.astype(f32)).astype(bf16)
    d_h_attn = dot(d_kv, w_kv, 1, 1) + dot(pick, high, 0, 0) + dot(pick, rest, 0, 0)
    d_x_attn, grad_attn = norm_back(x_embed, gains[0], d_h_attn)
    high = d_x_one.astype(bf16)
    rest = (d_x_one - high.astype(f32)).astype(bf16)
    d_x_embed = d_x_attn + dot(pick, high, 0, 0) + dot(pick, rest, 0, 0)

    scaled = (d_x_embed * emb_mult).astype(bf16)
    sending = [
        dot(spot_between(low, high), scaled, 0, 0).astype(bf16).reshape(devices, high - low, D)
        for low, high in zip(cuts_back, cuts_back[1:])
    ]
    if aligned:
        blocks = jnp.concatenate([jnp.zeros((1, 480, 640), bf16), grad_gu.reshape(2, 480, 640), down_pack(grad_down)[None]])
        share = lax.psum_scatter(blocks, "q", scatter_dimension=0, tiled=False)
        sending, d_q, d_kv, attended = lax.optimization_barrier((sending, d_q, d_kv, attended))
        share, d_q, d_kv, attended = lax.optimization_barrier((share, d_q, d_kv, attended))
    arrived = [exchange(blocks) for blocks in sending]
    grad_out = dot(attended, d_branch, 0, 0).astype(bf16)
    grad_q = dot(h_pick, d_q, 0, 0).astype(bf16)
    grad_kv = dot(h_attn, d_kv, 0, 0).astype(bf16)

    def norm_of(squares):
        sums = jnp.broadcast_to(jnp.stack([squares, my_loss])[None], (devices, 2))
        sums = jnp.sum(lax.all_to_all(sums, ALL, split_axis=0, concat_axis=0, tiled=True), axis=0)
        grad_norm = jnp.sqrt(sums[0])
        limit = CLIP_C / math.sqrt(loss_total)
        return sums[1] / loss_total, grad_norm, limit / jnp.maximum(grad_norm, limit)

    gain_grads = jnp.concatenate([grad_attn, grad_mlp, grad_final]).astype(bf16)
    if aligned:
        lower = jnp.concatenate([grad_q.reshape(5, TOP, D), grad_kv.reshape(5, SHARE - TOP, D)], axis=1)
        level = jnp.concatenate([lower, grad_out.reshape(3, SHARE, D)])
        room = jnp.zeros((8, ROOM, D), bf16).at[0, :3].set(gain_grads.reshape(3, D))
        level = jnp.concatenate([level, room], axis=1).reshape(4, 2, SHARE + ROOM, D)
        level, arrived[0] = lax.optimization_barrier((level, arrived[0]))
        keep = lax.dynamic_index_in_dim(level, c_index, 1, False)
        give = lax.dynamic_index_in_dim(level, 1 - c_index, 1, False)
        cores = [rows.reshape(2, 2, SHARE + ROOM, D) for rows in (keep, flip(give, "c", 1, 2))]
        middle = (SHARE + ROOM) // 2
        x_index, y_index = lax.axis_index("x"), lax.axis_index("y")

        def upper(index):
            return sum(pick_block(rows[:, :, :middle], index, 1).astype(f32) for rows in cores)

        def under(index):
            return sum(pick_block(rows[:, :, middle:], index, 0).astype(f32) for rows in cores)

        left = upper(x_index) + flip(upper(1 - x_index).astype(bf16), "x", 1, 2).astype(f32)
        right = under(y_index) + flip(under(1 - y_index).astype(bf16), "y", 1, 2).astype(f32)
        left = pick_block(left, y_index) + flip(pick_block(left, 1 - y_index).astype(bf16), "y", 1, 2).astype(f32)
        right = pick_block(right, x_index) + flip(pick_block(right, 1 - x_index).astype(bf16), "x", 1, 2).astype(f32)
        own = jnp.concatenate([left, right])
        own = own.reshape(4, (SHARE + ROOM) // 4, D)
        own, share, arrived[1] = lax.optimization_barrier((own, share, arrived[1]))
        got = lax.all_to_all(share.reshape(8, 60, 640), PLANE, split_axis=0, concat_axis=0, tiled=True)
        quarter = lax.dynamic_index_in_dim(own, q_index, 0, False)
        for k in (1, 2, 3):
            piece = lax.dynamic_index_in_dim(own, q_index ^ k, 0, False).astype(bf16)
            quarter = quarter + flip(piece, "q", k, 4).astype(f32)
        table_grad = head_grad
        for low, high, rows in zip(cuts_back, cuts_back[1:], arrived):
            table_grad = table_grad + dot(rows_between(low, high), rows, 0, 0)
        table_squares = jnp.sum(table_grad * table_grad)
        quarter = quarter.astype(bf16)
        squares = jnp.sum(quarter.astype(f32) ** 2) + jnp.sum(share.astype(f32) ** 2) + table_squares
        quarter, squares, got = lax.optimization_barrier((quarter, squares, got))
        quarters = [quarter] + [lax.ppermute(quarter, "q", [(k, 0)]) for k in (1, 2, 3)]
        loss, grad_norm, clip_factor = norm_of(squares)
        table_new = adamw_step(table_master, table_grad, table_m, table_v, clip_factor)
        quarters, table_new = lax.optimization_barrier((quarters, table_new))
        first = jnp.concatenate(quarters)
        gain_out = first[SHARE : SHARE + 3].reshape(-1)
        both = jnp.concatenate([first[:TOP], first[TOP:SHARE].reshape(TOP, KV)], axis=1)
        first = jnp.where(p_index < 5, both.reshape(-1), first[:SHARE].reshape(-1))
        by_share = got.reshape(8, 60, 2, UNIT).transpose(1, 2, 0, 3).reshape(-1)
        mine = jnp.where(q_index == 3, down_unpack(share).reshape(-1), by_share)
        mine = jnp.where(q_index == 0, first, mine)
    else:
        table_grad = head_grad
        for low, high, rows in zip(cuts_back, cuts_back[1:], arrived):
            table_grad = table_grad + dot(rows_between(low, high), rows, 0, 0)
        table_squares = jnp.sum(table_grad * table_grad)
        both = lax.dynamic_update_index_in_dim(jnp.zeros((D, 2, 8, UNIT), bf16), grad_gu.reshape(D, 2, UNIT), p_index, 2)
        downs = lax.dynamic_update_index_in_dim(jnp.zeros((8, SHARE, D), bf16), grad_down, p_index, 0)
        full = jnp.concatenate([part.reshape(-1, UNIT) for part in (jnp.concatenate([grad_q, grad_kv], axis=1), grad_out, both, downs)]).reshape(devices, units, UNIT)
        room = jnp.zeros((devices, 16, UNIT), bf16).at[0, :GAIN_UNITS].set(gain_grads.reshape(GAIN_UNITS, UNIT))
        full = jnp.concatenate([full, room], axis=1)
        summed = lax.psum_scatter(full, ALL, scatter_dimension=0, tiled=False)
        mine, gain_out = summed[:units].reshape(-1), summed[units : units + GAIN_UNITS].reshape(-1)
    behind = lax.ppermute(mine[span - GAINS :], ALL, [(i, i + 1) for i in range(devices - 1)])
    behind = jnp.where(me == 0, gain_out, behind)
    tail = max(0, drift * (devices - 1) + shard - GAINS - span)
    stream = jnp.concatenate([behind, mine, jnp.zeros((tail,), bf16)])
    layer_grad = lax.dynamic_slice(stream, (drift * me,), (shard,)).astype(f32)

    if not aligned:
        loss, grad_norm, clip_factor = norm_of(jnp.sum(layer_grad * layer_grad) + table_squares)
        table_new = adamw_step(table_master, table_grad, table_m, table_v, clip_factor)
    flat_new = adamw_step(flat_master, layer_grad, flat_m, flat_v, clip_factor)
    return (loss, grad_norm) + flat_new + table_new


def solution(mesh):
    count = mesh.devices.size
    grid = Mesh(mesh.devices.reshape(count // 8, 2, 2, 2), ALL)
    rows, matrix = P(ALL), P(ALL, None)
    in_specs = (rows,) * 6 + (matrix,) * 3
    out_specs = (P(), P()) + (rows,) * 3 + (matrix,) * 3
    return jax.shard_map(local, mesh=grid, in_specs=in_specs, out_specs=out_specs, check_vma=False)
```

```python
import math

import jax
import jax.numpy as jnp
import numpy as np
from jax import lax
from jax.sharding import Mesh, PartitionSpec as P

D = 960
QUERY_HEADS = 15
KEY_VALUE_HEADS = 5
HEAD_SIZE = 64
FF = 2560
V = 32000
PL = 256
CL = 128
STEP = 10
QKV = 1600

EPS = 1e-05
SMOOTH = 0.1
ZCOEF = 0.0001
BETA1 = 0.9
BETA2 = 0.95
ADAM_EPS = 1e-08
DECAY = 0.1
RATE = 0.03
CLIP_C = 25.0
NEGATIVE = -1e30

UNIT = 320
GAINS = 3 * D
GAIN_UNITS = GAINS // UNIT
QKV_UNITS = D * QKV // UNIT
OUT_UNITS = D * D // UNIT
GU_UNITS = D * 2 * FF // UNIT
DOWN_UNITS = FF * D // UNIT
ALL_UNITS = QKV_UNITS + OUT_UNITS + GU_UNITS + DOWN_UNITS
PLANE = ("y", "x", "c")
ALL = ("q", "y", "x", "c")
SHARE = FF // 8
TOP = D // 5
KV = QKV - D
ROOM = 32
WIDE = 1024

bf16 = jnp.bfloat16
f32 = jnp.float32


def dot(left, right, left_dim=1, right_dim=0):
    return lax.dot_general(
        left, right, (((left_dim,), (right_dim,)), ((), ())), preferred_element_type=f32
    )


def hot(index, count):
    return (index[:, None] == jnp.arange(count, dtype=jnp.int32)[None, :]).astype(bf16)


def scale_of(rows):
    return lax.rsqrt(jnp.mean(rows * rows, axis=-1, keepdims=True) + EPS)


def norm_back(rows, gain, grad):
    scale = scale_of(rows)
    normed = rows * scale
    grad_gain = jnp.sum(grad * normed, axis=0)
    scaled = grad * gain
    return scale * (scaled - normed * jnp.mean(scaled * normed, axis=-1, keepdims=True)), grad_gain


def flip(rows, axes, bits, size):
    return lax.ppermute(rows, axes, [(i, i ^ bits) for i in range(size)])


def rope_tables(count):
    row = np.arange(count)
    position = np.where(row < PL, row, PL + (row - PL) % CL).astype(np.float32)
    half = np.arange(HEAD_SIZE // 2, dtype=np.float32)
    freqs = np.float32(10000.0) ** (-(half * np.float32(2.0) / np.float32(HEAD_SIZE)))
    angles = (position[:, None] * freqs[None, :].astype(np.float32)).astype(np.float64)
    angles = np.concatenate([angles, angles], axis=-1)
    return np.cos(angles).astype(np.float32), np.sin(angles).astype(np.float32)


def rotate(rows, cosine, sine):
    heads = rows.reshape(rows.shape[0], -1, HEAD_SIZE)
    half = HEAD_SIZE // 2
    turned = jnp.concatenate([-heads[..., half:], heads[..., :half]], axis=-1)
    return (heads * cosine[:, None, :] + turned * sine[:, None, :]).reshape(rows.shape)


def rotate_back(grad, cosine, sine):
    heads = grad.reshape(grad.shape[0], -1, HEAD_SIZE)
    half = HEAD_SIZE // 2
    spun = heads * sine[:, None, :]
    turned = jnp.concatenate([spun[..., half:], -spun[..., :half]], axis=-1)
    return (heads * cosine[:, None, :] + turned).reshape(grad.shape)


def adamw_step(param, gradient, moment_one, moment_two, clip_factor):
    gradient = gradient * clip_factor
    new_one = BETA1 * moment_one + (1.0 - BETA1) * gradient
    new_two = BETA2 * moment_two + (1.0 - BETA2) * gradient * gradient
    ratio = new_one / (1.0 - BETA1**STEP) / (jnp.sqrt(new_two / (1.0 - BETA2**STEP)) + ADAM_EPS)
    return (new_one, new_two, -RATE * (ratio + DECAY * param))


def merge_stats(one, two):
    peak = jnp.maximum(one[0], two[0])
    total = one[1] * jnp.exp(one[0] - peak) + two[1] * jnp.exp(two[0] - peak)
    return jnp.stack([peak, total, one[2] + two[2], one[3] + two[3]])


def pick_block(blocks, index, axis=0):
    return lax.dynamic_index_in_dim(blocks, index, axis, False)


def widen(rows):
    return jnp.pad(rows, ((0, 0), (0, WIDE - D)))


def fold_plane(left, right, right_dim):
    c_index, yx_index = lax.axis_index("c"), lax.axis_index(("y", "x"))
    rows = left.reshape(4, 2, left.shape[0] // 8, left.shape[1])
    far = pick_block(rows, 1 - c_index, 1).reshape(-1, left.shape[1])
    near = pick_block(rows, c_index, 1).reshape(-1, left.shape[1])
    got = flip(dot(far, right, 1, right_dim).astype(bf16), "c", 1, 2)
    mine = (dot(near, right, 1, right_dim) + got.astype(f32)).reshape(4, -1, WIDE)
    low = mine.astype(bf16)
    total = pick_block(mine, yx_index)
    for k in (1, 2, 3):
        total = total + flip(pick_block(low, yx_index ^ k), ("y", "x"), k, 4).astype(f32)
    return total[:, :D]


def down_pack(rows):
    side = jnp.concatenate([rows[: SHARE // 2, 640:], rows[SHARE // 2 :, 640:]], axis=1)
    return jnp.concatenate([rows[:, :640], side])


def down_unpack(rows):
    side = jnp.concatenate([rows[SHARE:, :UNIT], rows[SHARE:, UNIT:]])
    return jnp.concatenate([rows[:SHARE], side], axis=1)


def spread_plane(rows):
    return widen(lax.all_gather(rows, PLANE).reshape(-1, D))


def local(
    token_ids, loss_rows, targets, flat_master, flat_m, flat_v, table_master, table_m, table_v
):
    devices = lax.axis_size(ALL)
    rows_q = lax.axis_size("q")
    me = lax.axis_index(ALL)
    q_index = lax.axis_index("q")
    p_index = lax.axis_index(PLANE)
    c_index = lax.axis_index("c")
    yx_index = lax.axis_index(("y", "x"))
    tokens = token_ids.shape[0]
    vocab_dev = table_master.shape[0]
    loss_dev = loss_rows.shape[0]
    loss_total = loss_dev * devices
    capacity = max(2, 2 * tokens // devices)
    slots = devices * capacity
    groups = QUERY_HEADS // KEY_VALUE_HEADS
    emb_mult = math.sqrt(D) * 0.5
    shard = flat_master.shape[0]
    units = ALL_UNITS // devices
    span = units * UNIT
    drift = shard - span
    aligned = devices == 32

    place = np.array([q * 8 + kyx * 2 + kc for kc in range(2) for kyx in range(4) for q in range(rows_q)])
    source_of = p_index ^ jnp.asarray(place, jnp.int32)

    table_low = table_master.astype(bf16)
    owner = token_ids // vocab_dev
    owner_hot = hot(owner, devices)
    before = (lax.broadcasted_iota(jnp.int32, (tokens, tokens), 0) > lax.broadcasted_iota(jnp.int32, (tokens, tokens), 1)).astype(bf16)
    slot = jnp.sum(dot(before, owner_hot) * owner_hot.astype(f32), axis=1).astype(jnp.int32)
    spot = hot(owner * capacity + slot, slots)

    def spot_between(low, high):
        inside = (slot >= low) & (slot < high)
        return hot(jnp.where(inside, owner * (high - low) + slot - low, -1), devices * (high - low))

    def rows_between(low, high):
        return hot(asked[:, low:high].reshape(-1) - me * vocab_dev, vocab_dev)

    def exchange(blocks):
        return lax.all_to_all(blocks, ALL, split_axis=0, concat_axis=0, tiled=True).reshape(-1, D)

    cuts_back = (0, capacity // 4, capacity)
    marked = token_ids + 1
    halves = jnp.stack([marked // 256, marked % 256]).astype(bf16)
    found = dot(halves, spot).astype(jnp.int32)
    requests = (found[0] * 256 + found[1] - 1).reshape(devices, capacity)
    ask = jnp.concatenate([requests, jnp.broadcast_to(targets[None], (devices, loss_dev))], axis=1)

    flat_low = flat_master.astype(bf16)
    ahead = lax.ppermute(flat_low[:GAINS], ALL, [(i + 1, i) for i in range(devices - 1)])
    back = max(0, drift * (devices - 1) - GAINS)
    pieces = [flat_low, ahead]
    if back:
        pieces = [lax.ppermute(flat_low[shard - back :], ALL, [(i, i + 1) for i in range(devices - 1)])] + pieces
    chunk = lax.dynamic_slice(jnp.concatenate(pieces), (back + GAINS - drift * me,), (span,))
    if aligned:
        sent = chunk.reshape(60, 2, 8, UNIT).transpose(2, 0, 1, 3).reshape(8, 60, 2 * UNIT)
        got = lax.all_to_all(sent, PLANE, split_axis=0, concat_axis=0, tiled=True)
        both = chunk.reshape(TOP, QKV)
        both = jnp.concatenate([both[:, :D], both[:, D:].reshape(SHARE - TOP, D)])
        first = jnp.where(p_index < 5, both, chunk.reshape(SHARE, D))
        first = jnp.concatenate([first, flat_low[:GAINS].reshape(3, D), jnp.zeros((5, D), bf16)])
        first, ask = lax.optimization_barrier((first, ask))
        asked = lax.all_to_all(ask, ALL, split_axis=0, concat_axis=0, tiled=True)
        answer = dot(rows_between(0, capacity), table_low).astype(bf16).reshape(devices, capacity, D)
        jumped = lax.ppermute(first, "q", [(0, 2)])
        first = jnp.where(q_index == 2, jumped, first)
        stepped = lax.ppermute(first, "q", [(0, 1), (2, 3)])
        first = jnp.where((q_index == 1) | (q_index == 3), stepped, first)
        answer, first, got = lax.optimization_barrier((answer, first, got))
        returned = exchange(answer)
        level = lax.all_gather(first, PLANE)
        mixed = jnp.where(q_index == 3, down_pack(chunk.reshape(SHARE, D)), got.reshape(480, 2 * UNIT))
        mixed, level = lax.optimization_barrier((mixed, level))
        gains = level[0, SHARE : SHARE + 3].astype(f32)
        w_q = level[:5, :TOP].reshape(D, D)
        w_kv = level[:5, TOP:SHARE].reshape(D, KV)
        w_out = level[5:, :SHARE].reshape(D, D)
        returned, w_q, w_kv, w_out = lax.optimization_barrier((returned, w_q, w_kv, w_out))
        column = lax.all_gather(mixed, "q")
    else:
        asked = lax.all_to_all(ask, ALL, split_axis=0, concat_axis=0, tiled=True)
        answer = dot(rows_between(0, capacity), table_low).astype(bf16).reshape(devices, capacity, D)
        returned = exchange(answer)
        extra = jnp.zeros((16 * UNIT,), bf16).at[:GAINS].set(flat_low[:GAINS])
        full = lax.all_gather(jnp.concatenate([chunk, extra]).reshape(units + 16, UNIT), ALL)
        gains = full[0, units : units + GAIN_UNITS].astype(f32).reshape(3, D)
        full = full[:, :units].reshape(ALL_UNITS, UNIT)
        edge = np.cumsum([QKV_UNITS, OUT_UNITS, GU_UNITS])
        w_qkv = full[: edge[0]].reshape(D, QKV)
        w_q, w_kv = w_qkv[:, :D], w_qkv[:, D:]
        w_out = full[edge[0] : edge[1]].reshape(D, D)
        both = lax.dynamic_index_in_dim(full[edge[1] : edge[2]].reshape(D, 2, 8, UNIT), p_index, 2, False)
        w_gu = both.reshape(D, 2 * SHARE)
        w_down = lax.dynamic_index_in_dim(full[edge[2] :].reshape(8, SHARE, D), p_index, 0, False)
    x_low = dot(spot, returned).astype(bf16)
    x_embed = x_low.astype(f32) * emb_mult

    pick = hot(loss_rows, tokens)
    cosine, sine = (jnp.asarray(t) for t in rope_tables(tokens))
    cosine_pick, sine_pick = cosine[loss_rows], sine[loss_rows]
    h_attn = (x_embed * scale_of(x_embed) * gains[0]).astype(bf16)
    h_pick = dot(pick, h_attn).astype(bf16)
    x_pick = dot(pick, x_low) * emb_mult
    query = rotate(dot(h_pick, w_q), cosine_pick, sine_pick).astype(bf16)
    key_value = dot(h_attn, w_kv)
    key = rotate(key_value[:, :UNIT], cosine, sine).astype(bf16)
    value = key_value[:, UNIT:].astype(bf16)

    def heads_of(rows):
        return rows.reshape(loss_dev, KEY_VALUE_HEADS, groups, HEAD_SIZE).transpose(1, 2, 0, 3).reshape(KEY_VALUE_HEADS, groups * loss_dev, HEAD_SIZE)

    def heads_back(rows):
        return rows.reshape(KEY_VALUE_HEADS, groups, loss_dev, HEAD_SIZE).transpose(2, 0, 1, 3).reshape(loss_dev, D)

    query_h = heads_of(query)
    key_h = key.reshape(tokens, KEY_VALUE_HEADS, HEAD_SIZE).transpose(1, 0, 2)
    value_h = value.reshape(tokens, KEY_VALUE_HEADS, HEAD_SIZE).transpose(1, 0, 2)
    key_pos = jnp.arange(tokens, dtype=jnp.int32)[None, :]
    ask_pos = jnp.tile(loss_rows, groups)[:, None]
    key_seg = jnp.where(key_pos < PL, 0, 1 + (key_pos - PL) // CL)
    ask_seg = jnp.where(ask_pos < PL, 0, 1 + (ask_pos - PL) // CL)
    allowed = (key_pos <= ask_pos) & ((key_seg == 0) | (key_seg == ask_seg))
    scores = jnp.einsum("hqd,hkd->hqk", query_h, key_h, preferred_element_type=f32) * HEAD_SIZE**-0.5
    scores = jnp.where(allowed[None], scores, NEGATIVE)
    exp_scores = jnp.exp(scores - jnp.max(scores, axis=-1, keepdims=True))
    probs = exp_scores / jnp.sum(exp_scores, axis=-1, keepdims=True)
    probs_low = probs.astype(bf16)
    mixed_heads = jnp.einsum("hqk,hkd->hqd", probs_low, value_h, preferred_element_type=f32)
    attended = heads_back(mixed_heads.astype(bf16))
    x_one = x_pick + dot(attended, w_out)

    h_mlp = (x_one * scale_of(x_one) * gains[1]).astype(bf16)
    h_all = spread_plane(h_mlp)
    if aligned:
        column, h_all = lax.optimization_barrier((column, h_all))
        w_gu = column[1:3].reshape(D, 2 * SHARE)
        w_down = down_unpack(column[3])
    w_gu = jnp.pad(w_gu, ((0, WIDE - D), (0, 0)))
    w_down = widen(w_down)
    gate_up = dot(h_all, w_gu)
    gate, up = gate_up[:, :SHARE], gate_up[:, SHARE:]
    sig = jax.nn.sigmoid(gate)
    act = (gate * sig * up).astype(bf16)
    x_two = x_one + fold_plane(act, w_down, 0)

    hidden = (x_two * scale_of(x_two) * gains[2]).astype(bf16)
    wide_table = widen(table_low)
    across = lax.all_gather(widen(hidden), "q")
    by_x, by_y = flip(across, "x", 1, 2), flip(across, "y", 1, 2)
    cut = rows_q // 2
    corner = [flip(by_x[:cut], "y", 1, 2), flip(by_y[cut:], "x", 1, 2)]
    near = jnp.concatenate([across, by_x, by_y] + corner).reshape(loss_total // 2, WIDE)
    sides = [near, flip(near, "c", 1, 2)]
    targets_all = jnp.take(asked[:, capacity:], source_of, axis=0).reshape(2, loss_total // 2)
    logits, hits, stats = [], [], []
    for side, rows in enumerate(sides):
        z = dot(rows, wide_table, 1, 1)
        column_id = targets_all[side] - me * vocab_dev
        hit = column_id[:, None] == jnp.arange(vocab_dev, dtype=jnp.int32)[None, :]
        local_peak = jnp.max(z, axis=1)
        local_total = jnp.sum(jnp.exp(z - local_peak[:, None]), axis=1)
        local_target = jnp.sum(jnp.where(hit, z, 0.0), axis=1)
        local_sum = jnp.sum(z, axis=1)
        logits.append(z)
        hits.append(hit)
        stats.append(jnp.stack([local_peak, local_total, local_target, local_sum]))
    stats = jnp.concatenate(stats, axis=1)
    block = rows_q * loss_dev
    for axis, bit in (("c", 4), ("x", 1), ("y", 2)):
        other = flip(stats, axis, 1, 2)
        other = jnp.concatenate([other[:, (k ^ bit) * block : ((k ^ bit) + 1) * block] for k in range(8)], axis=1)
        stats = merge_stats(stats, other)
    bit = 1
    while bit < rows_q:
        stats = merge_stats(stats, flip(stats, "q", bit, rows_q))
        bit *= 2
    log_total = stats[0] + jnp.log(stats[1])
    mine_at = q_index * loss_dev
    my_log, my_target, my_sum = (lax.dynamic_slice(row, (mine_at,), (loss_dev,)) for row in (log_total, stats[2], stats[3]))
    my_loss = jnp.sum(my_log - (1.0 - SMOOTH) * my_target - SMOOTH / V * my_sum + ZCOEF * my_log * my_log)
    log_total = log_total.reshape(2, loss_total // 2, 1)
    d_logits = [
        (
            (
                (1.0 + 2.0 * ZCOEF * log_total[side]) * jnp.exp(logits[side] - log_total[side])
                - jnp.where(hits[side], 1.0 - SMOOTH, 0.0)
                - SMOOTH / V
            )
            / loss_total
        ).astype(bf16)
        for side in (1, 0)
    ]
    got = flip(dot(d_logits[0], wide_table).astype(bf16), "c", 1, 2)
    d_hidden = (dot(d_logits[1], wide_table) + got.astype(f32)).reshape(4, rows_q, loss_dev, WIDE)
    d_low = d_hidden.astype(bf16)
    d_hidden = d_hidden[0]
    for k in (1, 2, 3):
        d_hidden = d_hidden + flip(d_low[k], ("y", "x"), k, 4).astype(f32)
    d_low = d_hidden.astype(bf16)
    total_hidden = pick_block(d_hidden, q_index)
    for k in range(1, rows_q):
        total_hidden = total_hidden + flip(pick_block(d_low, q_index ^ k), "q", k, rows_q).astype(f32)
    total_hidden = total_hidden[:, :D]
    head_grad = (dot(d_logits[1], sides[0], 0, 0) + dot(d_logits[0], sides[1], 0, 0))[:, :D]
    head_grad, total_hidden = lax.optimization_barrier((head_grad, total_hidden))

    d_x_two, grad_final = norm_back(x_two, gains[2], total_hidden)
    d_down = spread_plane(d_x_two.astype(bf16))
    d_act = dot(d_down, w_down, 1, 1)
    d_gate = d_act * up * sig * (1.0 + gate * (1.0 - sig))
    d_gu = jnp.concatenate([d_gate, d_act * gate * sig], axis=1).astype(bf16)
    d_h_mlp = fold_plane(d_gu, w_gu, 1)
    grad_down = dot(act, d_down, 0, 0)[:, :D].astype(bf16)
    grad_gu = dot(h_all, d_gu, 0, 0)[:D].astype(bf16)
    d_x_mlp, grad_mlp = norm_back(x_one, gains[1], d_h_mlp)
    d_x_one = d_x_two + d_x_mlp

    d_branch = d_x_one.astype(bf16)
    d_attended = dot(d_branch, w_out, 1, 1)
    d_mixed = heads_of(d_attended.astype(bf16))
    d_probs = jnp.einsum("hqd,hkd->hqk", d_mixed, value_h, preferred_element_type=f32)
    delta = jnp.sum(probs * d_probs, axis=-1, keepdims=True)
    d_scores = (probs * (d_probs - delta)).astype(bf16)
    d_query = jnp.einsum("hqk,hkd->hqd", d_scores, key_h, preferred_element_type=f32) * HEAD_SIZE**-0.5
    d_key = jnp.einsum("hqk,hqd->khd", d_scores, query_h, preferred_element_type=f32) * HEAD_SIZE**-0.5
    d_value = jnp.einsum("hqk,hqd->khd", probs_low, d_mixed, preferred_element_type=f32)
    d_q = rotate_back(heads_back(d_query), cosine_pick, sine_pick).astype(bf16)
    d_k = rotate_back(d_key.reshape(tokens, UNIT), cosine, sine)
    d_kv = jnp.concatenate([d_k, d_value.reshape(tokens, UNIT)], axis=1).astype(bf16)
    d_h_pick = dot(d_q, w_q, 1, 1)
    high = d_h_pick.astype(bf16)
    rest = (d_h_pick - high.astype(f32)).astype(bf16)
    d_h_attn = dot(d_kv, w_kv, 1, 1) + dot(pick, high, 0, 0) + dot(pick, rest, 0, 0)
    d_x_attn, grad_attn = norm_back(x_embed, gains[0], d_h_attn)
    high = d_x_one.astype(bf16)
    rest = (d_x_one - high.astype(f32)).astype(bf16)
    d_x_embed = d_x_attn + dot(pick, high, 0, 0) + dot(pick, rest, 0, 0)

    scaled = (d_x_embed * emb_mult).astype(bf16)
    sending = [
        dot(spot_between(low, high), scaled, 0, 0).astype(bf16).reshape(devices, high - low, D)
        for low, high in zip(cuts_back, cuts_back[1:])
    ]
    if aligned:
        blocks = jnp.concatenate([jnp.zeros((1, 480, 640), bf16), grad_gu.reshape(2, 480, 640), down_pack(grad_down)[None]])
        share = lax.psum_scatter(blocks, "q", scatter_dimension=0, tiled=False)
        sending, d_q, d_kv, attended = lax.optimization_barrier((sending, d_q, d_kv, attended))
        share, d_q, d_kv, attended = lax.optimization_barrier((share, d_q, d_kv, attended))
    arrived = [exchange(blocks) for blocks in sending]
    grad_out = dot(attended, d_branch, 0, 0).astype(bf16)
    grad_q = dot(h_pick, d_q, 0, 0).astype(bf16)
    grad_kv = dot(h_attn, d_kv, 0, 0).astype(bf16)

    def norm_of(squares):
        sums = jnp.stack([squares, my_loss])
        for axis, bit, size in [("c", 1, 2), ("x", 1, 2), ("y", 1, 2)] + [("q", 1 << k, rows_q) for k in range(rows_q.bit_length() - 1)]:
            sums = sums + flip(sums, axis, bit, size)
        grad_norm = jnp.sqrt(sums[0])
        limit = CLIP_C / math.sqrt(loss_total)
        return sums[1] / loss_total, grad_norm, limit / jnp.maximum(grad_norm, limit)

    gain_grads = jnp.concatenate([grad_attn, grad_mlp, grad_final]).astype(bf16)
    if aligned:
        lower = jnp.concatenate([grad_q.reshape(5, TOP, D), grad_kv.reshape(5, SHARE - TOP, D)], axis=1)
        level = jnp.concatenate([lower, grad_out.reshape(3, SHARE, D)])
        room = jnp.zeros((8, ROOM, D), bf16).at[0, :3].set(gain_grads.reshape(3, D))
        level = jnp.concatenate([level, room], axis=1).reshape(4, 2, SHARE + ROOM, D)
        level, arrived[0] = lax.optimization_barrier((level, arrived[0]))
        keep = lax.dynamic_index_in_dim(level, c_index, 1, False)
        give = lax.dynamic_index_in_dim(level, 1 - c_index, 1, False)
        cores = [rows.reshape(2, 2, SHARE + ROOM, D) for rows in (keep, flip(give, "c", 1, 2))]
        middle = (SHARE + ROOM) // 2
        x_index, y_index = lax.axis_index("x"), lax.axis_index("y")

        def upper(index):
            return sum(pick_block(rows[:, :, :middle], index, 1).astype(f32) for rows in cores)

        def under(index):
            return sum(pick_block(rows[:, :, middle:], index, 0).astype(f32) for rows in cores)

        left = upper(x_index) + flip(upper(1 - x_index).astype(bf16), "x", 1, 2).astype(f32)
        right = under(y_index) + flip(under(1 - y_index).astype(bf16), "y", 1, 2).astype(f32)
        left = pick_block(left, y_index) + flip(pick_block(left, 1 - y_index).astype(bf16), "y", 1, 2).astype(f32)
        right = pick_block(right, x_index) + flip(pick_block(right, 1 - x_index).astype(bf16), "x", 1, 2).astype(f32)
        own = jnp.concatenate([left, right])
        own = own.reshape(4, (SHARE + ROOM) // 4, D)
        own, share, arrived[1] = lax.optimization_barrier((own, share, arrived[1]))
        got = lax.all_to_all(share.reshape(8, 60, 640), PLANE, split_axis=0, concat_axis=0, tiled=True)
        quarter = lax.dynamic_index_in_dim(own, q_index, 0, False)
        for k in (1, 2, 3):
            piece = lax.dynamic_index_in_dim(own, q_index ^ k, 0, False).astype(bf16)
            quarter = quarter + flip(piece, "q", k, 4).astype(f32)
        table_grad = head_grad
        for low, high, rows in zip(cuts_back, cuts_back[1:], arrived):
            table_grad = table_grad + dot(rows_between(low, high), rows, 0, 0)
        table_squares = jnp.sum(table_grad * table_grad)
        quarter = quarter.astype(bf16)
        squares = jnp.sum(quarter.astype(f32) ** 2) + jnp.sum(share.astype(f32) ** 2) + table_squares
        quarters = [quarter] + [lax.ppermute(quarter, "q", [(k, 0)]) for k in (1, 2, 3)]
        first = jnp.concatenate(quarters)
        gain_out = first[SHARE : SHARE + 3].reshape(-1)
        both = jnp.concatenate([first[:TOP], first[TOP:SHARE].reshape(TOP, KV)], axis=1)
        first = jnp.where(p_index < 5, both.reshape(-1), first[:SHARE].reshape(-1))
        by_share = got.reshape(8, 60, 2, UNIT).transpose(1, 2, 0, 3).reshape(-1)
        mine = jnp.where(q_index == 3, down_unpack(share).reshape(-1), by_share)
        mine = jnp.where(q_index == 0, first, mine)
        loss, grad_norm, clip_factor = norm_of(squares)
        mine, clip_factor = lax.optimization_barrier((mine, clip_factor))
    else:
        table_grad = head_grad
        for low, high, rows in zip(cuts_back, cuts_back[1:], arrived):
            table_grad = table_grad + dot(rows_between(low, high), rows, 0, 0)
        table_squares = jnp.sum(table_grad * table_grad)
        both = lax.dynamic_update_index_in_dim(jnp.zeros((D, 2, 8, UNIT), bf16), grad_gu.reshape(D, 2, UNIT), p_index, 2)
        downs = lax.dynamic_update_index_in_dim(jnp.zeros((8, SHARE, D), bf16), grad_down, p_index, 0)
        full = jnp.concatenate([part.reshape(-1, UNIT) for part in (jnp.concatenate([grad_q, grad_kv], axis=1), grad_out, both, downs)]).reshape(devices, units, UNIT)
        room = jnp.zeros((devices, 16, UNIT), bf16).at[0, :GAIN_UNITS].set(gain_grads.reshape(GAIN_UNITS, UNIT))
        full = jnp.concatenate([full, room], axis=1)
        summed = lax.psum_scatter(full, ALL, scatter_dimension=0, tiled=False)
        mine, gain_out = summed[:units].reshape(-1), summed[units : units + GAIN_UNITS].reshape(-1)
    behind = lax.ppermute(mine[span - GAINS :], ALL, [(i, i + 1) for i in range(devices - 1)])
    behind = jnp.where(me == 0, gain_out, behind)
    tail = max(0, drift * (devices - 1) + shard - GAINS - span)
    stream = jnp.concatenate([behind, mine, jnp.zeros((tail,), bf16)])
    layer_grad = lax.dynamic_slice(stream, (drift * me,), (shard,)).astype(f32)

    if not aligned:
        loss, grad_norm, clip_factor = norm_of(jnp.sum(layer_grad * layer_grad) + table_squares)
    flat_new = adamw_step(flat_master, layer_grad, flat_m, flat_v, clip_factor)
    table_new = adamw_step(table_master, table_grad, table_m, table_v, clip_factor)
    return (loss, grad_norm) + flat_new + table_new


def solution(mesh):
    count = mesh.devices.size
    grid = Mesh(mesh.devices.reshape(count // 8, 2, 2, 2), ALL)
    rows, matrix = P(ALL), P(ALL, None)
    in_specs = (rows,) * 6 + (matrix,) * 3
    out_specs = (P(), P()) + (rows,) * 3 + (matrix,) * 3
    return jax.shard_map(local, mesh=grid, in_specs=in_specs, out_specs=out_specs, check_vma=False)
```

```python
import math

import jax
import jax.numpy as jnp
import numpy as np
from jax import lax
from jax.sharding import Mesh, PartitionSpec as P

D = 960
QUERY_HEADS = 15
KEY_VALUE_HEADS = 5
HEAD_SIZE = 64
FF = 2560
V = 32000
PL = 256
CL = 128
STEP = 10
QKV = 1600

EPS = 1e-05
SMOOTH = 0.1
ZCOEF = 0.0001
BETA1 = 0.9
BETA2 = 0.95
ADAM_EPS = 1e-08
DECAY = 0.1
RATE = 0.03
CLIP_C = 25.0
NEGATIVE = -1e30

UNIT = 320
GAINS = 3 * D
GAIN_UNITS = GAINS // UNIT
QKV_UNITS = D * QKV // UNIT
OUT_UNITS = D * D // UNIT
GU_UNITS = D * 2 * FF // UNIT
DOWN_UNITS = FF * D // UNIT
ALL_UNITS = QKV_UNITS + OUT_UNITS + GU_UNITS + DOWN_UNITS
PLANE = ("y", "x", "c")
ALL = ("q", "y", "x", "c")
SHARE = FF // 8
TOP = D // 5
KV = QKV - D
ROOM = 32
WIDE = 1024

bf16 = jnp.bfloat16
f32 = jnp.float32


def dot(left, right, left_dim=1, right_dim=0):
    return lax.dot_general(
        left, right, (((left_dim,), (right_dim,)), ((), ())), preferred_element_type=f32
    )


def hot(index, count):
    return (index[:, None] == jnp.arange(count, dtype=jnp.int32)[None, :]).astype(bf16)


def scale_of(rows):
    return lax.rsqrt(jnp.mean(rows * rows, axis=-1, keepdims=True) + EPS)


def norm_back(rows, gain, grad):
    scale = scale_of(rows)
    normed = rows * scale
    grad_gain = jnp.sum(grad * normed, axis=0)
    scaled = grad * gain
    return scale * (scaled - normed * jnp.mean(scaled * normed, axis=-1, keepdims=True)), grad_gain


def flip(rows, axes, bits, size):
    return lax.ppermute(rows, axes, [(i, i ^ bits) for i in range(size)])


def rope_tables(count):
    row = np.arange(count)
    position = np.where(row < PL, row, PL + (row - PL) % CL).astype(np.float32)
    half = np.arange(HEAD_SIZE // 2, dtype=np.float32)
    freqs = np.float32(10000.0) ** (-(half * np.float32(2.0) / np.float32(HEAD_SIZE)))
    angles = (position[:, None] * freqs[None, :].astype(np.float32)).astype(np.float64)
    angles = np.concatenate([angles, angles], axis=-1)
    return np.cos(angles).astype(np.float32), np.sin(angles).astype(np.float32)


def rotate(rows, cosine, sine):
    heads = rows.reshape(rows.shape[0], -1, HEAD_SIZE)
    half = HEAD_SIZE // 2
    turned = jnp.concatenate([-heads[..., half:], heads[..., :half]], axis=-1)
    return (heads * cosine[:, None, :] + turned * sine[:, None, :]).reshape(rows.shape)


def rotate_back(grad, cosine, sine):
    heads = grad.reshape(grad.shape[0], -1, HEAD_SIZE)
    half = HEAD_SIZE // 2
    spun = heads * sine[:, None, :]
    turned = jnp.concatenate([spun[..., half:], -spun[..., :half]], axis=-1)
    return (heads * cosine[:, None, :] + turned).reshape(grad.shape)


def adamw_step(param, gradient, moment_one, moment_two, clip_factor):
    gradient = gradient * clip_factor
    new_one = BETA1 * moment_one + (1.0 - BETA1) * gradient
    new_two = BETA2 * moment_two + (1.0 - BETA2) * gradient * gradient
    ratio = new_one / (1.0 - BETA1**STEP) / (jnp.sqrt(new_two / (1.0 - BETA2**STEP)) + ADAM_EPS)
    return (new_one, new_two, -RATE * (ratio + DECAY * param))


def merge_stats(one, two):
    peak = jnp.maximum(one[0], two[0])
    total = one[1] * jnp.exp(one[0] - peak) + two[1] * jnp.exp(two[0] - peak)
    return jnp.stack([peak, total, one[2] + two[2], one[3] + two[3]])


def pick_block(blocks, index, axis=0):
    return lax.dynamic_index_in_dim(blocks, index, axis, False)


def widen(rows):
    return jnp.pad(rows, ((0, 0), (0, WIDE - D)))


def fold_plane(left, right, right_dim):
    c_index, yx_index = lax.axis_index("c"), lax.axis_index(("y", "x"))
    rows = left.reshape(4, 2, left.shape[0] // 8, left.shape[1])
    far = pick_block(rows, 1 - c_index, 1).reshape(-1, left.shape[1])
    near = pick_block(rows, c_index, 1).reshape(-1, left.shape[1])
    got = flip(dot(far, right, 1, right_dim).astype(bf16), "c", 1, 2)
    mine = (dot(near, right, 1, right_dim) + got.astype(f32)).reshape(4, -1, WIDE)
    low = mine.astype(bf16)
    total = pick_block(mine, yx_index)
    for k in (1, 2, 3):
        total = total + flip(pick_block(low, yx_index ^ k), ("y", "x"), k, 4).astype(f32)
    return total[:, :D]


def down_pack(rows):
    side = jnp.concatenate([rows[: SHARE // 2, 640:], rows[SHARE // 2 :, 640:]], axis=1)
    return jnp.concatenate([rows[:, :640], side])


def down_unpack(rows):
    side = jnp.concatenate([rows[SHARE:, :UNIT], rows[SHARE:, UNIT:]])
    return jnp.concatenate([rows[:SHARE], side], axis=1)


def spread_plane(rows):
    return lax.all_gather(rows, PLANE).reshape(-1, D)


def local(
    token_ids, loss_rows, targets, flat_master, flat_m, flat_v, table_master, table_m, table_v
):
    devices = lax.axis_size(ALL)
    rows_q = lax.axis_size("q")
    me = lax.axis_index(ALL)
    q_index = lax.axis_index("q")
    p_index = lax.axis_index(PLANE)
    c_index = lax.axis_index("c")
    yx_index = lax.axis_index(("y", "x"))
    tokens = token_ids.shape[0]
    vocab_dev = table_master.shape[0]
    loss_dev = loss_rows.shape[0]
    loss_total = loss_dev * devices
    capacity = max(2, 2 * tokens // devices)
    slots = devices * capacity
    groups = QUERY_HEADS // KEY_VALUE_HEADS
    emb_mult = math.sqrt(D) * 0.5
    shard = flat_master.shape[0]
    units = ALL_UNITS // devices
    span = units * UNIT
    drift = shard - span
    aligned = devices == 32

    place = np.array([q * 8 + kyx * 2 + kc for kc in range(2) for kyx in range(4) for q in range(rows_q)])
    source_of = p_index ^ jnp.asarray(place, jnp.int32)

    table_low = table_master.astype(bf16)
    owner = token_ids // vocab_dev
    owner_hot = hot(owner, devices)
    before = (lax.broadcasted_iota(jnp.int32, (tokens, tokens), 0) > lax.broadcasted_iota(jnp.int32, (tokens, tokens), 1)).astype(bf16)
    slot = jnp.sum(dot(before, owner_hot) * owner_hot.astype(f32), axis=1).astype(jnp.int32)
    spot = hot(owner * capacity + slot, slots)

    def spot_between(low, high):
        inside = (slot >= low) & (slot < high)
        return hot(jnp.where(inside, owner * (high - low) + slot - low, -1), devices * (high - low))

    def rows_between(low, high):
        return hot(asked[:, low:high].reshape(-1) - me * vocab_dev, vocab_dev)

    def exchange(blocks):
        return lax.all_to_all(blocks, ALL, split_axis=0, concat_axis=0, tiled=True).reshape(-1, D)

    cuts_back = (0, capacity // 4, capacity)
    marked = token_ids + 1
    halves = jnp.stack([marked // 256, marked % 256]).astype(bf16)
    found = dot(halves, spot).astype(jnp.int32)
    requests = (found[0] * 256 + found[1] - 1).reshape(devices, capacity)
    ask = jnp.concatenate([requests, jnp.broadcast_to(targets[None], (devices, loss_dev))], axis=1)

    flat_low = flat_master.astype(bf16)
    ahead = lax.ppermute(flat_low[:GAINS], ALL, [(i + 1, i) for i in range(devices - 1)])
    back = max(0, drift * (devices - 1) - GAINS)
    pieces = [flat_low, ahead]
    if back:
        pieces = [lax.ppermute(flat_low[shard - back :], ALL, [(i, i + 1) for i in range(devices - 1)])] + pieces
    chunk = lax.dynamic_slice(jnp.concatenate(pieces), (back + GAINS - drift * me,), (span,))
    if aligned:
        sent = chunk.reshape(60, 2, 8, UNIT).transpose(2, 0, 1, 3).reshape(8, 60, 2 * UNIT)
        got = lax.all_to_all(sent, PLANE, split_axis=0, concat_axis=0, tiled=True)
        both = chunk.reshape(TOP, QKV)
        both = jnp.concatenate([both[:, :D], both[:, D:].reshape(SHARE - TOP, D)])
        first = jnp.where(p_index < 5, both, chunk.reshape(SHARE, D))
        first = jnp.concatenate([first, flat_low[:GAINS].reshape(3, D), jnp.zeros((5, D), bf16)])
        first, ask = lax.optimization_barrier((first, ask))
        asked = lax.all_to_all(ask, ALL, split_axis=0, concat_axis=0, tiled=True)
        answer = dot(rows_between(0, capacity), table_low).astype(bf16).reshape(devices, capacity, D)
        jumped = lax.ppermute(first, "q", [(0, 2)])
        first = jnp.where(q_index == 2, jumped, first)
        stepped = lax.ppermute(first, "q", [(0, 1), (2, 3)])
        first = jnp.where((q_index == 1) | (q_index == 3), stepped, first)
        answer, first, got = lax.optimization_barrier((answer, first, got))
        returned = exchange(answer)
        level = lax.all_gather(first, PLANE)
        mixed = jnp.where(q_index == 3, down_pack(chunk.reshape(SHARE, D)), got.reshape(480, 2 * UNIT))
        mixed, level = lax.optimization_barrier((mixed, level))
        gains = level[0, SHARE : SHARE + 3].astype(f32)
        w_q = level[:5, :TOP].reshape(D, D)
        w_kv = level[:5, TOP:SHARE].reshape(D, KV)
        w_out = level[5:, :SHARE].reshape(D, D)
        returned, w_q, w_kv, w_out = lax.optimization_barrier((returned, w_q, w_kv, w_out))
        column = lax.all_gather(mixed, "q")
    else:
        asked = lax.all_to_all(ask, ALL, split_axis=0, concat_axis=0, tiled=True)
        answer = dot(rows_between(0, capacity), table_low).astype(bf16).reshape(devices, capacity, D)
        returned = exchange(answer)
        extra = jnp.zeros((16 * UNIT,), bf16).at[:GAINS].set(flat_low[:GAINS])
        full = lax.all_gather(jnp.concatenate([chunk, extra]).reshape(units + 16, UNIT), ALL)
        gains = full[0, units : units + GAIN_UNITS].astype(f32).reshape(3, D)
        full = full[:, :units].reshape(ALL_UNITS, UNIT)
        edge = np.cumsum([QKV_UNITS, OUT_UNITS, GU_UNITS])
        w_qkv = full[: edge[0]].reshape(D, QKV)
        w_q, w_kv = w_qkv[:, :D], w_qkv[:, D:]
        w_out = full[edge[0] : edge[1]].reshape(D, D)
        both = lax.dynamic_index_in_dim(full[edge[1] : edge[2]].reshape(D, 2, 8, UNIT), p_index, 2, False)
        w_gu = both.reshape(D, 2 * SHARE)
        w_down = lax.dynamic_index_in_dim(full[edge[2] :].reshape(8, SHARE, D), p_index, 0, False)
    x_low = dot(spot, returned).astype(bf16)
    x_embed = x_low.astype(f32) * emb_mult

    pick = hot(loss_rows, tokens)
    cosine, sine = (jnp.asarray(t) for t in rope_tables(tokens))
    cosine_pick, sine_pick = cosine[loss_rows], sine[loss_rows]
    h_attn = (x_embed * scale_of(x_embed) * gains[0]).astype(bf16)
    h_pick = dot(pick, h_attn).astype(bf16)
    x_pick = dot(pick, x_low) * emb_mult
    query = rotate(dot(h_pick, w_q), cosine_pick, sine_pick).astype(bf16)
    key_value = dot(h_attn, w_kv)
    key = rotate(key_value[:, :UNIT], cosine, sine).astype(bf16)
    value = key_value[:, UNIT:].astype(bf16)

    def heads_of(rows):
        return rows.reshape(loss_dev, KEY_VALUE_HEADS, groups, HEAD_SIZE).transpose(1, 2, 0, 3).reshape(KEY_VALUE_HEADS, groups * loss_dev, HEAD_SIZE)

    def heads_back(rows):
        return rows.reshape(KEY_VALUE_HEADS, groups, loss_dev, HEAD_SIZE).transpose(2, 0, 1, 3).reshape(loss_dev, D)

    query_h = heads_of(query)
    key_h = key.reshape(tokens, KEY_VALUE_HEADS, HEAD_SIZE).transpose(1, 0, 2)
    value_h = value.reshape(tokens, KEY_VALUE_HEADS, HEAD_SIZE).transpose(1, 0, 2)
    key_pos = jnp.arange(tokens, dtype=jnp.int32)[None, :]
    ask_pos = jnp.tile(loss_rows, groups)[:, None]
    key_seg = jnp.where(key_pos < PL, 0, 1 + (key_pos - PL) // CL)
    ask_seg = jnp.where(ask_pos < PL, 0, 1 + (ask_pos - PL) // CL)
    allowed = (key_pos <= ask_pos) & ((key_seg == 0) | (key_seg == ask_seg))
    scores = jnp.einsum("hqd,hkd->hqk", query_h, key_h, preferred_element_type=f32) * HEAD_SIZE**-0.5
    scores = jnp.where(allowed[None], scores, NEGATIVE)
    exp_scores = jnp.exp(scores - jnp.max(scores, axis=-1, keepdims=True))
    probs = exp_scores / jnp.sum(exp_scores, axis=-1, keepdims=True)
    probs_low = probs.astype(bf16)
    mixed_heads = jnp.einsum("hqk,hkd->hqd", probs_low, value_h, preferred_element_type=f32)
    attended = heads_back(mixed_heads.astype(bf16))
    x_one = x_pick + dot(attended, w_out)

    h_mlp = (x_one * scale_of(x_one) * gains[1]).astype(bf16)
    h_all = spread_plane(h_mlp)
    if aligned:
        column, h_all = lax.optimization_barrier((column, h_all))
        w_gu = column[1:3].reshape(D, 2 * SHARE)
        w_down = down_unpack(column[3])
    wide_gu = jnp.pad(w_gu, ((0, WIDE - D), (0, 0)))
    gate_up = dot(h_all, w_gu)
    gate, up = gate_up[:, :SHARE], gate_up[:, SHARE:]
    sig = jax.nn.sigmoid(gate)
    act = (gate * sig * up).astype(bf16)
    x_two = x_one + fold_plane(act, widen(w_down), 0)

    hidden = (x_two * scale_of(x_two) * gains[2]).astype(bf16)
    wide_table = widen(table_low)
    across = lax.all_gather(widen(hidden), "q")
    by_x, by_y = flip(across, "x", 1, 2), flip(across, "y", 1, 2)
    cut = rows_q // 2
    corner = [flip(by_x[:cut], "y", 1, 2), flip(by_y[cut:], "x", 1, 2)]
    near = jnp.concatenate([across, by_x, by_y] + corner).reshape(loss_total // 2, WIDE)
    sides = [near, flip(near, "c", 1, 2)]
    targets_all = jnp.take(asked[:, capacity:], source_of, axis=0).reshape(2, loss_total // 2)
    logits, hits, stats = [], [], []
    for side, rows in enumerate(sides):
        z = dot(rows, wide_table, 1, 1)
        column_id = targets_all[side] - me * vocab_dev
        hit = column_id[:, None] == jnp.arange(vocab_dev, dtype=jnp.int32)[None, :]
        local_peak = jnp.max(z, axis=1)
        local_total = jnp.sum(jnp.exp(z - local_peak[:, None]), axis=1)
        local_target = jnp.sum(jnp.where(hit, z, 0.0), axis=1)
        local_sum = jnp.sum(z, axis=1)
        logits.append(z)
        hits.append(hit)
        stats.append(jnp.stack([local_peak, local_total, local_target, local_sum]))
    stats = jnp.concatenate(stats, axis=1)
    block = rows_q * loss_dev
    for axis, bit in (("c", 4), ("x", 1), ("y", 2)):
        other = flip(stats, axis, 1, 2)
        other = jnp.concatenate([other[:, (k ^ bit) * block : ((k ^ bit) + 1) * block] for k in range(8)], axis=1)
        stats = merge_stats(stats, other)
    bit = 1
    while bit < rows_q:
        stats = merge_stats(stats, flip(stats, "q", bit, rows_q))
        bit *= 2
    log_total = stats[0] + jnp.log(stats[1])
    mine_at = q_index * loss_dev
    my_log, my_target, my_sum = (lax.dynamic_slice(row, (mine_at,), (loss_dev,)) for row in (log_total, stats[2], stats[3]))
    my_loss = jnp.sum(my_log - (1.0 - SMOOTH) * my_target - SMOOTH / V * my_sum + ZCOEF * my_log * my_log)
    log_total = log_total.reshape(2, loss_total // 2, 1)
    d_logits = [
        (
            (
                (1.0 + 2.0 * ZCOEF * log_total[side]) * jnp.exp(logits[side] - log_total[side])
                - jnp.where(hits[side], 1.0 - SMOOTH, 0.0)
                - SMOOTH / V
            )
            / loss_total
        ).astype(bf16)
        for side in (1, 0)
    ]
    got = flip(dot(d_logits[0], wide_table).astype(bf16), "c", 1, 2)
    d_hidden = (dot(d_logits[1], wide_table) + got.astype(f32)).reshape(4, rows_q, loss_dev, WIDE)
    d_low = d_hidden.astype(bf16)
    d_hidden = d_hidden[0]
    for k in (1, 2, 3):
        d_hidden = d_hidden + flip(d_low[k], ("y", "x"), k, 4).astype(f32)
    d_low = d_hidden.astype(bf16)
    total_hidden = pick_block(d_hidden, q_index)
    for k in range(1, rows_q):
        total_hidden = total_hidden + flip(pick_block(d_low, q_index ^ k), "q", k, rows_q).astype(f32)
    total_hidden = total_hidden[:, :D]
    head_grad = (dot(d_logits[1], sides[0], 0, 0) + dot(d_logits[0], sides[1], 0, 0))[:, :D]
    head_grad, total_hidden = lax.optimization_barrier((head_grad, total_hidden))

    d_x_two, grad_final = norm_back(x_two, gains[2], total_hidden)
    d_down = spread_plane(d_x_two.astype(bf16))
    d_act = dot(d_down, w_down, 1, 1)
    d_gate = d_act * up * sig * (1.0 + gate * (1.0 - sig))
    d_gu = jnp.concatenate([d_gate, d_act * gate * sig], axis=1).astype(bf16)
    d_h_mlp = fold_plane(d_gu, wide_gu, 1)
    grad_down = dot(act, d_down, 0, 0).astype(bf16)
    grad_gu = dot(h_all, d_gu, 0, 0).astype(bf16)
    d_x_mlp, grad_mlp = norm_back(x_one, gains[1], d_h_mlp)
    d_x_one = d_x_two + d_x_mlp

    d_branch = d_x_one.astype(bf16)
    d_attended = dot(d_branch, w_out, 1, 1)
    d_mixed = heads_of(d_attended.astype(bf16))
    d_probs = jnp.einsum("hqd,hkd->hqk", d_mixed, value_h, preferred_element_type=f32)
    delta = jnp.sum(probs * d_probs, axis=-1, keepdims=True)
    d_scores = (probs * (d_probs - delta)).astype(bf16)
    d_query = jnp.einsum("hqk,hkd->hqd", d_scores, key_h, preferred_element_type=f32) * HEAD_SIZE**-0.5
    d_key = jnp.einsum("hqk,hqd->khd", d_scores, query_h, preferred_element_type=f32) * HEAD_SIZE**-0.5
    d_value = jnp.einsum("hqk,hqd->khd", probs_low, d_mixed, preferred_element_type=f32)
    d_q = rotate_back(heads_back(d_query), cosine_pick, sine_pick).astype(bf16)
    d_k = rotate_back(d_key.reshape(tokens, UNIT), cosine, sine)
    d_kv = jnp.concatenate([d_k, d_value.reshape(tokens, UNIT)], axis=1).astype(bf16)
    d_h_pick = dot(d_q, w_q, 1, 1)
    high = d_h_pick.astype(bf16)
    rest = (d_h_pick - high.astype(f32)).astype(bf16)
    d_h_attn = dot(d_kv, w_kv, 1, 1) + dot(pick, high, 0, 0) + dot(pick, rest, 0, 0)
    d_x_attn, grad_attn = norm_back(x_embed, gains[0], d_h_attn)
    high = d_x_one.astype(bf16)
    rest = (d_x_one - high.astype(f32)).astype(bf16)
    d_x_embed = d_x_attn + dot(pick, high, 0, 0) + dot(pick, rest, 0, 0)

    scaled = (d_x_embed * emb_mult).astype(bf16)
    sending = [
        dot(spot_between(low, high), scaled, 0, 0).astype(bf16).reshape(devices, high - low, D)
        for low, high in zip(cuts_back, cuts_back[1:])
    ]
    if aligned:
        blocks = jnp.concatenate([jnp.zeros((1, 480, 640), bf16), grad_gu.reshape(2, 480, 640), down_pack(grad_down)[None]])
        share = lax.psum_scatter(blocks, "q", scatter_dimension=0, tiled=False)
        sending, d_q, d_kv, attended = lax.optimization_barrier((sending, d_q, d_kv, attended))
        share, d_q, d_kv, attended = lax.optimization_barrier((share, d_q, d_kv, attended))
    arrived = [exchange(blocks) for blocks in sending]
    grad_out = dot(attended, d_branch, 0, 0).astype(bf16)
    grad_q = dot(h_pick, d_q, 0, 0).astype(bf16)
    grad_kv = dot(h_attn, d_kv, 0, 0).astype(bf16)

    def norm_of(squares):
        sums = jnp.broadcast_to(jnp.stack([squares, my_loss])[None], (devices, 2))
        sums = jnp.sum(lax.all_to_all(sums, ALL, split_axis=0, concat_axis=0, tiled=True), axis=0)
        grad_norm = jnp.sqrt(sums[0])
        limit = CLIP_C / math.sqrt(loss_total)
        return sums[1] / loss_total, grad_norm, limit / jnp.maximum(grad_norm, limit)

    gain_grads = jnp.concatenate([grad_attn, grad_mlp, grad_final]).astype(bf16)
    if aligned:
        lower = jnp.concatenate([grad_q.reshape(5, TOP, D), grad_kv.reshape(5, SHARE - TOP, D)], axis=1)
        level = jnp.concatenate([lower, grad_out.reshape(3, SHARE, D)])
        room = jnp.zeros((8, ROOM, D), bf16).at[0, :3].set(gain_grads.reshape(3, D))
        level = jnp.concatenate([level, room], axis=1).reshape(4, 2, SHARE + ROOM, D)
        level, arrived[0] = lax.optimization_barrier((level, arrived[0]))
        keep = lax.dynamic_index_in_dim(level, c_index, 1, False)
        give = lax.dynamic_index_in_dim(level, 1 - c_index, 1, False)
        cores = [rows.reshape(2, 2, SHARE + ROOM, D) for rows in (keep, flip(give, "c", 1, 2))]
        middle = (SHARE + ROOM) // 2
        x_index, y_index = lax.axis_index("x"), lax.axis_index("y")

        def upper(index):
            return sum(pick_block(rows[:, :, :middle], index, 1).astype(f32) for rows in cores)

        def under(index):
            return sum(pick_block(rows[:, :, middle:], index, 0).astype(f32) for rows in cores)

        left = upper(x_index) + flip(upper(1 - x_index).astype(bf16), "x", 1, 2).astype(f32)
        right = under(y_index) + flip(under(1 - y_index).astype(bf16), "y", 1, 2).astype(f32)
        left = pick_block(left, y_index) + flip(pick_block(left, 1 - y_index).astype(bf16), "y", 1, 2).astype(f32)
        right = pick_block(right, x_index) + flip(pick_block(right, 1 - x_index).astype(bf16), "x", 1, 2).astype(f32)
        own = jnp.concatenate([left, right])
        own = own.reshape(4, (SHARE + ROOM) // 4, D)
        own, share, arrived[1] = lax.optimization_barrier((own, share, arrived[1]))
        got = lax.all_to_all(share.reshape(8, 60, 640), PLANE, split_axis=0, concat_axis=0, tiled=True)
        quarter = lax.dynamic_index_in_dim(own, q_index, 0, False)
        for k in (1, 2, 3):
            piece = lax.dynamic_index_in_dim(own, q_index ^ k, 0, False).astype(bf16)
            quarter = quarter + flip(piece, "q", k, 4).astype(f32)
        table_grad = head_grad
        for low, high, rows in zip(cuts_back, cuts_back[1:], arrived):
            table_grad = table_grad + dot(rows_between(low, high), rows, 0, 0)
        table_squares = jnp.sum(table_grad * table_grad)
        quarter = quarter.astype(bf16)
        squares = jnp.sum(quarter.astype(f32) ** 2) + jnp.sum(share.astype(f32) ** 2) + table_squares
        quarter, squares, got = lax.optimization_barrier((quarter, squares, got))
        quarters = [quarter] + [lax.ppermute(quarter, "q", [(k, 0)]) for k in (1, 2, 3)]
        loss, grad_norm, clip_factor = norm_of(squares)
        table_new = adamw_step(table_master, table_grad, table_m, table_v, clip_factor)
        quarters, table_new = lax.optimization_barrier((quarters, table_new))
        first = jnp.concatenate(quarters)
        gain_out = first[SHARE : SHARE + 3].reshape(-1)
        both = jnp.concatenate([first[:TOP], first[TOP:SHARE].reshape(TOP, KV)], axis=1)
        first = jnp.where(p_index < 5, both.reshape(-1), first[:SHARE].reshape(-1))
        by_share = got.reshape(8, 60, 2, UNIT).transpose(1, 2, 0, 3).reshape(-1)
        mine = jnp.where(q_index == 3, down_unpack(share).reshape(-1), by_share)
        mine = jnp.where(q_index == 0, first, mine)
    else:
        table_grad = head_grad
        for low, high, rows in zip(cuts_back, cuts_back[1:], arrived):
            table_grad = table_grad + dot(rows_between(low, high), rows, 0, 0)
        table_squares = jnp.sum(table_grad * table_grad)
        both = lax.dynamic_update_index_in_dim(jnp.zeros((D, 2, 8, UNIT), bf16), grad_gu.reshape(D, 2, UNIT), p_index, 2)
        downs = lax.dynamic_update_index_in_dim(jnp.zeros((8, SHARE, D), bf16), grad_down, p_index, 0)
        full = jnp.concatenate([part.reshape(-1, UNIT) for part in (jnp.concatenate([grad_q, grad_kv], axis=1), grad_out, both, downs)]).reshape(devices, units, UNIT)
        room = jnp.zeros((devices, 16, UNIT), bf16).at[0, :GAIN_UNITS].set(gain_grads.reshape(GAIN_UNITS, UNIT))
        full = jnp.concatenate([full, room], axis=1)
        summed = lax.psum_scatter(full, ALL, scatter_dimension=0, tiled=False)
        mine, gain_out = summed[:units].reshape(-1), summed[units : units + GAIN_UNITS].reshape(-1)
    behind = lax.ppermute(mine[span - GAINS :], ALL, [(i, i + 1) for i in range(devices - 1)])
    behind = jnp.where(me == 0, gain_out, behind)
    tail = max(0, drift * (devices - 1) + shard - GAINS - span)
    stream = jnp.concatenate([behind, mine, jnp.zeros((tail,), bf16)])
    layer_grad = lax.dynamic_slice(stream, (drift * me,), (shard,)).astype(f32)

    if not aligned:
        loss, grad_norm, clip_factor = norm_of(jnp.sum(layer_grad * layer_grad) + table_squares)
        table_new = adamw_step(table_master, table_grad, table_m, table_v, clip_factor)
    flat_new = adamw_step(flat_master, layer_grad, flat_m, flat_v, clip_factor)
    return (loss, grad_norm) + flat_new + table_new


def solution(mesh):
    count = mesh.devices.size
    grid = Mesh(mesh.devices.reshape(count // 8, 2, 2, 2), ALL)
    rows, matrix = P(ALL), P(ALL, None)
    in_specs = (rows,) * 6 + (matrix,) * 3
    out_specs = (P(), P()) + (rows,) * 3 + (matrix,) * 3
    return jax.shard_map(local, mesh=grid, in_specs=in_specs, out_specs=out_specs, check_vma=False)
```

```python
import math

import jax
import jax.numpy as jnp
import numpy as np
from jax import lax
from jax.sharding import Mesh, PartitionSpec as P

D = 960
QUERY_HEADS = 15
KEY_VALUE_HEADS = 5
HEAD_SIZE = 64
FF = 2560
V = 32000
PL = 256
CL = 128
STEP = 10
QKV = 1600

EPS = 1e-05
SMOOTH = 0.1
ZCOEF = 0.0001
BETA1 = 0.9
BETA2 = 0.95
ADAM_EPS = 1e-08
DECAY = 0.1
RATE = 0.03
CLIP_C = 25.0
NEGATIVE = -1e30

UNIT = 320
GAINS = 3 * D
GAIN_UNITS = GAINS // UNIT
QKV_UNITS = D * QKV // UNIT
OUT_UNITS = D * D // UNIT
GU_UNITS = D * 2 * FF // UNIT
DOWN_UNITS = FF * D // UNIT
ALL_UNITS = QKV_UNITS + OUT_UNITS + GU_UNITS + DOWN_UNITS
PLANE = ("y", "x", "c")
ALL = ("q", "y", "x", "c")
SHARE = FF // 8
TOP = D // 5
KV = QKV - D
ROOM = 32
WIDE = 1024

bf16 = jnp.bfloat16
f32 = jnp.float32


def dot(left, right, left_dim=1, right_dim=0):
    return lax.dot_general(
        left, right, (((left_dim,), (right_dim,)), ((), ())), preferred_element_type=f32
    )


def hot(index, count):
    return (index[:, None] == jnp.arange(count, dtype=jnp.int32)[None, :]).astype(bf16)


def scale_of(rows):
    return lax.rsqrt(jnp.mean(rows * rows, axis=-1, keepdims=True) + EPS)


def norm_back(rows, gain, grad):
    scale = scale_of(rows)
    normed = rows * scale
    grad_gain = jnp.sum(grad * normed, axis=0)
    scaled = grad * gain
    return scale * (scaled - normed * jnp.mean(scaled * normed, axis=-1, keepdims=True)), grad_gain


def flip(rows, axes, bits, size):
    return lax.ppermute(rows, axes, [(i, i ^ bits) for i in range(size)])


def rope_tables(count):
    row = np.arange(count)
    position = np.where(row < PL, row, PL + (row - PL) % CL).astype(np.float32)
    half = np.arange(HEAD_SIZE // 2, dtype=np.float32)
    freqs = np.float32(10000.0) ** (-(half * np.float32(2.0) / np.float32(HEAD_SIZE)))
    angles = (position[:, None] * freqs[None, :].astype(np.float32)).astype(np.float64)
    angles = np.concatenate([angles, angles], axis=-1)
    return np.cos(angles).astype(np.float32), np.sin(angles).astype(np.float32)


def rotate(rows, cosine, sine):
    heads = rows.reshape(rows.shape[0], -1, HEAD_SIZE)
    half = HEAD_SIZE // 2
    turned = jnp.concatenate([-heads[..., half:], heads[..., :half]], axis=-1)
    return (heads * cosine[:, None, :] + turned * sine[:, None, :]).reshape(rows.shape)


def rotate_back(grad, cosine, sine):
    heads = grad.reshape(grad.shape[0], -1, HEAD_SIZE)
    half = HEAD_SIZE // 2
    spun = heads * sine[:, None, :]
    turned = jnp.concatenate([spun[..., half:], -spun[..., :half]], axis=-1)
    return (heads * cosine[:, None, :] + turned).reshape(grad.shape)


def adamw_step(param, gradient, moment_one, moment_two, clip_factor):
    gradient = gradient * clip_factor
    new_one = BETA1 * moment_one + (1.0 - BETA1) * gradient
    new_two = BETA2 * moment_two + (1.0 - BETA2) * gradient * gradient
    ratio = new_one / (1.0 - BETA1**STEP) / (jnp.sqrt(new_two / (1.0 - BETA2**STEP)) + ADAM_EPS)
    return (new_one, new_two, -RATE * (ratio + DECAY * param))


def merge_stats(one, two):
    peak = jnp.maximum(one[0], two[0])
    total = one[1] * jnp.exp(one[0] - peak) + two[1] * jnp.exp(two[0] - peak)
    return jnp.stack([peak, total, one[2] + two[2], one[3] + two[3]])


def pick_block(blocks, index, axis=0):
    return lax.dynamic_index_in_dim(blocks, index, axis, False)


def widen(rows):
    return jnp.pad(rows, ((0, 0), (0, WIDE - D)))


def fold_plane(left, right, right_dim):
    c_index, yx_index = lax.axis_index("c"), lax.axis_index(("y", "x"))
    rows = left.reshape(4, 2, left.shape[0] // 8, left.shape[1])
    far = pick_block(rows, 1 - c_index, 1).reshape(-1, left.shape[1])
    near = pick_block(rows, c_index, 1).reshape(-1, left.shape[1])
    got = flip(dot(far, right, 1, right_dim).astype(bf16), "c", 1, 2)
    mine = (dot(near, right, 1, right_dim) + got.astype(f32)).reshape(4, -1, WIDE)
    low = mine.astype(bf16)
    total = pick_block(mine, yx_index)
    for k in (1, 2, 3):
        total = total + flip(pick_block(low, yx_index ^ k), ("y", "x"), k, 4).astype(f32)
    return total[:, :D]


def down_pack(rows):
    side = jnp.concatenate([rows[: SHARE // 2, 640:], rows[SHARE // 2 :, 640:]], axis=1)
    return jnp.concatenate([rows[:, :640], side])


def down_unpack(rows):
    side = jnp.concatenate([rows[SHARE:, :UNIT], rows[SHARE:, UNIT:]])
    return jnp.concatenate([rows[:SHARE], side], axis=1)


def spread_plane(rows):
    return widen(lax.all_gather(rows, PLANE).reshape(-1, D))


def local(
    token_ids, loss_rows, targets, flat_master, flat_m, flat_v, table_master, table_m, table_v
):
    devices = lax.axis_size(ALL)
    rows_q = lax.axis_size("q")
    me = lax.axis_index(ALL)
    q_index = lax.axis_index("q")
    p_index = lax.axis_index(PLANE)
    c_index = lax.axis_index("c")
    yx_index = lax.axis_index(("y", "x"))
    tokens = token_ids.shape[0]
    vocab_dev = table_master.shape[0]
    loss_dev = loss_rows.shape[0]
    loss_total = loss_dev * devices
    capacity = max(2, 2 * tokens // devices)
    slots = devices * capacity
    groups = QUERY_HEADS // KEY_VALUE_HEADS
    emb_mult = math.sqrt(D) * 0.5
    shard = flat_master.shape[0]
    units = ALL_UNITS // devices
    span = units * UNIT
    drift = shard - span
    aligned = devices == 32

    place = np.array([q * 8 + kyx * 2 + kc for kc in range(2) for kyx in range(4) for q in range(rows_q)])
    source_of = p_index ^ jnp.asarray(place, jnp.int32)

    table_low = table_master.astype(bf16)
    owner = token_ids // vocab_dev
    owner_hot = hot(owner, devices)
    before = (lax.broadcasted_iota(jnp.int32, (tokens, tokens), 0) > lax.broadcasted_iota(jnp.int32, (tokens, tokens), 1)).astype(bf16)
    slot = jnp.sum(dot(before, owner_hot) * owner_hot.astype(f32), axis=1).astype(jnp.int32)
    spot = hot(owner * capacity + slot, slots)

    def spot_between(low, high):
        inside = (slot >= low) & (slot < high)
        return hot(jnp.where(inside, owner * (high - low) + slot - low, -1), devices * (high - low))

    def rows_between(low, high):
        return hot(asked[:, low:high].reshape(-1) - me * vocab_dev, vocab_dev)

    def exchange(blocks):
        return lax.all_to_all(blocks, ALL, split_axis=0, concat_axis=0, tiled=True).reshape(-1, D)

    cuts_back = (0, capacity // 4, capacity)
    marked = token_ids + 1
    halves = jnp.stack([marked // 256, marked % 256]).astype(bf16)
    found = dot(halves, spot).astype(jnp.int32)
    requests = (found[0] * 256 + found[1] - 1).reshape(devices, capacity)
    ask = jnp.concatenate([requests, jnp.broadcast_to(targets[None], (devices, loss_dev))], axis=1)

    flat_low = flat_master.astype(bf16)
    ahead = lax.ppermute(flat_low[:GAINS], ALL, [(i + 1, i) for i in range(devices - 1)])
    back = max(0, drift * (devices - 1) - GAINS)
    pieces = [flat_low, ahead]
    if back:
        pieces = [lax.ppermute(flat_low[shard - back :], ALL, [(i, i + 1) for i in range(devices - 1)])] + pieces
    chunk = lax.dynamic_slice(jnp.concatenate(pieces), (back + GAINS - drift * me,), (span,))
    if aligned:
        sent = chunk.reshape(60, 2, 8, UNIT).transpose(2, 0, 1, 3).reshape(8, 60, 2 * UNIT)
        got = lax.all_to_all(sent, PLANE, split_axis=0, concat_axis=0, tiled=True)
        both = chunk.reshape(TOP, QKV)
        both = jnp.concatenate([both[:, :D], both[:, D:].reshape(SHARE - TOP, D)])
        first = jnp.where(p_index < 5, both, chunk.reshape(SHARE, D))
        first = jnp.concatenate([first, flat_low[:GAINS].reshape(3, D), jnp.zeros((5, D), bf16)])
        first, ask = lax.optimization_barrier((first, ask))
        asked = lax.all_to_all(ask, ALL, split_axis=0, concat_axis=0, tiled=True)
        answer = dot(rows_between(0, capacity), table_low).astype(bf16).reshape(devices, capacity, D)
        jumped = lax.ppermute(first, "q", [(0, 2)])
        first = jnp.where(q_index == 2, jumped, first)
        stepped = lax.ppermute(first, "q", [(0, 1), (2, 3)])
        first = jnp.where((q_index == 1) | (q_index == 3), stepped, first)
        answer, first, got = lax.optimization_barrier((answer, first, got))
        returned = exchange(answer)
        level = lax.all_gather(first, PLANE)
        mixed = jnp.where(q_index == 3, down_pack(chunk.reshape(SHARE, D)), got.reshape(480, 2 * UNIT))
        mixed, level = lax.optimization_barrier((mixed, level))
        gains = level[0, SHARE : SHARE + 3].astype(f32)
        w_q = level[:5, :TOP].reshape(D, D)
        w_kv = level[:5, TOP:SHARE].reshape(D, KV)
        w_out = level[5:, :SHARE].reshape(D, D)
        returned, w_q, w_kv, w_out = lax.optimization_barrier((returned, w_q, w_kv, w_out))
        column = lax.all_gather(mixed, "q")
    else:
        asked = lax.all_to_all(ask, ALL, split_axis=0, concat_axis=0, tiled=True)
        answer = dot(rows_between(0, capacity), table_low).astype(bf16).reshape(devices, capacity, D)
        returned = exchange(answer)
        extra = jnp.zeros((16 * UNIT,), bf16).at[:GAINS].set(flat_low[:GAINS])
        full = lax.all_gather(jnp.concatenate([chunk, extra]).reshape(units + 16, UNIT), ALL)
        gains = full[0, units : units + GAIN_UNITS].astype(f32).reshape(3, D)
        full = full[:, :units].reshape(ALL_UNITS, UNIT)
        edge = np.cumsum([QKV_UNITS, OUT_UNITS, GU_UNITS])
        w_qkv = full[: edge[0]].reshape(D, QKV)
        w_q, w_kv = w_qkv[:, :D], w_qkv[:, D:]
        w_out = full[edge[0] : edge[1]].reshape(D, D)
        both = lax.dynamic_index_in_dim(full[edge[1] : edge[2]].reshape(D, 2, 8, UNIT), p_index, 2, False)
        w_gu = both.reshape(D, 2 * SHARE)
        w_down = lax.dynamic_index_in_dim(full[edge[2] :].reshape(8, SHARE, D), p_index, 0, False)
    x_low = dot(spot, returned).astype(bf16)
    x_embed = x_low.astype(f32) * emb_mult

    pick = hot(loss_rows, tokens)
    cosine, sine = (jnp.asarray(t) for t in rope_tables(tokens))
    cosine_pick, sine_pick = cosine[loss_rows], sine[loss_rows]
    h_attn = (x_embed * scale_of(x_embed) * gains[0]).astype(bf16)
    h_pick = dot(pick, h_attn).astype(bf16)
    x_pick = dot(pick, x_low) * emb_mult
    query = rotate(dot(h_pick, w_q), cosine_pick, sine_pick).astype(bf16)
    key_value = dot(h_attn, w_kv)
    key = rotate(key_value[:, :UNIT], cosine, sine).astype(bf16)
    value = key_value[:, UNIT:].astype(bf16)

    def heads_of(rows):
        return rows.reshape(loss_dev, KEY_VALUE_HEADS, groups, HEAD_SIZE).transpose(1, 2, 0, 3).reshape(KEY_VALUE_HEADS, groups * loss_dev, HEAD_SIZE)

    def heads_back(rows):
        return rows.reshape(KEY_VALUE_HEADS, groups, loss_dev, HEAD_SIZE).transpose(2, 0, 1, 3).reshape(loss_dev, D)

    query_h = heads_of(query)
    key_h = key.reshape(tokens, KEY_VALUE_HEADS, HEAD_SIZE).transpose(1, 0, 2)
    value_h = value.reshape(tokens, KEY_VALUE_HEADS, HEAD_SIZE).transpose(1, 0, 2)
    key_pos = jnp.arange(tokens, dtype=jnp.int32)[None, :]
    ask_pos = jnp.tile(loss_rows, groups)[:, None]
    key_seg = jnp.where(key_pos < PL, 0, 1 + (key_pos - PL) // CL)
    ask_seg = jnp.where(ask_pos < PL, 0, 1 + (ask_pos - PL) // CL)
    allowed = (key_pos <= ask_pos) & ((key_seg == 0) | (key_seg == ask_seg))
    scores = jnp.einsum("hqd,hkd->hqk", query_h, key_h, preferred_element_type=f32) * HEAD_SIZE**-0.5
    scores = jnp.where(allowed[None], scores, NEGATIVE)
    exp_scores = jnp.exp(scores - jnp.max(scores, axis=-1, keepdims=True))
    probs = exp_scores / jnp.sum(exp_scores, axis=-1, keepdims=True)
    probs_low = probs.astype(bf16)
    mixed_heads = jnp.einsum("hqk,hkd->hqd", probs_low, value_h, preferred_element_type=f32)
    attended = heads_back(mixed_heads.astype(bf16))
    x_one = x_pick + dot(attended, w_out)

    h_mlp = (x_one * scale_of(x_one) * gains[1]).astype(bf16)
    h_all = spread_plane(h_mlp)
    if aligned:
        column, h_all = lax.optimization_barrier((column, h_all))
        w_gu = column[1:3].reshape(D, 2 * SHARE)
        w_down = down_unpack(column[3])
    w_gu = jnp.pad(w_gu, ((0, WIDE - D), (0, 0)))
    w_down = widen(w_down)
    gate_up = dot(h_all, w_gu)
    gate, up = gate_up[:, :SHARE], gate_up[:, SHARE:]
    sig = jax.nn.sigmoid(gate)
    act = (gate * sig * up).astype(bf16)
    x_two = x_one + fold_plane(act, w_down, 0)

    hidden = (x_two * scale_of(x_two) * gains[2]).astype(bf16)
    wide_table = widen(table_low)
    across = lax.all_gather(widen(hidden), "q")
    by_x, by_y = flip(across, "x", 1, 2), flip(across, "y", 1, 2)
    cut = rows_q // 2
    corner = [flip(by_x[:cut], "y", 1, 2), flip(by_y[cut:], "x", 1, 2)]
    near = jnp.concatenate([across, by_x, by_y] + corner).reshape(loss_total // 2, WIDE)
    sides = [near, flip(near, "c", 1, 2)]
    targets_all = jnp.take(asked[:, capacity:], source_of, axis=0).reshape(2, loss_total // 2)
    logits, hits, stats = [], [], []
    for side, rows in enumerate(sides):
        z = dot(rows, wide_table, 1, 1)
        column_id = targets_all[side] - me * vocab_dev
        hit = column_id[:, None] == jnp.arange(vocab_dev, dtype=jnp.int32)[None, :]
        local_peak = jnp.max(z, axis=1)
        local_total = jnp.sum(jnp.exp(z - local_peak[:, None]), axis=1)
        local_target = jnp.sum(jnp.where(hit, z, 0.0), axis=1)
        local_sum = jnp.sum(z, axis=1)
        logits.append(z)
        hits.append(hit)
        stats.append(jnp.stack([local_peak, local_total, local_target, local_sum]))
    stats = jnp.concatenate(stats, axis=1)
    block = rows_q * loss_dev
    for axis, bit in (("c", 4), ("x", 1), ("y", 2)):
        other = flip(stats, axis, 1, 2)
        other = jnp.concatenate([other[:, (k ^ bit) * block : ((k ^ bit) + 1) * block] for k in range(8)], axis=1)
        stats = merge_stats(stats, other)
    bit = 1
    while bit < rows_q:
        stats = merge_stats(stats, flip(stats, "q", bit, rows_q))
        bit *= 2
    log_total = stats[0] + jnp.log(stats[1])
    mine_at = q_index * loss_dev
    my_log, my_target, my_sum = (lax.dynamic_slice(row, (mine_at,), (loss_dev,)) for row in (log_total, stats[2], stats[3]))
    my_loss = jnp.sum(my_log - (1.0 - SMOOTH) * my_target - SMOOTH / V * my_sum + ZCOEF * my_log * my_log)
    log_total = log_total.reshape(2, loss_total // 2, 1)
    d_logits = [
        (
            (
                (1.0 + 2.0 * ZCOEF * log_total[side]) * jnp.exp(logits[side] - log_total[side])
                - jnp.where(hits[side], 1.0 - SMOOTH, 0.0)
                - SMOOTH / V
            )
            / loss_total
        ).astype(bf16)
        for side in (1, 0)
    ]
    got = flip(dot(d_logits[0], wide_table).astype(bf16), "c", 1, 2)
    d_hidden = (dot(d_logits[1], wide_table) + got.astype(f32)).reshape(4, rows_q, loss_dev, WIDE)
    d_low = d_hidden.astype(bf16)
    d_hidden = d_hidden[0]
    for k in (1, 2, 3):
        d_hidden = d_hidden + flip(d_low[k], ("y", "x"), k, 4).astype(f32)
    d_low = d_hidden.astype(bf16)
    total_hidden = pick_block(d_hidden, q_index)
    for k in range(1, rows_q):
        total_hidden = total_hidden + flip(pick_block(d_low, q_index ^ k), "q", k, rows_q).astype(f32)
    total_hidden = total_hidden[:, :D]
    head_grad = (dot(d_logits[1], sides[0], 0, 0) + dot(d_logits[0], sides[1], 0, 0))[:, :D]
    head_grad, total_hidden = lax.optimization_barrier((head_grad, total_hidden))

    d_x_two, grad_final = norm_back(x_two, gains[2], total_hidden)
    d_down = spread_plane(d_x_two.astype(bf16))
    d_act = dot(d_down, w_down, 1, 1)
    d_gate = d_act * up * sig * (1.0 + gate * (1.0 - sig))
    d_gu = jnp.concatenate([d_gate, d_act * gate * sig], axis=1).astype(bf16)
    d_h_mlp = fold_plane(d_gu, w_gu, 1)
    grad_down = dot(act, d_down, 0, 0)[:, :D].astype(bf16)
    grad_gu = dot(h_all, d_gu, 0, 0)[:D].astype(bf16)
    d_x_mlp, grad_mlp = norm_back(x_one, gains[1], d_h_mlp)
    d_x_one = d_x_two + d_x_mlp

    d_branch = d_x_one.astype(bf16)
    d_attended = dot(d_branch, w_out, 1, 1)
    d_mixed = heads_of(d_attended.astype(bf16))
    d_probs = jnp.einsum("hqd,hkd->hqk", d_mixed, value_h, preferred_element_type=f32)
    delta = jnp.sum(probs * d_probs, axis=-1, keepdims=True)
    d_scores = (probs * (d_probs - delta)).astype(bf16)
    d_query = jnp.einsum("hqk,hkd->hqd", d_scores, key_h, preferred_element_type=f32) * HEAD_SIZE**-0.5
    d_key = jnp.einsum("hqk,hqd->khd", d_scores, query_h, preferred_element_type=f32) * HEAD_SIZE**-0.5
    d_value = jnp.einsum("hqk,hqd->khd", probs_low, d_mixed, preferred_element_type=f32)
    d_q = rotate_back(heads_back(d_query), cosine_pick, sine_pick).astype(bf16)
    d_k = rotate_back(d_key.reshape(tokens, UNIT), cosine, sine)
    d_kv = jnp.concatenate([d_k, d_value.reshape(tokens, UNIT)], axis=1).astype(bf16)
    d_h_pick = dot(d_q, w_q, 1, 1)
    high = d_h_pick.astype(bf16)
    rest = (d_h_pick - high.astype(f32)).astype(bf16)
    d_h_attn = dot(d_kv, w_kv, 1, 1) + dot(pick, high, 0, 0) + dot(pick, rest, 0, 0)
    d_x_attn, grad_attn = norm_back(x_embed, gains[0], d_h_attn)
    high = d_x_one.astype(bf16)
    rest = (d_x_one - high.astype(f32)).astype(bf16)
    d_x_embed = d_x_attn + dot(pick, high, 0, 0) + dot(pick, rest, 0, 0)

    scaled = (d_x_embed * emb_mult).astype(bf16)
    sending = [
        dot(spot_between(low, high), scaled, 0, 0).astype(bf16).reshape(devices, high - low, D)
        for low, high in zip(cuts_back, cuts_back[1:])
    ]
    if aligned:
        blocks = jnp.concatenate([jnp.zeros((1, 480, 640), bf16), grad_gu.reshape(2, 480, 640), down_pack(grad_down)[None]])
        share = lax.psum_scatter(blocks, "q", scatter_dimension=0, tiled=False)
        sending, d_q, d_kv, attended = lax.optimization_barrier((sending, d_q, d_kv, attended))
        share, d_q, d_kv, attended = lax.optimization_barrier((share, d_q, d_kv, attended))
    arrived = [exchange(blocks) for blocks in sending]
    grad_out = dot(attended, d_branch, 0, 0).astype(bf16)
    grad_q = dot(h_pick, d_q, 0, 0).astype(bf16)
    grad_kv = dot(h_attn, d_kv, 0, 0).astype(bf16)

    def begun(squares):
        sums = jnp.stack([squares, my_loss])
        for axis in ("c", "x"):
            sums = sums + flip(sums, axis, 1, 2)
        return sums

    def norm_of(sums):
        for axis, bit, size in [("y", 1, 2)] + [("q", 1 << k, rows_q) for k in range(rows_q.bit_length() - 1)]:
            sums = sums + flip(sums, axis, bit, size)
        grad_norm = jnp.sqrt(sums[0])
        limit = CLIP_C / math.sqrt(loss_total)
        return sums[1] / loss_total, grad_norm, limit / jnp.maximum(grad_norm, limit)

    gain_grads = jnp.concatenate([grad_attn, grad_mlp, grad_final]).astype(bf16)
    if aligned:
        lower = jnp.concatenate([grad_q.reshape(5, TOP, D), grad_kv.reshape(5, SHARE - TOP, D)], axis=1)
        level = jnp.concatenate([lower, grad_out.reshape(3, SHARE, D)])
        room = jnp.zeros((8, ROOM, D), bf16).at[0, :3].set(gain_grads.reshape(3, D))
        level = jnp.concatenate([level, room], axis=1).reshape(4, 2, SHARE + ROOM, D)
        level, arrived[0] = lax.optimization_barrier((level, arrived[0]))
        keep = lax.dynamic_index_in_dim(level, c_index, 1, False)
        give = lax.dynamic_index_in_dim(level, 1 - c_index, 1, False)
        cores = [rows.reshape(2, 2, SHARE + ROOM, D) for rows in (keep, flip(give, "c", 1, 2))]
        middle = (SHARE + ROOM) // 2
        x_index, y_index = lax.axis_index("x"), lax.axis_index("y")

        def upper(index):
            return sum(pick_block(rows[:, :, :middle], index, 1).astype(f32) for rows in cores)

        def under(index):
            return sum(pick_block(rows[:, :, middle:], index, 0).astype(f32) for rows in cores)

        left = upper(x_index) + flip(upper(1 - x_index).astype(bf16), "x", 1, 2).astype(f32)
        right = under(y_index) + flip(under(1 - y_index).astype(bf16), "y", 1, 2).astype(f32)
        left = pick_block(left, y_index) + flip(pick_block(left, 1 - y_index).astype(bf16), "y", 1, 2).astype(f32)
        right = pick_block(right, x_index) + flip(pick_block(right, 1 - x_index).astype(bf16), "x", 1, 2).astype(f32)
        own = jnp.concatenate([left, right])
        own = own.reshape(4, (SHARE + ROOM) // 4, D)
        own, share, arrived[1] = lax.optimization_barrier((own, share, arrived[1]))
        got = lax.all_to_all(share.reshape(8, 60, 640), PLANE, split_axis=0, concat_axis=0, tiled=True)
        quarter = lax.dynamic_index_in_dim(own, q_index, 0, False)
        for k in (1, 2, 3):
            piece = lax.dynamic_index_in_dim(own, q_index ^ k, 0, False).astype(bf16)
            quarter = quarter + flip(piece, "q", k, 4).astype(f32)
        table_grad = head_grad
        for low, high, rows in zip(cuts_back, cuts_back[1:], arrived):
            table_grad = table_grad + dot(rows_between(low, high), rows, 0, 0)
        table_squares = jnp.sum(table_grad * table_grad)
        quarter = quarter.astype(bf16)
        squares = jnp.sum(quarter.astype(f32) ** 2) + jnp.sum(share.astype(f32) ** 2) + table_squares
        quarter, sums = lax.optimization_barrier((quarter, begun(squares)))
        quarters = [quarter] + [lax.ppermute(quarter, "q", [(k, 0)]) for k in (1, 2, 3)]
        first = jnp.concatenate(quarters)
        gain_out = first[SHARE : SHARE + 3].reshape(-1)
        both = jnp.concatenate([first[:TOP], first[TOP:SHARE].reshape(TOP, KV)], axis=1)
        first = jnp.where(p_index < 5, both.reshape(-1), first[:SHARE].reshape(-1))
        by_share = got.reshape(8, 60, 2, UNIT).transpose(1, 2, 0, 3).reshape(-1)
        mine = jnp.where(q_index == 3, down_unpack(share).reshape(-1), by_share)
        mine = jnp.where(q_index == 0, first, mine)
        loss, grad_norm, clip_factor = norm_of(sums)
        mine, clip_factor = lax.optimization_barrier((mine, clip_factor))
    else:
        table_grad = head_grad
        for low, high, rows in zip(cuts_back, cuts_back[1:], arrived):
            table_grad = table_grad + dot(rows_between(low, high), rows, 0, 0)
        table_squares = jnp.sum(table_grad * table_grad)
        both = lax.dynamic_update_index_in_dim(jnp.zeros((D, 2, 8, UNIT), bf16), grad_gu.reshape(D, 2, UNIT), p_index, 2)
        downs = lax.dynamic_update_index_in_dim(jnp.zeros((8, SHARE, D), bf16), grad_down, p_index, 0)
        full = jnp.concatenate([part.reshape(-1, UNIT) for part in (jnp.concatenate([grad_q, grad_kv], axis=1), grad_out, both, downs)]).reshape(devices, units, UNIT)
        room = jnp.zeros((devices, 16, UNIT), bf16).at[0, :GAIN_UNITS].set(gain_grads.reshape(GAIN_UNITS, UNIT))
        full = jnp.concatenate([full, room], axis=1)
        summed = lax.psum_scatter(full, ALL, scatter_dimension=0, tiled=False)
        mine, gain_out = summed[:units].reshape(-1), summed[units : units + GAIN_UNITS].reshape(-1)
    behind = lax.ppermute(mine[span - GAINS :], ALL, [(i, i + 1) for i in range(devices - 1)])
    behind = jnp.where(me == 0, gain_out, behind)
    tail = max(0, drift * (devices - 1) + shard - GAINS - span)
    stream = jnp.concatenate([behind, mine, jnp.zeros((tail,), bf16)])
    layer_grad = lax.dynamic_slice(stream, (drift * me,), (shard,)).astype(f32)

    if not aligned:
        loss, grad_norm, clip_factor = norm_of(begun(jnp.sum(layer_grad * layer_grad) + table_squares))
    flat_new = adamw_step(flat_master, layer_grad, flat_m, flat_v, clip_factor)
    table_new = adamw_step(table_master, table_grad, table_m, table_v, clip_factor)
    return (loss, grad_norm) + flat_new + table_new


def solution(mesh):
    count = mesh.devices.size
    grid = Mesh(mesh.devices.reshape(count // 8, 2, 2, 2), ALL)
    rows, matrix = P(ALL), P(ALL, None)
    in_specs = (rows,) * 6 + (matrix,) * 3
    out_specs = (P(), P()) + (rows,) * 3 + (matrix,) * 3
    return jax.shard_map(local, mesh=grid, in_specs=in_specs, out_specs=out_specs, check_vma=False)
```
